32 devices in a mesh: seq: 4 (over z), fsdp: 8 (over y, x, core).
Axes of the slice: x: 2, y: 2, z: 4, core: 2. Of those that a mesh axis runs over, the one named last changes fastest.
Arguments:
- inputs: bfloat16 [2, 8, 1024, 1536], P(None, 'fsdp', 'seq'), may hold values from -6 to 6
- lengths: int32 [2, 8], P(None, 'fsdp'), may hold values from 256 to 1024, as said below
- expert_ids: int32 [2, 8, 1024, 8], P(None, 'fsdp', 'seq'), may hold values from 0 to 15, all different within a row; in each aligned block of 256 rows (0 to 255, 256 to 511, ..., all dimensions but the last counted through in order) at most 192 rows name the same one
- cotangent: bfloat16 [2, 8, 1024, 1536], P(None, 'fsdp', 'seq'), may hold values from -6 to 6
- gain_attn: bfloat16 [1536], P('fsdp'), may hold values from 0.5 to 1.5
- w_query: bfloat16 [1536, 1536], P('fsdp'), may hold values from -0.15625 to 0.15625
- key_projection: bfloat16 [1536, 512], P('fsdp'), may hold values from -0.15625 to 0.15625
- value_projection: bfloat16 [1536, 512], P('fsdp'), may hold values from -0.15625 to 0.15625
- w_out: bfloat16 [1536, 1536], P('fsdp'), may hold values from -1.75 to 1.75
- gain_moe: bfloat16 [1536], P('fsdp'), may hold values from 0.5 to 1.5
- router: bfloat16 [1536, 16], P('fsdp'), may hold values from -0.078125 to 0.078125
- w_gate: bfloat16 [16, 1536, 512], P('fsdp'), may hold values from -0.15625 to 0.15625
- w_up: bfloat16 [16, 1536, 512], P('fsdp'), may hold values from -0.15625 to 0.15625
- w_down: bfloat16 [16, 512, 1536], P('fsdp'), may hold values from -1.5 to 1.5
Outputs:
- out: bfloat16 [2, 8, 1024, 1536], P(None, 'fsdp', 'seq')
- d_input: bfloat16 [2, 8, 1024, 1536], P(None, 'fsdp', 'seq')
- d_gain_attn: float32 [1536], P('fsdp')
- d_query: float32 [1536, 1536], P('fsdp')
- d_key: float32 [1536, 512], P('fsdp')
- d_value: float32 [1536, 512], P('fsdp')
- d_out: float32 [1536, 1536], P('fsdp')
- d_gain_moe: float32 [1536], P('fsdp')
- d_router: float32 [1536, 16], P('fsdp')
- d_gate: float32 [16, 1536, 512], P('fsdp')
- d_up: float32 [16, 1536, 512], P('fsdp')
- d_down: float32 [16, 512, 1536], P('fsdp')
The draws below stay inside these ranges and needn't reach their ends.
Inputs may be any that keep to these rules, and one draw needn't show every extreme that they name: `lengths`: rows at or after a sequence's length are padding. In every draw some sequence has exactly 1024 valid tokens. `expert_ids`: each token names 8 different experts. Among the rows of one device (aligned blocks of 1024 // 4 positions of one sequence) no expert is named by more than 192 rows, a bound that some block reaches.
All inputs are finite; a program needn't handle non-finite values.
Results may differ from the reference program's by a relative error of at most 0.024.
Values may be sent and summed in bfloat16 or wider, within the bound.
No kernel may reach another device: no remote copies, remote signals or barrier semaphores. Data moves between devices by JAX's collectives and lax.ppermute only.
A program may use at most 320 MiB of HBM per device.

```python
import math
import jax
import jax.numpy as jnp
import numpy as np
from jax import lax

MODEL_DIM = 1536
QUERY_HEAD_COUNT = 24
KEY_HEAD_COUNT = 8
HEAD_SIZE = 64
F = 512
TOPK = 8
E = 16
MB = 2
SEQUENCE_SLOTS = 1024
BATCH = 8
SLOTS = 192
N_SEQ = 4


def draw_lengths(key, part):
    key_one, key_two = jax.random.split(jax.random.fold_in(key, 17))
    values = jax.random.randint(key_one, (MB * BATCH,), SEQUENCE_SLOTS // 4, SEQUENCE_SLOTS + 1)
    place = jax.random.randint(key_two, (), 0, MB * BATCH)
    values = jnp.where(jnp.arange(MB * BATCH) == place, SEQUENCE_SLOTS, values)
    return values.reshape(MB, BATCH).astype(jnp.int32)


def block_scale(own_key, extent, shards, least, largest):
    gain, own = 1.0, jax.random.fold_in(own_key, 6)
    for position, blocks in shards:
        draws = jnp.exp(jax.random.uniform(jax.random.fold_in(own, position), (blocks,), jnp.float32, least / len(shards), largest / len(shards)))
        gain = gain * jnp.repeat(draws, extent[position] // blocks).reshape([-1 if axis == position else 1 for axis in range(len(extent))])
    return gain


def assign_block(rng, own, number, rows, count, top, most, slope):
    sequence = jax.random.permutation(rng, count)
    heavy_load, common = load_shares(count, rows * top, most, slope, True), load_shares(count, rows * top, most, slope, False)
    places = jnp.arange(count)

    def named(sizes, rotation):
        used = int((sizes > 0).sum())
        fixed = max(1, used // 4)
        shifted = fixed + (places - fixed + rotation * (used - fixed)) % max(1, count - fixed)
        return jnp.zeros((count,), jnp.int32).at[sequence[jnp.where(places < fixed, places, shifted)]].set(jnp.asarray(sizes, jnp.int32))

    sizes = jnp.where(number % 4 == 0, named(heavy_load, number // 4), named(common, number - number // 4 - 1))
    mixed = jax.random.permutation(jax.random.fold_in(own, 3), count)
    giver, taker = mixed[0:count // 2 * 2:2], mixed[1:count // 2 * 2:2]
    margin = jnp.minimum(sizes[giver] - 1, most - sizes[taker]) // 2
    margin = jnp.where((giver == sequence[0]) | (taker == sequence[0]) | (sizes[taker] == 0), 0, jnp.maximum(margin, 0))
    shifted = jax.random.randint(jax.random.fold_in(own, 4), (count // 2,), 0, 1 << 20) % (margin + 1)
    sizes = sizes.at[giver].add(-shifted).at[taker].add(shifted)
    items = jnp.searchsorted(jnp.cumsum(sizes), jnp.arange(rows * top), side="right").astype(jnp.int32)
    table = items.reshape(top, rows).T
    table = table[jax.random.permutation(jax.random.fold_in(own, 1), rows)]
    rotation = jax.random.randint(jax.random.fold_in(own, 2), (rows, 1), 0, top)
    return jnp.take_along_axis(table, (jnp.arange(top)[None, :] + rotation) % top, axis=1)


def load_shares(number_of, total, limit, skew, full):
    loads = [(1 << 20) // math.isqrt(rank ** skew) + 1 for rank in range(1, number_of + 1)]
    largest = limit if full else min(limit, max(-(-total // number_of), total * loads[0] // sum(loads)))
    least = 1 if total - largest >= number_of - 1 else 0
    given, surplus = [largest] + [least] * (number_of - 1), total - largest - least * (number_of - 1)
    while surplus > 0:
        free = [i for i in range(1, number_of) if given[i] < largest] or [i for i in range(1, number_of) if given[i] < limit]
        pool, budget = sum([loads[i] for i in free]), surplus
        for i in free:
            extra = min(limit - given[i], max(1, budget * loads[i] // pool), surplus)
            given[i] = given[i] + extra
            surplus = surplus - extra
    return np.array(given)


def normal_values(rng, shape, width, limit, shards=(), held_as=jnp.bfloat16):
    values = jax.random.normal(rng, shape, jnp.float32) * width
    if len(shards) > 0:
        values = block_scale(rng, shape, shards, -0.22, 0.18) * values
    return jnp.clip(values, min=-limit, max=limit).astype(held_as)


def setup_inputs(seed: int = 0) -> dict:
    key_of = jax.random.split(jax.random.key(seed), 15)
    inputs = normal_values(key_of[0], (MB, BATCH, SEQUENCE_SLOTS, MODEL_DIM), 1.0, 6.0, ((1, 8), (2, 4)))
    lengths = draw_lengths(jax.random.fold_in(key_of[14], 71), 0)
    expert_ids_keys = jax.random.split(jax.random.fold_in(key_of[2], 1), MB * BATCH * SEQUENCE_SLOTS // (SEQUENCE_SLOTS // N_SEQ))
    expert_ids_turns = jax.random.permutation(jax.random.fold_in(key_of[2], 3), MB * BATCH * SEQUENCE_SLOTS // (SEQUENCE_SLOTS // N_SEQ))
    expert_ids = jax.vmap(lambda own, number: assign_block(jax.random.fold_in(key_of[2], 2), own, number, SEQUENCE_SLOTS // N_SEQ, E, TOPK, SLOTS, 1))(expert_ids_keys, expert_ids_turns).reshape((MB, BATCH, SEQUENCE_SLOTS, TOPK))
    cotangent = normal_values(key_of[3], (MB, BATCH, SEQUENCE_SLOTS, MODEL_DIM), 1.0, 6.0, ((1, 8), (2, 4)))
    gain_attn = jnp.clip(1.0 + 0.1 * jax.random.normal(key_of[4], (MODEL_DIM,), jnp.float32), 0.5, 1.5).astype(jnp.bfloat16)
    w_query = normal_values(key_of[5], (MODEL_DIM, QUERY_HEAD_COUNT * HEAD_SIZE), MODEL_DIM ** -0.5, 0.15625, ((0, 8),))
    key_projection = normal_values(key_of[6], (MODEL_DIM, KEY_HEAD_COUNT * HEAD_SIZE), MODEL_DIM ** -0.5, 0.15625, ((0, 8),))
    value_projection = normal_values(key_of[7], (MODEL_DIM, KEY_HEAD_COUNT * HEAD_SIZE), MODEL_DIM ** -0.5, 0.15625, ((0, 8),))
    w_out = normal_values(key_of[8], (QUERY_HEAD_COUNT * HEAD_SIZE, MODEL_DIM), (max(MODEL_DIM // 128, 4)) ** -0.5, 1.75, ((0, 8),))
    gain_moe = jnp.clip(1.0 + 0.1 * jax.random.normal(key_of[9], (MODEL_DIM,), jnp.float32), 0.5, 1.5).astype(jnp.bfloat16)
    router = normal_values(key_of[10], (MODEL_DIM, E), (4 * MODEL_DIM) ** -0.5, 0.078125, ((0, 8),))
    w_gate = normal_values(key_of[11], (E, MODEL_DIM, F), MODEL_DIM ** -0.5, 0.15625, ((0, 8),))
    w_up = normal_values(key_of[12], (E, MODEL_DIM, F), MODEL_DIM ** -0.5, 0.15625, ((0, 8),))
    w_down = normal_values(key_of[13], (E, F, MODEL_DIM), (max(F // 32, 2)) ** -0.5, 1.5, ((0, 8),))
    return {"inputs": inputs, "lengths": lengths, "expert_ids": expert_ids, "cotangent": cotangent, "gain_attn": gain_attn, "w_query": w_query, "key_projection": key_projection, "value_projection": value_projection, "w_out": w_out, "gain_moe": gain_moe, "router": router, "w_gate": w_gate, "w_up": w_up, "w_down": w_down}


EPS = 1e-06
THETA = 10000.0
NEGATIVE = -1e+30
HIGHEST = lax.Precision.HIGHEST

@jax.custom_vjp
def low(v):
    return lax.optimization_barrier(v.astype(jnp.bfloat16)).astype(jnp.float32)

@jax.custom_vjp
def low_back(v):
    return v

def low_keep(v):
    return (low(v), None)

def low_pass(kept, grad):
    return (grad,)

def back_keep(v):
    return (v, None)

def back_low(kept, grad):
    return (low(grad),)
low.defvjp(low_keep, low_pass)
low_back.defvjp(back_keep, back_low)

def matrix_product(left_side, right_side):
    return jnp.dot(left_side, right_side, precision=HIGHEST, preferred_element_type=jnp.float32)

def rope_tables(positions):
    half_dim = HEAD_SIZE // 2
    frequency = THETA ** (-(jnp.arange(half_dim, dtype=jnp.float32) * 2.0) / HEAD_SIZE)
    angles = positions.astype(jnp.float32)[:, None] * frequency[None, :]
    return (jnp.cos(angles)[:, None, :], jnp.sin(angles)[:, None, :])

def apply_rotary(values, cosine_table, sine_table):
    half_dim = values.shape[-1] // 2
    first_half = values[..., :half_dim]
    second_half = values[..., half_dim:]
    return jnp.concatenate([first_half * cosine_table - second_half * sine_table, second_half * cosine_table + first_half * sine_table], axis=-1)

def attend(query_row_data, key_row_data, value_row_data, seq_length):
    rows_per_block = min(512, SEQUENCE_SLOTS)
    number_of_blocks = SEQUENCE_SLOTS // rows_per_block
    query_group_width = QUERY_HEAD_COUNT // KEY_HEAD_COUNT
    score_scale = HEAD_SIZE ** (-0.5)
    query_block_list = query_row_data.reshape(number_of_blocks, rows_per_block, KEY_HEAD_COUNT, query_group_width, HEAD_SIZE)
    per_head_keys = key_row_data.reshape(SEQUENCE_SLOTS, KEY_HEAD_COUNT, HEAD_SIZE)
    per_head_values = value_row_data.reshape(SEQUENCE_SLOTS, KEY_HEAD_COUNT, HEAD_SIZE)
    key_pos = jnp.arange(SEQUENCE_SLOTS, dtype=jnp.int32)

    def one_block(pieces):
        query_block, first_row = pieces
        raw_scores = jnp.einsum('qkgd,skd->kgqs', query_block, per_head_keys, precision=HIGHEST) * score_scale
        scores = low_back(raw_scores)
        query_pos = first_row + jnp.arange(rows_per_block, dtype=jnp.int32)
        allowed = (key_pos[None, :] <= query_pos[:, None]) & (key_pos[None, :] < seq_length)
        scores = jnp.where(allowed[None, None], scores, NEGATIVE)
        top_score = lax.optimization_barrier(jnp.max(scores, axis=-1, keepdims=True))
        exponent = jnp.exp(scores - top_score)
        attn_probs = low(exponent / lax.optimization_barrier(jnp.sum(exponent, axis=-1, keepdims=True)))
        block_out = jnp.einsum('kgqs,skd->qkgd', attn_probs, per_head_values, precision=HIGHEST)
        return block_out.reshape(rows_per_block, QUERY_HEAD_COUNT * HEAD_SIZE)
    starts = jnp.arange(number_of_blocks, dtype=jnp.int32) * rows_per_block
    outputs = lax.map(jax.checkpoint(one_block), (query_block_list, starts))
    return outputs.reshape(SEQUENCE_SLOTS, QUERY_HEAD_COUNT * HEAD_SIZE)

def seq_forward(weights, seq_in, seq_length, seq_ids):
    gain_first, query_w, key_weight_local, value_w, out_w, gain_second, router_w, gate_w, up_w, down_w = weights
    positions = jnp.arange(SEQUENCE_SLOTS, dtype=jnp.int32)
    valid_rows = positions < seq_length
    cosine_table, sine_table = rope_tables(positions)
    unit_one = seq_in * lax.rsqrt(lax.optimization_barrier(jnp.mean(seq_in * seq_in, axis=-1, keepdims=True)) + EPS)
    first_normed_rows = low(unit_one * gain_first)
    query_row_data = low_back(matrix_product(first_normed_rows, query_w)).reshape(SEQUENCE_SLOTS, QUERY_HEAD_COUNT, HEAD_SIZE)
    query_row_data = low_back(low(apply_rotary(query_row_data, cosine_table, sine_table))).reshape(SEQUENCE_SLOTS, QUERY_HEAD_COUNT * HEAD_SIZE)
    key_row_data = low_back(matrix_product(first_normed_rows, key_weight_local)).reshape(SEQUENCE_SLOTS, KEY_HEAD_COUNT, HEAD_SIZE)
    key_row_data = low_back(low(apply_rotary(key_row_data, cosine_table, sine_table))).reshape(SEQUENCE_SLOTS, KEY_HEAD_COUNT * HEAD_SIZE)
    value_row_data = low_back(low(matrix_product(first_normed_rows, value_w)))
    head_rows = low_back(low(attend(query_row_data, key_row_data, value_row_data, seq_length)))
    residual = seq_in + low_back(matrix_product(head_rows, out_w))
    unit_two = residual * lax.rsqrt(lax.optimization_barrier(jnp.mean(residual * residual, axis=-1, keepdims=True)) + EPS)
    normed_two = low(unit_two * gain_second)
    logits = matrix_product(normed_two, router_w)
    chosen = lax.optimization_barrier(jnp.sum((seq_ids[:, :, None] == jnp.arange(E, dtype=jnp.int32)[None, None, :]).astype(jnp.float32), axis=1))
    top_logit = lax.optimization_barrier(jnp.max(jnp.where(chosen > 0, logits, NEGATIVE), axis=-1, keepdims=True))
    exponent = jnp.exp(logits - top_logit) * chosen
    gates = low(exponent / lax.optimization_barrier(jnp.sum(exponent, axis=-1, keepdims=True)))
    pre_gate = low_back(jnp.einsum('td,edf->etf', normed_two, gate_w, precision=HIGHEST))
    pre_up = low_back(jnp.einsum('td,edf->etf', normed_two, up_w, precision=HIGHEST))
    hidden = low(jax.nn.silu(pre_gate) * pre_up)
    expert_out = low_back(jnp.einsum('etf,efd->etd', hidden, down_w, precision=HIGHEST))
    moe_sum = jnp.einsum('te,etd->td', gates, expert_out, precision=HIGHEST)
    return jnp.where(valid_rows[:, None], residual + moe_sum, 0.0)

def reference(inputs, lengths, expert_ids, cotangent, gain_attn, w_query, key_projection, value_projection, w_out, gain_moe, router, w_gate, w_up, w_down):
    params = tuple((weight_arr.astype(jnp.float32) for weight_arr in (gain_attn, w_query, key_projection, value_projection, w_out, gain_moe, router, w_gate, w_up, w_down)))
    seq_inputs = inputs.astype(jnp.float32).reshape(MB * BATCH, SEQUENCE_SLOTS, MODEL_DIM)
    seq_lengths = lengths.reshape(MB * BATCH).astype(jnp.int32)
    seq_ids = expert_ids.reshape(MB * BATCH, SEQUENCE_SLOTS, TOPK).astype(jnp.int32)

    def forward(weights, seq_data):

        def one_seq(pieces):
            return seq_forward(weights, pieces[0], pieces[1], pieces[2])
        return lax.map(jax.checkpoint(one_seq), (seq_data, seq_lengths, seq_ids))
    result, pullback = jax.vjp(forward, params, seq_inputs)
    grad_params, grad_inputs = pullback(cotangent.astype(jnp.float32).reshape(MB * BATCH, SEQUENCE_SLOTS, MODEL_DIM))
    return (result.reshape(inputs.shape).astype(jnp.bfloat16), grad_inputs.reshape(inputs.shape).astype(jnp.bfloat16), grad_params[0], grad_params[1], grad_params[2], grad_params[3], grad_params[4], grad_params[5], grad_params[6], grad_params[7], grad_params[8], grad_params[9])
```

```python
import functools

import jax
import jax.numpy as jnp
from jax import lax
from jax.experimental import pallas as pl
from jax.experimental.pallas import tpu as pltpu
from jax.sharding import PartitionSpec as P

HEAD = 64
HALF = HEAD // 2
GROUP = 3
TOPK = 8
EPS = 1e-06
THETA = 10000.0
NEGATIVE = -1e30
LANES = 128
SCALE = HEAD ** (-0.5)
BF = jnp.bfloat16
F32 = jnp.float32
VMEM_BYTES = 60 * 1024 * 1024

NN = (((1,), (0,)), ((), ()))
NT = (((1,), (1,)), ((), ()))
TN = (((0,), (0,)), ((), ()))


def dot(a, b, dims=NN):
    return lax.dot_general(a, b, dims, preferred_element_type=F32)


def params():
    return pltpu.CompilerParams(vmem_limit_bytes=VMEM_BYTES)


def cost(flops, moved, trans=0):
    return pl.CostEstimate(flops=int(flops), bytes_accessed=int(moved), transcendentals=int(trans))


def whole(shape):
    zeros = (0,) * len(shape)
    return pl.BlockSpec(shape, lambda *_: zeros)


def smem():
    return pl.BlockSpec(memory_space=pltpu.SMEM)


def rotate(rows, cosine, sine, sign):
    pieces = []
    for h in range(rows.shape[0] // HEAD):
        a = rows[h * HEAD : h * HEAD + HALF]
        b = rows[h * HEAD + HALF : (h + 1) * HEAD]
        if sign > 0:
            pieces += [a * cosine - b * sine, b * cosine + a * sine]
        else:
            pieces += [a * cosine + b * sine, b * cosine - a * sine]
    return jnp.concatenate(pieces, axis=0)


def kv_kernel(x_ref, gain_ref, w_ref, cos_ref, sin_ref, kv_ref, normed_ref):
    step = pl.program_id(0)

    @pl.when(step == 0)
    def _():
        x = x_ref[...].astype(F32)
        inv = lax.rsqrt(jnp.mean(x * x, axis=-1, keepdims=True) + EPS)
        normed_ref[...] = (x * inv * gain_ref[...]).astype(BF)
        r = dot(normed_ref[...], w_ref[...])
        r = rotate(r.T, cos_ref[...], sin_ref[...], 1)
        kv_ref[...] = r.T.astype(BF)

    @pl.when(step == 1)
    def _():
        kv_ref[...] = dot(normed_ref[...], w_ref[...]).astype(BF)


def kv_project(x, gain, w, cosine, sine):
    rows, dim = x.shape
    width = w.shape[1] // 2
    return pl.pallas_call(
        kv_kernel,
        name="kv_project",
        grid=(2,),
        in_specs=[
            whole((rows, dim)),
            whole((1, dim)),
            pl.BlockSpec((dim, width), lambda i: (0, i)),
            whole((HALF, rows)),
            whole((HALF, rows)),
        ],
        out_specs=[pl.BlockSpec((rows, width), lambda i: (0, i)), whole((rows, dim))],
        out_shape=[
            jax.ShapeDtypeStruct((rows, 2 * width), BF),
            jax.ShapeDtypeStruct((rows, dim), BF),
        ],
        compiler_params=params(),
        cost_estimate=cost(2 * rows * dim * 2 * width, 2 * (2 * rows * dim + dim * 2 * width)),
    )(x, gain, w, cosine, sine)


def q_kernel(normed_ref, w_ref, cos_ref, sin_ref, q_ref):
    r = dot(normed_ref[...], w_ref[...])
    r = rotate(r.T, cos_ref[...], sin_ref[...], 1)
    q_ref[...] = r.astype(BF) * BF(SCALE)


def q_project(normed, w, cosine, sine):
    rows, dim = normed.shape
    width = w.shape[1]
    tile = 512
    return pl.pallas_call(
        q_kernel,
        name="q_project",
        grid=(width // tile,),
        in_specs=[
            whole((rows, dim)),
            pl.BlockSpec((dim, tile), lambda i: (0, i)),
            whole((HALF, rows)),
            whole((HALF, rows)),
        ],
        out_specs=pl.BlockSpec((tile, rows), lambda i: (i, 0)),
        out_shape=jax.ShapeDtypeStruct((width, rows), BF),
        compiler_params=params(),
        cost_estimate=cost(2 * rows * dim * width, 2 * (2 * rows * dim + dim * width)),
    )(normed, w, cosine, sine)


def side_by_side(ref, j):
    base = j * GROUP * HEAD
    return jnp.concatenate(
        [ref[base + h * HEAD : base + (h + 1) * HEAD, :] for h in range(GROUP)], axis=1
    )


def diagonal_mask(tokens, own_len):
    key = lax.broadcasted_iota(jnp.int32, (tokens, tokens), 0)
    query = lax.broadcasted_iota(jnp.int32, (tokens, tokens), 1)
    one = (key <= query) & (key < own_len)
    return jnp.concatenate([one.astype(jnp.int32)] * GROUP, axis=1) > 0


def attend_kernel(n, info_ref, q_ref, *refs):
    k_refs, v_refs = refs[:n], refs[n : 2 * n]
    o_ref, ot_ref, lse_ref, m_ref, l_ref, acc_ref = refs[2 * n :]
    tokens = q_ref.shape[1]
    s = info_ref[0]
    own_len = info_ref[1] - s * tokens
    active = own_len > 0

    @pl.when(jnp.logical_not(active))
    def _():
        o_ref[...] = jnp.zeros_like(o_ref)
        ot_ref[...] = jnp.zeros_like(ot_ref)
        lse_ref[...] = jnp.zeros_like(lse_ref)

    @pl.when(active)
    def _():
        for d in range(n):

            def block(d=d):
                mask = diagonal_mask(tokens, own_len) if d == 0 else None
                for j in range(2):
                    cols = slice(j * HEAD, (j + 1) * HEAD)
                    scores = dot(k_refs[d][:, cols], side_by_side(q_ref, j))
                    value_t = v_refs[d][:, cols].astype(F32).T.astype(BF)
                    if d == 0:
                        scores = jnp.where(mask, scores, NEGATIVE)
                        top = jnp.max(scores, axis=0, keepdims=True)
                        p = jnp.exp(scores - top)
                        l_ref[j : j + 1] = jnp.sum(p, axis=0, keepdims=True)
                        acc_ref[j] = dot(value_t, p.astype(BF))
                    else:
                        old = m_ref[j : j + 1]
                        top = jnp.maximum(old, jnp.max(scores, axis=0, keepdims=True))
                        keep = jnp.exp(old - top)
                        p = jnp.exp(scores - top)
                        l_ref[j : j + 1] = l_ref[j : j + 1] * keep + jnp.sum(
                            p, axis=0, keepdims=True
                        )
                        acc_ref[j] = acc_ref[j] * keep + dot(value_t, p.astype(BF))
                    m_ref[j : j + 1] = top

            if d == 0:
                block()
            else:
                pl.when(d <= s)(block)
        pieces = []
        for j in range(2):
            out = acc_ref[j] / l_ref[j : j + 1]
            lse_ref[j : j + 1] = m_ref[j : j + 1] + jnp.log(l_ref[j : j + 1])
            pieces += [out[:, h * tokens : (h + 1) * tokens] for h in range(GROUP)]
        out = jnp.concatenate(pieces, axis=0)
        ot_ref[...] = out.astype(BF)
        o_ref[...] = out.T.astype(BF)


def attend(info, q_t, kvs, micro, tokens):
    n = len(kvs)
    width = q_t.shape[0]
    kv_width = kvs[0].shape[1] // 2
    steps = kv_width // LANES
    qw = width // steps
    v_first = kv_width // LANES
    return pl.pallas_call(
        functools.partial(attend_kernel, n),
        name="attend",
        grid=(steps,),
        in_specs=[smem(), pl.BlockSpec((qw, tokens), lambda i: (i, micro))]
        + [pl.BlockSpec((tokens, LANES), lambda i: (0, i))] * n
        + [pl.BlockSpec((tokens, LANES), lambda i: (0, v_first + i))] * n,
        out_specs=[
            pl.BlockSpec((tokens, qw), lambda i: (0, i)),
            pl.BlockSpec((qw, tokens), lambda i: (i, 0)),
            pl.BlockSpec((8, GROUP * tokens), lambda i: (i, 0)),
        ],
        out_shape=[
            jax.ShapeDtypeStruct((tokens, width), BF),
            jax.ShapeDtypeStruct((width, tokens), BF),
            jax.ShapeDtypeStruct((8 * steps, GROUP * tokens), F32),
        ],
        scratch_shapes=[
            pltpu.VMEM((8, GROUP * tokens), F32),
            pltpu.VMEM((8, GROUP * tokens), F32),
            pltpu.VMEM((2, HEAD, GROUP * tokens), F32),
        ],
        compiler_params=params(),
        cost_estimate=cost(
            4 * 4 * width * tokens * tokens * n,
            2 * (3 * width * tokens + n * tokens * 2 * kv_width),
            width // HEAD * tokens * tokens * n,
        ),
    )(info, q_t, *kvs, *kvs)


def attend_back_kernel(n, info_ref, q_ref, g_ref, o_ref, lse_ref, cos_ref, sin_ref, *refs):
    k_refs, v_refs = refs[:n], refs[n : 2 * n]
    gq_ref = refs[2 * n]
    dk_refs, dv_refs = refs[2 * n + 1 : 3 * n + 1], refs[3 * n + 1 : 4 * n + 1]
    acc_ref = refs[4 * n + 1]
    tokens = q_ref.shape[1]
    s = info_ref[0]
    own_len = info_ref[1] - s * tokens
    active = own_len > 0

    @pl.when(jnp.logical_not(active))
    def _():
        gq_ref[...] = jnp.zeros_like(gq_ref)
        for d in range(n):
            dk_refs[d][...] = jnp.zeros_like(dk_refs[d])
            dv_refs[d][...] = jnp.zeros_like(dv_refs[d])

    @pl.when(active)
    def _():
        for d in range(n):

            def block(d=d):
                mask = diagonal_mask(tokens, own_len) if d == 0 else None
                dks, dvs = [], []
                for j in range(2):
                    cols = slice(j * HEAD, (j + 1) * HEAD)
                    key, value = k_refs[d][:, cols], v_refs[d][:, cols]
                    query, grad = side_by_side(q_ref, j), side_by_side(g_ref, j)
                    out = side_by_side(o_ref, j)
                    inner = jnp.sum(
                        grad.astype(F32) * out.astype(F32), axis=0, keepdims=True
                    )
                    p = jnp.exp(dot(key, query) - lse_ref[j : j + 1])
                    if d == 0:
                        p = jnp.where(mask, p, 0.0)
                    dp = dot(value, grad)
                    ds = (p * (dp - inner)).astype(BF)
                    dvs.append(dot(p.astype(BF), grad, NT))
                    dks.append(dot(ds, query, NT))
                    part = dot(key.astype(F32).T.astype(BF), ds)
                    if d == 0:
                        acc_ref[j] = part
                    else:
                        acc_ref[j] += part
                dk_refs[d][...] = jnp.concatenate(dks, axis=1).astype(BF)
                dv_refs[d][...] = jnp.concatenate(dvs, axis=1).astype(BF)

            if d == 0:
                block()
            else:
                pl.when(d <= s)(block)
        pieces = []
        for j in range(2):
            for h in range(GROUP):
                piece = acc_ref[j, :, h * tokens : (h + 1) * tokens] * SCALE
                pieces.append(piece.astype(BF).astype(F32))
        grad_q = rotate(jnp.concatenate(pieces, axis=0), cos_ref[...], sin_ref[...], -1)
        gq_ref[...] = grad_q.T.astype(BF)


def attend_back(info, q_t, g_t, o_t, lse, cosine, sine, kvs, micro, tokens):
    n = len(kvs)
    width = q_t.shape[0]
    kv_width = kvs[0].shape[1] // 2
    steps = kv_width // LANES
    qw = width // steps
    v_first = kv_width // LANES
    transposed = pl.BlockSpec((qw, tokens), lambda i: (i, 0))
    kv_block = pl.BlockSpec((tokens, LANES), lambda i: (0, i))
    got = pl.pallas_call(
        functools.partial(attend_back_kernel, n),
        name="attend_back",
        grid=(steps,),
        in_specs=[
            smem(),
            pl.BlockSpec((qw, tokens), lambda i: (i, micro)),
            transposed,
            transposed,
            pl.BlockSpec((8, GROUP * tokens), lambda i: (i, 0)),
            whole((HALF, tokens)),
            whole((HALF, tokens)),
        ]
        + [kv_block] * n
        + [pl.BlockSpec((tokens, LANES), lambda i: (0, v_first + i))] * n,
        out_specs=[pl.BlockSpec((tokens, qw), lambda i: (0, i))] + [kv_block] * (2 * n),
        out_shape=[jax.ShapeDtypeStruct((tokens, width), BF)]
        + [jax.ShapeDtypeStruct((tokens, kv_width), BF)] * (2 * n),
        scratch_shapes=[pltpu.VMEM((2, HEAD, GROUP * tokens), F32)],
        compiler_params=params(),
        cost_estimate=cost(
            10 * 4 * width * tokens * tokens * n,
            2 * (4 * width * tokens + 2 * n * tokens * 2 * kv_width),
            width // HEAD * tokens * tokens * n,
        ),
    )(info, q_t, g_t, o_t, lse, cosine, sine, *kvs, *kvs)
    return got[0], got[1 : n + 1], got[n + 1 :]


def after_kernel(
    steps, a_ref, w_ref, x_ref, gain_ref, router_ref, chosen_ref, res_ref, xg_ref, ge_ref, acc_ref
):
    step = pl.program_id(0)
    part = dot(a_ref[...], w_ref[...])

    @pl.when(step == 0)
    def _():
        acc_ref[...] = part

    @pl.when(step > 0)
    def _():
        acc_ref[...] += part

    @pl.when(step == steps - 1)
    def _():
        dim = x_ref.shape[1]
        residual = x_ref[...].astype(F32) + acc_ref[...]
        res_ref[...] = residual
        inv = lax.rsqrt(jnp.mean(residual * residual, axis=-1, keepdims=True) + EPS)
        normed = (residual * inv * gain_ref[...]).astype(BF)
        logits = dot(normed, router_ref[...])
        chosen = chosen_ref[...] > 0
        logits = jnp.where(chosen, logits, NEGATIVE)
        top = jnp.max(logits, axis=-1, keepdims=True)
        e = jnp.where(chosen, jnp.exp(logits - top), 0.0)
        exact = e / jnp.sum(e, axis=-1, keepdims=True)
        ge_ref[...] = exact
        xg_ref[:, :dim] = normed
        xg_ref[:, dim:] = exact.astype(BF)


def after_attention(attn, w_out, x, micro, gain, router, chosen):
    tokens, width = attn.shape
    dim = w_out.shape[1]
    tile = 512
    steps = width // tile
    return pl.pallas_call(
        functools.partial(after_kernel, steps),
        name="after_attention",
        grid=(steps,),
        in_specs=[
            pl.BlockSpec((tokens, tile), lambda i: (0, i)),
            pl.BlockSpec((tile, dim), lambda i: (i, 0)),
            pl.BlockSpec((tokens, dim), lambda i: (micro, 0)),
            whole((1, dim)),
            whole((dim, LANES)),
            pl.BlockSpec((tokens, LANES), lambda i: (micro, 0)),
        ],
        out_specs=[
            whole((tokens, dim)),
            whole((tokens, dim + LANES)),
            whole((tokens, LANES)),
        ],
        out_shape=[
            jax.ShapeDtypeStruct((tokens, dim), F32),
            jax.ShapeDtypeStruct((tokens, dim + LANES), BF),
            jax.ShapeDtypeStruct((tokens, LANES), F32),
        ],
        scratch_shapes=[pltpu.VMEM((tokens, dim), F32)],
        compiler_params=params(),
        cost_estimate=cost(2 * tokens * width * dim, 2 * width * dim + 10 * tokens * dim),
    )(attn, w_out, x, gain, router, chosen)


def expert_kernel(
    experts, own_ref, xg_ref, g_ref, wg_ref, wu_ref, wd_ref, y_ref, back_ref, hg_ref, gp_ref
):
    dim = g_ref.shape[1]
    hidden = wg_ref.shape[2]
    rows = g_ref.shape[0]
    x = xg_ref[:, :dim]
    g = g_ref[...]
    gates = xg_ref[:, dim:].astype(F32)
    lane = lax.broadcasted_iota(jnp.int32, (rows, LANES), 1)
    gate_cols = jnp.zeros((rows, LANES), F32)
    for e in range(experts):
        mine = lane == own_ref[0] + e
        gate = jnp.sum(jnp.where(mine, gates, 0.0), axis=1, keepdims=True)
        pre_gate = dot(x, wg_ref[e])
        pre_up = dot(x, wu_ref[e])
        grad_hidden = dot(g, wd_ref[e], NT)
        sig = 1.0 / (1.0 + jnp.exp(-pre_gate))
        silu = pre_gate * sig
        h = (silu * pre_up).astype(BF).astype(F32)
        per_gate = jnp.sum(h * grad_hidden, axis=1, keepdims=True)
        gate_cols = jnp.where(mine, per_gate, gate_cols)
        hg_ref[:, e * hidden : (e + 1) * hidden] = (gate * h).astype(BF)
        gh = gate * grad_hidden
        base = 2 * e * hidden
        gp_ref[:, base : base + hidden] = (
            gh * pre_up * (sig * (1.0 + pre_gate * (1.0 - sig)))
        ).astype(BF)
        gp_ref[:, base + hidden : base + 2 * hidden] = (gh * silu).astype(BF)
    y = dot(hg_ref[:, :hidden], wd_ref[0])
    for e in range(1, experts):
        y += dot(hg_ref[:, e * hidden : (e + 1) * hidden], wd_ref[e])
    y_ref[...] = y.astype(BF)
    back = None
    for e in range(experts):
        base = 2 * e * hidden
        part = dot(gp_ref[:, base : base + hidden], wg_ref[e], NT)
        part += dot(gp_ref[:, base + hidden : base + 2 * hidden], wu_ref[e], NT)
        back = part if back is None else back + part
    back_ref[:, :dim] = back.astype(BF)
    back_ref[:, dim:] = gate_cols.astype(BF)


def run_experts(own, xg, g, w_gate, w_up, w_down):
    rows, dim = g.shape
    experts, _, hidden = w_gate.shape
    tile = 256
    row_block = lambda width: pl.BlockSpec((tile, width), lambda i: (i, 0))
    return pl.pallas_call(
        functools.partial(expert_kernel, experts),
        name="run_experts",
        grid=(rows // tile,),
        in_specs=[
            smem(),
            row_block(dim + LANES),
            row_block(dim),
            whole(w_gate.shape),
            whole(w_up.shape),
            whole(w_down.shape),
        ],
        out_specs=[
            row_block(dim),
            row_block(dim + LANES),
            row_block(experts * hidden),
            row_block(2 * experts * hidden),
        ],
        out_shape=[
            jax.ShapeDtypeStruct((rows, dim), BF),
            jax.ShapeDtypeStruct((rows, dim + LANES), BF),
            jax.ShapeDtypeStruct((rows, experts * hidden), BF),
            jax.ShapeDtypeStruct((rows, 2 * experts * hidden), BF),
        ],
        compiler_params=params(),
        cost_estimate=cost(
            12 * rows * dim * hidden * experts,
            2 * (4 * rows * dim + 3 * rows * experts * hidden + 3 * experts * dim * hidden),
            rows * experts * hidden,
        ),
    )(own, xg, g, w_gate, w_up, w_down)


def wide_grad_kernel(steps, micros, *refs):
    a_refs, b_refs = refs[:micros], refs[micros : 2 * micros]
    out_ref, acc_ref = refs[2 * micros :]
    step = pl.program_id(0)
    for m in range(micros):

        @pl.when((step >= m * steps) & (step < (m + 1) * steps))
        def _(m=m):
            part = dot(a_refs[m][...], b_refs[m][...], TN)
            if m == 0:

                @pl.when(step == 0)
                def _():
                    acc_ref[...] = part

                @pl.when(step > 0)
                def _():
                    acc_ref[...] += part
            else:
                acc_ref[...] += part

    @pl.when(step == micros * steps - 1)
    def _():
        out_ref[...] = acc_ref[...].astype(BF)


def wide_grad(lefts, left_block, left_width, rights, right_block, right_width, tile=512):
    micros, rows = len(lefts), lefts[0].shape[0]
    steps = rows // tile

    def spec(m, width, column):
        return pl.BlockSpec(
            (tile, width), lambda i: (jnp.clip(i - m * steps, 0, steps - 1), column)
        )

    return pl.pallas_call(
        functools.partial(wide_grad_kernel, steps, micros),
        name="wide_grad",
        grid=(micros * steps,),
        in_specs=[spec(m, left_width, left_block) for m in range(micros)]
        + [spec(m, right_width, right_block) for m in range(micros)],
        out_specs=whole((left_width, right_width)),
        out_shape=jax.ShapeDtypeStruct((left_width, right_width), BF),
        scratch_shapes=[pltpu.VMEM((left_width, right_width), F32)],
        compiler_params=params(),
        cost_estimate=cost(
            2 * micros * rows * left_width * right_width,
            2 * (micros * rows * (left_width + right_width) + left_width * right_width),
        ),
    )(*lefts, *rights)


def before_kernel(
    ret_ref, res_ref, ge_ref, gout_ref, gain_ref, router_ref, w_ref, gres_ref, ga_ref, gt_ref, small_ref
):
    dim = res_ref.shape[1]

    @pl.when(pl.program_id(0) == 0)
    def _():
        ge = ge_ref[...]
        gg = ret_ref[:, dim:].astype(F32)
        gl = ge * (gg - jnp.sum(ge * gg, axis=-1, keepdims=True))
        high = gl.astype(BF)
        low = (gl - high.astype(F32)).astype(BF)
        router = router_ref[...]
        gn = ret_ref[:, :dim].astype(F32) + (dot(high, router, NT) + dot(low, router, NT))
        residual = res_ref[...]
        gain = gain_ref[...]
        inv = lax.rsqrt(jnp.mean(residual * residual, axis=-1, keepdims=True) + EPS)
        unit = residual * inv
        normed = (unit * gain).astype(BF)
        small_ref[:LANES] = dot(high, normed, TN) + dot(low, normed, TN)
        gain_row = jnp.sum(gn * unit, axis=0, keepdims=True)
        small_ref[LANES:] = jnp.broadcast_to(gain_row, (8, dim))
        u = gn * gain
        gres = gout_ref[...].astype(F32) + inv * (
            u - unit * jnp.mean(u * unit, axis=-1, keepdims=True)
        )
        gres_ref[...] = gres
        ga_ref[...] = gres.astype(BF)

    gt_ref[...] = dot(w_ref[...], ga_ref[...], NT).astype(BF)


def before_attention(returned, residual, exact, gout, gain, router, w_out):
    tokens, dim = residual.shape
    width = w_out.shape[0]
    tile = 512
    return pl.pallas_call(
        before_kernel,
        name="before_attention",
        grid=(width // tile,),
        in_specs=[
            whole((tokens, dim + LANES)),
            whole((tokens, dim)),
            whole((tokens, LANES)),
            whole((tokens, dim)),
            whole((1, dim)),
            whole((dim, LANES)),
            pl.BlockSpec((tile, dim), lambda i: (i, 0)),
        ],
        out_specs=[
            whole((tokens, dim)),
            whole((tokens, dim)),
            pl.BlockSpec((tile, tokens), lambda i: (i, 0)),
            whole((LANES + 8, dim)),
        ],
        out_shape=[
            jax.ShapeDtypeStruct((tokens, dim), F32),
            jax.ShapeDtypeStruct((tokens, dim), BF),
            jax.ShapeDtypeStruct((width, tokens), BF),
            jax.ShapeDtypeStruct((LANES + 8, dim), F32),
        ],
        compiler_params=params(),
        cost_estimate=cost(2 * tokens * width * dim, 2 * width * dim + 14 * tokens * dim),
    )(returned, residual, exact, gout, gain, router, w_out)


def last_kernel(
    q_steps, steps, gq_ref, dkv_ref, wq_ref, wkv_ref, x_ref, gain_ref, gres_ref, din_ref, small_ref, acc_ref
):
    step = pl.program_id(0)

    @pl.when(step == 0)
    def _():
        acc_ref[...] = dot(gq_ref[...], wq_ref[...], NT)

    @pl.when((step > 0) & (step < q_steps))
    def _():
        acc_ref[...] += dot(gq_ref[...], wq_ref[...], NT)

    @pl.when(step >= q_steps)
    def _():
        acc_ref[...] += dot(dkv_ref[...], wkv_ref[...], NT)

    @pl.when(step == steps - 1)
    def _():
        x = x_ref[...].astype(F32)
        gain = gain_ref[...]
        inv = lax.rsqrt(jnp.mean(x * x, axis=-1, keepdims=True) + EPS)
        unit = x * inv
        gn = acc_ref[...]
        small_ref[...] = jnp.broadcast_to(
            jnp.sum(gn * unit, axis=0, keepdims=True), small_ref.shape
        )
        w = gn * gain
        grad = inv * (w - unit * jnp.mean(w * unit, axis=-1, keepdims=True))
        din_ref[...] = (grad + gres_ref[...]).astype(BF)


def last_step(gq, dkv, w_q, w_kv, x, micro, gain, gres):
    tokens, dim = gres.shape
    tile = 512
    q_steps = gq.shape[1] // tile
    steps = q_steps + dkv.shape[1] // tile
    q_at = lambda i: (0, jnp.minimum(i, q_steps - 1))
    kv_at = lambda i: (0, jnp.maximum(i - q_steps, 0))
    return pl.pallas_call(
        functools.partial(last_kernel, q_steps, steps),
        name="last_step",
        grid=(steps,),
        in_specs=[
            pl.BlockSpec((tokens, tile), q_at),
            pl.BlockSpec((tokens, tile), kv_at),
            pl.BlockSpec((dim, tile), q_at),
            pl.BlockSpec((dim, tile), kv_at),
            pl.BlockSpec((tokens, dim), lambda i: (micro, 0)),
            whole((1, dim)),
            whole((tokens, dim)),
        ],
        out_specs=[whole((tokens, dim)), whole((8, dim))],
        out_shape=[
            jax.ShapeDtypeStruct((tokens, dim), BF),
            jax.ShapeDtypeStruct((8, dim), F32),
        ],
        scratch_shapes=[pltpu.VMEM((tokens, dim), F32)],
        compiler_params=params(),
        cost_estimate=cost(
            2 * tokens * steps * tile * dim, 2 * steps * tile * dim + 12 * tokens * dim
        ),
    )(gq, dkv, w_q, w_kv, x, gain, gres)


def add_low(a, b):
    return (a.astype(F32) + b.astype(F32)).astype(BF)


def line_sum(x, n):
    if n == 1:
        return x
    if n % 2:
        return lax.psum(x, "seq")
    half = n // 2
    at = lax.axis_index("seq")
    for k in range(half - 1):
        x = add_low(x, lax.ppermute(x, "seq", [(k, k + 1), (n - 1 - k, n - 2 - k)]))
    x = add_low(x, lax.ppermute(x, "seq", [(half - 1, half), (half, half - 1)]))
    for k in reversed(range(half - 1)):
        got = lax.ppermute(x, "seq", [(k + 1, k), (n - 2 - k, n - 1 - k)])
        x = jnp.where((at == k) | (at == n - 1 - k), got, x)
    return x


def gather_rows(x):
    return lax.all_gather(x, "fsdp", axis=0, tiled=True)


def scatter_rows(x):
    return lax.psum_scatter(x, "fsdp", scatter_dimension=0, tiled=True)


def on_device(
    n_seq,
    inputs,
    lengths,
    expert_ids,
    cotangent,
    gain_attn,
    w_query,
    key_projection,
    value_projection,
    w_out,
    gain_moe,
    router,
    w_gate,
    w_up,
    w_down,
):
    micros, local_seqs, tokens, dim = inputs.shape
    assert local_seqs == 1
    rows = micros * tokens
    experts, _, hidden = w_gate.shape
    n_experts = router.shape[1]
    kv_width = key_projection.shape[1]
    at = lax.axis_index("seq")
    own = (lax.axis_index("fsdp") * experts).astype(jnp.int32).reshape(1)

    small = jnp.concatenate(
        [router, gain_attn[:, None], gain_moe[:, None]], axis=1
    )
    small = jnp.pad(small, ((0, 0), (0, LANES - small.shape[1])))
    kv_all = gather_rows(jnp.concatenate([key_projection, value_projection, small], axis=1))
    q_all = gather_rows(w_query)
    out_all = gather_rows(w_out)
    small_all = kv_all[:, 2 * kv_width :]
    gain_one = small_all[:, n_experts].astype(F32).reshape(1, dim)
    gain_two = small_all[:, n_experts + 1].astype(F32).reshape(1, dim)
    router_all = jnp.where(
        lax.broadcasted_iota(jnp.int32, small_all.shape, 1) < n_experts, small_all, BF(0)
    )
    kv_w = kv_all[:, : 2 * kv_width]

    positions = at * tokens + jnp.arange(tokens, dtype=jnp.int32)
    frequency = THETA ** (-(jnp.arange(HALF, dtype=F32) * 2.0) / HEAD)
    angles = frequency[:, None] * positions.astype(F32)[None, :]
    cosine, sine = jnp.cos(angles), jnp.sin(angles)
    cosine_all, sine_all = jnp.tile(cosine, (1, micros)), jnp.tile(sine, (1, micros))

    x = inputs.reshape(rows, dim)
    chosen = jnp.sum(
        (
            expert_ids.reshape(rows, TOPK)[:, :, None]
            == jnp.arange(LANES, dtype=jnp.int32)[None, None, :]
        ).astype(F32),
        axis=1,
    )
    valid = positions[None, :] < lengths[:, :1]
    gout = jnp.where(valid[:, :, None], cotangent.reshape(micros, tokens, dim), BF(0))
    infos = [
        jnp.stack([at.astype(jnp.int32), lengths[m, 0].astype(jnp.int32)]) for m in range(micros)
    ]

    kv, normed_one = kv_project(x, gain_one, kv_w, cosine_all, sine_all)
    kvs = []
    for m in range(micros):
        mine = kv[m * tokens : (m + 1) * tokens]
        kvs.append(
            [mine]
            + [
                lax.ppermute(mine, "seq", [(i, i + d) for i in range(n_seq - d)])
                for d in range(1, n_seq)
            ]
        )
    q_t = q_project(normed_one, q_all, cosine_all, sine_all)

    state = []
    for m in range(micros):
        attn, attn_t, lse = attend(infos[m], q_t, kvs[m], m, tokens)
        residual, xg, exact = after_attention(
            attn, out_all, x, m, gain_two, router_all, chosen
        )
        state.append((attn_t, lse, residual, exact, gather_rows(xg), gather_rows(gout[m])))

    outs, passed = [], []
    for m in range(micros):
        attn_t, lse, residual, exact, xg_all, g_all = state[m]
        y, back, hg, gp = run_experts(own, xg_all, g_all, w_gate, w_up, w_down)
        passed.append((xg_all, g_all, hg, gp))
        returned = scatter_rows(back)
        moe = scatter_rows(y)
        outs.append(
            jnp.where(valid[m][:, None], residual + moe.astype(F32), 0.0).astype(BF)
        )
        state[m] = (attn_t, lse, residual, exact, returned)

    d_gate, d_up, d_down = [], [], []
    xs, gs = [p[0] for p in passed], [p[1] for p in passed]
    hgs, gps = [p[2] for p in passed], [p[3] for p in passed]
    for e in range(experts):
        d_down.append(line_sum(wide_grad(hgs, e, hidden, gs, 0, dim), n_seq))
        d_gate.append(line_sum(wide_grad(xs, 0, dim, gps, 2 * e, hidden), n_seq))
        d_up.append(line_sum(wide_grad(xs, 0, dim, gps, 2 * e + 1, hidden), n_seq))

    grads, smalls, d_out, d_q, d_kv = [], [], None, None, None
    for m in range(micros):
        attn_t, lse, residual, exact, returned = state[m]
        gres, g_attn, g_t, small_two = before_attention(
            returned, residual, exact, gout[m], gain_two, router_all, out_all
        )
        part = dot(attn_t, g_attn)
        d_out = part if d_out is None else d_out + part
        gq, dks, dvs = attend_back(
            infos[m], q_t, g_t, attn_t, lse, cosine, sine, kvs[m], m, tokens
        )
        dk, dv = dks[0].astype(F32), dvs[0].astype(F32)
        for d in range(1, n_seq):
            pairs = [(i, i - d) for i in range(d, n_seq)]
            dk += lax.ppermute(dks[d], "seq", pairs).astype(F32)
            dv += lax.ppermute(dvs[d], "seq", pairs).astype(F32)
        dk = dk.astype(BF).astype(F32)
        dk = rotate(dk.T, cosine, sine, -1).T
        dkv = jnp.concatenate([dk.astype(BF), dv.astype(BF)], axis=1)
        normed = normed_one[m * tokens : (m + 1) * tokens]
        part_q, part_kv = dot(normed, gq, TN), dot(normed, dkv, TN)
        d_q = part_q if d_q is None else d_q + part_q
        d_kv = part_kv if d_kv is None else d_kv + part_kv
        din, small_one = last_step(gq, dkv, q_all, kv_w, x, m, gain_one, gres)
        grads.append(din)
        smalls.append(
            jnp.concatenate(
                [small_two[:n_experts], small_one[:1], small_two[LANES : LANES + 1]], axis=0
            )
        )
    small_rows = functools.reduce(jnp.add, smalls)
    small_cols = jnp.pad(small_rows, ((0, LANES - small_rows.shape[0]), (0, 0))).T.astype(BF)
    d_out = line_sum(scatter_rows(d_out.astype(BF)), n_seq).astype(F32)
    rest = line_sum(
        scatter_rows(jnp.concatenate([d_q.astype(BF), d_kv.astype(BF), small_cols], axis=1)), n_seq
    ).astype(F32)
    q_width = d_q.shape[1]
    shape = (micros, 1, tokens, dim)
    ends = q_width + 2 * kv_width
    return (
        jnp.stack(outs).reshape(shape),
        jnp.stack(grads).reshape(shape),
        rest[:, ends + n_experts],
        rest[:, :q_width],
        rest[:, q_width : q_width + kv_width],
        rest[:, q_width + kv_width : ends],
        d_out,
        rest[:, ends + n_experts + 1],
        rest[:, ends : ends + n_experts],
        jnp.stack(d_gate).astype(F32),
        jnp.stack(d_up).astype(F32),
        jnp.stack(d_down).astype(F32),
    )


def solution(mesh):
    token_spec = P(None, "fsdp", "seq", None)
    row, matrix, cube = P("fsdp"), P("fsdp", None), P("fsdp", None, None)
    return jax.shard_map(
        functools.partial(on_device, mesh.shape["seq"]),
        mesh=mesh,
        in_specs=(
            token_spec,
            P(None, "fsdp"),
            token_spec,
            token_spec,
            row,
            matrix,
            matrix,
            matrix,
            matrix,
            row,
            matrix,
            cube,
            cube,
            cube,
        ),
        out_specs=(
            token_spec,
            token_spec,
            row,
            matrix,
            matrix,
            matrix,
            matrix,
            row,
            matrix,
            cube,
            cube,
            cube,
        ),
        check_vma=False,
    )
```

```python
import functools

import jax
import jax.numpy as jnp
from jax import lax
from jax.experimental import pallas as pl
from jax.experimental.pallas import tpu as pltpu
from jax.sharding import PartitionSpec as P

HEAD = 64
HALF = HEAD // 2
GROUP = 3
TOPK = 8
EPS = 1e-06
THETA = 10000.0
NEGATIVE = -1e30
LANES = 128
SCALE = HEAD ** (-0.5)
BF = jnp.bfloat16
F32 = jnp.float32
VMEM_BYTES = 60 * 1024 * 1024

NN = (((1,), (0,)), ((), ()))
NT = (((1,), (1,)), ((), ()))
TN = (((0,), (0,)), ((), ()))


def dot(a, b, dims=NN):
    return lax.dot_general(a, b, dims, preferred_element_type=F32)


def params():
    return pltpu.CompilerParams(vmem_limit_bytes=VMEM_BYTES)


def cost(flops, moved, trans=0):
    parts = (int(v) // 10 for v in (flops, moved, trans))
    flops, moved, trans = parts
    return pl.CostEstimate(flops=flops, bytes_accessed=moved, transcendentals=trans)


def whole(shape):
    zeros = (0,) * len(shape)
    return pl.BlockSpec(shape, lambda *_: zeros)


def smem():
    return pl.BlockSpec(memory_space=pltpu.SMEM)


def pick(at, first_ref, second_ref, index=None):
    half = first_ref.shape[0]
    if index is None:
        index = lax.rem(at, half)
    return jnp.where(at < half, first_ref[index], second_ref[index])


def in_order(place_ref, w_refs):
    devices = 2 * w_refs[0].shape[0]
    return jnp.concatenate([pick(place_ref[j], *w_refs) for j in range(devices)], axis=0)


def rotate(rows, cosine, sine, sign):
    pieces = []
    for h in range(rows.shape[0] // HEAD):
        a = rows[h * HEAD : h * HEAD + HALF]
        b = rows[h * HEAD + HALF : (h + 1) * HEAD]
        if sign > 0:
            pieces += [a * cosine - b * sine, b * cosine + a * sine]
        else:
            pieces += [a * cosine + b * sine, b * cosine - a * sine]
    return jnp.concatenate(pieces, axis=0)


def unpack_kernel(n_experts, place_ref, wa_ref, wb_ref, router_ref, rows_ref):
    w = in_order(place_ref, (wa_ref, wb_ref))
    lane = lax.broadcasted_iota(jnp.int32, w.shape, 1)
    router_ref[...] = jnp.where(lane < n_experts, w.astype(F32), 0.0).astype(BF)
    rows_ref[...] = w.astype(F32).T


def unpack(place, w, block, n_experts):
    dim = 2 * w[0].shape[0] * w[0].shape[1]
    return pl.pallas_call(
        functools.partial(unpack_kernel, n_experts),
        name="unpack",
        grid=(1,),
        in_specs=[smem(), *w_columns(w, LANES, lambda i: block)],
        out_specs=[whole((dim, LANES)), whole((LANES, dim))],
        out_shape=[
            jax.ShapeDtypeStruct((dim, LANES), BF),
            jax.ShapeDtypeStruct((LANES, dim), F32),
        ],
        compiler_params=params(),
        cost_estimate=cost(0, 12 * dim * LANES),
    )(place, *w)


def kv_kernel(place_ref, x_ref, gain_ref, wa_ref, wb_ref, cos_ref, sin_ref, kv_ref, normed_ref):
    step = pl.program_id(0)

    @pl.when(step == 0)
    def _():
        x = x_ref[...].astype(F32)
        inv = lax.rsqrt(jnp.mean(x * x, axis=-1, keepdims=True) + EPS)
        normed_ref[...] = (x * inv * gain_ref[...]).astype(BF)
        r = dot(normed_ref[...], in_order(place_ref, (wa_ref, wb_ref)))
        r = rotate(r.T, cos_ref[...], sin_ref[...], 1)
        kv_ref[...] = r.T.astype(BF)

    @pl.when(step == 1)
    def _():
        kv_ref[...] = dot(normed_ref[...], in_order(place_ref, (wa_ref, wb_ref))).astype(BF)


def w_columns(w, tile, at):
    return [pl.BlockSpec((*half.shape[:2], tile), lambda *i: (0, 0, at(*i))) for half in w]


def kv_project(place, x, gain, w, width, cosine, sine):
    rows, dim = x.shape
    return pl.pallas_call(
        kv_kernel,
        name="kv_project",
        grid=(2,),
        in_specs=[
            smem(),
            whole((rows, dim)),
            whole((1, dim)),
            *w_columns(w, width, lambda i: i),
            whole((HALF, rows)),
            whole((HALF, rows)),
        ],
        out_specs=[pl.BlockSpec((rows, width), lambda i: (0, i)), whole((rows, dim))],
        out_shape=[
            jax.ShapeDtypeStruct((rows, 2 * width), BF),
            jax.ShapeDtypeStruct((rows, dim), BF),
        ],
        compiler_params=params(),
        cost_estimate=cost(2 * rows * dim * 2 * width, 2 * (2 * rows * dim + dim * 2 * width)),
    )(place, x, gain, *w, cosine, sine)


def q_kernel(place_ref, normed_ref, wa_ref, wb_ref, cos_ref, sin_ref, q_ref):
    r = dot(normed_ref[...], in_order(place_ref, (wa_ref, wb_ref)))
    r = rotate(r.T, cos_ref[...], sin_ref[...], 1)
    q_ref[...] = r.astype(BF) * BF(SCALE)


def q_project(place, normed, w, cosine, sine):
    rows, dim = normed.shape
    width = w[0].shape[2]
    tile = 512
    return pl.pallas_call(
        q_kernel,
        name="q_project",
        grid=(width // tile,),
        in_specs=[
            smem(),
            whole((rows, dim)),
            *w_columns(w, tile, lambda i: i),
            whole((HALF, rows)),
            whole((HALF, rows)),
        ],
        out_specs=pl.BlockSpec((tile, rows), lambda i: (i, 0)),
        out_shape=jax.ShapeDtypeStruct((width, rows), BF),
        compiler_params=params(),
        cost_estimate=cost(2 * rows * dim * width, 2 * (2 * rows * dim + dim * width)),
    )(place, normed, *w, cosine, sine)


def side_by_side(ref, j):
    base = j * GROUP * HEAD
    return jnp.concatenate(
        [ref[base + h * HEAD : base + (h + 1) * HEAD, :] for h in range(GROUP)], axis=1
    )


def diagonal_mask(tokens, own_len):
    key = lax.broadcasted_iota(jnp.int32, (tokens, tokens), 0)
    query = lax.broadcasted_iota(jnp.int32, (tokens, tokens), 1)
    one = (key <= query) & (key < own_len)
    return jnp.concatenate([one.astype(jnp.int32)] * GROUP, axis=1) > 0


def attend_kernel(n, info_ref, q_ref, k_ref, v_ref, o_ref, ot_ref, lse_ref, m_ref, l_ref, acc_ref):
    tokens = q_ref.shape[1]
    d = pl.program_id(1)
    s = info_ref[0]
    own_len = info_ref[1] - s * tokens
    active = own_len > 0

    def pair(j):
        cols = slice(j * HEAD, (j + 1) * HEAD)
        scores = dot(k_ref[0, :, cols], side_by_side(q_ref, j))
        return scores, v_ref[0, :, cols].astype(F32).T.astype(BF)

    @pl.when(active & (d == 0))
    def _():
        mask = diagonal_mask(tokens, own_len)
        for j in range(2):
            scores, value_t = pair(j)
            scores = jnp.where(mask, scores, NEGATIVE)
            top = jnp.max(scores, axis=0, keepdims=True)
            p = jnp.exp(scores - top)
            l_ref[j : j + 1] = jnp.sum(p, axis=0, keepdims=True)
            acc_ref[j] = dot(value_t, p.astype(BF))
            m_ref[j : j + 1] = top

    @pl.when(active & (d > 0) & (d <= s))
    def _():
        for j in range(2):
            scores, value_t = pair(j)
            old = m_ref[j : j + 1]
            top = jnp.maximum(old, jnp.max(scores, axis=0, keepdims=True))
            keep = jnp.exp(old - top)
            p = jnp.exp(scores - top)
            l_ref[j : j + 1] = l_ref[j : j + 1] * keep + jnp.sum(p, axis=0, keepdims=True)
            acc_ref[j] = acc_ref[j] * keep + dot(value_t, p.astype(BF))
            m_ref[j : j + 1] = top

    @pl.when(active & (d == n - 1))
    def _():
        pieces = []
        for j in range(2):
            out = acc_ref[j] / l_ref[j : j + 1]
            lse_ref[j : j + 1] = m_ref[j : j + 1] + jnp.log(l_ref[j : j + 1])
            pieces += [out[:, h * tokens : (h + 1) * tokens] for h in range(GROUP)]
        out = jnp.concatenate(pieces, axis=0)
        ot_ref[...] = out.astype(BF)
        o_ref[...] = out.T.astype(BF)

    @pl.when(jnp.logical_not(active) & (d == 0))
    def _():
        o_ref[...] = jnp.zeros_like(o_ref)
        ot_ref[...] = jnp.zeros_like(ot_ref)
        lse_ref[...] = jnp.zeros_like(lse_ref)


def owner(info_ref, d, n):
    return lax.rem(info_ref[0] + n - d, n)


def attend(info, q_t, kv, micro, tokens):
    n = kv.shape[0]
    width = q_t.shape[0]
    kv_width = kv.shape[2] // 2
    steps = kv_width // LANES
    qw = width // steps
    return pl.pallas_call(
        functools.partial(attend_kernel, n),
        name="attend",
        grid_spec=pltpu.PrefetchScalarGridSpec(
            num_scalar_prefetch=1,
            grid=(steps, n),
            in_specs=[
                pl.BlockSpec((qw, tokens), lambda i, d, info: (i, micro)),
                pl.BlockSpec((1, tokens, LANES), lambda i, d, info: (owner(info, d, n), 0, i)),
                pl.BlockSpec(
                    (1, tokens, LANES), lambda i, d, info: (owner(info, d, n), 0, steps + i)
                ),
            ],
            out_specs=[
                pl.BlockSpec((tokens, qw), lambda i, d, info: (0, i)),
                pl.BlockSpec((qw, tokens), lambda i, d, info: (i, 0)),
                pl.BlockSpec((8, GROUP * tokens), lambda i, d, info: (i, 0)),
            ],
            scratch_shapes=[
                pltpu.VMEM((8, GROUP * tokens), F32),
                pltpu.VMEM((8, GROUP * tokens), F32),
                pltpu.VMEM((2, HEAD, GROUP * tokens), F32),
            ],
        ),
        out_shape=[
            jax.ShapeDtypeStruct((tokens, width), BF),
            jax.ShapeDtypeStruct((width, tokens), BF),
            jax.ShapeDtypeStruct((8 * steps, GROUP * tokens), F32),
        ],
        compiler_params=params(),
        cost_estimate=cost(
            4 * 4 * width * tokens * tokens * n,
            2 * (3 * width * tokens + n * tokens * 2 * kv_width),
            width // HEAD * tokens * tokens * n,
        ),
    )(info, q_t, kv, kv)


def attend_back_kernel(
    n, info_ref, q_ref, g_ref, o_ref, lse_ref, cos_ref, sin_ref, k_ref, v_ref, gq_ref, dkv_ref, acc_ref
):
    tokens = q_ref.shape[1]
    d = pl.program_id(1)
    s = info_ref[0]
    own_len = info_ref[1] - s * tokens
    active = own_len > 0

    def block(first):
        mask = diagonal_mask(tokens, own_len) if first else None
        dks, dvs = [], []
        for j in range(2):
            cols = slice(j * HEAD, (j + 1) * HEAD)
            key, value = k_ref[0, :, cols], v_ref[0, :, cols]
            query, grad = side_by_side(q_ref, j), side_by_side(g_ref, j)
            out = side_by_side(o_ref, j)
            inner = jnp.sum(grad.astype(F32) * out.astype(F32), axis=0, keepdims=True)
            p = jnp.exp(dot(key, query) - lse_ref[j : j + 1])
            if first:
                p = jnp.where(mask, p, 0.0)
            dp = dot(value, grad)
            ds = (p * (dp - inner)).astype(BF)
            dvs.append(dot(p.astype(BF), grad, NT))
            dks.append(dot(ds, query, NT))
            part = dot(key.astype(F32).T.astype(BF), ds)
            if first:
                acc_ref[j] = part
            else:
                acc_ref[j] += part
        dkv_ref[0, 0] = jnp.concatenate(dks, axis=1).astype(BF)
        dkv_ref[0, 1] = jnp.concatenate(dvs, axis=1).astype(BF)

    pl.when(active & (d == 0))(lambda: block(True))
    pl.when(active & (d > 0) & (d <= s))(lambda: block(False))

    @pl.when(active & (d == n - 1))
    def _():
        pieces = []
        for j in range(2):
            for h in range(GROUP):
                piece = acc_ref[j, :, h * tokens : (h + 1) * tokens] * SCALE
                pieces.append(piece.astype(BF).astype(F32))
        grad_q = rotate(jnp.concatenate(pieces, axis=0), cos_ref[...], sin_ref[...], -1)
        gq_ref[...] = grad_q.T.astype(BF)

    @pl.when(jnp.logical_not(active) | (d > s))
    def _():
        dkv_ref[...] = jnp.zeros_like(dkv_ref)

    @pl.when(jnp.logical_not(active) & (d == 0))
    def _():
        gq_ref[...] = jnp.zeros_like(gq_ref)


def attend_back(info, q_t, g_t, o_t, lse, cosine, sine, kv, micro, tokens):
    n = kv.shape[0]
    width = q_t.shape[0]
    kv_width = kv.shape[2] // 2
    steps = kv_width // LANES
    qw = width // steps
    transposed = pl.BlockSpec((qw, tokens), lambda i, d, info: (i, 0))
    return pl.pallas_call(
        functools.partial(attend_back_kernel, n),
        name="attend_back",
        grid_spec=pltpu.PrefetchScalarGridSpec(
            num_scalar_prefetch=1,
            grid=(steps, n),
            in_specs=[
            pl.BlockSpec((qw, tokens), lambda i, d, info: (i, micro)),
            transposed,
            transposed,
            pl.BlockSpec((8, GROUP * tokens), lambda i, d, info: (i, 0)),
            whole((HALF, tokens)),
            whole((HALF, tokens)),
            pl.BlockSpec((1, tokens, LANES), lambda i, d, info: (owner(info, d, n), 0, i)),
            pl.BlockSpec(
                (1, tokens, LANES), lambda i, d, info: (owner(info, d, n), 0, steps + i)
            ),
        ],
        out_specs=[
            pl.BlockSpec((tokens, qw), lambda i, d, info: (0, i)),
            pl.BlockSpec(
                (1, 2, tokens, LANES), lambda i, d, info: (owner(info, d, n), 0, 0, i)
            ),
        ],
            scratch_shapes=[pltpu.VMEM((2, HEAD, GROUP * tokens), F32)],
        ),
        out_shape=[
            jax.ShapeDtypeStruct((tokens, width), BF),
            jax.ShapeDtypeStruct((n, 2, tokens, kv_width), BF),
        ],
        compiler_params=params(),
        cost_estimate=cost(
            10 * 4 * width * tokens * tokens * n,
            2 * (4 * width * tokens + 2 * n * tokens * 2 * kv_width),
            width // HEAD * tokens * tokens * n,
        ),
    )(info, q_t, g_t, o_t, lse, cosine, sine, kv, kv)


def after_kernel(
    steps, place_ref, a_ref, wa_ref, wb_ref, x_ref, gain_ref, router_ref, chosen_ref, res_ref, xg_ref, ge_ref, acc_ref
):
    step = pl.program_id(0)
    acc_ref[step] = dot(a_ref[...], in_order(place_ref, (wa_ref, wb_ref)))

    @pl.when(step == steps - 1)
    def _():
        dim = x_ref.shape[1]
        product = jnp.concatenate([acc_ref[i] for i in range(steps)], axis=1)
        residual = x_ref[...].astype(F32) + product
        res_ref[...] = residual
        inv = lax.rsqrt(jnp.mean(residual * residual, axis=-1, keepdims=True) + EPS)
        normed = (residual * inv * gain_ref[...]).astype(BF)
        logits = dot(normed, router_ref[...])
        chosen = chosen_ref[...] > 0
        logits = jnp.where(chosen, logits, NEGATIVE)
        top = jnp.max(logits, axis=-1, keepdims=True)
        e = jnp.where(chosen, jnp.exp(logits - top), 0.0)
        exact = e / jnp.sum(e, axis=-1, keepdims=True)
        ge_ref[...] = exact
        xg_ref[:, :dim] = normed
        xg_ref[:, dim:] = exact.astype(BF)


def after_attention(place, attn, w_out, x, micro, gain, router, chosen):
    tokens, width = attn.shape
    dim = w_out[0].shape[2]
    tile = 512
    steps = dim // tile
    return pl.pallas_call(
        functools.partial(after_kernel, steps),
        name="after_attention",
        grid=(steps,),
        in_specs=[
            smem(),
            whole((tokens, width)),
            *w_columns(w_out, tile, lambda i: i),
            pl.BlockSpec((tokens, dim), lambda i: (micro, 0)),
            whole((1, dim)),
            whole((dim, LANES)),
            pl.BlockSpec((tokens, LANES), lambda i: (micro, 0)),
        ],
        out_specs=[
            whole((tokens, dim)),
            whole((tokens, dim + LANES)),
            whole((tokens, LANES)),
        ],
        out_shape=[
            jax.ShapeDtypeStruct((tokens, dim), F32),
            jax.ShapeDtypeStruct((tokens, dim + LANES), BF),
            jax.ShapeDtypeStruct((tokens, LANES), F32),
        ],
        scratch_shapes=[pltpu.VMEM((steps, tokens, tile), F32)],
        compiler_params=params(),
        cost_estimate=cost(2 * tokens * width * dim, 2 * width * dim + 10 * tokens * dim),
    )(place, attn, *w_out, x, gain, router, chosen)


def expert_kernel(
    experts, half, own_ref, place_ref, xg_ref, ga_ref, gb_ref, wg_ref, wu_ref, wd_ref, y_ref, back_ref, hg_ref, gp_ref
):
    rows, dim = ga_ref.shape
    hidden = wg_ref.shape[2]
    x = xg_ref[:, :dim]
    g = jnp.where(place_ref[pl.program_id(0)] < half, ga_ref[...], gb_ref[...])
    gates = xg_ref[:, dim:].astype(F32)
    lane = lax.broadcasted_iota(jnp.int32, (rows, LANES), 1)
    gate_cols = jnp.zeros((rows, LANES), F32)
    for e in range(experts):
        mine = lane == own_ref[0] + e
        gate = jnp.sum(jnp.where(mine, gates, 0.0), axis=1, keepdims=True)
        pre_gate = dot(x, wg_ref[e])
        pre_up = dot(x, wu_ref[e])
        grad_hidden = dot(g, wd_ref[e], NT)
        sig = 1.0 / (1.0 + jnp.exp(-pre_gate))
        silu = pre_gate * sig
        h = (silu * pre_up).astype(BF).astype(F32)
        per_gate = jnp.sum(h * grad_hidden, axis=1, keepdims=True)
        gate_cols = jnp.where(mine, per_gate, gate_cols)
        hg_ref[:, e * hidden : (e + 1) * hidden] = (gate * h).astype(BF)
        gh = gate * grad_hidden
        base = 2 * e * hidden
        gp_ref[:, base : base + hidden] = (
            gh * pre_up * (sig * (1.0 + pre_gate * (1.0 - sig)))
        ).astype(BF)
        gp_ref[:, base + hidden : base + 2 * hidden] = (gh * silu).astype(BF)
    y = dot(hg_ref[:, :hidden], wd_ref[0])
    for e in range(1, experts):
        y += dot(hg_ref[:, e * hidden : (e + 1) * hidden], wd_ref[e])
    y_ref[...] = y.astype(BF)
    back = None
    for e in range(experts):
        base = 2 * e * hidden
        part = dot(gp_ref[:, base : base + hidden], wg_ref[e], NT)
        part += dot(gp_ref[:, base + hidden : base + 2 * hidden], wu_ref[e], NT)
        back = part if back is None else back + part
    back_ref[:, :dim] = back.astype(BF)
    back_ref[:, dim:] = gate_cols.astype(BF)


def run_experts(own, place, xg, g, micro, micros, w_gate, w_up, w_down):
    rows = xg.shape[0]
    dim = g[0].shape[1]
    experts, _, hidden = w_gate.shape
    devices = place.shape[0]
    tile, half = rows // devices, devices // 2
    row_block = lambda width: pl.BlockSpec((tile, width), lambda i, *_: (i, 0))
    arrival = lambda width: pl.BlockSpec((tile, width), lambda i, own, place: (place[i], 0))
    g_block = pl.BlockSpec(
        (tile, dim), lambda i, own, place: (lax.rem(place[i], half) * micros + micro, 0)
    )
    return pl.pallas_call(
        functools.partial(expert_kernel, experts, half),
        name="run_experts",
        grid_spec=pltpu.PrefetchScalarGridSpec(
            num_scalar_prefetch=2,
            grid=(devices,),
            in_specs=[
                row_block(dim + LANES),
                g_block,
                g_block,
                whole(w_gate.shape),
                whole(w_up.shape),
                whole(w_down.shape),
            ],
            out_specs=[
                arrival(dim),
                row_block(dim + LANES),
                arrival(experts * hidden),
                row_block(2 * experts * hidden),
            ],
        ),
        out_shape=[
            jax.ShapeDtypeStruct((rows, dim), BF),
            jax.ShapeDtypeStruct((rows, dim + LANES), BF),
            jax.ShapeDtypeStruct((rows, experts * hidden), BF),
            jax.ShapeDtypeStruct((rows, 2 * experts * hidden), BF),
        ],
        compiler_params=params(),
        cost_estimate=cost(
            12 * rows * dim * hidden * experts,
            2 * (4 * rows * dim + 3 * rows * experts * hidden + 3 * experts * dim * hidden),
            rows * experts * hidden,
        ),
    )(own, place, xg, *g, w_gate, w_up, w_down)


def wide_grad_kernel(steps, micros, *refs):
    a_refs, b_refs = refs[:micros], refs[micros : 2 * micros]
    out_ref, acc_ref = refs[2 * micros :]
    step = pl.program_id(0)
    for m in range(micros):

        @pl.when((step >= m * steps) & (step < (m + 1) * steps))
        def _(m=m):
            part = dot(a_refs[m][...], b_refs[m][...], TN)
            if m == 0:

                @pl.when(step == 0)
                def _():
                    acc_ref[...] = part

                @pl.when(step > 0)
                def _():
                    acc_ref[...] += part
            else:
                acc_ref[...] += part

    @pl.when(step == micros * steps - 1)
    def _():
        out_ref[...] = acc_ref[...].astype(BF)


def wide_grad(lefts, left_block, left_width, rights, right_block, right_width, tile=512):
    micros, rows = len(lefts), lefts[0].shape[0]
    steps = rows // tile

    def spec(m, width, column):
        return pl.BlockSpec(
            (tile, width), lambda i: (jnp.clip(i - m * steps, 0, steps - 1), column)
        )

    return pl.pallas_call(
        functools.partial(wide_grad_kernel, steps, micros),
        name="wide_grad",
        grid=(micros * steps,),
        in_specs=[spec(m, left_width, left_block) for m in range(micros)]
        + [spec(m, right_width, right_block) for m in range(micros)],
        out_specs=whole((left_width, right_width)),
        out_shape=jax.ShapeDtypeStruct((left_width, right_width), BF),
        scratch_shapes=[pltpu.VMEM((left_width, right_width), F32)],
        compiler_params=params(),
        cost_estimate=cost(
            2 * micros * rows * left_width * right_width,
            2 * (micros * rows * (left_width + right_width) + left_width * right_width),
        ),
    )(*lefts, *rights)


def down_grad_kernel(micros, devices, *refs):
    hg_refs, ga_ref, gb_ref, out_ref, acc_ref = refs[:micros], *refs[micros:]
    step = pl.program_id(0)
    g = jnp.where(step < devices // 2, ga_ref[...], gb_ref[...])
    hg = jnp.concatenate([r[...] for r in hg_refs], axis=0)
    part = dot(hg, g, TN)

    @pl.when(step == 0)
    def _():
        acc_ref[...] = part

    @pl.when(step > 0)
    def _():
        acc_ref[...] += part

    @pl.when(step == devices - 1)
    def _():
        out_ref[...] = acc_ref[...].astype(BF)


def down_grad(hgs, expert, hidden, g, devices):
    micros, rows = len(hgs), hgs[0].shape[0]
    tile, half = rows // devices, devices // 2
    dim = g[0].shape[1]
    return pl.pallas_call(
        functools.partial(down_grad_kernel, micros, devices),
        name="down_grad",
        grid=(devices,),
        in_specs=[pl.BlockSpec((tile, hidden), lambda i: (i, expert))] * micros
        + [
            pl.BlockSpec((micros * tile, dim), lambda i: (jnp.minimum(i, half - 1), 0)),
            pl.BlockSpec((micros * tile, dim), lambda i: (jnp.maximum(i - half, 0), 0)),
        ],
        out_specs=whole((hidden, dim)),
        out_shape=jax.ShapeDtypeStruct((hidden, dim), BF),
        scratch_shapes=[pltpu.VMEM((hidden, dim), F32)],
        compiler_params=params(),
        cost_estimate=cost(2 * micros * rows * hidden * dim, 2 * micros * rows * (hidden + dim)),
    )(*hgs, *g)


def before_kernel(
    steps, place_ref, ret_ref, res_ref, ge_ref, gout_ref, gain_ref, router_ref, wa_ref, wb_ref, gres_ref, ga_ref, gt_ref, small_ref, cut_ref, acc_ref
):
    dim = res_ref.shape[1]

    step = pl.program_id(0)
    tile = dim // steps

    @pl.when(step == 0)
    def _():
        ge = ge_ref[...]
        gg = ret_ref[:, dim:].astype(F32)
        gl = ge * (gg - jnp.sum(ge * gg, axis=-1, keepdims=True))
        high = gl.astype(BF)
        low = (gl - high.astype(F32)).astype(BF)
        router = router_ref[...]
        gn = ret_ref[:, :dim].astype(F32) + (dot(high, router, NT) + dot(low, router, NT))
        residual = res_ref[...]
        gain = gain_ref[...]
        inv = lax.rsqrt(jnp.mean(residual * residual, axis=-1, keepdims=True) + EPS)
        unit = residual * inv
        normed = (unit * gain).astype(BF)
        small_ref[:LANES] = dot(high, normed, TN) + dot(low, normed, TN)
        gain_row = jnp.sum(gn * unit, axis=0, keepdims=True)
        small_ref[LANES:] = jnp.broadcast_to(gain_row, (8, dim))
        u = gn * gain
        gres = gout_ref[...].astype(F32) + inv * (
            u - unit * jnp.mean(u * unit, axis=-1, keepdims=True)
        )
        gres_ref[...] = gres
        low_gres = gres.astype(BF)
        ga_ref[...] = low_gres
        for i in range(steps):
            cut_ref[i] = low_gres[:, i * tile : (i + 1) * tile]
        acc_ref[...] = jnp.zeros_like(acc_ref)

    acc_ref[...] += dot(in_order(place_ref, (wa_ref, wb_ref)), cut_ref[step], NT)

    @pl.when(step == steps - 1)
    def _():
        gt_ref[...] = acc_ref[...].astype(BF)


def before_attention(place, returned, residual, exact, gout, gain, router, w_out):
    tokens, dim = residual.shape
    width = 2 * w_out[0].shape[0] * w_out[0].shape[1]
    tile = 512
    steps = dim // tile
    return pl.pallas_call(
        functools.partial(before_kernel, steps),
        name="before_attention",
        grid=(steps,),
        in_specs=[
            smem(),
            whole((tokens, dim + LANES)),
            whole((tokens, dim)),
            whole((tokens, LANES)),
            whole((tokens, dim)),
            whole((1, dim)),
            whole((dim, LANES)),
            *w_columns(w_out, tile, lambda i: i),
        ],
        out_specs=[
            whole((tokens, dim)),
            whole((tokens, dim)),
            whole((width, tokens)),
            whole((LANES + 8, dim)),
        ],
        out_shape=[
            jax.ShapeDtypeStruct((tokens, dim), F32),
            jax.ShapeDtypeStruct((tokens, dim), BF),
            jax.ShapeDtypeStruct((width, tokens), BF),
            jax.ShapeDtypeStruct((LANES + 8, dim), F32),
        ],
        scratch_shapes=[
            pltpu.VMEM((steps, tokens, tile), BF),
            pltpu.VMEM((width, tokens), F32),
        ],
        compiler_params=params(),
        cost_estimate=cost(2 * tokens * width * dim, 2 * width * dim + 14 * tokens * dim),
    )(place, returned, residual, exact, gout, gain, router, *w_out)


def last_kernel(
    q_steps, steps, place_ref, gq_ref, dkv_ref, qa_ref, qb_ref, kva_ref, kvb_ref, x_ref, gain_ref, gres_ref, din_ref, small_ref, acc_ref
):
    step = pl.program_id(0)

    @pl.when(step == 0)
    def _():
        acc_ref[...] = dot(gq_ref[...], in_order(place_ref, (qa_ref, qb_ref)), NT)

    @pl.when((step > 0) & (step < q_steps))
    def _():
        acc_ref[...] += dot(gq_ref[...], in_order(place_ref, (qa_ref, qb_ref)), NT)

    @pl.when(step >= q_steps)
    def _():
        acc_ref[...] += dot(dkv_ref[...], in_order(place_ref, (kva_ref, kvb_ref)), NT)

    @pl.when(step == steps - 1)
    def _():
        x = x_ref[...].astype(F32)
        gain = gain_ref[...]
        inv = lax.rsqrt(jnp.mean(x * x, axis=-1, keepdims=True) + EPS)
        unit = x * inv
        gn = acc_ref[...]
        small_ref[...] = jnp.broadcast_to(
            jnp.sum(gn * unit, axis=0, keepdims=True), small_ref.shape
        )
        w = gn * gain
        grad = inv * (w - unit * jnp.mean(w * unit, axis=-1, keepdims=True))
        din_ref[...] = (grad + gres_ref[...]).astype(BF)


def last_step(place, gq, dkv, w_q, w_kv, x, micro, gain, gres):
    tokens, dim = gres.shape
    tile = 512
    q_steps, kv_steps = gq.shape[1] // tile, dkv.shape[1] // tile
    steps = q_steps + kv_steps
    q_at = lambda i: (0, jnp.minimum(i, q_steps - 1))
    kv_at = lambda i: (0, jnp.maximum(i - q_steps, 0))
    return pl.pallas_call(
        functools.partial(last_kernel, q_steps, steps),
        name="last_step",
        grid=(steps,),
        in_specs=[
            smem(),
            pl.BlockSpec((tokens, tile), q_at),
            pl.BlockSpec((tokens, tile), kv_at),
            *w_columns(w_q, tile, lambda i: q_at(i)[1]),
            *w_columns(w_kv, tile, lambda i: kv_at(i)[1]),
            pl.BlockSpec((tokens, dim), lambda i: (micro, 0)),
            whole((1, dim)),
            whole((tokens, dim)),
        ],
        out_specs=[whole((tokens, dim)), whole((8, dim))],
        out_shape=[
            jax.ShapeDtypeStruct((tokens, dim), BF),
            jax.ShapeDtypeStruct((8, dim), F32),
        ],
        scratch_shapes=[pltpu.VMEM((tokens, dim), F32)],
        compiler_params=params(),
        cost_estimate=cost(
            2 * tokens * steps * tile * dim, 2 * steps * tile * dim + 12 * tokens * dim
        ),
    )(place, gq, dkv, *w_q, *w_kv, x, gain, gres)


def add_low(a, b):
    return (a.astype(F32) + b.astype(F32)).astype(BF)


def line_sum(x, n):
    if n == 1:
        return x
    if n % 2:
        return lax.psum(x, "seq")
    half = n // 2
    at = lax.axis_index("seq")
    for k in range(half - 1):
        x = add_low(x, lax.ppermute(x, "seq", [(k, k + 1), (n - 1 - k, n - 2 - k)]))
    x = add_low(x, lax.ppermute(x, "seq", [(half - 1, half), (half, half - 1)]))
    for k in reversed(range(half - 1)):
        got = lax.ppermute(x, "seq", [(k + 1, k), (n - 2 - k, n - 1 - k)])
        x = jnp.where((at == k) | (at == n - 1 - k), got, x)
    return x


class Line:
    def __init__(self, n):
        self.n = n
        self.held = {}
        self.count = 0
        self.results = []

    def sums(self):
        at = lax.axis_index("seq")
        middle = (at == 1) | (at == 2)
        return [r[0] if len(r) == 1 else jnp.where(middle, *r) for r in self.results]

    def step(self, chunk):
        n = self.n
        if n != 4:
            if chunk is not None:
                self.results.append((line_sum(chunk, n),))
            return
        held, self.held = self.held, {}
        crossing, leaving = held.get("crossing"), held.get("leaving")
        arrived = None
        if chunk is not None:
            arrived = lax.ppermute(chunk, "seq", [(0, 1), (3, 2)])
        if leaving is not None:
            self.results.append((leaving, lax.ppermute(leaving, "seq", [(1, 0), (2, 3)])))
        if crossing is not None:
            other = lax.ppermute(crossing, "seq", [(1, 2), (2, 1)])
            self.held["leaving"] = add_low(crossing, other)
        if chunk is not None:
            self.held["crossing"] = add_low(chunk, arrived)


def gate(x, *others):
    return lax.optimization_barrier((x, others))[0]


CORE, ALONG_X, ALONG_Y = 1, 2, 4


def swap(x, mask):
    return lax.ppermute(x, "fsdp", [(i, i ^ mask) for i in range(8)])


def gather_rows(x):
    return lax.all_gather(x, "fsdp", axis=0, tiled=True)


def assemble_kernel(x_ref, top_x_ref, low_y_ref, top_far_ref, low_far_ref, out_ref):
    rows = x_ref.shape[0]
    half = rows // 2
    out_ref[:rows] = x_ref[...]
    out_ref[rows : rows + half] = top_x_ref[...]
    out_ref[rows + half : 2 * rows] = low_far_ref[:half]
    out_ref[2 * rows : 2 * rows + half] = top_far_ref[:half]
    out_ref[2 * rows + half : 3 * rows] = low_y_ref[...]
    out_ref[3 * rows : 3 * rows + half] = top_far_ref[half:]
    out_ref[3 * rows + half :] = low_far_ref[half:]


def assemble(*pieces):
    rows, width = pieces[0].shape
    block = lambda n: pl.BlockSpec((n, width // 3), lambda i: (0, i))
    return pl.pallas_call(
        assemble_kernel,
        name="assemble",
        grid=(3,),
        in_specs=[block(p.shape[0]) for p in pieces],
        out_specs=block(4 * rows),
        out_shape=jax.ShapeDtypeStruct((4 * rows, width), pieces[0].dtype),
        compiler_params=params(),
        cost_estimate=cost(0, 16 * rows * width),
    )(*pieces)


def gather_near(x, n):
    if n != 8:
        every = gather_rows(x)
        half = every.shape[0] // 2
        return every[:half], every[half:]
    gather = Gather(x, n)
    gather.further()
    return gather.finish()


class Gather:
    def __init__(self, x, n):
        self.n, self.x = n, x
        if n != 8:
            self.halves = gather_near(x, n)
            self.near = self.far = ()
            return
        half = x.shape[0] // 2
        self.near = swap(x[:half], ALONG_X), swap(x[half:], ALONG_Y)

    def further(self, *others):
        if self.n != 8:
            return
        half = self.x.shape[0] // 2
        x, (top_x, low_y) = gate((self.x, self.near), *others)
        self.near = top_x, low_y
        top_far = swap(jnp.concatenate([x[:half], top_x]), ALONG_Y)
        low_far = swap(jnp.concatenate([x[half:], low_y]), ALONG_X)
        self.far = top_far, low_far

    def finish(self, *others):
        if self.n != 8:
            return self.halves
        near, far = gate((self.near, self.far), *others)
        mine = assemble(self.x, *near, *far)
        return mine, swap(mine, CORE)


class Scatter:
    def __init__(self, arrays, n):
        self.arrays, self.n, self.stage = list(arrays), n, 0
        self.rows = arrays[0].shape[0] // n

    def advance(self):
        held, self.stage = self.arrays, self.stage + 1
        rows, half = self.rows, self.rows // 2
        if self.n != 8:
            if self.stage == 1:
                self.arrays = [scatter_rows(a) for a in held]
            return
        if self.stage == 1:
            self.arrays = [add_low(a[: 4 * rows], swap(a[4 * rows :], CORE)) for a in held]
        if self.stage == 2:
            tops = [a[k * rows : k * rows + half] for a in held for k in (2, 3)]
            lows = [a[k * rows + half : (k + 1) * rows] for a in held for k in (1, 3)]
            tops = swap(jnp.concatenate(tops), ALONG_Y)
            lows = swap(jnp.concatenate(lows), ALONG_X)
            self.arrays = []
            for i, a in enumerate(held):
                at = 2 * i * half
                self.arrays.append(
                    (
                        add_low(a[:half], tops[at : at + half]),
                        add_low(a[half:rows], lows[at : at + half]),
                        add_low(a[rows : rows + half], tops[at + half : at + rows]),
                        add_low(a[2 * rows + half : 3 * rows], lows[at + half : at + rows]),
                    )
                )
        if self.stage == 3:
            over_x = swap(jnp.concatenate([a[2] for a in held]), ALONG_X)
            over_y = swap(jnp.concatenate([a[3] for a in held]), ALONG_Y)
            self.arrays = [
                jnp.concatenate(
                    [
                        add_low(a[0], over_x[i * half : (i + 1) * half]),
                        add_low(a[1], over_y[i * half : (i + 1) * half]),
                    ]
                )
                for i, a in enumerate(held)
            ]


def block_places(n):
    if n != 8:
        return jnp.arange(n, dtype=jnp.int32)
    mask = lax.axis_index("fsdp").astype(jnp.int32) ^ jnp.arange(n, dtype=jnp.int32)
    return (mask >> 1) + 4 * (mask & 1)


def scatter_rows(x):
    return lax.psum_scatter(x, "fsdp", scatter_dimension=0, tiled=True)


def on_device(
    n_seq,
    n_fsdp,
    inputs,
    lengths,
    expert_ids,
    cotangent,
    gain_attn,
    w_query,
    key_projection,
    value_projection,
    w_out,
    gain_moe,
    router,
    w_gate,
    w_up,
    w_down,
):
    micros, local_seqs, tokens, dim = inputs.shape
    assert local_seqs == 1
    rows = micros * tokens
    experts, _, hidden = w_gate.shape
    n_experts = router.shape[1]
    kv_width = key_projection.shape[1]
    at = lax.axis_index("seq")
    own = (lax.axis_index("fsdp") * experts).astype(jnp.int32).reshape(1)

    small = jnp.concatenate(
        [router, gain_attn[:, None], gain_moe[:, None]], axis=1
    )
    small = jnp.pad(small, ((0, 0), (0, LANES - small.shape[1])))
    place = block_places(n_fsdp)

    def weights(w):
        return [h.reshape(n_fsdp // 2, -1, h.shape[1]) for h in gather_near(w, n_fsdp)]

    w_kv = weights(jnp.concatenate([key_projection, value_projection, small], axis=1))
    router_all, rows_all = unpack(place, w_kv, 2 * kv_width // LANES, n_experts)
    gain_one = rows_all[n_experts : n_experts + 1]
    gain_two = rows_all[n_experts + 1 : n_experts + 2]

    positions = at * tokens + jnp.arange(tokens, dtype=jnp.int32)
    frequency = THETA ** (-(jnp.arange(HALF, dtype=F32) * 2.0) / HEAD)
    angles = frequency[:, None] * positions.astype(F32)[None, :]
    cosine, sine = jnp.cos(angles), jnp.sin(angles)
    cosine_all, sine_all = jnp.tile(cosine, (1, micros)), jnp.tile(sine, (1, micros))

    x = inputs.reshape(rows, dim)
    chosen = jnp.sum(
        (
            expert_ids.reshape(rows, TOPK)[:, :, None]
            == jnp.arange(LANES, dtype=jnp.int32)[None, None, :]
        ).astype(F32),
        axis=1,
    )
    valid = positions[None, :] < lengths[:, :1]
    gout = jnp.where(valid[:, :, None], cotangent.reshape(micros, tokens, dim), BF(0))
    infos = [
        jnp.stack([at.astype(jnp.int32), lengths[m, 0].astype(jnp.int32)]) for m in range(micros)
    ]

    kv, normed_one = kv_project(place, x, gain_one, w_kv, kv_width, cosine_all, sine_all)
    w_q = weights(gate(w_query, kv))
    q_t = q_project(place, normed_one, w_q, cosine_all, sine_all)
    kvs = []
    for m in range(micros):
        mine = kv[m * tokens : (m + 1) * tokens]
        every = lax.all_gather(mine, "seq", axis=0, tiled=True)
        kvs.append(every.reshape(n_seq, tokens, 2 * kv_width))

    out_all = weights(gate(w_out, w_q[0]))
    g_gather = Gather(gate(gout.reshape(rows, dim), w_q[0]), n_fsdp)

    state, xg_all = [], []
    for m in range(micros):
        if m == 0:
            info = gate(infos[m], g_gather.near)
            g_gather.further()
        else:
            info = gate(infos[m], state[-1][2], g_gather.far)
            g_all = g_gather.finish()
        attn, attn_t, lse = attend(info, q_t, kvs[m], m, tokens)
        residual, xg, exact = after_attention(
            place, attn, out_all, x, m, gain_two, router_all, chosen
        )
        state.append((attn_t, lse, residual, exact))
        xg_all.append(gather_rows(xg))

    xg_all[0] = gate(xg_all[0], state[-1][2])
    passed, backs = [], []
    for m in range(micros):
        y, back, hg, gp = run_experts(
            own, place, xg_all[m], g_all, m, micros, w_gate, w_up, w_down
        )
        passed.append((xg_all[m], hg, gp))
        backs.append((scatter_rows(back), y))

    names = [("down", e) for e in range(experts)]
    names += [(name, e) for e in range(experts) for name in ("gate", "up")]

    def expert_grad(name, e, got):
        xs, hgs, gps = ([p[i] for p in got] for i in range(3))
        if name == "down":
            return down_grad(hgs, e, hidden, g_all, n_fsdp)
        return wide_grad(xs, 0, dim, gps, 2 * e + (name == "up"), hidden)

    line = Line(n_seq)
    found = [{} for _ in range(micros)]

    def to_heads(m):
        attn_t, lse, residual, exact = state[m]
        gres, g_attn, g_t, small_two = before_attention(
            place, backs[m][0], residual, exact, gout[m], gain_two, router_all, out_all
        )
        found[m].update(gres=gres, g_attn=g_attn, g_t=g_t, small_two=small_two)

    def through_heads(m):
        attn_t, lse = state[m][:2]
        gq, by_owner = attend_back(
            infos[m], q_t, found[m]["g_t"], attn_t, lse, cosine, sine, kvs[m], m, tokens
        )
        found[m].update(gq=gq, by_owner=by_owner)

    owned = {}

    def to_owners(m):
        by_owner = found[m].pop("by_owner")
        shape = by_owner.shape
        owned[m] = lax.psum_scatter(
            by_owner.reshape(n_seq * shape[1] * tokens, shape[3]),
            "seq",
            scatter_dimension=0,
            tiled=True,
        ).reshape(shape[1:])

    def own_grads(m):
        dk = rotate(owned[m][0].astype(F32).T, cosine, sine, -1).T
        return jnp.concatenate([dk.astype(BF), owned[m][1]], axis=1)

    def finish(m):
        f = found[m]
        f["dkv"] = own_grads(m)
        din, small_one = last_step(
            place, f["gq"], f["dkv"], w_q, w_kv, x, m, gain_one, f["gres"]
        )
        small_rows = jnp.concatenate(
            [f["small_two"][:n_experts], small_one[:1], f["small_two"][LANES : LANES + 1]], axis=0
        )
        f.update(din=din, small_rows=small_rows)

    def out_grad():
        total = None
        for m in range(micros):
            part = dot(state[m][0], found[m]["g_attn"])
            total = part if total is None else total + part
        return total.astype(BF)

    def projection_grads():
        d_q = d_kv = None
        for m in range(micros):
            normed = normed_one[m * tokens : (m + 1) * tokens]
            part_q = dot(normed, found[m]["gq"], TN)
            part_kv = dot(normed, found[m]["dkv"], TN)
            d_q = part_q if d_q is None else d_q + part_q
            d_kv = part_kv if d_kv is None else d_kv + part_kv
        small_rows = functools.reduce(jnp.add, [f["small_rows"] for f in found])
        pad = ((0, LANES - small_rows.shape[0]), (0, 0))
        small_cols = jnp.pad(small_rows, pad).T
        columns = jnp.concatenate([d_q, d_kv, small_cols], axis=1).astype(BF)
        return scatter_rows(columns)

    n_grads = len(names)
    work = {
        0: [("grad", 1), (to_heads, 0)],
        1: [("grad", 2), (through_heads, 0)],
        2: [("grad", 3), (to_heads, 1)],
        3: [("grad", 4), (through_heads, 1)],
        4: [("grad", 5)],
    }
    chunks = {0: expert_grad(*names[0], passed)}
    chunks.update({i: expert_grad(*names[i], passed) for i in range(6, n_grads)})
    slots = max(n_grads, 6)
    moe = Scatter([b[1] for b in backs], n_fsdp)
    for t in range(slots + 4):
        chunks, line.held, line.results, passed, found, moe.arrays = lax.optimization_barrier(
            (chunks, line.held, line.results, passed, found, moe.arrays)
        )
        sent = chunks.pop(t, None)
        if t == 2:
            to_owners(0)
        if t == 4:
            to_owners(1)
            out_part = scatter_rows(found[0].pop("out"))
        for kind, i in work.get(t, []):
            if kind != "grad":
                kind(i)
            elif i < n_grads:
                chunks[i] = expert_grad(*names[i], passed)
        if t == 3:
            found[0]["out"] = out_grad()
        if t == 5:
            finish(0)
            finish(1)
            rest_part = projection_grads()
        if t == slots - 1:
            chunks[slots] = out_part
        if t == slots:
            chunks[slots + 1] = rest_part
        if t in (4, 5, 6):
            moe.advance()
        line.step(sent)
    totals = line.sums()
    sums = dict(zip(names, totals))
    d_down = [sums["down", e] for e in range(experts)]
    d_gate = [sums["gate", e] for e in range(experts)]
    d_up = [sums["up", e] for e in range(experts)]
    d_out, rest = [part.astype(F32) for part in totals[n_grads:]]

    outs = []
    for m in range(micros):
        outs.append(
            jnp.where(valid[m][:, None], state[m][2] + moe.arrays[m].astype(F32), 0.0).astype(BF)
        )
    grads = [f["din"] for f in found]
    q_width = w_query.shape[1]
    shape = (micros, 1, tokens, dim)
    ends = q_width + 2 * kv_width
    return (
        jnp.stack(outs).reshape(shape),
        jnp.stack(grads).reshape(shape),
        rest[:, ends + n_experts],
        rest[:, :q_width],
        rest[:, q_width : q_width + kv_width],
        rest[:, q_width + kv_width : ends],
        d_out,
        rest[:, ends + n_experts + 1],
        rest[:, ends : ends + n_experts],
        jnp.stack(d_gate).astype(F32),
        jnp.stack(d_up).astype(F32),
        jnp.stack(d_down).astype(F32),
    )


def solution(mesh):
    token_spec = P(None, "fsdp", "seq", None)
    row, matrix, cube = P("fsdp"), P("fsdp", None), P("fsdp", None, None)
    return jax.shard_map(
        functools.partial(on_device, mesh.shape["seq"], mesh.shape["fsdp"]),
        mesh=mesh,
        in_specs=(
            token_spec,
            P(None, "fsdp"),
            token_spec,
            token_spec,
            row,
            matrix,
            matrix,
            matrix,
            matrix,
            row,
            matrix,
            cube,
            cube,
            cube,
        ),
        out_specs=(
            token_spec,
            token_spec,
            row,
            matrix,
            matrix,
            matrix,
            matrix,
            row,
            matrix,
            cube,
            cube,
            cube,
        ),
        check_vma=False,
    )
```

```python
import functools

import jax
import jax.numpy as jnp
from jax import lax
from jax.experimental import pallas as pl
from jax.experimental.pallas import tpu as pltpu
from jax.sharding import PartitionSpec as P

HEAD = 64
HALF = HEAD // 2
GROUP = 3
TOPK = 8
EPS = 1e-06
THETA = 10000.0
NEGATIVE = -1e30
LANES = 128
SCALE = HEAD ** (-0.5)
BF = jnp.bfloat16
F32 = jnp.float32
VMEM_BYTES = 60 * 1024 * 1024

NN = (((1,), (0,)), ((), ()))
NT = (((1,), (1,)), ((), ()))
TN = (((0,), (0,)), ((), ()))


def dot(a, b, dims=NN):
    return lax.dot_general(a, b, dims, preferred_element_type=F32)


def params():
    return pltpu.CompilerParams(vmem_limit_bytes=VMEM_BYTES)


def cost(flops, moved, trans=0):
    parts = (int(v) // 10 for v in (flops, moved, trans))
    flops, moved, trans = parts
    return pl.CostEstimate(flops=flops, bytes_accessed=moved, transcendentals=trans)


def whole(shape):
    zeros = (0,) * len(shape)
    return pl.BlockSpec(shape, lambda *_: zeros)


def smem():
    return pl.BlockSpec(memory_space=pltpu.SMEM)


def pick(at, first_ref, second_ref, index=None):
    half = first_ref.shape[0]
    if index is None:
        index = lax.rem(at, half)
    return jnp.where(at < half, first_ref[index], second_ref[index])


def in_order(place_ref, w_refs):
    devices = 2 * w_refs[0].shape[0]
    return jnp.concatenate([pick(place_ref[j], *w_refs) for j in range(devices)], axis=0)


def rotate(rows, cosine, sine, sign):
    pieces = []
    for h in range(rows.shape[0] // HEAD):
        a = rows[h * HEAD : h * HEAD + HALF]
        b = rows[h * HEAD + HALF : (h + 1) * HEAD]
        if sign > 0:
            pieces += [a * cosine - b * sine, b * cosine + a * sine]
        else:
            pieces += [a * cosine + b * sine, b * cosine - a * sine]
    return jnp.concatenate(pieces, axis=0)


def unpack_kernel(n_experts, place_ref, wa_ref, wb_ref, router_ref, rows_ref):
    w = in_order(place_ref, (wa_ref, wb_ref))
    lane = lax.broadcasted_iota(jnp.int32, w.shape, 1)
    router_ref[...] = jnp.where(lane < n_experts, w.astype(F32), 0.0).astype(BF)
    rows_ref[...] = w.astype(F32).T


def unpack(place, w, block, n_experts):
    dim = 2 * w[0].shape[0] * w[0].shape[1]
    return pl.pallas_call(
        functools.partial(unpack_kernel, n_experts),
        name="unpack",
        grid=(1,),
        in_specs=[smem(), *w_columns(w, LANES, lambda i: block)],
        out_specs=[whole((dim, LANES)), whole((LANES, dim))],
        out_shape=[
            jax.ShapeDtypeStruct((dim, LANES), BF),
            jax.ShapeDtypeStruct((LANES, dim), F32),
        ],
        compiler_params=params(),
        cost_estimate=cost(0, 12 * dim * LANES),
    )(place, *w)


def kv_kernel(place_ref, x_ref, gain_ref, wa_ref, wb_ref, cos_ref, sin_ref, kv_ref, normed_ref):
    step = pl.program_id(0)

    @pl.when(step == 0)
    def _():
        x = x_ref[...].astype(F32)
        inv = lax.rsqrt(jnp.mean(x * x, axis=-1, keepdims=True) + EPS)
        normed_ref[...] = (x * inv * gain_ref[...]).astype(BF)
        r = dot(normed_ref[...], in_order(place_ref, (wa_ref, wb_ref)))
        r = rotate(r.T, cos_ref[...], sin_ref[...], 1)
        kv_ref[...] = r.T.astype(BF)

    @pl.when(step == 1)
    def _():
        kv_ref[...] = dot(normed_ref[...], in_order(place_ref, (wa_ref, wb_ref))).astype(BF)


def w_columns(w, tile, at):
    return [pl.BlockSpec((*half.shape[:2], tile), lambda *i: (0, 0, at(*i))) for half in w]


def kv_project(place, x, gain, w, width, cosine, sine):
    rows, dim = x.shape
    return pl.pallas_call(
        kv_kernel,
        name="kv_project",
        grid=(2,),
        in_specs=[
            smem(),
            whole((rows, dim)),
            whole((1, dim)),
            *w_columns(w, width, lambda i: i),
            whole((HALF, rows)),
            whole((HALF, rows)),
        ],
        out_specs=[pl.BlockSpec((rows, width), lambda i: (0, i)), whole((rows, dim))],
        out_shape=[
            jax.ShapeDtypeStruct((rows, 2 * width), BF),
            jax.ShapeDtypeStruct((rows, dim), BF),
        ],
        compiler_params=params(),
        cost_estimate=cost(2 * rows * dim * 2 * width, 2 * (2 * rows * dim + dim * 2 * width)),
    )(place, x, gain, *w, cosine, sine)


def q_kernel(place_ref, normed_ref, wa_ref, wb_ref, cos_ref, sin_ref, q_ref):
    r = dot(normed_ref[...], in_order(place_ref, (wa_ref, wb_ref)))
    r = rotate(r.T, cos_ref[...], sin_ref[...], 1)
    q_ref[...] = r.astype(BF) * BF(SCALE)


def q_project(place, normed, w, width, cosine, sine):
    rows, dim = normed.shape
    tile = 512
    return pl.pallas_call(
        q_kernel,
        name="q_project",
        grid=(width // tile,),
        in_specs=[
            smem(),
            whole((rows, dim)),
            *w_columns(w, tile, lambda i: i),
            whole((HALF, rows)),
            whole((HALF, rows)),
        ],
        out_specs=pl.BlockSpec((tile, rows), lambda i: (i, 0)),
        out_shape=jax.ShapeDtypeStruct((width, rows), BF),
        compiler_params=params(),
        cost_estimate=cost(2 * rows * dim * width, 2 * (2 * rows * dim + dim * width)),
    )(place, normed, *w, cosine, sine)


def side_by_side(ref, j):
    base = j * GROUP * HEAD
    return jnp.concatenate(
        [ref[base + h * HEAD : base + (h + 1) * HEAD, :] for h in range(GROUP)], axis=1
    )


def diagonal_mask(tokens, own_len):
    key = lax.broadcasted_iota(jnp.int32, (tokens, tokens), 0)
    query = lax.broadcasted_iota(jnp.int32, (tokens, tokens), 1)
    one = (key <= query) & (key < own_len)
    return jnp.concatenate([one.astype(jnp.int32)] * GROUP, axis=1) > 0


def attend_kernel(n, info_ref, q_ref, k_ref, v_ref, o_ref, ot_ref, lse_ref, m_ref, l_ref, acc_ref):
    tokens = q_ref.shape[1]
    d = pl.program_id(1)
    s = info_ref[0]
    own_len = info_ref[1] - s * tokens
    active = own_len > 0

    def pair(j):
        cols = slice(j * HEAD, (j + 1) * HEAD)
        scores = dot(k_ref[0, :, cols], side_by_side(q_ref, j))
        return scores, v_ref[0, :, cols].astype(F32).T.astype(BF)

    @pl.when(active & (d == 0))
    def _():
        mask = diagonal_mask(tokens, own_len)
        for j in range(2):
            scores, value_t = pair(j)
            scores = jnp.where(mask, scores, NEGATIVE)
            top = jnp.max(scores, axis=0, keepdims=True)
            p = jnp.exp(scores - top)
            l_ref[j : j + 1] = jnp.sum(p, axis=0, keepdims=True)
            acc_ref[j] = dot(value_t, p.astype(BF))
            m_ref[j : j + 1] = top

    @pl.when(active & (d > 0) & (d <= s))
    def _():
        for j in range(2):
            scores, value_t = pair(j)
            old = m_ref[j : j + 1]
            top = jnp.maximum(old, jnp.max(scores, axis=0, keepdims=True))
            keep = jnp.exp(old - top)
            p = jnp.exp(scores - top)
            l_ref[j : j + 1] = l_ref[j : j + 1] * keep + jnp.sum(p, axis=0, keepdims=True)
            acc_ref[j] = acc_ref[j] * keep + dot(value_t, p.astype(BF))
            m_ref[j : j + 1] = top

    @pl.when(active & (d == n - 1))
    def _():
        pieces = []
        for j in range(2):
            out = acc_ref[j] / l_ref[j : j + 1]
            lse_ref[j : j + 1] = m_ref[j : j + 1] + jnp.log(l_ref[j : j + 1])
            pieces += [out[:, h * tokens : (h + 1) * tokens] for h in range(GROUP)]
        out = jnp.concatenate(pieces, axis=0)
        ot_ref[...] = out.astype(BF)
        o_ref[...] = out.T.astype(BF)

    @pl.when(jnp.logical_not(active) & (d == 0))
    def _():
        o_ref[...] = jnp.zeros_like(o_ref)
        ot_ref[...] = jnp.zeros_like(ot_ref)
        lse_ref[...] = jnp.zeros_like(lse_ref)


def owner(info_ref, d, n):
    return lax.rem(info_ref[0] + n - d, n)


def attend(info, q_t, kv, micro, tokens):
    n = kv.shape[0]
    width = q_t.shape[0]
    kv_width = kv.shape[2] // 2
    steps = kv_width // LANES
    qw = width // steps
    return pl.pallas_call(
        functools.partial(attend_kernel, n),
        name="attend",
        grid_spec=pltpu.PrefetchScalarGridSpec(
            num_scalar_prefetch=1,
            grid=(steps, n),
            in_specs=[
                pl.BlockSpec((qw, tokens), lambda i, d, info: (i, micro)),
                pl.BlockSpec((1, tokens, LANES), lambda i, d, info: (owner(info, d, n), 0, i)),
                pl.BlockSpec(
                    (1, tokens, LANES), lambda i, d, info: (owner(info, d, n), 0, steps + i)
                ),
            ],
            out_specs=[
                pl.BlockSpec((tokens, qw), lambda i, d, info: (0, i)),
                pl.BlockSpec((qw, tokens), lambda i, d, info: (i, 0)),
                pl.BlockSpec((8, GROUP * tokens), lambda i, d, info: (i, 0)),
            ],
            scratch_shapes=[
                pltpu.VMEM((8, GROUP * tokens), F32),
                pltpu.VMEM((8, GROUP * tokens), F32),
                pltpu.VMEM((2, HEAD, GROUP * tokens), F32),
            ],
        ),
        out_shape=[
            jax.ShapeDtypeStruct((tokens, width), BF),
            jax.ShapeDtypeStruct((width, tokens), BF),
            jax.ShapeDtypeStruct((8 * steps, GROUP * tokens), F32),
        ],
        compiler_params=params(),
        cost_estimate=cost(
            4 * 4 * width * tokens * tokens * n,
            2 * (3 * width * tokens + n * tokens * 2 * kv_width),
            width // HEAD * tokens * tokens * n,
        ),
    )(info, q_t, kv, kv)


def attend_back_kernel(
    n, info_ref, q_ref, g_ref, o_ref, lse_ref, cos_ref, sin_ref, k_ref, v_ref, gq_ref, dkv_ref, acc_ref
):
    tokens = q_ref.shape[1]
    d = pl.program_id(1)
    s = info_ref[0]
    own_len = info_ref[1] - s * tokens
    active = own_len > 0

    def block(first):
        mask = diagonal_mask(tokens, own_len) if first else None
        dks, dvs = [], []
        for j in range(2):
            cols = slice(j * HEAD, (j + 1) * HEAD)
            key, value = k_ref[0, :, cols], v_ref[0, :, cols]
            query, grad = side_by_side(q_ref, j), side_by_side(g_ref, j)
            out = side_by_side(o_ref, j)
            inner = jnp.sum(grad.astype(F32) * out.astype(F32), axis=0, keepdims=True)
            p = jnp.exp(dot(key, query) - lse_ref[j : j + 1])
            if first:
                p = jnp.where(mask, p, 0.0)
            dp = dot(value, grad)
            ds = (p * (dp - inner)).astype(BF)
            dvs.append(dot(p.astype(BF), grad, NT))
            dks.append(dot(ds, query, NT))
            part = dot(key.astype(F32).T.astype(BF), ds)
            if first:
                acc_ref[j] = part
            else:
                acc_ref[j] += part
        dkv_ref[0, 0] = jnp.concatenate(dks, axis=1).astype(BF)
        dkv_ref[0, 1] = jnp.concatenate(dvs, axis=1).astype(BF)

    pl.when(active & (d == 0))(lambda: block(True))
    pl.when(active & (d > 0) & (d <= s))(lambda: block(False))

    @pl.when(active & (d == n - 1))
    def _():
        pieces = []
        for j in range(2):
            for h in range(GROUP):
                piece = acc_ref[j, :, h * tokens : (h + 1) * tokens] * SCALE
                pieces.append(piece.astype(BF).astype(F32))
        grad_q = rotate(jnp.concatenate(pieces, axis=0), cos_ref[...], sin_ref[...], -1)
        gq_ref[...] = grad_q.T.astype(BF)

    @pl.when(jnp.logical_not(active) | (d > s))
    def _():
        dkv_ref[...] = jnp.zeros_like(dkv_ref)

    @pl.when(jnp.logical_not(active) & (d == 0))
    def _():
        gq_ref[...] = jnp.zeros_like(gq_ref)


def attend_back(info, q_t, g_t, o_t, lse, cosine, sine, kv, micro, tokens):
    n = kv.shape[0]
    width = q_t.shape[0]
    kv_width = kv.shape[2] // 2
    steps = kv_width // LANES
    qw = width // steps
    transposed = pl.BlockSpec((qw, tokens), lambda i, d, info: (i, 0))
    return pl.pallas_call(
        functools.partial(attend_back_kernel, n),
        name="attend_back",
        grid_spec=pltpu.PrefetchScalarGridSpec(
            num_scalar_prefetch=1,
            grid=(steps, n),
            in_specs=[
            pl.BlockSpec((qw, tokens), lambda i, d, info: (i, micro)),
            transposed,
            transposed,
            pl.BlockSpec((8, GROUP * tokens), lambda i, d, info: (i, 0)),
            whole((HALF, tokens)),
            whole((HALF, tokens)),
            pl.BlockSpec((1, tokens, LANES), lambda i, d, info: (owner(info, d, n), 0, i)),
            pl.BlockSpec(
                (1, tokens, LANES), lambda i, d, info: (owner(info, d, n), 0, steps + i)
            ),
        ],
        out_specs=[
            pl.BlockSpec((tokens, qw), lambda i, d, info: (0, i)),
            pl.BlockSpec(
                (1, 2, tokens, LANES), lambda i, d, info: (owner(info, d, n), 0, 0, i)
            ),
        ],
            scratch_shapes=[pltpu.VMEM((2, HEAD, GROUP * tokens), F32)],
        ),
        out_shape=[
            jax.ShapeDtypeStruct((tokens, width), BF),
            jax.ShapeDtypeStruct((n, 2, tokens, kv_width), BF),
        ],
        compiler_params=params(),
        cost_estimate=cost(
            10 * 4 * width * tokens * tokens * n,
            2 * (4 * width * tokens + 2 * n * tokens * 2 * kv_width),
            width // HEAD * tokens * tokens * n,
        ),
    )(info, q_t, g_t, o_t, lse, cosine, sine, kv, kv)


def after_kernel(
    steps, place_ref, a_ref, wa_ref, wb_ref, x_ref, gain_ref, router_ref, chosen_ref, res_ref, xg_ref, ge_ref, acc_ref
):
    step = pl.program_id(0)
    acc_ref[step] = dot(a_ref[...], in_order(place_ref, (wa_ref, wb_ref)))

    @pl.when(step == steps - 1)
    def _():
        dim = x_ref.shape[1]
        product = jnp.concatenate([acc_ref[i] for i in range(steps)], axis=1)
        residual = x_ref[...].astype(F32) + product
        res_ref[...] = residual
        inv = lax.rsqrt(jnp.mean(residual * residual, axis=-1, keepdims=True) + EPS)
        normed = (residual * inv * gain_ref[...]).astype(BF)
        logits = dot(normed, router_ref[...])
        chosen = chosen_ref[...] > 0
        logits = jnp.where(chosen, logits, NEGATIVE)
        top = jnp.max(logits, axis=-1, keepdims=True)
        e = jnp.where(chosen, jnp.exp(logits - top), 0.0)
        exact = e / jnp.sum(e, axis=-1, keepdims=True)
        ge_ref[...] = exact
        xg_ref[:, :dim] = normed
        xg_ref[:, dim:] = exact.astype(BF)


def after_attention(place, attn, w, first, x, micro, gain, router, chosen):
    tokens, width = attn.shape
    dim = x.shape[1]
    tile = 512
    steps = dim // tile
    return pl.pallas_call(
        functools.partial(after_kernel, steps),
        name="after_attention",
        grid=(steps,),
        in_specs=[
            smem(),
            whole((tokens, width)),
            *w_columns(w, tile, lambda i: first // tile + i),
            pl.BlockSpec((tokens, dim), lambda i: (micro, 0)),
            whole((1, dim)),
            whole((dim, LANES)),
            pl.BlockSpec((tokens, LANES), lambda i: (micro, 0)),
        ],
        out_specs=[
            whole((tokens, dim)),
            whole((tokens, dim + LANES)),
            whole((tokens, LANES)),
        ],
        out_shape=[
            jax.ShapeDtypeStruct((tokens, dim), F32),
            jax.ShapeDtypeStruct((tokens, dim + LANES), BF),
            jax.ShapeDtypeStruct((tokens, LANES), F32),
        ],
        scratch_shapes=[pltpu.VMEM((steps, tokens, tile), F32)],
        compiler_params=params(),
        cost_estimate=cost(2 * tokens * width * dim, 2 * width * dim + 10 * tokens * dim),
    )(place, attn, *w, x, gain, router, chosen)


def expert_kernel(
    experts, half, own_ref, order_ref, xg_ref, ga_ref, gb_ref, wg_ref, wu_ref, wd_ref, ya_ref, yb_ref, back_ref, hg_ref, gp_ref
):
    rows, dim = ga_ref.shape
    hidden = wg_ref.shape[2]
    x = xg_ref[:, :dim]
    step = pl.program_id(0)
    g = jnp.where(step < half, ga_ref[...], gb_ref[...])
    gates = xg_ref[:, dim:].astype(F32)
    lane = lax.broadcasted_iota(jnp.int32, (rows, LANES), 1)
    gate_cols = jnp.zeros((rows, LANES), F32)
    for e in range(experts):
        mine = lane == own_ref[0] + e
        gate = jnp.sum(jnp.where(mine, gates, 0.0), axis=1, keepdims=True)
        pre_gate = dot(x, wg_ref[e])
        pre_up = dot(x, wu_ref[e])
        grad_hidden = dot(g, wd_ref[e], NT)
        sig = 1.0 / (1.0 + jnp.exp(-pre_gate))
        silu = pre_gate * sig
        h = (silu * pre_up).astype(BF).astype(F32)
        per_gate = jnp.sum(h * grad_hidden, axis=1, keepdims=True)
        gate_cols = jnp.where(mine, per_gate, gate_cols)
        hg_ref[:, e * hidden : (e + 1) * hidden] = (gate * h).astype(BF)
        gh = gate * grad_hidden
        base = 2 * e * hidden
        gp_ref[:, base : base + hidden] = (
            gh * pre_up * (sig * (1.0 + pre_gate * (1.0 - sig)))
        ).astype(BF)
        gp_ref[:, base + hidden : base + 2 * hidden] = (gh * silu).astype(BF)
    y = dot(hg_ref[:, :hidden], wd_ref[0])
    for e in range(1, experts):
        y += dot(hg_ref[:, e * hidden : (e + 1) * hidden], wd_ref[e])

    @pl.when(step < half)
    def _():
        ya_ref[...] = y.astype(BF)

    @pl.when(step >= half)
    def _():
        yb_ref[...] = y.astype(BF)

    back = None
    for e in range(experts):
        base = 2 * e * hidden
        part = dot(gp_ref[:, base : base + hidden], wg_ref[e], NT)
        part += dot(gp_ref[:, base + hidden : base + 2 * hidden], wu_ref[e], NT)
        back = part if back is None else back + part
    back_ref[:, :dim] = back.astype(BF)
    back_ref[:, dim:] = gate_cols.astype(BF)


def run_experts(own, order, xg, g, w_gate, w_up, w_down):
    rows = xg.shape[0]
    dim = g[0].shape[1]
    experts, _, hidden = w_gate.shape
    devices = order.shape[0]
    tile, half = rows // devices, devices // 2
    named = lambda width: pl.BlockSpec((tile, width), lambda i, own, order: (order[i], 0))
    first = lambda i: jnp.minimum(i, half - 1)
    second = lambda i: jnp.maximum(i - half, 0)
    return pl.pallas_call(
        functools.partial(expert_kernel, experts, half),
        name="run_experts",
        grid_spec=pltpu.PrefetchScalarGridSpec(
            num_scalar_prefetch=2,
            grid=(devices,),
            in_specs=[
                named(dim + LANES),
                pl.BlockSpec((tile, dim), lambda i, *_: (first(i), 0)),
                pl.BlockSpec((tile, dim), lambda i, *_: (second(i), 0)),
                whole(w_gate.shape),
                whole(w_up.shape),
                whole(w_down.shape),
            ],
            out_specs=[
                pl.BlockSpec((tile, dim), lambda i, *_: (first(i), 0)),
                pl.BlockSpec((tile, dim), lambda i, *_: (second(i), 0)),
                named(dim + LANES),
                pl.BlockSpec((tile, experts * hidden), lambda i, *_: (i, 0)),
                named(2 * experts * hidden),
            ],
        ),
        out_shape=[
            jax.ShapeDtypeStruct((rows // 2, dim), BF),
            jax.ShapeDtypeStruct((rows // 2, dim), BF),
            jax.ShapeDtypeStruct((rows, dim + LANES), BF),
            jax.ShapeDtypeStruct((rows, experts * hidden), BF),
            jax.ShapeDtypeStruct((rows, 2 * experts * hidden), BF),
        ],
        compiler_params=params(),
        cost_estimate=cost(
            12 * rows * dim * hidden * experts,
            2 * (4 * rows * dim + 3 * rows * experts * hidden + 3 * experts * dim * hidden),
            rows * experts * hidden,
        ),
    )(own, order, xg, *g, w_gate, w_up, w_down)


def wide_grad_kernel(steps, micros, *refs):
    a_refs, b_refs = refs[:micros], refs[micros : 2 * micros]
    out_ref, acc_ref = refs[2 * micros :]
    step = pl.program_id(0)
    for m in range(micros):

        @pl.when((step >= m * steps) & (step < (m + 1) * steps))
        def _(m=m):
            part = dot(a_refs[m][...], b_refs[m][...], TN)
            if m == 0:

                @pl.when(step == 0)
                def _():
                    acc_ref[...] = part

                @pl.when(step > 0)
                def _():
                    acc_ref[...] += part
            else:
                acc_ref[...] += part

    @pl.when(step == micros * steps - 1)
    def _():
        out_ref[...] = acc_ref[...].astype(BF)


def wide_grad(lefts, left_block, left_width, rights, right_block, right_width, tile=512):
    micros, rows = len(lefts), lefts[0].shape[0]
    steps = rows // tile

    def spec(m, width, column):
        return pl.BlockSpec(
            (tile, width), lambda i: (jnp.clip(i - m * steps, 0, steps - 1), column)
        )

    return pl.pallas_call(
        functools.partial(wide_grad_kernel, steps, micros),
        name="wide_grad",
        grid=(micros * steps,),
        in_specs=[spec(m, left_width, left_block) for m in range(micros)]
        + [spec(m, right_width, right_block) for m in range(micros)],
        out_specs=whole((left_width, right_width)),
        out_shape=jax.ShapeDtypeStruct((left_width, right_width), BF),
        scratch_shapes=[pltpu.VMEM((left_width, right_width), F32)],
        compiler_params=params(),
        cost_estimate=cost(
            2 * micros * rows * left_width * right_width,
            2 * (micros * rows * (left_width + right_width) + left_width * right_width),
        ),
    )(*lefts, *rights)


def down_grad_kernel(micros, devices, *refs):
    hg_refs, refs = refs[:micros], refs[micros:]
    ga_refs, gb_refs = refs[:micros], refs[micros : 2 * micros]
    out_ref, acc_ref = refs[2 * micros :]
    step = pl.program_id(0)
    g = [jnp.where(step < devices // 2, a[...], b[...]) for a, b in zip(ga_refs, gb_refs)]
    part = dot(jnp.concatenate(g), jnp.concatenate([r[...] for r in hg_refs]), TN)

    @pl.when(step == 0)
    def _():
        acc_ref[...] = part

    @pl.when(step > 0)
    def _():
        acc_ref[...] += part

    @pl.when(step == devices - 1)
    def _():
        out_ref[...] = acc_ref[...].astype(BF)


def down_grad(hgs, expert, hidden, gs, devices):
    micros, rows = len(hgs), hgs[0].shape[0]
    tile, half = rows // devices, devices // 2
    dim = gs[0][0].shape[1]
    return pl.pallas_call(
        functools.partial(down_grad_kernel, micros, devices),
        name="down_grad",
        grid=(devices,),
        in_specs=[pl.BlockSpec((tile, hidden), lambda i: (i, expert))] * micros
        + [pl.BlockSpec((tile, dim), lambda i: (jnp.minimum(i, half - 1), 0))] * micros
        + [pl.BlockSpec((tile, dim), lambda i: (jnp.maximum(i - half, 0), 0))] * micros,
        out_specs=whole((dim, hidden)),
        out_shape=jax.ShapeDtypeStruct((dim, hidden), BF),
        scratch_shapes=[pltpu.VMEM((dim, hidden), F32)],
        compiler_params=params(),
        cost_estimate=cost(2 * micros * rows * hidden * dim, 2 * micros * rows * (hidden + dim)),
    )(*hgs, *[g[0] for g in gs], *[g[1] for g in gs])


def before_kernel(
    steps, place_ref, ret_ref, res_ref, ge_ref, gout_ref, gain_ref, router_ref, wa_ref, wb_ref, gres_ref, ga_ref, gt_ref, small_ref, cut_ref, acc_ref
):
    dim = res_ref.shape[1]

    step = pl.program_id(0)
    tile = dim // steps

    @pl.when(step == 0)
    def _():
        ge = ge_ref[...]
        gg = ret_ref[:, dim:].astype(F32)
        gl = ge * (gg - jnp.sum(ge * gg, axis=-1, keepdims=True))
        high = gl.astype(BF)
        low = (gl - high.astype(F32)).astype(BF)
        router = router_ref[...]
        gn = ret_ref[:, :dim].astype(F32) + (dot(high, router, NT) + dot(low, router, NT))
        residual = res_ref[...]
        gain = gain_ref[...]
        inv = lax.rsqrt(jnp.mean(residual * residual, axis=-1, keepdims=True) + EPS)
        unit = residual * inv
        normed = (unit * gain).astype(BF)
        small_ref[:LANES] = dot(high, normed, TN) + dot(low, normed, TN)
        gain_row = jnp.sum(gn * unit, axis=0, keepdims=True)
        small_ref[LANES:] = jnp.broadcast_to(gain_row, (8, dim))
        u = gn * gain
        gres = gout_ref[...].astype(F32) + inv * (
            u - unit * jnp.mean(u * unit, axis=-1, keepdims=True)
        )
        gres_ref[...] = gres
        low_gres = gres.astype(BF)
        ga_ref[...] = low_gres
        for i in range(steps):
            cut_ref[i] = low_gres[:, i * tile : (i + 1) * tile]
        acc_ref[...] = jnp.zeros_like(acc_ref)

    acc_ref[...] += dot(in_order(place_ref, (wa_ref, wb_ref)), cut_ref[step], NT)

    @pl.when(step == steps - 1)
    def _():
        gt_ref[...] = acc_ref[...].astype(BF)


def before_attention(place, returned, residual, exact, gout, gain, router, w, first):
    tokens, dim = residual.shape
    width = 2 * w[0].shape[0] * w[0].shape[1]
    tile = 512
    steps = dim // tile
    return pl.pallas_call(
        functools.partial(before_kernel, steps),
        name="before_attention",
        grid=(steps,),
        in_specs=[
            smem(),
            whole((tokens, dim + LANES)),
            whole((tokens, dim)),
            whole((tokens, LANES)),
            whole((tokens, dim)),
            whole((1, dim)),
            whole((dim, LANES)),
            *w_columns(w, tile, lambda i: first // tile + i),
        ],
        out_specs=[
            whole((tokens, dim)),
            whole((tokens, dim)),
            whole((width, tokens)),
            whole((LANES + 8, dim)),
        ],
        out_shape=[
            jax.ShapeDtypeStruct((tokens, dim), F32),
            jax.ShapeDtypeStruct((tokens, dim), BF),
            jax.ShapeDtypeStruct((width, tokens), BF),
            jax.ShapeDtypeStruct((LANES + 8, dim), F32),
        ],
        scratch_shapes=[
            pltpu.VMEM((steps, tokens, tile), BF),
            pltpu.VMEM((width, tokens), F32),
        ],
        compiler_params=params(),
        cost_estimate=cost(2 * tokens * width * dim, 2 * width * dim + 14 * tokens * dim),
    )(place, returned, residual, exact, gout, gain, router, *w)


def last_kernel(
    q_steps, steps, place_ref, gq_ref, dkv_ref, qa_ref, qb_ref, kva_ref, kvb_ref, x_ref, gain_ref, gres_ref, din_ref, small_ref, acc_ref
):
    step = pl.program_id(0)

    @pl.when(step == 0)
    def _():
        acc_ref[...] = dot(gq_ref[...], in_order(place_ref, (qa_ref, qb_ref)), NT)

    @pl.when((step > 0) & (step < q_steps))
    def _():
        acc_ref[...] += dot(gq_ref[...], in_order(place_ref, (qa_ref, qb_ref)), NT)

    @pl.when(step >= q_steps)
    def _():
        acc_ref[...] += dot(dkv_ref[...], in_order(place_ref, (kva_ref, kvb_ref)), NT)

    @pl.when(step == steps - 1)
    def _():
        x = x_ref[...].astype(F32)
        gain = gain_ref[...]
        inv = lax.rsqrt(jnp.mean(x * x, axis=-1, keepdims=True) + EPS)
        unit = x * inv
        gn = acc_ref[...]
        small_ref[...] = jnp.broadcast_to(
            jnp.sum(gn * unit, axis=0, keepdims=True), small_ref.shape
        )
        w = gn * gain
        grad = inv * (w - unit * jnp.mean(w * unit, axis=-1, keepdims=True))
        din_ref[...] = (grad + gres_ref[...]).astype(BF)


def last_step(place, gq, dkv, w_q, w_kv, x, micro, gain, gres):
    tokens, dim = gres.shape
    tile = 512
    q_steps, kv_steps = gq.shape[1] // tile, dkv.shape[1] // tile
    steps = q_steps + kv_steps
    q_at = lambda i: (0, jnp.minimum(i, q_steps - 1))
    kv_at = lambda i: (0, jnp.maximum(i - q_steps, 0))
    return pl.pallas_call(
        functools.partial(last_kernel, q_steps, steps),
        name="last_step",
        grid=(steps,),
        in_specs=[
            smem(),
            pl.BlockSpec((tokens, tile), q_at),
            pl.BlockSpec((tokens, tile), kv_at),
            *w_columns(w_q, tile, lambda i: q_at(i)[1]),
            *w_columns(w_kv, tile, lambda i: kv_at(i)[1]),
            pl.BlockSpec((tokens, dim), lambda i: (micro, 0)),
            whole((1, dim)),
            whole((tokens, dim)),
        ],
        out_specs=[whole((tokens, dim)), whole((8, dim))],
        out_shape=[
            jax.ShapeDtypeStruct((tokens, dim), BF),
            jax.ShapeDtypeStruct((8, dim), F32),
        ],
        scratch_shapes=[pltpu.VMEM((tokens, dim), F32)],
        compiler_params=params(),
        cost_estimate=cost(
            2 * tokens * steps * tile * dim, 2 * steps * tile * dim + 12 * tokens * dim
        ),
    )(place, gq, dkv, *w_q, *w_kv, x, gain, gres)


def out_grad_kernel(micros, half, order_ref, *refs):
    t_refs, g_refs, (first_ref, second_ref) = refs[:micros], refs[micros : 2 * micros], refs[2 * micros :]
    step = pl.program_id(0)
    total = dot(t_refs[0][...], g_refs[0][...])
    for t_ref, g_ref in zip(t_refs[1:], g_refs[1:]):
        total += dot(t_ref[...], g_ref[...])

    @pl.when(step < half)
    def _():
        first_ref[...] = total.astype(BF)

    @pl.when(step >= half)
    def _():
        second_ref[...] = total.astype(BF)


def out_grad(order, heads_t, grads):
    micros, devices = len(heads_t), order.shape[0]
    width, tokens = heads_t[0].shape
    dim = grads[0].shape[1]
    tile, half = width // devices, devices // 2
    return pl.pallas_call(
        functools.partial(out_grad_kernel, micros, half),
        name="out_grad",
        grid_spec=pltpu.PrefetchScalarGridSpec(
            num_scalar_prefetch=1,
            grid=(devices,),
            in_specs=[pl.BlockSpec((tile, tokens), lambda i, order: (order[i], 0))] * micros
            + [whole((tokens, dim))] * micros,
            out_specs=[
                pl.BlockSpec((tile, dim), lambda i, order: (jnp.minimum(i, half - 1), 0)),
                pl.BlockSpec((tile, dim), lambda i, order: (jnp.maximum(i - half, 0), 0)),
            ],
        ),
        out_shape=[jax.ShapeDtypeStruct((width // 2, dim), BF)] * 2,
        compiler_params=params(),
        cost_estimate=cost(2 * micros * tokens * width * dim, 4 * width * dim),
    )(order, *heads_t, *grads)


def turn_kernel(kv_ref, cos_ref, sin_ref, out_ref):
    width = kv_ref.shape[2]
    key = rotate(kv_ref[0].astype(F32).T, cos_ref[...], sin_ref[...], -1)
    out_ref[:, :width] = key.T.astype(BF)
    out_ref[:, width:] = kv_ref[1]


def turn_back(kv, cosine, sine):
    _, tokens, width = kv.shape
    return pl.pallas_call(
        turn_kernel,
        name="turn_back",
        out_shape=jax.ShapeDtypeStruct((tokens, 2 * width), BF),
        compiler_params=params(),
        cost_estimate=cost(0, 8 * tokens * width),
    )(kv, cosine, sine)


def projection_kernel(micros, q_steps, steps, n_experts, normed_ref, *refs):
    gq_refs, refs = refs[:micros], refs[micros:]
    dkv_refs, refs = refs[:micros], refs[micros:]
    two_refs, refs = refs[:micros], refs[micros:]
    one_refs, (out_ref, turned_ref) = refs[:micros], refs[micros:]
    step = pl.program_id(0)
    tile = gq_refs[0].shape[1]

    @pl.when(step == 0)
    def _():
        turned_ref[...] = normed_ref[...].astype(F32).T.astype(BF)
        rows = functools.reduce(jnp.add, [r[:LANES] for r in two_refs])
        gain_two = functools.reduce(jnp.add, [r[LANES : LANES + 1] for r in two_refs])
        gain_one = functools.reduce(jnp.add, [r[:1] for r in one_refs])
        at = lax.broadcasted_iota(jnp.int32, rows.shape, 0)
        rows = jnp.where(at == n_experts, gain_one, rows)
        rows = jnp.where(at == n_experts + 1, gain_two, rows)
        out_ref[:, steps * tile :] = rows.T.astype(BF)

    q = jnp.concatenate([r[...] for r in gq_refs], axis=0)
    kv = jnp.concatenate([r[...] for r in dkv_refs], axis=0)
    g = jnp.where(step < q_steps, q, kv)
    out_ref[:, pl.ds(pl.multiple_of(step * tile, tile), tile)] = dot(turned_ref[...], g).astype(BF)


def projection_grads(normed, gqs, dkvs, twos, ones, n_experts):
    rows, dim = normed.shape
    micros, tokens, tile = len(gqs), gqs[0].shape[0], 512
    q_steps, kv_steps = gqs[0].shape[1] // tile, dkvs[0].shape[1] // tile
    steps = q_steps + kv_steps
    width = steps * tile + LANES
    return pl.pallas_call(
        functools.partial(projection_kernel, micros, q_steps, steps, n_experts),
        name="projection_grads",
        grid=(steps,),
        in_specs=[whole((rows, dim))]
        + [pl.BlockSpec((tokens, tile), lambda i: (0, jnp.minimum(i, q_steps - 1)))] * micros
        + [pl.BlockSpec((tokens, tile), lambda i: (0, jnp.maximum(i - q_steps, 0)))] * micros
        + [whole(twos[0].shape)] * micros
        + [whole(ones[0].shape)] * micros,
        out_specs=whole((dim, width)),
        out_shape=jax.ShapeDtypeStruct((dim, width), BF),
        scratch_shapes=[pltpu.VMEM((dim, rows), BF)],
        compiler_params=params(),
        cost_estimate=cost(2 * rows * dim * width, 2 * rows * (dim + width) + 2 * dim * width),
    )(normed, *gqs, *dkvs, *twos, *ones)


def add_low(a, b):
    return (a.astype(F32) + b.astype(F32)).astype(BF)


def line_sum(x, n):
    if n == 1:
        return x
    if n % 2:
        return lax.psum(x, "seq")
    half = n // 2
    at = lax.axis_index("seq")
    for k in range(half - 1):
        x = add_low(x, lax.ppermute(x, "seq", [(k, k + 1), (n - 1 - k, n - 2 - k)]))
    x = add_low(x, lax.ppermute(x, "seq", [(half - 1, half), (half, half - 1)]))
    for k in reversed(range(half - 1)):
        got = lax.ppermute(x, "seq", [(k + 1, k), (n - 2 - k, n - 1 - k)])
        x = jnp.where((at == k) | (at == n - 1 - k), got, x)
    return x


class Line:
    def __init__(self, n):
        self.n = n
        self.held = {}
        self.results = []

    def sums(self):
        at = lax.axis_index("seq")
        middle = (at == 1) | (at == 2)
        return [r[0] if len(r) == 1 else jnp.where(middle, *r) for r in self.results]

    def step(self, chunk, beside):
        n = self.n
        if n != 4:
            if chunk is not None:
                self.results.append((line_sum(chunk, n),))
            return
        at = lax.axis_index("seq")
        middle = (at == 1) | (at == 2)
        come, go = [(0, 1), (3, 2)], [(1, 0), (2, 3)]
        held, self.held = self.held, {}
        summed = held.get("summed")
        if summed is not None:
            summed = add_low(*summed)
        crossing = held.get("crossing")
        if crossing is not None:
            crossing = add_low(*crossing)
            self.held["summed"] = (crossing, lax.ppermute(crossing, "seq", [(1, 2), (2, 1)]))
        if chunk is not None and summed is not None and chunk.shape == summed.shape:
            sent = jnp.where(middle, summed, chunk)
            got = lax.ppermute(sent, "seq", come + go)
            self.results.append((sent, got))
            self.held["crossing"] = (chunk, got)
        else:
            if summed is not None:
                self.results.append((summed, lax.ppermute(summed, "seq", go)))
            if chunk is not None:
                self.held["crossing"] = (chunk, lax.ppermute(chunk, "seq", come))
        self.held, self.results = gate((self.held, self.results), beside)


def gate(x, *others):
    return lax.optimization_barrier((x, others))[0]


CORE, ALONG_X, ALONG_Y = 1, 2, 4


def swap(x, mask):
    return lax.ppermute(x, "fsdp", [(i, i ^ mask) for i in range(8)])


def gather_rows(x):
    return lax.all_gather(x, "fsdp", axis=0, tiled=True)


def assemble_kernel(x_ref, top_x_ref, low_y_ref, top_far_ref, low_far_ref, out_ref):
    rows = x_ref.shape[0]
    half = rows // 2
    out_ref[:rows] = x_ref[...]
    out_ref[rows : rows + half] = top_x_ref[...]
    out_ref[rows + half : 2 * rows] = low_far_ref[:half]
    out_ref[2 * rows : 2 * rows + half] = top_far_ref[:half]
    out_ref[2 * rows + half : 3 * rows] = low_y_ref[...]
    out_ref[3 * rows : 3 * rows + half] = top_far_ref[half:]
    out_ref[3 * rows + half :] = low_far_ref[half:]


def assemble(*pieces):
    rows, width = pieces[0].shape
    block = lambda n: pl.BlockSpec((n, width // 3), lambda i: (0, i))
    return pl.pallas_call(
        assemble_kernel,
        name="assemble",
        grid=(3,),
        in_specs=[block(p.shape[0]) for p in pieces],
        out_specs=block(4 * rows),
        out_shape=jax.ShapeDtypeStruct((4 * rows, width), pieces[0].dtype),
        compiler_params=params(),
        cost_estimate=cost(0, 16 * rows * width),
    )(*pieces)


def gather_near(x, n):
    if n != 8:
        every = gather_rows(x)
        half = every.shape[0] // 2
        return every[:half], every[half:]
    gather = Gather(x, n)
    gather.further()
    return gather.finish()


class Gather:
    def __init__(self, x, n):
        self.n, self.x = n, x
        if n != 8:
            self.halves = gather_near(x, n)
            self.near = self.far = ()
            return
        half = x.shape[0] // 2
        self.near = swap(x[:half], ALONG_X), swap(x[half:], ALONG_Y)

    def further(self, *others):
        if self.n != 8:
            return
        half = self.x.shape[0] // 2
        x, (top_x, low_y) = gate((self.x, self.near), *others)
        self.near = top_x, low_y
        top_far = swap(jnp.concatenate([x[:half], top_x]), ALONG_Y)
        low_far = swap(jnp.concatenate([x[half:], low_y]), ALONG_X)
        self.far = top_far, low_far

    def finish(self, *others):
        if self.n != 8:
            return self.halves
        near, far = gate((self.near, self.far), *others)
        mine = assemble(self.x, *near, *far)
        return mine, swap(mine, CORE)


class Scatter:
    def __init__(self, arrays, n):
        self.arrays, self.n, self.stage = list(arrays), n, 0
        self.rows = 2 * arrays[0][0].shape[0] // n

    def advance(self):
        held, self.stage = self.arrays, self.stage + 1
        rows, half = self.rows, self.rows // 2
        if self.n != 8:
            if self.stage == 1:
                self.arrays = [scatter_rows(jnp.concatenate(a)) for a in held]
            return
        if self.stage == 1:
            self.arrays = [add_low(mine, swap(other, CORE)) for mine, other in held]
        if self.stage == 2:
            tops = [a[k * rows : k * rows + half] for a in held for k in (2, 3)]
            lows = [a[k * rows + half : (k + 1) * rows] for a in held for k in (1, 3)]
            tops = swap(jnp.concatenate(tops), ALONG_Y)
            lows = swap(jnp.concatenate(lows), ALONG_X)
            self.arrays = []
            for i, a in enumerate(held):
                at = 2 * i * half
                self.arrays.append(
                    (
                        add_low(a[:half], tops[at : at + half]),
                        add_low(a[half:rows], lows[at : at + half]),
                        add_low(a[rows : rows + half], tops[at + half : at + rows]),
                        add_low(a[2 * rows + half : 3 * rows], lows[at + half : at + rows]),
                    )
                )
        if self.stage == 3:
            over_x = swap(jnp.concatenate([a[2] for a in held]), ALONG_X)
            over_y = swap(jnp.concatenate([a[3] for a in held]), ALONG_Y)
            self.arrays = [
                jnp.concatenate(
                    [
                        add_low(a[0], over_x[i * half : (i + 1) * half]),
                        add_low(a[1], over_y[i * half : (i + 1) * half]),
                    ]
                )
                for i, a in enumerate(held)
            ]


def block_order(n):
    at = jnp.arange(n, dtype=jnp.int32)
    if n != 8:
        return at
    return lax.axis_index("fsdp").astype(jnp.int32) ^ (2 * lax.rem(at, 4) + at // 4)


def block_places(n):
    if n != 8:
        return jnp.arange(n, dtype=jnp.int32)
    mask = lax.axis_index("fsdp").astype(jnp.int32) ^ jnp.arange(n, dtype=jnp.int32)
    return (mask >> 1) + 4 * (mask & 1)


def scatter_rows(x):
    return lax.psum_scatter(x, "fsdp", scatter_dimension=0, tiled=True)


def on_device(
    n_seq,
    n_fsdp,
    inputs,
    lengths,
    expert_ids,
    cotangent,
    gain_attn,
    w_query,
    key_projection,
    value_projection,
    w_out,
    gain_moe,
    router,
    w_gate,
    w_up,
    w_down,
):
    micros, local_seqs, tokens, dim = inputs.shape
    assert local_seqs == 1
    rows = micros * tokens
    experts, _, hidden = w_gate.shape
    n_experts = router.shape[1]
    kv_width = key_projection.shape[1]
    at = lax.axis_index("seq")
    own = (lax.axis_index("fsdp") * experts).astype(jnp.int32).reshape(1)

    small = jnp.concatenate(
        [router, gain_attn[:, None], gain_moe[:, None]], axis=1
    )
    small = jnp.pad(small, ((0, 0), (0, LANES - small.shape[1])))
    place, order = block_places(n_fsdp), block_order(n_fsdp)

    def weights(w):
        return [h.reshape(n_fsdp // 2, -1, h.shape[1]) for h in gather_near(w, n_fsdp)]

    w_kv = weights(jnp.concatenate([key_projection, value_projection, small], axis=1))
    router_all, rows_all = unpack(place, w_kv, 2 * kv_width // LANES, n_experts)
    gain_one = rows_all[n_experts : n_experts + 1]
    gain_two = rows_all[n_experts + 1 : n_experts + 2]

    positions = at * tokens + jnp.arange(tokens, dtype=jnp.int32)
    frequency = THETA ** (-(jnp.arange(HALF, dtype=F32) * 2.0) / HEAD)
    angles = frequency[:, None] * positions.astype(F32)[None, :]
    cosine, sine = jnp.cos(angles), jnp.sin(angles)
    cosine_all, sine_all = jnp.tile(cosine, (1, micros)), jnp.tile(sine, (1, micros))

    x = inputs.reshape(rows, dim)
    chosen = jnp.sum(
        (
            expert_ids.reshape(rows, TOPK)[:, :, None]
            == jnp.arange(LANES, dtype=jnp.int32)[None, None, :]
        ).astype(F32),
        axis=1,
    )
    valid = positions[None, :] < lengths[:, :1]
    gout = jnp.where(valid[:, :, None], cotangent.reshape(micros, tokens, dim), BF(0))
    infos = [
        jnp.stack([at.astype(jnp.int32), lengths[m, 0].astype(jnp.int32)]) for m in range(micros)
    ]

    kv, normed_one = kv_project(place, x, gain_one, w_kv, kv_width, cosine_all, sine_all)
    q_width = w_query.shape[1]
    w_gather = Gather(gate(jnp.concatenate([w_query, w_out], axis=1), kv), n_fsdp)
    w_gather.further()
    kvs = []
    for m in range(micros):
        mine = kv[m * tokens : (m + 1) * tokens]
        every = lax.all_gather(mine, "seq", axis=0, tiled=True)
        kvs.append(every.reshape(n_seq, tokens, 2 * kv_width))
    w_qo = [h.reshape(n_fsdp // 2, -1, h.shape[1]) for h in w_gather.finish(kvs[0])]
    g_gathers = [Gather(gate(gout[0], w_gather.far), n_fsdp)]
    for m in range(1, micros):
        g_gathers.append(Gather(gate(gout[m], g_gathers[-1].near), n_fsdp))
    q_t = q_project(
        place, gate(normed_one, kvs[0]), w_qo, q_width, cosine_all, sine_all
    )

    state, xg_all = [], []
    for m in range(micros):
        if m == 0:
            info = gate(infos[m], g_gathers[0].near)
            g_gathers[0].further(q_t)
        else:
            info = gate(infos[m], state[-1][2], g_gathers[m].far)
            g_all = [g.finish() for g in g_gathers]
        attn, attn_t, lse = attend(info, q_t, kvs[m], m, tokens)
        if m == 0:
            attn = gate(attn, g_gathers[0].far)
            for g in g_gathers[1:]:
                g.further(g_gathers[0].far)
        residual, xg, exact = after_attention(
            place, attn, w_qo, q_width, x, m, gain_two, router_all, chosen
        )
        state.append((attn_t, lse, residual, exact))
        xg_all.append(gather_rows(xg))

    xg_all[0] = gate(xg_all[0], state[-1][2], g_all)
    passed, backs = [], []
    for m in range(micros):
        *y, back, hg, gp = run_experts(
            own, order, xg_all[m], g_all[m], w_gate, w_up, w_down
        )
        passed.append((xg_all[m], hg, gp))
        backs.append((scatter_rows(back), y))

    names = [(name, e) for name in ("down", "gate", "up") for e in range(experts)]

    def expert_grad(name, e, got):
        xs, hgs, gps = ([p[i] for p in got] for i in range(3))
        if name == "down":
            return down_grad(hgs, e, hidden, g_all, n_fsdp)
        return wide_grad(xs, 0, dim, gps, 2 * e + (name == "up"), hidden)

    line = Line(n_seq)
    found = [{} for _ in range(micros)]

    def to_heads(m):
        attn_t, lse, residual, exact = state[m]
        gres, g_attn, g_t, small_two = before_attention(
            place, backs[m][0], residual, exact, gout[m], gain_two, router_all, w_qo, q_width
        )
        found[m].update(gres=gres, g_attn=g_attn, g_t=g_t, small_two=small_two)

    def through_heads(m):
        attn_t, lse = state[m][:2]
        gq, by_owner = attend_back(
            infos[m], q_t, found[m]["g_t"], attn_t, lse, cosine, sine, kvs[m], m, tokens
        )
        found[m].update(gq=gq, by_owner=by_owner)

    owned = {}

    def to_owners(m):
        by_owner = found[m].pop("by_owner")
        shape = by_owner.shape
        owned[m] = lax.psum_scatter(
            by_owner.reshape(n_seq * shape[1] * tokens, shape[3]),
            "seq",
            scatter_dimension=0,
            tiled=True,
        ).reshape(shape[1:])

    def finish(m):
        f = found[m]
        f["dkv"] = turn_back(f["mine"], cosine, sine)
        f["din"], f["small_one"] = last_step(
            place, f["gq"], f["dkv"], w_qo, w_kv, x, m, gain_one, f["gres"]
        )

    def rest_grads():
        every = lambda name: [f[name] for f in found]
        return projection_grads(
            normed_one, every("gq"), every("dkv"), every("small_two"), every("small_one"), n_experts
        )

    n_grads = len(names)
    work = {
        0: [("grad", 1), (to_heads, 0)],
        1: [("grad", 2), (through_heads, 0)],
        2: [("grad", 3), (to_heads, 1), (through_heads, 1)],
        3: [("grad", 4), (finish, 0), ("grad", 5)],
        4: [(finish, 1)],
    }
    def widen(parts, turned):
        return jnp.stack([(p.T if turned else p).astype(F32) for p in parts])

    experts_out = []
    chunks = {0: expert_grad(*names[0], passed)}
    chunks.update({i: expert_grad(*names[i], passed) for i in range(6, n_grads)})
    slots = max(n_grads, 6)
    moe = Scatter([b[1] for b in backs], n_fsdp)
    for t in range(slots + 3):
        if t in (3, 4):
            found[t - 3]["mine"] = owned[t - 3]
        if t == 3:
            heads = Scatter([found[0].pop("out")], n_fsdp)
        if t in (6, 8):
            found[0]["rest"] = rest
        held = (chunks, line.held, line.results, passed, found, moe.arrays)
        if t >= 3:
            *held, heads.arrays = lax.optimization_barrier((*held, heads.arrays))
        else:
            held = lax.optimization_barrier(held)
        chunks, line.held, line.results, passed, found, moe.arrays = held
        if t == 6:
            rest = lax.psum(found[0].pop("rest"), "seq")
        if len(line.results) in (experts, 2 * experts) and t < slots + 2:
            pair = line.sums()[-experts:]
            experts_out.append(widen(pair, len(experts_out) == 0))
            found[1]["wide"] = experts_out[-1]
        if t == slots:
            chunks[slots] = heads.arrays[0]
        sent = chunks.pop(t, None)
        if t in (2, 3):
            to_owners(t - 2)
        for kind, i in work.get(t, []):
            if kind != "grad":
                kind(i)
            elif i < n_grads:
                chunks[i] = expert_grad(*names[i], passed)
        if t == 2:
            found[0]["out"] = out_grad(
                order, [st[0] for st in state], [f["g_attn"] for f in found]
            )
        if t == 4:
            rest = scatter_rows(rest_grads())
        if t in (2, 3, 4):
            moe.advance()
        if t in (3, 4, 5):
            heads.advance()
        line.step(sent, (chunks, found))
    rest = found[0]["rest"].astype(F32)
    totals = line.sums()
    for i in range(len(experts_out), 3):
        experts_out.append(widen(totals[i * experts : (i + 1) * experts], i == 0))
    d_out = totals[n_grads].astype(F32)

    outs = []
    for m in range(micros):
        outs.append(
            jnp.where(valid[m][:, None], state[m][2] + moe.arrays[m].astype(F32), 0.0).astype(BF)
        )
    grads = [f["din"] for f in found]
    assert len(totals) == n_grads + 1
    shape = (micros, 1, tokens, dim)
    ends = q_width + 2 * kv_width
    return (
        jnp.stack(outs).reshape(shape),
        jnp.stack(grads).reshape(shape),
        rest[:, ends + n_experts],
        rest[:, :q_width],
        rest[:, q_width : q_width + kv_width],
        rest[:, q_width + kv_width : ends],
        d_out,
        rest[:, ends + n_experts + 1],
        rest[:, ends : ends + n_experts],
        *experts_out[1:],
        experts_out[0],
    )


def solution(mesh):
    token_spec = P(None, "fsdp", "seq", None)
    row, matrix, cube = P("fsdp"), P("fsdp", None), P("fsdp", None, None)
    return jax.shard_map(
        functools.partial(on_device, mesh.shape["seq"], mesh.shape["fsdp"]),
        mesh=mesh,
        in_specs=(
            token_spec,
            P(None, "fsdp"),
            token_spec,
            token_spec,
            row,
            matrix,
            matrix,
            matrix,
            matrix,
            row,
            matrix,
            cube,
            cube,
            cube,
        ),
        out_specs=(
            token_spec,
            token_spec,
            row,
            matrix,
            matrix,
            matrix,
            matrix,
            row,
            matrix,
            cube,
            cube,
            cube,
        ),
        check_vma=False,
    )
```

```python
import functools

import jax
import jax.numpy as jnp
from jax import lax
from jax.experimental import pallas as pl
from jax.experimental.pallas import tpu as pltpu
from jax.sharding import PartitionSpec as P

HEAD = 64
HALF = HEAD // 2
GROUP = 3
TOPK = 8
EPS = 1e-06
THETA = 10000.0
NEGATIVE = -1e30
LANES = 128
SCALE = HEAD ** (-0.5)
BF = jnp.bfloat16
F32 = jnp.float32
VMEM_BYTES = 60 * 1024 * 1024

NN = (((1,), (0,)), ((), ()))
NT = (((1,), (1,)), ((), ()))
TN = (((0,), (0,)), ((), ()))


def dot(a, b, dims=NN):
    return lax.dot_general(a, b, dims, preferred_element_type=F32)


def params():
    return pltpu.CompilerParams(vmem_limit_bytes=VMEM_BYTES)


def cost(flops, moved, trans=0):
    parts = (int(v) // 10 for v in (flops, moved, trans))
    flops, moved, trans = parts
    return pl.CostEstimate(flops=flops, bytes_accessed=moved, transcendentals=trans)


def whole(shape):
    zeros = (0,) * len(shape)
    return pl.BlockSpec(shape, lambda *_: zeros)


def smem():
    return pl.BlockSpec(memory_space=pltpu.SMEM)


def pick(at, first_ref, second_ref, index=None):
    half = first_ref.shape[0]
    if index is None:
        index = lax.rem(at, half)
    return jnp.where(at < half, first_ref[index], second_ref[index])


def in_order(place_ref, w_refs):
    devices = 2 * w_refs[0].shape[0]
    return jnp.concatenate([pick(place_ref[j], *w_refs) for j in range(devices)], axis=0)


def rotate(rows, cosine, sine, sign):
    pieces = []
    for h in range(rows.shape[0] // HEAD):
        a = rows[h * HEAD : h * HEAD + HALF]
        b = rows[h * HEAD + HALF : (h + 1) * HEAD]
        if sign > 0:
            pieces += [a * cosine - b * sine, b * cosine + a * sine]
        else:
            pieces += [a * cosine + b * sine, b * cosine - a * sine]
    return jnp.concatenate(pieces, axis=0)


def unpack_kernel(n_experts, place_ref, wa_ref, wb_ref, router_ref, rows_ref):
    w = in_order(place_ref, (wa_ref, wb_ref))
    lane = lax.broadcasted_iota(jnp.int32, w.shape, 1)
    router_ref[...] = jnp.where(lane < n_experts, w.astype(F32), 0.0).astype(BF)
    rows_ref[...] = w.astype(F32).T


def unpack(place, w, block, n_experts):
    dim = 2 * w[0].shape[0] * w[0].shape[1]
    return pl.pallas_call(
        functools.partial(unpack_kernel, n_experts),
        name="unpack",
        grid=(1,),
        in_specs=[smem(), *w_columns(w, LANES, lambda i: block)],
        out_specs=[whole((dim, LANES)), whole((LANES, dim))],
        out_shape=[
            jax.ShapeDtypeStruct((dim, LANES), BF),
            jax.ShapeDtypeStruct((LANES, dim), F32),
        ],
        compiler_params=params(),
        cost_estimate=cost(0, 12 * dim * LANES),
    )(place, *w)


def kv_kernel(place_ref, x_ref, gain_ref, wa_ref, wb_ref, cos_ref, sin_ref, kv_ref, normed_ref):
    step = pl.program_id(0)

    @pl.when(step == 0)
    def _():
        x = x_ref[...].astype(F32)
        inv = lax.rsqrt(jnp.mean(x * x, axis=-1, keepdims=True) + EPS)
        normed_ref[...] = (x * inv * gain_ref[...]).astype(BF)
        r = dot(normed_ref[...], in_order(place_ref, (wa_ref, wb_ref)))
        r = rotate(r.T, cos_ref[...], sin_ref[...], 1)
        kv_ref[...] = r.T.astype(BF)

    @pl.when(step == 1)
    def _():
        kv_ref[...] = dot(normed_ref[...], in_order(place_ref, (wa_ref, wb_ref))).astype(BF)


def w_columns(w, tile, at):
    return [pl.BlockSpec((*half.shape[:2], tile), lambda *i: (0, 0, at(*i))) for half in w]


def kv_project(place, x, gain, w, width, cosine, sine):
    rows, dim = x.shape
    return pl.pallas_call(
        kv_kernel,
        name="kv_project",
        grid=(2,),
        in_specs=[
            smem(),
            whole((rows, dim)),
            whole((1, dim)),
            *w_columns(w, width, lambda i: i),
            whole((HALF, rows)),
            whole((HALF, rows)),
        ],
        out_specs=[pl.BlockSpec((rows, width), lambda i: (0, i)), whole((rows, dim))],
        out_shape=[
            jax.ShapeDtypeStruct((rows, 2 * width), BF),
            jax.ShapeDtypeStruct((rows, dim), BF),
        ],
        compiler_params=params(),
        cost_estimate=cost(2 * rows * dim * 2 * width, 2 * (2 * rows * dim + dim * 2 * width)),
    )(place, x, gain, *w, cosine, sine)


def q_kernel(place_ref, normed_ref, wa_ref, wb_ref, cos_ref, sin_ref, q_ref):
    r = dot(normed_ref[...], in_order(place_ref, (wa_ref, wb_ref)))
    r = rotate(r.T, cos_ref[...], sin_ref[...], 1)
    q_ref[...] = r.astype(BF) * BF(SCALE)


def q_project(place, normed, w, width, cosine, sine):
    rows, dim = normed.shape
    tile = 512
    return pl.pallas_call(
        q_kernel,
        name="q_project",
        grid=(width // tile,),
        in_specs=[
            smem(),
            whole((rows, dim)),
            *w_columns(w, tile, lambda i: i),
            whole((HALF, rows)),
            whole((HALF, rows)),
        ],
        out_specs=pl.BlockSpec((tile, rows), lambda i: (i, 0)),
        out_shape=jax.ShapeDtypeStruct((width, rows), BF),
        compiler_params=params(),
        cost_estimate=cost(2 * rows * dim * width, 2 * (2 * rows * dim + dim * width)),
    )(place, normed, *w, cosine, sine)


def side_by_side(ref, j):
    base = j * GROUP * HEAD
    return jnp.concatenate(
        [ref[base + h * HEAD : base + (h + 1) * HEAD, :] for h in range(GROUP)], axis=1
    )


def diagonal_mask(tokens, own_len):
    key = lax.broadcasted_iota(jnp.int32, (tokens, tokens), 0)
    query = lax.broadcasted_iota(jnp.int32, (tokens, tokens), 1)
    one = (key <= query) & (key < own_len)
    return jnp.concatenate([one.astype(jnp.int32)] * GROUP, axis=1) > 0


def attend_kernel(n, info_ref, q_ref, k_ref, v_ref, o_ref, ot_ref, lse_ref, m_ref, l_ref, acc_ref):
    tokens = q_ref.shape[1]
    d = pl.program_id(1)
    s = info_ref[0]
    own_len = info_ref[1] - s * tokens
    active = own_len > 0

    def pair(j):
        cols = slice(j * HEAD, (j + 1) * HEAD)
        scores = dot(k_ref[0, :, cols], side_by_side(q_ref, j))
        return scores, v_ref[0, :, cols].astype(F32).T.astype(BF)

    @pl.when(active & (d == 0))
    def _():
        mask = diagonal_mask(tokens, own_len)
        for j in range(2):
            scores, value_t = pair(j)
            scores = jnp.where(mask, scores, NEGATIVE)
            top = jnp.max(scores, axis=0, keepdims=True)
            p = jnp.exp(scores - top)
            l_ref[j : j + 1] = jnp.sum(p, axis=0, keepdims=True)
            acc_ref[j] = dot(value_t, p.astype(BF))
            m_ref[j : j + 1] = top

    @pl.when(active & (d > 0) & (d <= s))
    def _():
        for j in range(2):
            scores, value_t = pair(j)
            old = m_ref[j : j + 1]
            top = jnp.maximum(old, jnp.max(scores, axis=0, keepdims=True))
            keep = jnp.exp(old - top)
            p = jnp.exp(scores - top)
            l_ref[j : j + 1] = l_ref[j : j + 1] * keep + jnp.sum(p, axis=0, keepdims=True)
            acc_ref[j] = acc_ref[j] * keep + dot(value_t, p.astype(BF))
            m_ref[j : j + 1] = top

    @pl.when(active & (d == n - 1))
    def _():
        pieces = []
        for j in range(2):
            out = acc_ref[j] / l_ref[j : j + 1]
            lse_ref[j : j + 1] = m_ref[j : j + 1] + jnp.log(l_ref[j : j + 1])
            pieces += [out[:, h * tokens : (h + 1) * tokens] for h in range(GROUP)]
        out = jnp.concatenate(pieces, axis=0)
        ot_ref[...] = out.astype(BF)
        o_ref[...] = out.T.astype(BF)

    @pl.when(jnp.logical_not(active) & (d == 0))
    def _():
        o_ref[...] = jnp.zeros_like(o_ref)
        ot_ref[...] = jnp.zeros_like(ot_ref)
        lse_ref[...] = jnp.zeros_like(lse_ref)


def owner(info_ref, d, n):
    return lax.rem(info_ref[0] + n - d, n)


def attend(info, q_t, kv, micro, tokens):
    n = kv.shape[0]
    width = q_t.shape[0]
    kv_width = kv.shape[2] // 2
    steps = kv_width // LANES
    qw = width // steps
    return pl.pallas_call(
        functools.partial(attend_kernel, n),
        name="attend",
        grid_spec=pltpu.PrefetchScalarGridSpec(
            num_scalar_prefetch=1,
            grid=(steps, n),
            in_specs=[
                pl.BlockSpec((qw, tokens), lambda i, d, info: (i, micro)),
                pl.BlockSpec((1, tokens, LANES), lambda i, d, info: (owner(info, d, n), 0, i)),
                pl.BlockSpec(
                    (1, tokens, LANES), lambda i, d, info: (owner(info, d, n), 0, steps + i)
                ),
            ],
            out_specs=[
                pl.BlockSpec((tokens, qw), lambda i, d, info: (0, i)),
                pl.BlockSpec((qw, tokens), lambda i, d, info: (i, 0)),
                pl.BlockSpec((8, GROUP * tokens), lambda i, d, info: (i, 0)),
            ],
            scratch_shapes=[
                pltpu.VMEM((8, GROUP * tokens), F32),
                pltpu.VMEM((8, GROUP * tokens), F32),
                pltpu.VMEM((2, HEAD, GROUP * tokens), F32),
            ],
        ),
        out_shape=[
            jax.ShapeDtypeStruct((tokens, width), BF),
            jax.ShapeDtypeStruct((width, tokens), BF),
            jax.ShapeDtypeStruct((8 * steps, GROUP * tokens), F32),
        ],
        compiler_params=params(),
        cost_estimate=cost(
            4 * 4 * width * tokens * tokens * n,
            2 * (3 * width * tokens + n * tokens * 2 * kv_width),
            width // HEAD * tokens * tokens * n,
        ),
    )(info, q_t, kv, kv)


def attend_back_kernel(
    n, info_ref, q_ref, g_ref, o_ref, lse_ref, cos_ref, sin_ref, k_ref, v_ref, gq_ref, dkv_ref, acc_ref
):
    tokens = q_ref.shape[1]
    d = pl.program_id(1)
    s = info_ref[0]
    own_len = info_ref[1] - s * tokens
    active = own_len > 0

    def block(first):
        mask = diagonal_mask(tokens, own_len) if first else None
        dks, dvs = [], []
        for j in range(2):
            cols = slice(j * HEAD, (j + 1) * HEAD)
            key, value = k_ref[0, :, cols], v_ref[0, :, cols]
            query, grad = side_by_side(q_ref, j), side_by_side(g_ref, j)
            out = side_by_side(o_ref, j)
            inner = jnp.sum(grad.astype(F32) * out.astype(F32), axis=0, keepdims=True)
            p = jnp.exp(dot(key, query) - lse_ref[j : j + 1])
            if first:
                p = jnp.where(mask, p, 0.0)
            dp = dot(value, grad)
            ds = (p * (dp - inner)).astype(BF)
            dvs.append(dot(p.astype(BF), grad, NT))
            dks.append(dot(ds, query, NT))
            part = dot(key.astype(F32).T.astype(BF), ds)
            if first:
                acc_ref[j] = part
            else:
                acc_ref[j] += part
        dkv_ref[0, 0] = jnp.concatenate(dks, axis=1).astype(BF)
        dkv_ref[0, 1] = jnp.concatenate(dvs, axis=1).astype(BF)

    pl.when(active & (d == 0))(lambda: block(True))
    pl.when(active & (d > 0) & (d <= s))(lambda: block(False))

    @pl.when(active & (d == n - 1))
    def _():
        pieces = []
        for j in range(2):
            for h in range(GROUP):
                piece = acc_ref[j, :, h * tokens : (h + 1) * tokens] * SCALE
                pieces.append(piece.astype(BF).astype(F32))
        grad_q = rotate(jnp.concatenate(pieces, axis=0), cos_ref[...], sin_ref[...], -1)
        gq_ref[...] = grad_q.T.astype(BF)

    @pl.when(jnp.logical_not(active) | (d > s))
    def _():
        dkv_ref[...] = jnp.zeros_like(dkv_ref)

    @pl.when(jnp.logical_not(active) & (d == 0))
    def _():
        gq_ref[...] = jnp.zeros_like(gq_ref)


def attend_back(info, q_t, g_t, o_t, lse, cosine, sine, kv, micro, tokens):
    n = kv.shape[0]
    width = q_t.shape[0]
    kv_width = kv.shape[2] // 2
    steps = kv_width // LANES
    qw = width // steps
    transposed = pl.BlockSpec((qw, tokens), lambda i, d, info: (i, 0))
    return pl.pallas_call(
        functools.partial(attend_back_kernel, n),
        name="attend_back",
        grid_spec=pltpu.PrefetchScalarGridSpec(
            num_scalar_prefetch=1,
            grid=(steps, n),
            in_specs=[
            pl.BlockSpec((qw, tokens), lambda i, d, info: (i, micro)),
            transposed,
            transposed,
            pl.BlockSpec((8, GROUP * tokens), lambda i, d, info: (i, 0)),
            whole((HALF, tokens)),
            whole((HALF, tokens)),
            pl.BlockSpec((1, tokens, LANES), lambda i, d, info: (owner(info, d, n), 0, i)),
            pl.BlockSpec(
                (1, tokens, LANES), lambda i, d, info: (owner(info, d, n), 0, steps + i)
            ),
        ],
        out_specs=[
            pl.BlockSpec((tokens, qw), lambda i, d, info: (0, i)),
            pl.BlockSpec(
                (1, 2, tokens, LANES), lambda i, d, info: (owner(info, d, n), 0, 0, i)
            ),
        ],
            scratch_shapes=[pltpu.VMEM((2, HEAD, GROUP * tokens), F32)],
        ),
        out_shape=[
            jax.ShapeDtypeStruct((tokens, width), BF),
            jax.ShapeDtypeStruct((n, 2, tokens, kv_width), BF),
        ],
        compiler_params=params(),
        cost_estimate=cost(
            10 * 4 * width * tokens * tokens * n,
            2 * (4 * width * tokens + 2 * n * tokens * 2 * kv_width),
            width // HEAD * tokens * tokens * n,
        ),
    )(info, q_t, g_t, o_t, lse, cosine, sine, kv, kv)


def after_kernel(
    steps, place_ref, a_ref, wa_ref, wb_ref, x_ref, gain_ref, router_ref, chosen_ref, res_ref, xg_ref, ge_ref, acc_ref
):
    step = pl.program_id(0)
    acc_ref[step] = dot(a_ref[...], in_order(place_ref, (wa_ref, wb_ref)))

    @pl.when(step == steps - 1)
    def _():
        dim = x_ref.shape[1]
        product = jnp.concatenate([acc_ref[i] for i in range(steps)], axis=1)
        residual = x_ref[...].astype(F32) + product
        res_ref[...] = residual
        inv = lax.rsqrt(jnp.mean(residual * residual, axis=-1, keepdims=True) + EPS)
        normed = (residual * inv * gain_ref[...]).astype(BF)
        logits = dot(normed, router_ref[...])
        chosen = chosen_ref[...] > 0
        logits = jnp.where(chosen, logits, NEGATIVE)
        top = jnp.max(logits, axis=-1, keepdims=True)
        e = jnp.where(chosen, jnp.exp(logits - top), 0.0)
        exact = e / jnp.sum(e, axis=-1, keepdims=True)
        ge_ref[...] = exact
        xg_ref[:, :dim] = normed
        xg_ref[:, dim:] = exact.astype(BF)


def after_attention(place, attn, w, first, x, micro, gain, router, chosen):
    tokens, width = attn.shape
    dim = x.shape[1]
    tile = 512
    steps = dim // tile
    return pl.pallas_call(
        functools.partial(after_kernel, steps),
        name="after_attention",
        grid=(steps,),
        in_specs=[
            smem(),
            whole((tokens, width)),
            *w_columns(w, tile, lambda i: first // tile + i),
            pl.BlockSpec((tokens, dim), lambda i: (micro, 0)),
            whole((1, dim)),
            whole((dim, LANES)),
            pl.BlockSpec((tokens, LANES), lambda i: (micro, 0)),
        ],
        out_specs=[
            whole((tokens, dim)),
            whole((tokens, dim + LANES)),
            whole((tokens, LANES)),
        ],
        out_shape=[
            jax.ShapeDtypeStruct((tokens, dim), F32),
            jax.ShapeDtypeStruct((tokens, dim + LANES), BF),
            jax.ShapeDtypeStruct((tokens, LANES), F32),
        ],
        scratch_shapes=[pltpu.VMEM((steps, tokens, tile), F32)],
        compiler_params=params(),
        cost_estimate=cost(2 * tokens * width * dim, 2 * width * dim + 10 * tokens * dim),
    )(place, attn, *w, x, gain, router, chosen)


def expert_kernel(
    experts, half, own_ref, order_ref, xg_ref, ga_ref, gb_ref, wg_ref, wu_ref, wd_ref, ya_ref, yb_ref, back_ref, hg_ref, gp_ref
):
    rows, dim = ga_ref.shape
    hidden = wg_ref.shape[2]
    x = xg_ref[:, :dim]
    step = pl.program_id(0)
    g = jnp.where(step < half, ga_ref[...], gb_ref[...])
    gates = xg_ref[:, dim:].astype(F32)
    lane = lax.broadcasted_iota(jnp.int32, (rows, LANES), 1)
    gate_cols = jnp.zeros((rows, LANES), F32)
    for e in range(experts):
        mine = lane == own_ref[0] + e
        gate = jnp.sum(jnp.where(mine, gates, 0.0), axis=1, keepdims=True)
        pre_gate = dot(x, wg_ref[e])
        pre_up = dot(x, wu_ref[e])
        grad_hidden = dot(g, wd_ref[e], NT)
        sig = 1.0 / (1.0 + jnp.exp(-pre_gate))
        silu = pre_gate * sig
        h = (silu * pre_up).astype(BF).astype(F32)
        per_gate = jnp.sum(h * grad_hidden, axis=1, keepdims=True)
        gate_cols = jnp.where(mine, per_gate, gate_cols)
        hg_ref[:, e * hidden : (e + 1) * hidden] = (gate * h).astype(BF)
        gh = gate * grad_hidden
        base = 2 * e * hidden
        gp_ref[:, base : base + hidden] = (
            gh * pre_up * (sig * (1.0 + pre_gate * (1.0 - sig)))
        ).astype(BF)
        gp_ref[:, base + hidden : base + 2 * hidden] = (gh * silu).astype(BF)
    y = dot(hg_ref[:, :hidden], wd_ref[0])
    for e in range(1, experts):
        y += dot(hg_ref[:, e * hidden : (e + 1) * hidden], wd_ref[e])

    @pl.when(step < half)
    def _():
        ya_ref[...] = y.astype(BF)

    @pl.when(step >= half)
    def _():
        yb_ref[...] = y.astype(BF)

    back = None
    for e in range(experts):
        base = 2 * e * hidden
        part = dot(gp_ref[:, base : base + hidden], wg_ref[e], NT)
        part += dot(gp_ref[:, base + hidden : base + 2 * hidden], wu_ref[e], NT)
        back = part if back is None else back + part
    back_ref[:, :dim] = back.astype(BF)
    back_ref[:, dim:] = gate_cols.astype(BF)


def run_experts(own, order, xg, g, w_gate, w_up, w_down):
    rows = xg.shape[0]
    dim = g[0].shape[1]
    experts, _, hidden = w_gate.shape
    devices = order.shape[0]
    tile, half = rows // devices, devices // 2
    named = lambda width: pl.BlockSpec((tile, width), lambda i, own, order: (order[i], 0))
    first = lambda i: jnp.minimum(i, half - 1)
    second = lambda i: jnp.maximum(i - half, 0)
    return pl.pallas_call(
        functools.partial(expert_kernel, experts, half),
        name="run_experts",
        grid_spec=pltpu.PrefetchScalarGridSpec(
            num_scalar_prefetch=2,
            grid=(devices,),
            in_specs=[
                named(dim + LANES),
                pl.BlockSpec((tile, dim), lambda i, *_: (first(i), 0)),
                pl.BlockSpec((tile, dim), lambda i, *_: (second(i), 0)),
                whole(w_gate.shape),
                whole(w_up.shape),
                whole(w_down.shape),
            ],
            out_specs=[
                pl.BlockSpec((tile, dim), lambda i, *_: (first(i), 0)),
                pl.BlockSpec((tile, dim), lambda i, *_: (second(i), 0)),
                named(dim + LANES),
                pl.BlockSpec((tile, experts * hidden), lambda i, *_: (i, 0)),
                named(2 * experts * hidden),
            ],
        ),
        out_shape=[
            jax.ShapeDtypeStruct((rows // 2, dim), BF),
            jax.ShapeDtypeStruct((rows // 2, dim), BF),
            jax.ShapeDtypeStruct((rows, dim + LANES), BF),
            jax.ShapeDtypeStruct((rows, experts * hidden), BF),
            jax.ShapeDtypeStruct((rows, 2 * experts * hidden), BF),
        ],
        compiler_params=params(),
        cost_estimate=cost(
            12 * rows * dim * hidden * experts,
            2 * (4 * rows * dim + 3 * rows * experts * hidden + 3 * experts * dim * hidden),
            rows * experts * hidden,
        ),
    )(own, order, xg, *g, w_gate, w_up, w_down)


def wide_grad_kernel(steps, micros, *refs):
    a_refs, b_refs = refs[:micros], refs[micros : 2 * micros]
    out_ref, acc_ref = refs[2 * micros :]
    step = pl.program_id(0)
    for m in range(micros):

        @pl.when((step >= m * steps) & (step < (m + 1) * steps))
        def _(m=m):
            part = dot(a_refs[m][...], b_refs[m][...], TN)
            if m == 0:

                @pl.when(step == 0)
                def _():
                    acc_ref[...] = part

                @pl.when(step > 0)
                def _():
                    acc_ref[...] += part
            else:
                acc_ref[...] += part

    @pl.when(step == micros * steps - 1)
    def _():
        out_ref[...] = acc_ref[...].astype(BF)


def wide_grad(lefts, left_block, left_width, rights, right_block, right_width, tile=512):
    micros, rows = len(lefts), lefts[0].shape[0]
    steps = rows // tile

    def spec(m, width, column):
        return pl.BlockSpec(
            (tile, width), lambda i: (jnp.clip(i - m * steps, 0, steps - 1), column)
        )

    return pl.pallas_call(
        functools.partial(wide_grad_kernel, steps, micros),
        name="wide_grad",
        grid=(micros * steps,),
        in_specs=[spec(m, left_width, left_block) for m in range(micros)]
        + [spec(m, right_width, right_block) for m in range(micros)],
        out_specs=whole((left_width, right_width)),
        out_shape=jax.ShapeDtypeStruct((left_width, right_width), BF),
        scratch_shapes=[pltpu.VMEM((left_width, right_width), F32)],
        compiler_params=params(),
        cost_estimate=cost(
            2 * micros * rows * left_width * right_width,
            2 * (micros * rows * (left_width + right_width) + left_width * right_width),
        ),
    )(*lefts, *rights)


def down_grad_kernel(micros, devices, *refs):
    hg_refs, refs = refs[:micros], refs[micros:]
    ga_refs, gb_refs = refs[:micros], refs[micros : 2 * micros]
    out_ref, acc_ref = refs[2 * micros :]
    step = pl.program_id(0)
    g = [jnp.where(step < devices // 2, a[...], b[...]) for a, b in zip(ga_refs, gb_refs)]
    part = dot(jnp.concatenate(g), jnp.concatenate([r[...] for r in hg_refs]), TN)

    @pl.when(step == 0)
    def _():
        acc_ref[...] = part

    @pl.when(step > 0)
    def _():
        acc_ref[...] += part

    @pl.when(step == devices - 1)
    def _():
        out_ref[...] = acc_ref[...].astype(BF)


def down_grad(hgs, expert, hidden, gs, devices):
    micros, rows = len(hgs), hgs[0].shape[0]
    tile, half = rows // devices, devices // 2
    dim = gs[0][0].shape[1]
    return pl.pallas_call(
        functools.partial(down_grad_kernel, micros, devices),
        name="down_grad",
        grid=(devices,),
        in_specs=[pl.BlockSpec((tile, hidden), lambda i: (i, expert))] * micros
        + [pl.BlockSpec((tile, dim), lambda i: (jnp.minimum(i, half - 1), 0))] * micros
        + [pl.BlockSpec((tile, dim), lambda i: (jnp.maximum(i - half, 0), 0))] * micros,
        out_specs=whole((dim, hidden)),
        out_shape=jax.ShapeDtypeStruct((dim, hidden), BF),
        scratch_shapes=[pltpu.VMEM((dim, hidden), F32)],
        compiler_params=params(),
        cost_estimate=cost(2 * micros * rows * hidden * dim, 2 * micros * rows * (hidden + dim)),
    )(*hgs, *[g[0] for g in gs], *[g[1] for g in gs])


def before_kernel(
    steps, place_ref, ret_ref, res_ref, ge_ref, gout_ref, gain_ref, router_ref, wa_ref, wb_ref, gres_ref, ga_ref, gt_ref, small_ref, cut_ref, acc_ref
):
    dim = res_ref.shape[1]

    step = pl.program_id(0)
    tile = dim // steps

    @pl.when(step == 0)
    def _():
        ge = ge_ref[...]
        gg = ret_ref[:, dim:].astype(F32)
        gl = ge * (gg - jnp.sum(ge * gg, axis=-1, keepdims=True))
        high = gl.astype(BF)
        low = (gl - high.astype(F32)).astype(BF)
        router = router_ref[...]
        gn = ret_ref[:, :dim].astype(F32) + (dot(high, router, NT) + dot(low, router, NT))
        residual = res_ref[...]
        gain = gain_ref[...]
        inv = lax.rsqrt(jnp.mean(residual * residual, axis=-1, keepdims=True) + EPS)
        unit = residual * inv
        normed = (unit * gain).astype(BF)
        small_ref[:LANES] = dot(high, normed, TN) + dot(low, normed, TN)
        gain_row = jnp.sum(gn * unit, axis=0, keepdims=True)
        small_ref[LANES:] = jnp.broadcast_to(gain_row, (8, dim))
        u = gn * gain
        gres = gout_ref[...].astype(F32) + inv * (
            u - unit * jnp.mean(u * unit, axis=-1, keepdims=True)
        )
        gres_ref[...] = gres
        low_gres = gres.astype(BF)
        ga_ref[...] = low_gres
        for i in range(steps):
            cut_ref[i] = low_gres[:, i * tile : (i + 1) * tile]
        acc_ref[...] = jnp.zeros_like(acc_ref)

    acc_ref[...] += dot(in_order(place_ref, (wa_ref, wb_ref)), cut_ref[step], NT)

    @pl.when(step == steps - 1)
    def _():
        gt_ref[...] = acc_ref[...].astype(BF)


def before_attention(place, returned, residual, exact, gout, gain, router, w, first):
    tokens, dim = residual.shape
    width = 2 * w[0].shape[0] * w[0].shape[1]
    tile = 512
    steps = dim // tile
    return pl.pallas_call(
        functools.partial(before_kernel, steps),
        name="before_attention",
        grid=(steps,),
        in_specs=[
            smem(),
            whole((tokens, dim + LANES)),
            whole((tokens, dim)),
            whole((tokens, LANES)),
            whole((tokens, dim)),
            whole((1, dim)),
            whole((dim, LANES)),
            *w_columns(w, tile, lambda i: first // tile + i),
        ],
        out_specs=[
            whole((tokens, dim)),
            whole((tokens, dim)),
            whole((width, tokens)),
            whole((LANES + 8, dim)),
        ],
        out_shape=[
            jax.ShapeDtypeStruct((tokens, dim), F32),
            jax.ShapeDtypeStruct((tokens, dim), BF),
            jax.ShapeDtypeStruct((width, tokens), BF),
            jax.ShapeDtypeStruct((LANES + 8, dim), F32),
        ],
        scratch_shapes=[
            pltpu.VMEM((steps, tokens, tile), BF),
            pltpu.VMEM((width, tokens), F32),
        ],
        compiler_params=params(),
        cost_estimate=cost(2 * tokens * width * dim, 2 * width * dim + 14 * tokens * dim),
    )(place, returned, residual, exact, gout, gain, router, *w)


def last_kernel(
    q_steps, steps, place_ref, gq_ref, dkv_ref, qa_ref, qb_ref, kva_ref, kvb_ref, x_ref, gain_ref, gres_ref, din_ref, small_ref, acc_ref
):
    step = pl.program_id(0)

    @pl.when(step == 0)
    def _():
        acc_ref[...] = dot(gq_ref[...], in_order(place_ref, (qa_ref, qb_ref)), NT)

    @pl.when((step > 0) & (step < q_steps))
    def _():
        acc_ref[...] += dot(gq_ref[...], in_order(place_ref, (qa_ref, qb_ref)), NT)

    @pl.when(step >= q_steps)
    def _():
        acc_ref[...] += dot(dkv_ref[...], in_order(place_ref, (kva_ref, kvb_ref)), NT)

    @pl.when(step == steps - 1)
    def _():
        x = x_ref[...].astype(F32)
        gain = gain_ref[...]
        inv = lax.rsqrt(jnp.mean(x * x, axis=-1, keepdims=True) + EPS)
        unit = x * inv
        gn = acc_ref[...]
        small_ref[...] = jnp.broadcast_to(
            jnp.sum(gn * unit, axis=0, keepdims=True), small_ref.shape
        )
        w = gn * gain
        grad = inv * (w - unit * jnp.mean(w * unit, axis=-1, keepdims=True))
        din_ref[...] = (grad + gres_ref[...]).astype(BF)


def last_step(place, gq, dkv, w_q, w_kv, x, micro, gain, gres):
    tokens, dim = gres.shape
    tile = 512
    q_steps, kv_steps = gq.shape[1] // tile, dkv.shape[1] // tile
    steps = q_steps + kv_steps
    q_at = lambda i: (0, jnp.minimum(i, q_steps - 1))
    kv_at = lambda i: (0, jnp.maximum(i - q_steps, 0))
    return pl.pallas_call(
        functools.partial(last_kernel, q_steps, steps),
        name="last_step",
        grid=(steps,),
        in_specs=[
            smem(),
            pl.BlockSpec((tokens, tile), q_at),
            pl.BlockSpec((tokens, tile), kv_at),
            *w_columns(w_q, tile, lambda i: q_at(i)[1]),
            *w_columns(w_kv, tile, lambda i: kv_at(i)[1]),
            pl.BlockSpec((tokens, dim), lambda i: (micro, 0)),
            whole((1, dim)),
            whole((tokens, dim)),
        ],
        out_specs=[whole((tokens, dim)), whole((8, dim))],
        out_shape=[
            jax.ShapeDtypeStruct((tokens, dim), BF),
            jax.ShapeDtypeStruct((8, dim), F32),
        ],
        scratch_shapes=[pltpu.VMEM((tokens, dim), F32)],
        compiler_params=params(),
        cost_estimate=cost(
            2 * tokens * steps * tile * dim, 2 * steps * tile * dim + 12 * tokens * dim
        ),
    )(place, gq, dkv, *w_q, *w_kv, x, gain, gres)


def out_grad_kernel(micros, half, order_ref, *refs):
    t_refs, g_refs, (first_ref, second_ref) = refs[:micros], refs[micros : 2 * micros], refs[2 * micros :]
    step = pl.program_id(0)
    total = dot(t_refs[0][...], g_refs[0][...])
    for t_ref, g_ref in zip(t_refs[1:], g_refs[1:]):
        total += dot(t_ref[...], g_ref[...])

    @pl.when(step < half)
    def _():
        first_ref[...] = total.astype(BF)

    @pl.when(step >= half)
    def _():
        second_ref[...] = total.astype(BF)


def out_grad(order, heads_t, grads):
    micros, devices = len(heads_t), order.shape[0]
    width, tokens = heads_t[0].shape
    dim = grads[0].shape[1]
    tile, half = width // devices, devices // 2
    return pl.pallas_call(
        functools.partial(out_grad_kernel, micros, half),
        name="out_grad",
        grid_spec=pltpu.PrefetchScalarGridSpec(
            num_scalar_prefetch=1,
            grid=(devices,),
            in_specs=[pl.BlockSpec((tile, tokens), lambda i, order: (order[i], 0))] * micros
            + [whole((tokens, dim))] * micros,
            out_specs=[
                pl.BlockSpec((tile, dim), lambda i, order: (jnp.minimum(i, half - 1), 0)),
                pl.BlockSpec((tile, dim), lambda i, order: (jnp.maximum(i - half, 0), 0)),
            ],
        ),
        out_shape=[jax.ShapeDtypeStruct((width // 2, dim), BF)] * 2,
        compiler_params=params(),
        cost_estimate=cost(2 * micros * tokens * width * dim, 4 * width * dim),
    )(order, *heads_t, *grads)


def turn_kernel(kv_ref, cos_ref, sin_ref, out_ref):
    width = kv_ref.shape[2]
    key = rotate(kv_ref[0].astype(F32).T, cos_ref[...], sin_ref[...], -1)
    out_ref[:, :width] = key.T.astype(BF)
    out_ref[:, width:] = kv_ref[1]


def turn_back(kv, cosine, sine):
    _, tokens, width = kv.shape
    return pl.pallas_call(
        turn_kernel,
        name="turn_back",
        out_shape=jax.ShapeDtypeStruct((tokens, 2 * width), BF),
        compiler_params=params(),
        cost_estimate=cost(0, 8 * tokens * width),
    )(kv, cosine, sine)


def projection_kernel(micros, q_steps, steps, n_experts, normed_ref, *refs):
    gq_refs, refs = refs[:micros], refs[micros:]
    dkv_refs, refs = refs[:micros], refs[micros:]
    two_refs, refs = refs[:micros], refs[micros:]
    one_refs, (out_ref, turned_ref) = refs[:micros], refs[micros:]
    step = pl.program_id(0)
    tile = gq_refs[0].shape[1]

    @pl.when(step == 0)
    def _():
        turned_ref[...] = normed_ref[...].astype(F32).T.astype(BF)
        rows = functools.reduce(jnp.add, [r[:LANES] for r in two_refs])
        gain_two = functools.reduce(jnp.add, [r[LANES : LANES + 1] for r in two_refs])
        gain_one = functools.reduce(jnp.add, [r[:1] for r in one_refs])
        at = lax.broadcasted_iota(jnp.int32, rows.shape, 0)
        rows = jnp.where(at == n_experts, gain_one, rows)
        rows = jnp.where(at == n_experts + 1, gain_two, rows)
        out_ref[:, steps * tile :] = rows.T.astype(BF)

    q = jnp.concatenate([r[...] for r in gq_refs], axis=0)
    kv = jnp.concatenate([r[...] for r in dkv_refs], axis=0)
    g = jnp.where(step < q_steps, q, kv)
    out_ref[:, pl.ds(pl.multiple_of(step * tile, tile), tile)] = dot(turned_ref[...], g).astype(BF)


def projection_grads(normed, gqs, dkvs, twos, ones, n_experts):
    rows, dim = normed.shape
    micros, tokens, tile = len(gqs), gqs[0].shape[0], 512
    q_steps, kv_steps = gqs[0].shape[1] // tile, dkvs[0].shape[1] // tile
    steps = q_steps + kv_steps
    width = steps * tile + LANES
    return pl.pallas_call(
        functools.partial(projection_kernel, micros, q_steps, steps, n_experts),
        name="projection_grads",
        grid=(steps,),
        in_specs=[whole((rows, dim))]
        + [pl.BlockSpec((tokens, tile), lambda i: (0, jnp.minimum(i, q_steps - 1)))] * micros
        + [pl.BlockSpec((tokens, tile), lambda i: (0, jnp.maximum(i - q_steps, 0)))] * micros
        + [whole(twos[0].shape)] * micros
        + [whole(ones[0].shape)] * micros,
        out_specs=whole((dim, width)),
        out_shape=jax.ShapeDtypeStruct((dim, width), BF),
        scratch_shapes=[pltpu.VMEM((dim, rows), BF)],
        compiler_params=params(),
        cost_estimate=cost(2 * rows * dim * width, 2 * rows * (dim + width) + 2 * dim * width),
    )(normed, *gqs, *dkvs, *twos, *ones)


def add_low(a, b):
    return (a.astype(F32) + b.astype(F32)).astype(BF)


def line_sum(x, n):
    if n == 1:
        return x
    if n % 2:
        return lax.psum(x, "seq")
    half = n // 2
    at = lax.axis_index("seq")
    for k in range(half - 1):
        x = add_low(x, lax.ppermute(x, "seq", [(k, k + 1), (n - 1 - k, n - 2 - k)]))
    x = add_low(x, lax.ppermute(x, "seq", [(half - 1, half), (half, half - 1)]))
    for k in reversed(range(half - 1)):
        got = lax.ppermute(x, "seq", [(k + 1, k), (n - 2 - k, n - 1 - k)])
        x = jnp.where((at == k) | (at == n - 1 - k), got, x)
    return x


class Line:
    def __init__(self, n):
        self.n = n
        self.held = {}
        self.results = []

    def sums(self):
        at = lax.axis_index("seq")
        middle = (at == 1) | (at == 2)
        return [r[0] if len(r) == 1 else jnp.where(middle, *r) for r in self.results]

    def step(self, chunk, beside):
        n = self.n
        if n != 4:
            if chunk is not None:
                self.results.append((line_sum(chunk, n),))
            return
        at = lax.axis_index("seq")
        middle = (at == 1) | (at == 2)
        come, go = [(0, 1), (3, 2)], [(1, 0), (2, 3)]
        held, self.held = self.held, {}
        summed = held.get("summed")
        if summed is not None:
            summed = add_low(*summed)
        crossing = held.get("crossing")
        if crossing is not None:
            crossing = add_low(*crossing)
            self.held["summed"] = (crossing, lax.ppermute(crossing, "seq", [(1, 2), (2, 1)]))
        if chunk is not None and summed is not None and chunk.shape == summed.shape:
            sent = jnp.where(middle, summed, chunk)
            got = lax.ppermute(sent, "seq", come + go)
            self.results.append((sent, got))
            self.held["crossing"] = (chunk, got)
        else:
            if summed is not None:
                self.results.append((summed, lax.ppermute(summed, "seq", go)))
            if chunk is not None:
                self.held["crossing"] = (chunk, lax.ppermute(chunk, "seq", come))
        self.held, self.results = gate((self.held, self.results), beside)


def gate(x, *others):
    return lax.optimization_barrier((x, others))[0]


CORE, ALONG_X, ALONG_Y = 1, 2, 4


def swap(x, mask):
    return lax.ppermute(x, "fsdp", [(i, i ^ mask) for i in range(8)])


def gather_rows(x):
    return lax.all_gather(x, "fsdp", axis=0, tiled=True)


def assemble_kernel(x_ref, top_x_ref, low_y_ref, top_far_ref, low_far_ref, out_ref):
    rows = x_ref.shape[0]
    half = rows // 2
    out_ref[:rows] = x_ref[...]
    out_ref[rows : rows + half] = top_x_ref[...]
    out_ref[rows + half : 2 * rows] = low_far_ref[:half]
    out_ref[2 * rows : 2 * rows + half] = top_far_ref[:half]
    out_ref[2 * rows + half : 3 * rows] = low_y_ref[...]
    out_ref[3 * rows : 3 * rows + half] = top_far_ref[half:]
    out_ref[3 * rows + half :] = low_far_ref[half:]


def assemble(*pieces):
    rows, width = pieces[0].shape
    block = lambda n: pl.BlockSpec((n, width // 3), lambda i: (0, i))
    return pl.pallas_call(
        assemble_kernel,
        name="assemble",
        grid=(3,),
        in_specs=[block(p.shape[0]) for p in pieces],
        out_specs=block(4 * rows),
        out_shape=jax.ShapeDtypeStruct((4 * rows, width), pieces[0].dtype),
        compiler_params=params(),
        cost_estimate=cost(0, 16 * rows * width),
    )(*pieces)


def gather_near(x, n):
    if n != 8:
        every = gather_rows(x)
        half = every.shape[0] // 2
        return every[:half], every[half:]
    gather = Gather(x, n)
    gather.further()
    return gather.finish()


class Gather:
    def __init__(self, x, n):
        self.n, self.x = n, x
        if n != 8:
            self.halves = gather_near(x, n)
            self.near = self.far = ()
            return
        half = x.shape[0] // 2
        self.near = swap(x[:half], ALONG_X), swap(x[half:], ALONG_Y)

    def further(self, *others):
        if self.n != 8:
            return
        half = self.x.shape[0] // 2
        x, (top_x, low_y) = gate((self.x, self.near), *others)
        self.near = top_x, low_y
        top_far = swap(jnp.concatenate([x[:half], top_x]), ALONG_Y)
        low_far = swap(jnp.concatenate([x[half:], low_y]), ALONG_X)
        self.far = top_far, low_far

    def finish(self, *others):
        if self.n != 8:
            return self.halves
        near, far = gate((self.near, self.far), *others)
        mine = assemble(self.x, *near, *far)
        return mine, swap(mine, CORE)


class Scatter:
    def __init__(self, arrays, n):
        self.arrays, self.n, self.stage = list(arrays), n, 0
        self.rows = 2 * arrays[0][0].shape[0] // n

    def advance(self):
        held, self.stage = self.arrays, self.stage + 1
        rows, half = self.rows, self.rows // 2
        if self.n != 8:
            if self.stage == 1:
                self.arrays = [scatter_rows(jnp.concatenate(a)) for a in held]
            return
        if self.stage == 1:
            self.arrays = [add_low(mine, swap(other, CORE)) for mine, other in held]
        if self.stage == 2:
            tops = [a[k * rows : k * rows + half] for a in held for k in (2, 3)]
            lows = [a[k * rows + half : (k + 1) * rows] for a in held for k in (1, 3)]
            tops = swap(jnp.concatenate(tops), ALONG_Y)
            lows = swap(jnp.concatenate(lows), ALONG_X)
            self.arrays = []
            for i, a in enumerate(held):
                at = 2 * i * half
                self.arrays.append(
                    (
                        add_low(a[:half], tops[at : at + half]),
                        add_low(a[half:rows], lows[at : at + half]),
                        add_low(a[rows : rows + half], tops[at + half : at + rows]),
                        add_low(a[2 * rows + half : 3 * rows], lows[at + half : at + rows]),
                    )
                )
        if self.stage == 3:
            over_x = swap(jnp.concatenate([a[2] for a in held]), ALONG_X)
            over_y = swap(jnp.concatenate([a[3] for a in held]), ALONG_Y)
            self.arrays = [
                jnp.concatenate(
                    [
                        add_low(a[0], over_x[i * half : (i + 1) * half]),
                        add_low(a[1], over_y[i * half : (i + 1) * half]),
                    ]
                )
                for i, a in enumerate(held)
            ]


def block_order(n):
    at = jnp.arange(n, dtype=jnp.int32)
    if n != 8:
        return at
    return lax.axis_index("fsdp").astype(jnp.int32) ^ (2 * lax.rem(at, 4) + at // 4)


def block_places(n):
    if n != 8:
        return jnp.arange(n, dtype=jnp.int32)
    mask = lax.axis_index("fsdp").astype(jnp.int32) ^ jnp.arange(n, dtype=jnp.int32)
    return (mask >> 1) + 4 * (mask & 1)


def scatter_rows(x):
    return lax.psum_scatter(x, "fsdp", scatter_dimension=0, tiled=True)


def on_device(
    n_seq,
    n_fsdp,
    inputs,
    lengths,
    expert_ids,
    cotangent,
    gain_attn,
    w_query,
    key_projection,
    value_projection,
    w_out,
    gain_moe,
    router,
    w_gate,
    w_up,
    w_down,
):
    micros, local_seqs, tokens, dim = inputs.shape
    assert local_seqs == 1
    rows = micros * tokens
    experts, _, hidden = w_gate.shape
    n_experts = router.shape[1]
    kv_width = key_projection.shape[1]
    at = lax.axis_index("seq")
    own = (lax.axis_index("fsdp") * experts).astype(jnp.int32).reshape(1)

    small = jnp.concatenate(
        [router, gain_attn[:, None], gain_moe[:, None]], axis=1
    )
    small = jnp.pad(small, ((0, 0), (0, LANES - small.shape[1])))
    place, order = block_places(n_fsdp), block_order(n_fsdp)

    def weights(w):
        return [h.reshape(n_fsdp // 2, -1, h.shape[1]) for h in gather_near(w, n_fsdp)]

    w_kv = weights(jnp.concatenate([key_projection, value_projection, small], axis=1))
    router_all, rows_all = unpack(place, w_kv, 2 * kv_width // LANES, n_experts)
    gain_one = rows_all[n_experts : n_experts + 1]
    gain_two = rows_all[n_experts + 1 : n_experts + 2]

    positions = at * tokens + jnp.arange(tokens, dtype=jnp.int32)
    frequency = THETA ** (-(jnp.arange(HALF, dtype=F32) * 2.0) / HEAD)
    angles = frequency[:, None] * positions.astype(F32)[None, :]
    cosine, sine = jnp.cos(angles), jnp.sin(angles)
    cosine_all, sine_all = jnp.tile(cosine, (1, micros)), jnp.tile(sine, (1, micros))

    x = inputs.reshape(rows, dim)
    chosen = jnp.sum(
        (
            expert_ids.reshape(rows, TOPK)[:, :, None]
            == jnp.arange(LANES, dtype=jnp.int32)[None, None, :]
        ).astype(F32),
        axis=1,
    )
    valid = positions[None, :] < lengths[:, :1]
    gout = jnp.where(valid[:, :, None], cotangent.reshape(micros, tokens, dim), BF(0))
    infos = [
        jnp.stack([at.astype(jnp.int32), lengths[m, 0].astype(jnp.int32)]) for m in range(micros)
    ]

    kv, normed_one = kv_project(place, x, gain_one, w_kv, kv_width, cosine_all, sine_all)
    q_width = w_query.shape[1]
    w_gather = Gather(gate(jnp.concatenate([w_query, w_out], axis=1), kv), n_fsdp)
    w_gather.further()
    kvs = []
    for m in range(micros):
        mine = kv[m * tokens : (m + 1) * tokens]
        every = lax.all_gather(mine, "seq", axis=0, tiled=True)
        kvs.append(every.reshape(n_seq, tokens, 2 * kv_width))
    w_qo = [h.reshape(n_fsdp // 2, -1, h.shape[1]) for h in w_gather.finish(kvs[0])]
    g_gathers = [Gather(gate(gout[0], w_gather.far), n_fsdp)]
    for m in range(1, micros):
        g_gathers.append(Gather(gate(gout[m], g_gathers[-1].near), n_fsdp))
    q_t = q_project(
        place, gate(normed_one, kvs[0]), w_qo, q_width, cosine_all, sine_all
    )

    state, xg_all = [], []
    for m in range(micros):
        if m == 0:
            info = gate(infos[m], g_gathers[0].near)
            g_gathers[0].further(q_t)
        else:
            info = gate(infos[m], state[-1][2], g_gathers[m].far)
            g_all = [g.finish() for g in g_gathers]
        attn, attn_t, lse = attend(info, q_t, kvs[m], m, tokens)
        if m == 0:
            attn = gate(attn, g_gathers[0].far)
            for g in g_gathers[1:]:
                g.further(g_gathers[0].far)
        residual, xg, exact = after_attention(
            place, attn, w_qo, q_width, x, m, gain_two, router_all, chosen
        )
        state.append((attn_t, lse, residual, exact))
        xg_all.append(gather_rows(xg))

    xg_all[0] = gate(xg_all[0], state[-1][2], g_all)
    passed, backs = [], []
    for m in range(micros):
        *y, back, hg, gp = run_experts(
            own, order, xg_all[m], g_all[m], w_gate, w_up, w_down
        )
        passed.append((xg_all[m], hg, gp))
        backs.append((scatter_rows(back), y))

    names = [(name, e) for name in ("down", "gate", "up") for e in range(experts)]

    def expert_grad(name, e, got):
        xs, hgs, gps = ([p[i] for p in got] for i in range(3))
        if name == "down":
            return down_grad(hgs, e, hidden, g_all, n_fsdp)
        return wide_grad(xs, 0, dim, gps, 2 * e + (name == "up"), hidden)

    line = Line(n_seq)
    found = [{} for _ in range(micros)]

    def to_heads(m):
        attn_t, lse, residual, exact = state[m]
        gres, g_attn, g_t, small_two = before_attention(
            place, backs[m][0], residual, exact, gout[m], gain_two, router_all, w_qo, q_width
        )
        found[m].update(gres=gres, g_attn=g_attn, g_t=g_t, small_two=small_two)

    def through_heads(m):
        attn_t, lse = state[m][:2]
        gq, by_owner = attend_back(
            infos[m], q_t, found[m]["g_t"], attn_t, lse, cosine, sine, kvs[m], m, tokens
        )
        found[m].update(gq=gq, by_owner=by_owner)

    owned = {}

    def to_owners(m):
        by_owner = found[m].pop("by_owner")
        shape = by_owner.shape
        owned[m] = lax.psum_scatter(
            by_owner.reshape(n_seq * shape[1] * tokens, shape[3]),
            "seq",
            scatter_dimension=0,
            tiled=True,
        ).reshape(shape[1:])

    def finish(m):
        f = found[m]
        f["dkv"] = turn_back(f["mine"], cosine, sine)
        f["din"], f["small_one"] = last_step(
            place, f["gq"], f["dkv"], w_qo, w_kv, x, m, gain_one, f["gres"]
        )

    def rest_grads():
        every = lambda name: [f[name] for f in found]
        return projection_grads(
            normed_one, every("gq"), every("dkv"), every("small_two"), every("small_one"), n_experts
        )

    n_grads = len(names)
    work = {
        0: [("grad", 1), (to_heads, 0)],
        1: [("grad", 2), (through_heads, 0)],
        2: [("grad", 3), (to_heads, 1), (through_heads, 1)],
        3: [("grad", 4), (finish, 0), ("grad", 5)],
        4: [(finish, 1)],
    }
    def widen(parts, turned):
        return jnp.stack([(p.T if turned else p).astype(F32) for p in parts])

    experts_out = []
    chunks = {0: expert_grad(*names[0], passed)}
    chunks.update({i: expert_grad(*names[i], passed) for i in range(6, n_grads)})
    slots = max(n_grads, 6)
    moe = Scatter([b[1] for b in backs], n_fsdp)
    for t in range(slots + 3):
        if t in (3, 4):
            found[t - 3]["mine"] = owned[t - 3]
        if t == 3:
            heads = Scatter([found[0].pop("out")], n_fsdp)
        if t in (6, 8):
            found[0]["rest"] = rest
        held = (chunks, line.held, line.results, passed, found, moe.arrays)
        if t >= 3:
            *held, heads.arrays = lax.optimization_barrier((*held, heads.arrays))
        else:
            held = lax.optimization_barrier(held)
        chunks, line.held, line.results, passed, found, moe.arrays = held
        if t == 6:
            rest = lax.psum(found[0].pop("rest"), "seq")
        if len(line.results) in (experts, 2 * experts) and t < slots + 2:
            pair = line.sums()[-experts:]
            experts_out.append(widen(pair, len(experts_out) == 0))
            found[1]["wide"] = experts_out[-1]
        if t == slots:
            chunks[slots] = heads.arrays[0]
        sent = chunks.pop(t, None)
        if t in (2, 3):
            to_owners(t - 2)
        for kind, i in work.get(t, []):
            if kind != "grad":
                kind(i)
            elif i < n_grads:
                chunks[i] = expert_grad(*names[i], passed)
        if t == 2:
            found[0]["out"] = out_grad(
                order, [st[0] for st in state], [f["g_attn"] for f in found]
            )
        if t == 4:
            rest = scatter_rows(rest_grads())
        if t in (5, 6, 7):
            moe.advance()
        for _ in range(3 if t == 3 else 0):
            heads.advance()
        line.step(sent, (chunks, found))
    rest = found[0]["rest"].astype(F32)
    totals = line.sums()
    for i in range(len(experts_out), 3):
        experts_out.append(widen(totals[i * experts : (i + 1) * experts], i == 0))
    d_out = totals[n_grads].astype(F32)

    outs = []
    for m in range(micros):
        outs.append(
            jnp.where(valid[m][:, None], state[m][2] + moe.arrays[m].astype(F32), 0.0).astype(BF)
        )
    grads = [f["din"] for f in found]
    assert len(totals) == n_grads + 1
    shape = (micros, 1, tokens, dim)
    ends = q_width + 2 * kv_width
    return (
        jnp.stack(outs).reshape(shape),
        jnp.stack(grads).reshape(shape),
        rest[:, ends + n_experts],
        rest[:, :q_width],
        rest[:, q_width : q_width + kv_width],
        rest[:, q_width + kv_width : ends],
        d_out,
        rest[:, ends + n_experts + 1],
        rest[:, ends : ends + n_experts],
        *experts_out[1:],
        experts_out[0],
    )


def solution(mesh):
    token_spec = P(None, "fsdp", "seq", None)
    row, matrix, cube = P("fsdp"), P("fsdp", None), P("fsdp", None, None)
    return jax.shard_map(
        functools.partial(on_device, mesh.shape["seq"], mesh.shape["fsdp"]),
        mesh=mesh,
        in_specs=(
            token_spec,
            P(None, "fsdp"),
            token_spec,
            token_spec,
            row,
            matrix,
            matrix,
            matrix,
            matrix,
            row,
            matrix,
            cube,
            cube,
            cube,
        ),
        out_specs=(
            token_spec,
            token_spec,
            row,
            matrix,
            matrix,
            matrix,
            matrix,
            row,
            matrix,
            cube,
            cube,
            cube,
        ),
        check_vma=False,
    )
```

```python
import functools

import jax
import jax.numpy as jnp
from jax import lax
from jax.experimental import pallas as pl
from jax.experimental.pallas import tpu as pltpu
from jax.sharding import PartitionSpec as P

HEAD = 64
HALF = HEAD // 2
GROUP = 3
TOPK = 8
EPS = 1e-06
THETA = 10000.0
NEGATIVE = -1e30
LANES = 128
SCALE = HEAD ** (-0.5)
BF = jnp.bfloat16
F32 = jnp.float32
VMEM_BYTES = 60 * 1024 * 1024

NN = (((1,), (0,)), ((), ()))
NT = (((1,), (1,)), ((), ()))
TN = (((0,), (0,)), ((), ()))


def dot(a, b, dims=NN):
    return lax.dot_general(a, b, dims, preferred_element_type=F32)


def params():
    return pltpu.CompilerParams(vmem_limit_bytes=VMEM_BYTES)


def cost(flops, moved, trans=0):
    parts = (int(v) // 10 for v in (flops, moved, trans))
    flops, moved, trans = parts
    return pl.CostEstimate(flops=flops, bytes_accessed=moved, transcendentals=trans)


def whole(shape):
    zeros = (0,) * len(shape)
    return pl.BlockSpec(shape, lambda *_: zeros)


def smem():
    return pl.BlockSpec(memory_space=pltpu.SMEM)


def pick(at, first_ref, second_ref, index=None):
    half = first_ref.shape[0]
    if index is None:
        index = lax.rem(at, half)
    return jnp.where(at < half, first_ref[index], second_ref[index])


def in_order(place_ref, w_refs):
    devices = 2 * w_refs[0].shape[0]
    return jnp.concatenate([pick(place_ref[j], *w_refs) for j in range(devices)], axis=0)


def rotate(rows, cosine, sine, sign):
    pieces = []
    for h in range(rows.shape[0] // HEAD):
        a = rows[h * HEAD : h * HEAD + HALF]
        b = rows[h * HEAD + HALF : (h + 1) * HEAD]
        if sign > 0:
            pieces += [a * cosine - b * sine, b * cosine + a * sine]
        else:
            pieces += [a * cosine + b * sine, b * cosine - a * sine]
    return jnp.concatenate(pieces, axis=0)


def unpack_kernel(n_experts, place_ref, wa_ref, wb_ref, router_ref, rows_ref):
    w = in_order(place_ref, (wa_ref, wb_ref))
    lane = lax.broadcasted_iota(jnp.int32, w.shape, 1)
    router_ref[...] = jnp.where(lane < n_experts, w.astype(F32), 0.0).astype(BF)
    rows_ref[...] = w.astype(F32).T


def unpack(place, w, block, n_experts):
    dim = 2 * w[0].shape[0] * w[0].shape[1]
    return pl.pallas_call(
        functools.partial(unpack_kernel, n_experts),
        name="unpack",
        grid=(1,),
        in_specs=[smem(), *w_columns(w, LANES, lambda i: block)],
        out_specs=[whole((dim, LANES)), whole((LANES, dim))],
        out_shape=[
            jax.ShapeDtypeStruct((dim, LANES), BF),
            jax.ShapeDtypeStruct((LANES, dim), F32),
        ],
        compiler_params=params(),
        cost_estimate=cost(0, 12 * dim * LANES),
    )(place, *w)


def kv_kernel(place_ref, x_ref, gain_ref, wa_ref, wb_ref, cos_ref, sin_ref, kv_ref, normed_ref):
    step = pl.program_id(0)

    @pl.when(step == 0)
    def _():
        x = x_ref[...].astype(F32)
        inv = lax.rsqrt(jnp.mean(x * x, axis=-1, keepdims=True) + EPS)
        normed_ref[...] = (x * inv * gain_ref[...]).astype(BF)
        r = dot(normed_ref[...], in_order(place_ref, (wa_ref, wb_ref)))
        r = rotate(r.T, cos_ref[...], sin_ref[...], 1)
        kv_ref[...] = r.T.astype(BF)

    @pl.when(step == 1)
    def _():
        kv_ref[...] = dot(normed_ref[...], in_order(place_ref, (wa_ref, wb_ref))).astype(BF)


def w_columns(w, tile, at):
    return [pl.BlockSpec((*half.shape[:2], tile), lambda *i: (0, 0, at(*i))) for half in w]


def kv_project(place, x, gain, w, width, cosine, sine):
    rows, dim = x.shape
    return pl.pallas_call(
        kv_kernel,
        name="kv_project",
        grid=(2,),
        in_specs=[
            smem(),
            whole((rows, dim)),
            whole((1, dim)),
            *w_columns(w, width, lambda i: i),
            whole((HALF, rows)),
            whole((HALF, rows)),
        ],
        out_specs=[pl.BlockSpec((rows, width), lambda i: (0, i)), whole((rows, dim))],
        out_shape=[
            jax.ShapeDtypeStruct((rows, 2 * width), BF),
            jax.ShapeDtypeStruct((rows, dim), BF),
        ],
        compiler_params=params(),
        cost_estimate=cost(2 * rows * dim * 2 * width, 2 * (2 * rows * dim + dim * 2 * width)),
    )(place, x, gain, *w, cosine, sine)


def q_kernel(place_ref, normed_ref, wa_ref, wb_ref, cos_ref, sin_ref, q_ref):
    r = dot(normed_ref[...], in_order(place_ref, (wa_ref, wb_ref)))
    r = rotate(r.T, cos_ref[...], sin_ref[...], 1)
    q_ref[...] = r.astype(BF) * BF(SCALE)


def q_project(place, normed, w, width, cosine, sine):
    rows, dim = normed.shape
    tile = 512
    return pl.pallas_call(
        q_kernel,
        name="q_project",
        grid=(width // tile,),
        in_specs=[
            smem(),
            whole((rows, dim)),
            *w_columns(w, tile, lambda i: i),
            whole((HALF, rows)),
            whole((HALF, rows)),
        ],
        out_specs=pl.BlockSpec((tile, rows), lambda i: (i, 0)),
        out_shape=jax.ShapeDtypeStruct((width, rows), BF),
        compiler_params=params(),
        cost_estimate=cost(2 * rows * dim * width, 2 * (2 * rows * dim + dim * width)),
    )(place, normed, *w, cosine, sine)


def side_by_side(ref, j):
    base = j * GROUP * HEAD
    return jnp.concatenate(
        [ref[base + h * HEAD : base + (h + 1) * HEAD, :] for h in range(GROUP)], axis=1
    )


def diagonal_mask(tokens, own_len):
    key = lax.broadcasted_iota(jnp.int32, (tokens, tokens), 0)
    query = lax.broadcasted_iota(jnp.int32, (tokens, tokens), 1)
    one = (key <= query) & (key < own_len)
    return jnp.concatenate([one.astype(jnp.int32)] * GROUP, axis=1) > 0


def attend_kernel(n, info_ref, q_ref, k_ref, v_ref, o_ref, ot_ref, lse_ref, m_ref, l_ref, acc_ref):
    tokens = q_ref.shape[1]
    d = pl.program_id(1)
    s = info_ref[0]
    own_len = info_ref[1] - s * tokens
    active = own_len > 0

    def pair(j):
        cols = slice(j * HEAD, (j + 1) * HEAD)
        scores = dot(k_ref[0, :, cols], side_by_side(q_ref, j))
        return scores, v_ref[0, :, cols].astype(F32).T.astype(BF)

    @pl.when(active & (d == 0))
    def _():
        mask = diagonal_mask(tokens, own_len)
        for j in range(2):
            scores, value_t = pair(j)
            scores = jnp.where(mask, scores, NEGATIVE)
            top = jnp.max(scores, axis=0, keepdims=True)
            p = jnp.exp(scores - top)
            l_ref[j : j + 1] = jnp.sum(p, axis=0, keepdims=True)
            acc_ref[j] = dot(value_t, p.astype(BF))
            m_ref[j : j + 1] = top

    @pl.when(active & (d > 0) & (d <= s))
    def _():
        for j in range(2):
            scores, value_t = pair(j)
            old = m_ref[j : j + 1]
            top = jnp.maximum(old, jnp.max(scores, axis=0, keepdims=True))
            keep = jnp.exp(old - top)
            p = jnp.exp(scores - top)
            l_ref[j : j + 1] = l_ref[j : j + 1] * keep + jnp.sum(p, axis=0, keepdims=True)
            acc_ref[j] = acc_ref[j] * keep + dot(value_t, p.astype(BF))
            m_ref[j : j + 1] = top

    @pl.when(active & (d == n - 1))
    def _():
        pieces = []
        for j in range(2):
            out = acc_ref[j] / l_ref[j : j + 1]
            lse_ref[j : j + 1] = m_ref[j : j + 1] + jnp.log(l_ref[j : j + 1])
            pieces += [out[:, h * tokens : (h + 1) * tokens] for h in range(GROUP)]
        out = jnp.concatenate(pieces, axis=0)
        ot_ref[...] = out.astype(BF)
        o_ref[...] = out.T.astype(BF)

    @pl.when(jnp.logical_not(active) & (d == 0))
    def _():
        o_ref[...] = jnp.zeros_like(o_ref)
        ot_ref[...] = jnp.zeros_like(ot_ref)
        lse_ref[...] = jnp.zeros_like(lse_ref)


def owner(info_ref, d, n):
    return lax.rem(info_ref[0] + n - d, n)


def attend(info, q_t, kv, micro, tokens):
    n = kv.shape[0]
    width = q_t.shape[0]
    kv_width = kv.shape[2] // 2
    steps = kv_width // LANES
    qw = width // steps
    return pl.pallas_call(
        functools.partial(attend_kernel, n),
        name="attend",
        grid_spec=pltpu.PrefetchScalarGridSpec(
            num_scalar_prefetch=1,
            grid=(steps, n),
            in_specs=[
                pl.BlockSpec((qw, tokens), lambda i, d, info: (i, micro)),
                pl.BlockSpec((1, tokens, LANES), lambda i, d, info: (owner(info, d, n), 0, i)),
                pl.BlockSpec(
                    (1, tokens, LANES), lambda i, d, info: (owner(info, d, n), 0, steps + i)
                ),
            ],
            out_specs=[
                pl.BlockSpec((tokens, qw), lambda i, d, info: (0, i)),
                pl.BlockSpec((qw, tokens), lambda i, d, info: (i, 0)),
                pl.BlockSpec((8, GROUP * tokens), lambda i, d, info: (i, 0)),
            ],
            scratch_shapes=[
                pltpu.VMEM((8, GROUP * tokens), F32),
                pltpu.VMEM((8, GROUP * tokens), F32),
                pltpu.VMEM((2, HEAD, GROUP * tokens), F32),
            ],
        ),
        out_shape=[
            jax.ShapeDtypeStruct((tokens, width), BF),
            jax.ShapeDtypeStruct((width, tokens), BF),
            jax.ShapeDtypeStruct((8 * steps, GROUP * tokens), F32),
        ],
        compiler_params=params(),
        cost_estimate=cost(
            4 * 4 * width * tokens * tokens * n,
            2 * (3 * width * tokens + n * tokens * 2 * kv_width),
            width // HEAD * tokens * tokens * n,
        ),
    )(info, q_t, kv, kv)


def attend_back_kernel(
    n, info_ref, q_ref, g_ref, o_ref, lse_ref, cos_ref, sin_ref, k_ref, v_ref, gq_ref, dkv_ref, acc_ref
):
    tokens = q_ref.shape[1]
    d = pl.program_id(1)
    s = info_ref[0]
    own_len = info_ref[1] - s * tokens
    active = own_len > 0

    def block(first):
        mask = diagonal_mask(tokens, own_len) if first else None
        dks, dvs = [], []
        for j in range(2):
            cols = slice(j * HEAD, (j + 1) * HEAD)
            key, value = k_ref[0, :, cols], v_ref[0, :, cols]
            query, grad = side_by_side(q_ref, j), side_by_side(g_ref, j)
            out = side_by_side(o_ref, j)
            inner = jnp.sum(grad.astype(F32) * out.astype(F32), axis=0, keepdims=True)
            p = jnp.exp(dot(key, query) - lse_ref[j : j + 1])
            if first:
                p = jnp.where(mask, p, 0.0)
            dp = dot(value, grad)
            ds = (p * (dp - inner)).astype(BF)
            dvs.append(dot(p.astype(BF), grad, NT))
            dks.append(dot(ds, query, NT))
            part = dot(key.astype(F32).T.astype(BF), ds)
            if first:
                acc_ref[j] = part
            else:
                acc_ref[j] += part
        dkv_ref[0, 0] = jnp.concatenate(dks, axis=1).astype(BF)
        dkv_ref[0, 1] = jnp.concatenate(dvs, axis=1).astype(BF)

    pl.when(active & (d == 0))(lambda: block(True))
    pl.when(active & (d > 0) & (d <= s))(lambda: block(False))

    @pl.when(active & (d == n - 1))
    def _():
        pieces = []
        for j in range(2):
            for h in range(GROUP):
                piece = acc_ref[j, :, h * tokens : (h + 1) * tokens] * SCALE
                pieces.append(piece.astype(BF).astype(F32))
        grad_q = rotate(jnp.concatenate(pieces, axis=0), cos_ref[...], sin_ref[...], -1)
        gq_ref[...] = grad_q.T.astype(BF)

    @pl.when(jnp.logical_not(active) | (d > s))
    def _():
        dkv_ref[...] = jnp.zeros_like(dkv_ref)

    @pl.when(jnp.logical_not(active) & (d == 0))
    def _():
        gq_ref[...] = jnp.zeros_like(gq_ref)


def attend_back(info, q_t, g_t, o_t, lse, cosine, sine, kv, micro, tokens):
    n = kv.shape[0]
    width = q_t.shape[0]
    kv_width = kv.shape[2] // 2
    steps = kv_width // LANES
    qw = width // steps
    transposed = pl.BlockSpec((qw, tokens), lambda i, d, info: (i, 0))
    return pl.pallas_call(
        functools.partial(attend_back_kernel, n),
        name="attend_back",
        grid_spec=pltpu.PrefetchScalarGridSpec(
            num_scalar_prefetch=1,
            grid=(steps, n),
            in_specs=[
            pl.BlockSpec((qw, tokens), lambda i, d, info: (i, micro)),
            transposed,
            transposed,
            pl.BlockSpec((8, GROUP * tokens), lambda i, d, info: (i, 0)),
            whole((HALF, tokens)),
            whole((HALF, tokens)),
            pl.BlockSpec((1, tokens, LANES), lambda i, d, info: (owner(info, d, n), 0, i)),
            pl.BlockSpec(
                (1, tokens, LANES), lambda i, d, info: (owner(info, d, n), 0, steps + i)
            ),
        ],
        out_specs=[
            pl.BlockSpec((tokens, qw), lambda i, d, info: (0, i)),
            pl.BlockSpec(
                (1, 2, tokens, LANES), lambda i, d, info: (owner(info, d, n), 0, 0, i)
            ),
        ],
            scratch_shapes=[pltpu.VMEM((2, HEAD, GROUP * tokens), F32)],
        ),
        out_shape=[
            jax.ShapeDtypeStruct((tokens, width), BF),
            jax.ShapeDtypeStruct((n, 2, tokens, kv_width), BF),
        ],
        compiler_params=params(),
        cost_estimate=cost(
            10 * 4 * width * tokens * tokens * n,
            2 * (4 * width * tokens + 2 * n * tokens * 2 * kv_width),
            width // HEAD * tokens * tokens * n,
        ),
    )(info, q_t, g_t, o_t, lse, cosine, sine, kv, kv)


def after_kernel(
    steps, place_ref, a_ref, wa_ref, wb_ref, x_ref, gain_ref, router_ref, chosen_ref, res_ref, xg_ref, ge_ref, acc_ref
):
    step = pl.program_id(0)
    acc_ref[step] = dot(a_ref[...], in_order(place_ref, (wa_ref, wb_ref)))

    @pl.when(step == steps - 1)
    def _():
        dim = x_ref.shape[1]
        product = jnp.concatenate([acc_ref[i] for i in range(steps)], axis=1)
        residual = x_ref[...].astype(F32) + product
        res_ref[...] = residual
        inv = lax.rsqrt(jnp.mean(residual * residual, axis=-1, keepdims=True) + EPS)
        normed = (residual * inv * gain_ref[...]).astype(BF)
        logits = dot(normed, router_ref[...])
        chosen = chosen_ref[...] > 0
        logits = jnp.where(chosen, logits, NEGATIVE)
        top = jnp.max(logits, axis=-1, keepdims=True)
        e = jnp.where(chosen, jnp.exp(logits - top), 0.0)
        exact = e / jnp.sum(e, axis=-1, keepdims=True)
        ge_ref[...] = exact
        xg_ref[:, :dim] = normed
        xg_ref[:, dim:] = exact.astype(BF)


def after_attention(place, attn, w, first, x, micro, gain, router, chosen):
    tokens, width = attn.shape
    dim = x.shape[1]
    tile = 512
    steps = dim // tile
    return pl.pallas_call(
        functools.partial(after_kernel, steps),
        name="after_attention",
        grid=(steps,),
        in_specs=[
            smem(),
            whole((tokens, width)),
            *w_columns(w, tile, lambda i: first // tile + i),
            pl.BlockSpec((tokens, dim), lambda i: (micro, 0)),
            whole((1, dim)),
            whole((dim, LANES)),
            pl.BlockSpec((tokens, LANES), lambda i: (micro, 0)),
        ],
        out_specs=[
            whole((tokens, dim)),
            whole((tokens, dim + LANES)),
            whole((tokens, LANES)),
        ],
        out_shape=[
            jax.ShapeDtypeStruct((tokens, dim), F32),
            jax.ShapeDtypeStruct((tokens, dim + LANES), BF),
            jax.ShapeDtypeStruct((tokens, LANES), F32),
        ],
        scratch_shapes=[pltpu.VMEM((steps, tokens, tile), F32)],
        compiler_params=params(),
        cost_estimate=cost(2 * tokens * width * dim, 2 * width * dim + 10 * tokens * dim),
    )(place, attn, *w, x, gain, router, chosen)


def expert_kernel(
    experts, half, own_ref, order_ref, xg_ref, ga_ref, gb_ref, wg_ref, wu_ref, wd_ref, ya_ref, yb_ref, back_ref, hg_ref, gp_ref
):
    rows, dim = ga_ref.shape
    hidden = wg_ref.shape[2]
    x = xg_ref[:, :dim]
    step = pl.program_id(0)
    g = jnp.where(step < half, ga_ref[...], gb_ref[...])
    gates = xg_ref[:, dim:].astype(F32)
    lane = lax.broadcasted_iota(jnp.int32, (rows, LANES), 1)
    gate_cols = jnp.zeros((rows, LANES), F32)
    for e in range(experts):
        mine = lane == own_ref[0] + e
        gate = jnp.sum(jnp.where(mine, gates, 0.0), axis=1, keepdims=True)
        pre_gate = dot(x, wg_ref[e])
        pre_up = dot(x, wu_ref[e])
        grad_hidden = dot(g, wd_ref[e], NT)
        sig = 1.0 / (1.0 + jnp.exp(-pre_gate))
        silu = pre_gate * sig
        h = (silu * pre_up).astype(BF).astype(F32)
        per_gate = jnp.sum(h * grad_hidden, axis=1, keepdims=True)
        gate_cols = jnp.where(mine, per_gate, gate_cols)
        hg_ref[:, e * hidden : (e + 1) * hidden] = (gate * h).astype(BF)
        gh = gate * grad_hidden
        base = 2 * e * hidden
        gp_ref[:, base : base + hidden] = (
            gh * pre_up * (sig * (1.0 + pre_gate * (1.0 - sig)))
        ).astype(BF)
        gp_ref[:, base + hidden : base + 2 * hidden] = (gh * silu).astype(BF)
    y = dot(hg_ref[:, :hidden], wd_ref[0])
    for e in range(1, experts):
        y += dot(hg_ref[:, e * hidden : (e + 1) * hidden], wd_ref[e])

    @pl.when(step < half)
    def _():
        ya_ref[...] = y.astype(BF)

    @pl.when(step >= half)
    def _():
        yb_ref[...] = y.astype(BF)

    back = None
    for e in range(experts):
        base = 2 * e * hidden
        part = dot(gp_ref[:, base : base + hidden], wg_ref[e], NT)
        part += dot(gp_ref[:, base + hidden : base + 2 * hidden], wu_ref[e], NT)
        back = part if back is None else back + part
    back_ref[:, :dim] = back.astype(BF)
    back_ref[:, dim:] = gate_cols.astype(BF)


def run_experts(own, order, xg, g, w_gate, w_up, w_down):
    rows = xg.shape[0]
    dim = g[0].shape[1]
    experts, _, hidden = w_gate.shape
    devices = order.shape[0]
    tile, half = rows // devices, devices // 2
    named = lambda width: pl.BlockSpec((tile, width), lambda i, own, order: (order[i], 0))
    first = lambda i: jnp.minimum(i, half - 1)
    second = lambda i: jnp.maximum(i - half, 0)
    return pl.pallas_call(
        functools.partial(expert_kernel, experts, half),
        name="run_experts",
        grid_spec=pltpu.PrefetchScalarGridSpec(
            num_scalar_prefetch=2,
            grid=(devices,),
            in_specs=[
                named(dim + LANES),
                pl.BlockSpec((tile, dim), lambda i, *_: (first(i), 0)),
                pl.BlockSpec((tile, dim), lambda i, *_: (second(i), 0)),
                whole(w_gate.shape),
                whole(w_up.shape),
                whole(w_down.shape),
            ],
            out_specs=[
                pl.BlockSpec((tile, dim), lambda i, *_: (first(i), 0)),
                pl.BlockSpec((tile, dim), lambda i, *_: (second(i), 0)),
                named(dim + LANES),
                pl.BlockSpec((tile, experts * hidden), lambda i, *_: (i, 0)),
                named(2 * experts * hidden),
            ],
        ),
        out_shape=[
            jax.ShapeDtypeStruct((rows // 2, dim), BF),
            jax.ShapeDtypeStruct((rows // 2, dim), BF),
            jax.ShapeDtypeStruct((rows, dim + LANES), BF),
            jax.ShapeDtypeStruct((rows, experts * hidden), BF),
            jax.ShapeDtypeStruct((rows, 2 * experts * hidden), BF),
        ],
        compiler_params=params(),
        cost_estimate=cost(
            12 * rows * dim * hidden * experts,
            2 * (4 * rows * dim + 3 * rows * experts * hidden + 3 * experts * dim * hidden),
            rows * experts * hidden,
        ),
    )(own, order, xg, *g, w_gate, w_up, w_down)


def wide_grad_kernel(steps, micros, *refs):
    a_refs, b_refs = refs[:micros], refs[micros : 2 * micros]
    out_ref, acc_ref = refs[2 * micros :]
    step = pl.program_id(0)
    for m in range(micros):

        @pl.when((step >= m * steps) & (step < (m + 1) * steps))
        def _(m=m):
            part = dot(a_refs[m][...], b_refs[m][...], TN)
            if m == 0:

                @pl.when(step == 0)
                def _():
                    acc_ref[...] = part

                @pl.when(step > 0)
                def _():
                    acc_ref[...] += part
            else:
                acc_ref[...] += part

    @pl.when(step == micros * steps - 1)
    def _():
        out_ref[...] = acc_ref[...].astype(BF)


def wide_grad(lefts, left_block, left_width, rights, right_block, right_width, tile=512):
    micros, rows = len(lefts), lefts[0].shape[0]
    steps = rows // tile

    def spec(m, width, column):
        return pl.BlockSpec(
            (tile, width), lambda i: (jnp.clip(i - m * steps, 0, steps - 1), column)
        )

    return pl.pallas_call(
        functools.partial(wide_grad_kernel, steps, micros),
        name="wide_grad",
        grid=(micros * steps,),
        in_specs=[spec(m, left_width, left_block) for m in range(micros)]
        + [spec(m, right_width, right_block) for m in range(micros)],
        out_specs=whole((left_width, right_width)),
        out_shape=jax.ShapeDtypeStruct((left_width, right_width), BF),
        scratch_shapes=[pltpu.VMEM((left_width, right_width), F32)],
        compiler_params=params(),
        cost_estimate=cost(
            2 * micros * rows * left_width * right_width,
            2 * (micros * rows * (left_width + right_width) + left_width * right_width),
        ),
    )(*lefts, *rights)


def down_grad_kernel(micros, devices, *refs):
    hg_refs, refs = refs[:micros], refs[micros:]
    ga_refs, gb_refs = refs[:micros], refs[micros : 2 * micros]
    out_ref, acc_ref = refs[2 * micros :]
    step = pl.program_id(0)
    g = [jnp.where(step < devices // 2, a[...], b[...]) for a, b in zip(ga_refs, gb_refs)]
    part = dot(jnp.concatenate(g), jnp.concatenate([r[...] for r in hg_refs]), TN)

    @pl.when(step == 0)
    def _():
        acc_ref[...] = part

    @pl.when(step > 0)
    def _():
        acc_ref[...] += part

    @pl.when(step == devices - 1)
    def _():
        out_ref[...] = acc_ref[...].astype(BF)


def down_grad(hgs, expert, hidden, gs, devices):
    micros, rows = len(hgs), hgs[0].shape[0]
    tile, half = rows // devices, devices // 2
    dim = gs[0][0].shape[1]
    return pl.pallas_call(
        functools.partial(down_grad_kernel, micros, devices),
        name="down_grad",
        grid=(devices,),
        in_specs=[pl.BlockSpec((tile, hidden), lambda i: (i, expert))] * micros
        + [pl.BlockSpec((tile, dim), lambda i: (jnp.minimum(i, half - 1), 0))] * micros
        + [pl.BlockSpec((tile, dim), lambda i: (jnp.maximum(i - half, 0), 0))] * micros,
        out_specs=whole((dim, hidden)),
        out_shape=jax.ShapeDtypeStruct((dim, hidden), BF),
        scratch_shapes=[pltpu.VMEM((dim, hidden), F32)],
        compiler_params=params(),
        cost_estimate=cost(2 * micros * rows * hidden * dim, 2 * micros * rows * (hidden + dim)),
    )(*hgs, *[g[0] for g in gs], *[g[1] for g in gs])


def before_kernel(
    steps, place_ref, ret_ref, res_ref, ge_ref, gout_ref, gain_ref, router_ref, wa_ref, wb_ref, gres_ref, ga_ref, gt_ref, small_ref, cut_ref, acc_ref
):
    dim = res_ref.shape[1]

    step = pl.program_id(0)
    tile = dim // steps

    @pl.when(step == 0)
    def _():
        ge = ge_ref[...]
        gg = ret_ref[:, dim:].astype(F32)
        gl = ge * (gg - jnp.sum(ge * gg, axis=-1, keepdims=True))
        high = gl.astype(BF)
        low = (gl - high.astype(F32)).astype(BF)
        router = router_ref[...]
        gn = ret_ref[:, :dim].astype(F32) + (dot(high, router, NT) + dot(low, router, NT))
        residual = res_ref[...]
        gain = gain_ref[...]
        inv = lax.rsqrt(jnp.mean(residual * residual, axis=-1, keepdims=True) + EPS)
        unit = residual * inv
        normed = (unit * gain).astype(BF)
        small_ref[:LANES] = dot(high, normed, TN) + dot(low, normed, TN)
        gain_row = jnp.sum(gn * unit, axis=0, keepdims=True)
        small_ref[LANES:] = jnp.broadcast_to(gain_row, (8, dim))
        u = gn * gain
        gres = gout_ref[...].astype(F32) + inv * (
            u - unit * jnp.mean(u * unit, axis=-1, keepdims=True)
        )
        gres_ref[...] = gres
        low_gres = gres.astype(BF)
        ga_ref[...] = low_gres
        for i in range(steps):
            cut_ref[i] = low_gres[:, i * tile : (i + 1) * tile]
        acc_ref[...] = jnp.zeros_like(acc_ref)

    acc_ref[...] += dot(in_order(place_ref, (wa_ref, wb_ref)), cut_ref[step], NT)

    @pl.when(step == steps - 1)
    def _():
        gt_ref[...] = acc_ref[...].astype(BF)


def before_attention(place, returned, residual, exact, gout, gain, router, w, first):
    tokens, dim = residual.shape
    width = 2 * w[0].shape[0] * w[0].shape[1]
    tile = 512
    steps = dim // tile
    return pl.pallas_call(
        functools.partial(before_kernel, steps),
        name="before_attention",
        grid=(steps,),
        in_specs=[
            smem(),
            whole((tokens, dim + LANES)),
            whole((tokens, dim)),
            whole((tokens, LANES)),
            whole((tokens, dim)),
            whole((1, dim)),
            whole((dim, LANES)),
            *w_columns(w, tile, lambda i: first // tile + i),
        ],
        out_specs=[
            whole((tokens, dim)),
            whole((tokens, dim)),
            whole((width, tokens)),
            whole((LANES + 8, dim)),
        ],
        out_shape=[
            jax.ShapeDtypeStruct((tokens, dim), F32),
            jax.ShapeDtypeStruct((tokens, dim), BF),
            jax.ShapeDtypeStruct((width, tokens), BF),
            jax.ShapeDtypeStruct((LANES + 8, dim), F32),
        ],
        scratch_shapes=[
            pltpu.VMEM((steps, tokens, tile), BF),
            pltpu.VMEM((width, tokens), F32),
        ],
        compiler_params=params(),
        cost_estimate=cost(2 * tokens * width * dim, 2 * width * dim + 14 * tokens * dim),
    )(place, returned, residual, exact, gout, gain, router, *w)


def last_kernel(
    q_steps, steps, place_ref, gq_ref, dkv_ref, qa_ref, qb_ref, kva_ref, kvb_ref, x_ref, gain_ref, gres_ref, din_ref, small_ref, acc_ref
):
    step = pl.program_id(0)

    @pl.when(step == 0)
    def _():
        acc_ref[...] = dot(gq_ref[...], in_order(place_ref, (qa_ref, qb_ref)), NT)

    @pl.when((step > 0) & (step < q_steps))
    def _():
        acc_ref[...] += dot(gq_ref[...], in_order(place_ref, (qa_ref, qb_ref)), NT)

    @pl.when(step >= q_steps)
    def _():
        acc_ref[...] += dot(dkv_ref[...], in_order(place_ref, (kva_ref, kvb_ref)), NT)

    @pl.when(step == steps - 1)
    def _():
        x = x_ref[...].astype(F32)
        gain = gain_ref[...]
        inv = lax.rsqrt(jnp.mean(x * x, axis=-1, keepdims=True) + EPS)
        unit = x * inv
        gn = acc_ref[...]
        small_ref[...] = jnp.broadcast_to(
            jnp.sum(gn * unit, axis=0, keepdims=True), small_ref.shape
        )
        w = gn * gain
        grad = inv * (w - unit * jnp.mean(w * unit, axis=-1, keepdims=True))
        din_ref[...] = (grad + gres_ref[...]).astype(BF)


def last_step(place, gq, dkv, w_q, w_kv, x, micro, gain, gres):
    tokens, dim = gres.shape
    tile = 512
    q_steps, kv_steps = gq.shape[1] // tile, dkv.shape[1] // tile
    steps = q_steps + kv_steps
    q_at = lambda i: (0, jnp.minimum(i, q_steps - 1))
    kv_at = lambda i: (0, jnp.maximum(i - q_steps, 0))
    return pl.pallas_call(
        functools.partial(last_kernel, q_steps, steps),
        name="last_step",
        grid=(steps,),
        in_specs=[
            smem(),
            pl.BlockSpec((tokens, tile), q_at),
            pl.BlockSpec((tokens, tile), kv_at),
            *w_columns(w_q, tile, lambda i: q_at(i)[1]),
            *w_columns(w_kv, tile, lambda i: kv_at(i)[1]),
            pl.BlockSpec((tokens, dim), lambda i: (micro, 0)),
            whole((1, dim)),
            whole((tokens, dim)),
        ],
        out_specs=[whole((tokens, dim)), whole((8, dim))],
        out_shape=[
            jax.ShapeDtypeStruct((tokens, dim), BF),
            jax.ShapeDtypeStruct((8, dim), F32),
        ],
        scratch_shapes=[pltpu.VMEM((tokens, dim), F32)],
        compiler_params=params(),
        cost_estimate=cost(
            2 * tokens * steps * tile * dim, 2 * steps * tile * dim + 12 * tokens * dim
        ),
    )(place, gq, dkv, *w_q, *w_kv, x, gain, gres)


def out_grad_kernel(micros, half, order_ref, *refs):
    t_refs, g_refs, (first_ref, second_ref) = refs[:micros], refs[micros : 2 * micros], refs[2 * micros :]
    step = pl.program_id(0)
    total = dot(t_refs[0][...], g_refs[0][...])
    for t_ref, g_ref in zip(t_refs[1:], g_refs[1:]):
        total += dot(t_ref[...], g_ref[...])

    @pl.when(step < half)
    def _():
        first_ref[...] = total.astype(BF)

    @pl.when(step >= half)
    def _():
        second_ref[...] = total.astype(BF)


def out_grad(order, heads_t, grads):
    micros, devices = len(heads_t), order.shape[0]
    width, tokens = heads_t[0].shape
    dim = grads[0].shape[1]
    tile, half = width // devices, devices // 2
    return pl.pallas_call(
        functools.partial(out_grad_kernel, micros, half),
        name="out_grad",
        grid_spec=pltpu.PrefetchScalarGridSpec(
            num_scalar_prefetch=1,
            grid=(devices,),
            in_specs=[pl.BlockSpec((tile, tokens), lambda i, order: (order[i], 0))] * micros
            + [whole((tokens, dim))] * micros,
            out_specs=[
                pl.BlockSpec((tile, dim), lambda i, order: (jnp.minimum(i, half - 1), 0)),
                pl.BlockSpec((tile, dim), lambda i, order: (jnp.maximum(i - half, 0), 0)),
            ],
        ),
        out_shape=[jax.ShapeDtypeStruct((width // 2, dim), BF)] * 2,
        compiler_params=params(),
        cost_estimate=cost(2 * micros * tokens * width * dim, 4 * width * dim),
    )(order, *heads_t, *grads)


def turn_kernel(kv_ref, cos_ref, sin_ref, out_ref):
    width = kv_ref.shape[2]
    key = rotate(kv_ref[0].astype(F32).T, cos_ref[...], sin_ref[...], -1)
    out_ref[:, :width] = key.T.astype(BF)
    out_ref[:, width:] = kv_ref[1]


def turn_back(kv, cosine, sine):
    _, tokens, width = kv.shape
    return pl.pallas_call(
        turn_kernel,
        name="turn_back",
        out_shape=jax.ShapeDtypeStruct((tokens, 2 * width), BF),
        compiler_params=params(),
        cost_estimate=cost(0, 8 * tokens * width),
    )(kv, cosine, sine)


def projection_kernel(micros, q_steps, steps, n_experts, normed_ref, *refs):
    gq_refs, refs = refs[:micros], refs[micros:]
    dkv_refs, refs = refs[:micros], refs[micros:]
    two_refs, refs = refs[:micros], refs[micros:]
    one_refs, (out_ref, turned_ref) = refs[:micros], refs[micros:]
    step = pl.program_id(0)
    tile = gq_refs[0].shape[1]

    @pl.when(step == 0)
    def _():
        turned_ref[...] = normed_ref[...].astype(F32).T.astype(BF)
        rows = functools.reduce(jnp.add, [r[:LANES] for r in two_refs])
        gain_two = functools.reduce(jnp.add, [r[LANES : LANES + 1] for r in two_refs])
        gain_one = functools.reduce(jnp.add, [r[:1] for r in one_refs])
        at = lax.broadcasted_iota(jnp.int32, rows.shape, 0)
        rows = jnp.where(at == n_experts, gain_one, rows)
        rows = jnp.where(at == n_experts + 1, gain_two, rows)
        out_ref[:, steps * tile :] = rows.T.astype(BF)

    q = jnp.concatenate([r[...] for r in gq_refs], axis=0)
    kv = jnp.concatenate([r[...] for r in dkv_refs], axis=0)
    g = jnp.where(step < q_steps, q, kv)
    out_ref[:, pl.ds(pl.multiple_of(step * tile, tile), tile)] = dot(turned_ref[...], g).astype(BF)


def projection_grads(normed, gqs, dkvs, twos, ones, n_experts):
    rows, dim = normed.shape
    micros, tokens, tile = len(gqs), gqs[0].shape[0], 512
    q_steps, kv_steps = gqs[0].shape[1] // tile, dkvs[0].shape[1] // tile
    steps = q_steps + kv_steps
    width = steps * tile + LANES
    return pl.pallas_call(
        functools.partial(projection_kernel, micros, q_steps, steps, n_experts),
        name="projection_grads",
        grid=(steps,),
        in_specs=[whole((rows, dim))]
        + [pl.BlockSpec((tokens, tile), lambda i: (0, jnp.minimum(i, q_steps - 1)))] * micros
        + [pl.BlockSpec((tokens, tile), lambda i: (0, jnp.maximum(i - q_steps, 0)))] * micros
        + [whole(twos[0].shape)] * micros
        + [whole(ones[0].shape)] * micros,
        out_specs=whole((dim, width)),
        out_shape=jax.ShapeDtypeStruct((dim, width), BF),
        scratch_shapes=[pltpu.VMEM((dim, rows), BF)],
        compiler_params=params(),
        cost_estimate=cost(2 * rows * dim * width, 2 * rows * (dim + width) + 2 * dim * width),
    )(normed, *gqs, *dkvs, *twos, *ones)


def add_low(a, b):
    return (a.astype(F32) + b.astype(F32)).astype(BF)


def line_sum(x, n):
    if n == 1:
        return x
    if n % 2:
        return lax.psum(x, "seq")
    half = n // 2
    at = lax.axis_index("seq")
    for k in range(half - 1):
        x = add_low(x, lax.ppermute(x, "seq", [(k, k + 1), (n - 1 - k, n - 2 - k)]))
    x = add_low(x, lax.ppermute(x, "seq", [(half - 1, half), (half, half - 1)]))
    for k in reversed(range(half - 1)):
        got = lax.ppermute(x, "seq", [(k + 1, k), (n - 2 - k, n - 1 - k)])
        x = jnp.where((at == k) | (at == n - 1 - k), got, x)
    return x


class Line:
    def __init__(self, n):
        self.n = n
        self.held = {}
        self.results = []

    def sums(self):
        at = lax.axis_index("seq")
        middle = (at == 1) | (at == 2)
        return [r[0] if len(r) == 1 else jnp.where(middle, *r) for r in self.results]

    def step(self, chunk, beside):
        n = self.n
        if n != 4:
            if chunk is not None:
                self.results.append((line_sum(chunk, n),))
            return
        at = lax.axis_index("seq")
        middle = (at == 1) | (at == 2)
        come, go = [(0, 1), (3, 2)], [(1, 0), (2, 3)]
        held, self.held = self.held, {}
        summed = held.get("summed")
        if summed is not None:
            summed = add_low(*summed)
        crossing = held.get("crossing")
        if crossing is not None:
            crossing = add_low(*crossing)
            self.held["summed"] = (crossing, lax.ppermute(crossing, "seq", [(1, 2), (2, 1)]))
        if chunk is not None and summed is not None and chunk.shape == summed.shape:
            sent = jnp.where(middle, summed, chunk)
            got = lax.ppermute(sent, "seq", come + go)
            self.results.append((sent, got))
            self.held["crossing"] = (chunk, got)
        else:
            if summed is not None:
                self.results.append((summed, lax.ppermute(summed, "seq", go)))
            if chunk is not None:
                self.held["crossing"] = (chunk, lax.ppermute(chunk, "seq", come))
        self.held, self.results = gate((self.held, self.results), beside)


def gate(x, *others):
    return lax.optimization_barrier((x, others))[0]


CORE, ALONG_X, ALONG_Y = 1, 2, 4


def swap(x, mask):
    return lax.ppermute(x, "fsdp", [(i, i ^ mask) for i in range(8)])


def gather_rows(x):
    return lax.all_gather(x, "fsdp", axis=0, tiled=True)


def assemble_kernel(x_ref, top_x_ref, low_y_ref, top_far_ref, low_far_ref, out_ref):
    rows = x_ref.shape[0]
    half = rows // 2
    out_ref[:rows] = x_ref[...]
    out_ref[rows : rows + half] = top_x_ref[...]
    out_ref[rows + half : 2 * rows] = low_far_ref[:half]
    out_ref[2 * rows : 2 * rows + half] = top_far_ref[:half]
    out_ref[2 * rows + half : 3 * rows] = low_y_ref[...]
    out_ref[3 * rows : 3 * rows + half] = top_far_ref[half:]
    out_ref[3 * rows + half :] = low_far_ref[half:]


def assemble(*pieces):
    rows, width = pieces[0].shape
    block = lambda n: pl.BlockSpec((n, width // 3), lambda i: (0, i))
    return pl.pallas_call(
        assemble_kernel,
        name="assemble",
        grid=(3,),
        in_specs=[block(p.shape[0]) for p in pieces],
        out_specs=block(4 * rows),
        out_shape=jax.ShapeDtypeStruct((4 * rows, width), pieces[0].dtype),
        compiler_params=params(),
        cost_estimate=cost(0, 16 * rows * width),
    )(*pieces)


def gather_near(x, n):
    if n != 8:
        every = gather_rows(x)
        half = every.shape[0] // 2
        return every[:half], every[half:]
    gather = Gather(x, n)
    gather.further()
    return gather.finish()


class Gather:
    def __init__(self, x, n):
        self.n, self.x = n, x
        if n != 8:
            self.halves = gather_near(x, n)
            self.near = self.far = ()
            return
        half = x.shape[0] // 2
        self.near = swap(x[:half], ALONG_X), swap(x[half:], ALONG_Y)

    def further(self, *others):
        if self.n != 8:
            return
        half = self.x.shape[0] // 2
        x, (top_x, low_y) = gate((self.x, self.near), *others)
        self.near = top_x, low_y
        top_far = swap(jnp.concatenate([x[:half], top_x]), ALONG_Y)
        low_far = swap(jnp.concatenate([x[half:], low_y]), ALONG_X)
        self.far = top_far, low_far

    def finish(self, *others):
        if self.n != 8:
            return self.halves
        near, far = gate((self.near, self.far), *others)
        mine = assemble(self.x, *near, *far)
        return mine, swap(mine, CORE)


class Scatter:
    def __init__(self, arrays, n):
        self.arrays, self.n, self.stage = list(arrays), n, 0
        self.rows = 2 * arrays[0][0].shape[0] // n

    def advance(self):
        held, self.stage = self.arrays, self.stage + 1
        rows, half = self.rows, self.rows // 2
        if self.n != 8:
            if self.stage == 1:
                self.arrays = [scatter_rows(jnp.concatenate(a)) for a in held]
            return
        if self.stage == 1:
            self.arrays = [add_low(mine, swap(other, CORE)) for mine, other in held]
        if self.stage == 2:
            tops = [a[k * rows : k * rows + half] for a in held for k in (2, 3)]
            lows = [a[k * rows + half : (k + 1) * rows] for a in held for k in (1, 3)]
            tops = swap(jnp.concatenate(tops), ALONG_Y)
            lows = swap(jnp.concatenate(lows), ALONG_X)
            self.arrays = []
            for i, a in enumerate(held):
                at = 2 * i * half
                self.arrays.append(
                    (
                        add_low(a[:half], tops[at : at + half]),
                        add_low(a[half:rows], lows[at : at + half]),
                        add_low(a[rows : rows + half], tops[at + half : at + rows]),
                        add_low(a[2 * rows + half : 3 * rows], lows[at + half : at + rows]),
                    )
                )
        if self.stage == 3:
            over_x = swap(jnp.concatenate([a[2] for a in held]), ALONG_X)
            over_y = swap(jnp.concatenate([a[3] for a in held]), ALONG_Y)
            self.arrays = [
                jnp.concatenate(
                    [
                        add_low(a[0], over_x[i * half : (i + 1) * half]),
                        add_low(a[1], over_y[i * half : (i + 1) * half]),
                    ]
                )
                for i, a in enumerate(held)
            ]


def block_order(n):
    at = jnp.arange(n, dtype=jnp.int32)
    if n != 8:
        return at
    return lax.axis_index("fsdp").astype(jnp.int32) ^ (2 * lax.rem(at, 4) + at // 4)


def block_places(n):
    if n != 8:
        return jnp.arange(n, dtype=jnp.int32)
    mask = lax.axis_index("fsdp").astype(jnp.int32) ^ jnp.arange(n, dtype=jnp.int32)
    return (mask >> 1) + 4 * (mask & 1)


def scatter_rows(x):
    return lax.psum_scatter(x, "fsdp", scatter_dimension=0, tiled=True)


def on_device(
    n_seq,
    n_fsdp,
    inputs,
    lengths,
    expert_ids,
    cotangent,
    gain_attn,
    w_query,
    key_projection,
    value_projection,
    w_out,
    gain_moe,
    router,
    w_gate,
    w_up,
    w_down,
):
    micros, local_seqs, tokens, dim = inputs.shape
    assert local_seqs == 1
    rows = micros * tokens
    experts, _, hidden = w_gate.shape
    n_experts = router.shape[1]
    kv_width = key_projection.shape[1]
    at = lax.axis_index("seq")
    own = (lax.axis_index("fsdp") * experts).astype(jnp.int32).reshape(1)

    small = jnp.concatenate(
        [router, gain_attn[:, None], gain_moe[:, None]], axis=1
    )
    small = jnp.pad(small, ((0, 0), (0, LANES - small.shape[1])))
    place, order = block_places(n_fsdp), block_order(n_fsdp)

    def weights(w):
        return [h.reshape(n_fsdp // 2, -1, h.shape[1]) for h in gather_near(w, n_fsdp)]

    w_kv = weights(jnp.concatenate([key_projection, value_projection, small], axis=1))
    router_all, rows_all = unpack(place, w_kv, 2 * kv_width // LANES, n_experts)
    gain_one = rows_all[n_experts : n_experts + 1]
    gain_two = rows_all[n_experts + 1 : n_experts + 2]

    positions = at * tokens + jnp.arange(tokens, dtype=jnp.int32)
    frequency = THETA ** (-(jnp.arange(HALF, dtype=F32) * 2.0) / HEAD)
    angles = frequency[:, None] * positions.astype(F32)[None, :]
    cosine, sine = jnp.cos(angles), jnp.sin(angles)
    cosine_all, sine_all = jnp.tile(cosine, (1, micros)), jnp.tile(sine, (1, micros))

    x = inputs.reshape(rows, dim)
    chosen = jnp.sum(
        (
            expert_ids.reshape(rows, TOPK)[:, :, None]
            == jnp.arange(LANES, dtype=jnp.int32)[None, None, :]
        ).astype(F32),
        axis=1,
    )
    valid = positions[None, :] < lengths[:, :1]
    gout = jnp.where(valid[:, :, None], cotangent.reshape(micros, tokens, dim), BF(0))
    infos = [
        jnp.stack([at.astype(jnp.int32), lengths[m, 0].astype(jnp.int32)]) for m in range(micros)
    ]

    kv, normed_one = kv_project(place, x, gain_one, w_kv, kv_width, cosine_all, sine_all)
    q_width = w_query.shape[1]
    w_gather = Gather(gate(jnp.concatenate([w_query, w_out], axis=1), kv), n_fsdp)
    w_gather.further()
    kvs = []
    for m in range(micros):
        mine = kv[m * tokens : (m + 1) * tokens]
        every = lax.all_gather(mine, "seq", axis=0, tiled=True)
        kvs.append(every.reshape(n_seq, tokens, 2 * kv_width))
    w_qo = [h.reshape(n_fsdp // 2, -1, h.shape[1]) for h in w_gather.finish(kvs[0], chosen, infos)]
    g_gathers = [Gather(gate(gout[0], w_gather.far), n_fsdp)]
    for m in range(1, micros):
        g_gathers.append(Gather(gate(gout[m], g_gathers[-1].near), n_fsdp))
    q_t = q_project(
        place, gate(normed_one, kvs[0]), w_qo, q_width, cosine_all, sine_all
    )

    state, xg_all = [], []
    for m in range(micros):
        if m == 0:
            info = gate(infos[m], g_gathers[0].near)
            g_gathers[0].further(q_t)
        else:
            info = gate(infos[m], state[-1][2])
        attn, attn_t, lse = attend(info, q_t, kvs[m], m, tokens)
        if m == 0:
            attn = gate(attn, g_gathers[0].far, [g.near for g in g_gathers[1:]])
            for g in g_gathers[1:]:
                g.further(g_gathers[0].far)
        else:
            attn = gate(attn, g_gathers[m].far)
        residual, xg, exact = after_attention(
            place, attn, w_qo, q_width, x, m, gain_two, router_all, chosen
        )
        state.append((attn_t, lse, residual, exact))
        xg_all.append(gather_rows(xg))

    g_all = [g.finish(state[-1][2]) for g in g_gathers]
    xg_all[0] = gate(xg_all[0], state[-1][2], g_all)
    passed, backs = [], []
    for m in range(micros):
        *y, back, hg, gp = run_experts(
            own, order, xg_all[m], g_all[m], w_gate, w_up, w_down
        )
        passed.append((xg_all[m], hg, gp))
        backs.append((scatter_rows(back), y))

    names = [(name, e) for name in ("down", "gate", "up") for e in range(experts)]

    def expert_grad(name, e, got):
        xs, hgs, gps = ([p[i] for p in got] for i in range(3))
        if name == "down":
            return down_grad(hgs, e, hidden, g_all, n_fsdp)
        return wide_grad(xs, 0, dim, gps, 2 * e + (name == "up"), hidden)

    line = Line(n_seq)
    found = [{} for _ in range(micros)]

    def to_heads(m):
        attn_t, lse, residual, exact = state[m]
        gres, g_attn, g_t, small_two = before_attention(
            place, backs[m][0], residual, exact, gout[m], gain_two, router_all, w_qo, q_width
        )
        found[m].update(gres=gres, g_attn=g_attn, g_t=g_t, small_two=small_two)

    def through_heads(m):
        attn_t, lse = state[m][:2]
        gq, by_owner = attend_back(
            infos[m], q_t, found[m]["g_t"], attn_t, lse, cosine, sine, kvs[m], m, tokens
        )
        found[m].update(gq=gq, by_owner=by_owner)

    owned = {}

    def to_owners(m):
        by_owner = found[m].pop("by_owner")
        shape = by_owner.shape
        owned[m] = lax.psum_scatter(
            by_owner.reshape(n_seq * shape[1] * tokens, shape[3]),
            "seq",
            scatter_dimension=0,
            tiled=True,
        ).reshape(shape[1:])

    def finish(m):
        f = found[m]
        f["dkv"] = turn_back(f["mine"], cosine, sine)
        f["din"], f["small_one"] = last_step(
            place, f["gq"], f["dkv"], w_qo, w_kv, x, m, gain_one, f["gres"]
        )

    def rest_grads():
        every = lambda name: [f[name] for f in found]
        return projection_grads(
            normed_one, every("gq"), every("dkv"), every("small_two"), every("small_one"), n_experts
        )

    n_grads = len(names)
    work = {
        0: [("grad", 1), (to_heads, 0)],
        1: [("grad", 2), (through_heads, 0)],
        2: [("grad", 3), (to_heads, 1), (through_heads, 1)],
        3: [("grad", 4), (finish, 0), ("grad", 5)],
        4: [(finish, 1)],
    }
    def widen(parts, turned):
        return jnp.stack([(p.T if turned else p).astype(F32) for p in parts])

    experts_out = []
    chunks = {0: expert_grad(*names[0], passed)}
    chunks.update({i: expert_grad(*names[i], passed) for i in range(6, n_grads)})
    slots = max(n_grads, 6)
    moe = Scatter([b[1] for b in backs], n_fsdp)
    for t in range(slots + 3):
        if t in (3, 4):
            found[t - 3]["mine"] = owned[t - 3]
        if t == 3:
            heads = Scatter([found[0].pop("out")], n_fsdp)
        if t in (6, 8):
            found[0]["rest"] = rest
        held = (chunks, line.held, line.results, passed, found, moe.arrays)
        if t >= 3:
            *held, heads.arrays = lax.optimization_barrier((*held, heads.arrays))
        else:
            held = lax.optimization_barrier(held)
        chunks, line.held, line.results, passed, found, moe.arrays = held
        if t == 6:
            rest = lax.psum(found[0].pop("rest"), "seq")
        if len(line.results) in (experts, 2 * experts) and t < slots + 2:
            pair = line.sums()[-experts:]
            experts_out.append(widen(pair, len(experts_out) == 0))
            found[1]["wide"] = experts_out[-1]
        if t == slots:
            chunks[slots] = heads.arrays[0]
        sent = chunks.pop(t, None)
        if t in (2, 3):
            to_owners(t - 2)
        for kind, i in work.get(t, []):
            if kind != "grad":
                kind(i)
            elif i < n_grads:
                chunks[i] = expert_grad(*names[i], passed)
        if t == 2:
            found[0]["out"] = out_grad(
                order, [st[0] for st in state], [f["g_attn"] for f in found]
            )
        if t == 4:
            rest = scatter_rows(rest_grads())
        if t in (5, 6, 7):
            moe.advance()
        for _ in range(3 if t == 3 else 0):
            heads.advance()
        line.step(sent, (chunks, found))
    rest = found[0]["rest"].astype(F32)
    totals = line.sums()
    for i in range(len(experts_out), 3):
        experts_out.append(widen(totals[i * experts : (i + 1) * experts], i == 0))
    d_out = totals[n_grads].astype(F32)

    outs = []
    for m in range(micros):
        outs.append(
            jnp.where(valid[m][:, None], state[m][2] + moe.arrays[m].astype(F32), 0.0).astype(BF)
        )
    grads = [f["din"] for f in found]
    assert len(totals) == n_grads + 1
    shape = (micros, 1, tokens, dim)
    ends = q_width + 2 * kv_width
    return (
        jnp.stack(outs).reshape(shape),
        jnp.stack(grads).reshape(shape),
        rest[:, ends + n_experts],
        rest[:, :q_width],
        rest[:, q_width : q_width + kv_width],
        rest[:, q_width + kv_width : ends],
        d_out,
        rest[:, ends + n_experts + 1],
        rest[:, ends : ends + n_experts],
        *experts_out[1:],
        experts_out[0],
    )


def solution(mesh):
    token_spec = P(None, "fsdp", "seq", None)
    row, matrix, cube = P("fsdp"), P("fsdp", None), P("fsdp", None, None)
    return jax.shard_map(
        functools.partial(on_device, mesh.shape["seq"], mesh.shape["fsdp"]),
        mesh=mesh,
        in_specs=(
            token_spec,
            P(None, "fsdp"),
            token_spec,
            token_spec,
            row,
            matrix,
            matrix,
            matrix,
            matrix,
            row,
            matrix,
            cube,
            cube,
            cube,
        ),
        out_specs=(
            token_spec,
            token_spec,
            row,
            matrix,
            matrix,
            matrix,
            matrix,
            row,
            matrix,
            cube,
            cube,
            cube,
        ),
        check_vma=False,
    )
```

```python
import functools

import jax
import jax.numpy as jnp
from jax import lax
from jax.experimental import pallas as pl
from jax.experimental.pallas import tpu as pltpu
from jax.sharding import PartitionSpec as P

HEAD = 64
HALF = HEAD // 2
GROUP = 3
TOPK = 8
EPS = 1e-06
THETA = 10000.0
NEGATIVE = -1e30
LANES = 128
SCALE = HEAD ** (-0.5)
BF = jnp.bfloat16
F32 = jnp.float32
VMEM_BYTES = 60 * 1024 * 1024

NN = (((1,), (0,)), ((), ()))
NT = (((1,), (1,)), ((), ()))
TN = (((0,), (0,)), ((), ()))


def dot(a, b, dims=NN):
    return lax.dot_general(a, b, dims, preferred_element_type=F32)


def params():
    return pltpu.CompilerParams(vmem_limit_bytes=VMEM_BYTES)


def cost(flops, moved, trans=0):
    parts = (int(v) // 10 for v in (flops, moved, trans))
    flops, moved, trans = parts
    return pl.CostEstimate(flops=flops, bytes_accessed=moved, transcendentals=trans)


def whole(shape):
    zeros = (0,) * len(shape)
    return pl.BlockSpec(shape, lambda *_: zeros)


def smem():
    return pl.BlockSpec(memory_space=pltpu.SMEM)


def pick(at, first_ref, second_ref, index=None):
    half = first_ref.shape[0]
    if index is None:
        index = lax.rem(at, half)
    return jnp.where(at < half, first_ref[index], second_ref[index])


def in_order(place_ref, w_refs):
    devices = 2 * w_refs[0].shape[0]
    return jnp.concatenate([pick(place_ref[j], *w_refs) for j in range(devices)], axis=0)


def rotate(rows, cosine, sine, sign):
    pieces = []
    for h in range(rows.shape[0] // HEAD):
        a = rows[h * HEAD : h * HEAD + HALF]
        b = rows[h * HEAD + HALF : (h + 1) * HEAD]
        if sign > 0:
            pieces += [a * cosine - b * sine, b * cosine + a * sine]
        else:
            pieces += [a * cosine + b * sine, b * cosine - a * sine]
    return jnp.concatenate(pieces, axis=0)


def unpack_kernel(n_experts, place_ref, wa_ref, wb_ref, router_ref, rows_ref):
    w = in_order(place_ref, (wa_ref, wb_ref))
    lane = lax.broadcasted_iota(jnp.int32, w.shape, 1)
    router_ref[...] = jnp.where(lane < n_experts, w.astype(F32), 0.0).astype(BF)
    rows_ref[...] = w.astype(F32).T


def unpack(place, w, block, n_experts):
    dim = 2 * w[0].shape[0] * w[0].shape[1]
    return pl.pallas_call(
        functools.partial(unpack_kernel, n_experts),
        name="unpack",
        grid=(1,),
        in_specs=[smem(), *w_columns(w, LANES, lambda i: block)],
        out_specs=[whole((dim, LANES)), whole((LANES, dim))],
        out_shape=[
            jax.ShapeDtypeStruct((dim, LANES), BF),
            jax.ShapeDtypeStruct((LANES, dim), F32),
        ],
        compiler_params=params(),
        cost_estimate=cost(0, 12 * dim * LANES),
    )(place, *w)


def kv_kernel(place_ref, x_ref, gain_ref, wa_ref, wb_ref, cos_ref, sin_ref, kv_ref, normed_ref):
    step = pl.program_id(0)

    @pl.when(step == 0)
    def _():
        x = x_ref[...].astype(F32)
        inv = lax.rsqrt(jnp.mean(x * x, axis=-1, keepdims=True) + EPS)
        normed_ref[...] = (x * inv * gain_ref[...]).astype(BF)
        r = dot(normed_ref[...], in_order(place_ref, (wa_ref, wb_ref)))
        r = rotate(r.T, cos_ref[...], sin_ref[...], 1)
        kv_ref[...] = r.T.astype(BF)

    @pl.when(step == 1)
    def _():
        kv_ref[...] = dot(normed_ref[...], in_order(place_ref, (wa_ref, wb_ref))).astype(BF)


def w_columns(w, tile, at):
    return [pl.BlockSpec((*half.shape[:2], tile), lambda *i: (0, 0, at(*i))) for half in w]


def kv_project(place, x, gain, w, width, cosine, sine):
    rows, dim = x.shape
    return pl.pallas_call(
        kv_kernel,
        name="kv_project",
        grid=(2,),
        in_specs=[
            smem(),
            whole((rows, dim)),
            whole((1, dim)),
            *w_columns(w, width, lambda i: i),
            whole((HALF, rows)),
            whole((HALF, rows)),
        ],
        out_specs=[pl.BlockSpec((rows, width), lambda i: (0, i)), whole((rows, dim))],
        out_shape=[
            jax.ShapeDtypeStruct((rows, 2 * width), BF),
            jax.ShapeDtypeStruct((rows, dim), BF),
        ],
        compiler_params=params(),
        cost_estimate=cost(2 * rows * dim * 2 * width, 2 * (2 * rows * dim + dim * 2 * width)),
    )(place, x, gain, *w, cosine, sine)


def q_kernel(place_ref, normed_ref, wa_ref, wb_ref, cos_ref, sin_ref, q_ref):
    r = dot(normed_ref[...], in_order(place_ref, (wa_ref, wb_ref)))
    r = rotate(r.T, cos_ref[...], sin_ref[...], 1)
    q_ref[...] = r.astype(BF) * BF(SCALE)


def q_project(place, normed, w, width, cosine, sine):
    rows, dim = normed.shape
    tile = 512
    return pl.pallas_call(
        q_kernel,
        name="q_project",
        grid=(width // tile,),
        in_specs=[
            smem(),
            whole((rows, dim)),
            *w_columns(w, tile, lambda i: i),
            whole((HALF, rows)),
            whole((HALF, rows)),
        ],
        out_specs=pl.BlockSpec((tile, rows), lambda i: (i, 0)),
        out_shape=jax.ShapeDtypeStruct((width, rows), BF),
        compiler_params=params(),
        cost_estimate=cost(2 * rows * dim * width, 2 * (2 * rows * dim + dim * width)),
    )(place, normed, *w, cosine, sine)


def side_by_side(ref, j):
    base = j * GROUP * HEAD
    return jnp.concatenate(
        [ref[base + h * HEAD : base + (h + 1) * HEAD, :] for h in range(GROUP)], axis=1
    )


def diagonal_mask(tokens, own_len):
    key = lax.broadcasted_iota(jnp.int32, (tokens, tokens), 0)
    query = lax.broadcasted_iota(jnp.int32, (tokens, tokens), 1)
    one = (key <= query) & (key < own_len)
    return jnp.concatenate([one.astype(jnp.int32)] * GROUP, axis=1) > 0


def attend_kernel(n, info_ref, q_ref, k_ref, v_ref, o_ref, ot_ref, lse_ref, m_ref, l_ref, acc_ref):
    tokens = q_ref.shape[1]
    d = pl.program_id(1)
    s = info_ref[0]
    own_len = info_ref[1] - s * tokens
    active = own_len > 0

    def pair(j):
        cols = slice(j * HEAD, (j + 1) * HEAD)
        scores = dot(k_ref[0, :, cols], side_by_side(q_ref, j))
        return scores, v_ref[0, :, cols].astype(F32).T.astype(BF)

    @pl.when(active & (d == 0))
    def _():
        mask = diagonal_mask(tokens, own_len)
        for j in range(2):
            scores, value_t = pair(j)
            scores = jnp.where(mask, scores, NEGATIVE)
            top = jnp.max(scores, axis=0, keepdims=True)
            p = jnp.exp(scores - top)
            l_ref[j : j + 1] = jnp.sum(p, axis=0, keepdims=True)
            acc_ref[j] = dot(value_t, p.astype(BF))
            m_ref[j : j + 1] = top

    @pl.when(active & (d > 0) & (d <= s))
    def _():
        for j in range(2):
            scores, value_t = pair(j)
            old = m_ref[j : j + 1]
            top = jnp.maximum(old, jnp.max(scores, axis=0, keepdims=True))
            keep = jnp.exp(old - top)
            p = jnp.exp(scores - top)
            l_ref[j : j + 1] = l_ref[j : j + 1] * keep + jnp.sum(p, axis=0, keepdims=True)
            acc_ref[j] = acc_ref[j] * keep + dot(value_t, p.astype(BF))
            m_ref[j : j + 1] = top

    @pl.when(active & (d == n - 1))
    def _():
        pieces = []
        for j in range(2):
            out = acc_ref[j] / l_ref[j : j + 1]
            lse_ref[j : j + 1] = m_ref[j : j + 1] + jnp.log(l_ref[j : j + 1])
            pieces += [out[:, h * tokens : (h + 1) * tokens] for h in range(GROUP)]
        out = jnp.concatenate(pieces, axis=0)
        ot_ref[...] = out.astype(BF)
        o_ref[...] = out.T.astype(BF)

    @pl.when(jnp.logical_not(active) & (d == 0))
    def _():
        o_ref[...] = jnp.zeros_like(o_ref)
        ot_ref[...] = jnp.zeros_like(ot_ref)
        lse_ref[...] = jnp.zeros_like(lse_ref)


def owner(info_ref, d, n):
    return lax.rem(info_ref[0] + n - d, n)


def attend(info, q_t, kv, micro, tokens):
    n = kv.shape[0]
    width = q_t.shape[0]
    kv_width = kv.shape[2] // 2
    steps = kv_width // LANES
    qw = width // steps
    return pl.pallas_call(
        functools.partial(attend_kernel, n),
        name="attend",
        grid_spec=pltpu.PrefetchScalarGridSpec(
            num_scalar_prefetch=1,
            grid=(steps, n),
            in_specs=[
                pl.BlockSpec((qw, tokens), lambda i, d, info: (i, micro)),
                pl.BlockSpec((1, tokens, LANES), lambda i, d, info: (owner(info, d, n), 0, i)),
                pl.BlockSpec(
                    (1, tokens, LANES), lambda i, d, info: (owner(info, d, n), 0, steps + i)
                ),
            ],
            out_specs=[
                pl.BlockSpec((tokens, qw), lambda i, d, info: (0, i)),
                pl.BlockSpec((qw, tokens), lambda i, d, info: (i, 0)),
                pl.BlockSpec((8, GROUP * tokens), lambda i, d, info: (i, 0)),
            ],
            scratch_shapes=[
                pltpu.VMEM((8, GROUP * tokens), F32),
                pltpu.VMEM((8, GROUP * tokens), F32),
                pltpu.VMEM((2, HEAD, GROUP * tokens), F32),
            ],
        ),
        out_shape=[
            jax.ShapeDtypeStruct((tokens, width), BF),
            jax.ShapeDtypeStruct((width, tokens), BF),
            jax.ShapeDtypeStruct((8 * steps, GROUP * tokens), F32),
        ],
        compiler_params=params(),
        cost_estimate=cost(
            4 * 4 * width * tokens * tokens * n,
            2 * (3 * width * tokens + n * tokens * 2 * kv_width),
            width // HEAD * tokens * tokens * n,
        ),
    )(info, q_t, kv, kv)


def attend_back_kernel(
    n, info_ref, q_ref, g_ref, o_ref, lse_ref, cos_ref, sin_ref, k_ref, v_ref, gq_ref, dkv_ref, acc_ref
):
    tokens = q_ref.shape[1]
    d = pl.program_id(1)
    s = info_ref[0]
    own_len = info_ref[1] - s * tokens
    active = own_len > 0

    def block(first):
        mask = diagonal_mask(tokens, own_len) if first else None
        dks, dvs = [], []
        for j in range(2):
            cols = slice(j * HEAD, (j + 1) * HEAD)
            key, value = k_ref[0, :, cols], v_ref[0, :, cols]
            query, grad = side_by_side(q_ref, j), side_by_side(g_ref, j)
            out = side_by_side(o_ref, j)
            inner = jnp.sum(grad.astype(F32) * out.astype(F32), axis=0, keepdims=True)
            p = jnp.exp(dot(key, query) - lse_ref[j : j + 1])
            if first:
                p = jnp.where(mask, p, 0.0)
            dp = dot(value, grad)
            ds = (p * (dp - inner)).astype(BF)
            dvs.append(dot(p.astype(BF), grad, NT))
            dks.append(dot(ds, query, NT))
            part = dot(key.astype(F32).T.astype(BF), ds)
            if first:
                acc_ref[j] = part
            else:
                acc_ref[j] += part
        dkv_ref[0, 0] = jnp.concatenate(dks, axis=1).astype(BF)
        dkv_ref[0, 1] = jnp.concatenate(dvs, axis=1).astype(BF)

    pl.when(active & (d == 0))(lambda: block(True))
    pl.when(active & (d > 0) & (d <= s))(lambda: block(False))

    @pl.when(active & (d == n - 1))
    def _():
        pieces = []
        for j in range(2):
            for h in range(GROUP):
                piece = acc_ref[j, :, h * tokens : (h + 1) * tokens] * SCALE
                pieces.append(piece.astype(BF).astype(F32))
        grad_q = rotate(jnp.concatenate(pieces, axis=0), cos_ref[...], sin_ref[...], -1)
        gq_ref[...] = grad_q.T.astype(BF)

    @pl.when(jnp.logical_not(active) | (d > s))
    def _():
        dkv_ref[...] = jnp.zeros_like(dkv_ref)

    @pl.when(jnp.logical_not(active) & (d == 0))
    def _():
        gq_ref[...] = jnp.zeros_like(gq_ref)


def attend_back(info, q_t, g_t, o_t, lse, cosine, sine, kv, micro, tokens):
    n = kv.shape[0]
    width = q_t.shape[0]
    kv_width = kv.shape[2] // 2
    steps = kv_width // LANES
    qw = width // steps
    transposed = pl.BlockSpec((qw, tokens), lambda i, d, info: (i, 0))
    return pl.pallas_call(
        functools.partial(attend_back_kernel, n),
        name="attend_back",
        grid_spec=pltpu.PrefetchScalarGridSpec(
            num_scalar_prefetch=1,
            grid=(steps, n),
            in_specs=[
            pl.BlockSpec((qw, tokens), lambda i, d, info: (i, micro)),
            transposed,
            transposed,
            pl.BlockSpec((8, GROUP * tokens), lambda i, d, info: (i, 0)),
            whole((HALF, tokens)),
            whole((HALF, tokens)),
            pl.BlockSpec((1, tokens, LANES), lambda i, d, info: (owner(info, d, n), 0, i)),
            pl.BlockSpec(
                (1, tokens, LANES), lambda i, d, info: (owner(info, d, n), 0, steps + i)
            ),
        ],
        out_specs=[
            pl.BlockSpec((tokens, qw), lambda i, d, info: (0, i)),
            pl.BlockSpec(
                (1, 2, tokens, LANES), lambda i, d, info: (owner(info, d, n), 0, 0, i)
            ),
        ],
            scratch_shapes=[pltpu.VMEM((2, HEAD, GROUP * tokens), F32)],
        ),
        out_shape=[
            jax.ShapeDtypeStruct((tokens, width), BF),
            jax.ShapeDtypeStruct((n, 2, tokens, kv_width), BF),
        ],
        compiler_params=params(),
        cost_estimate=cost(
            10 * 4 * width * tokens * tokens * n,
            2 * (4 * width * tokens + 2 * n * tokens * 2 * kv_width),
            width // HEAD * tokens * tokens * n,
        ),
    )(info, q_t, g_t, o_t, lse, cosine, sine, kv, kv)


def after_kernel(
    steps, place_ref, a_ref, wa_ref, wb_ref, x_ref, gain_ref, router_ref, chosen_ref, res_ref, xg_ref, ge_ref, acc_ref
):
    step = pl.program_id(0)
    acc_ref[step] = dot(a_ref[...], in_order(place_ref, (wa_ref, wb_ref)))

    @pl.when(step == steps - 1)
    def _():
        dim = x_ref.shape[1]
        product = jnp.concatenate([acc_ref[i] for i in range(steps)], axis=1)
        residual = x_ref[...].astype(F32) + product
        res_ref[...] = residual
        inv = lax.rsqrt(jnp.mean(residual * residual, axis=-1, keepdims=True) + EPS)
        normed = (residual * inv * gain_ref[...]).astype(BF)
        logits = dot(normed, router_ref[...])
        chosen = chosen_ref[...] > 0
        logits = jnp.where(chosen, logits, NEGATIVE)
        top = jnp.max(logits, axis=-1, keepdims=True)
        e = jnp.where(chosen, jnp.exp(logits - top), 0.0)
        exact = e / jnp.sum(e, axis=-1, keepdims=True)
        ge_ref[...] = exact
        xg_ref[:, :dim] = normed
        xg_ref[:, dim:] = exact.astype(BF)


def after_attention(place, attn, w, first, x, micro, gain, router, chosen):
    tokens, width = attn.shape
    dim = x.shape[1]
    tile = 512
    steps = dim // tile
    return pl.pallas_call(
        functools.partial(after_kernel, steps),
        name="after_attention",
        grid=(steps,),
        in_specs=[
            smem(),
            whole((tokens, width)),
            *w_columns(w, tile, lambda i: first // tile + i),
            pl.BlockSpec((tokens, dim), lambda i: (micro, 0)),
            whole((1, dim)),
            whole((dim, LANES)),
            pl.BlockSpec((tokens, LANES), lambda i: (micro, 0)),
        ],
        out_specs=[
            whole((tokens, dim)),
            whole((tokens, dim + LANES)),
            whole((tokens, LANES)),
        ],
        out_shape=[
            jax.ShapeDtypeStruct((tokens, dim), F32),
            jax.ShapeDtypeStruct((tokens, dim + LANES), BF),
            jax.ShapeDtypeStruct((tokens, LANES), F32),
        ],
        scratch_shapes=[pltpu.VMEM((steps, tokens, tile), F32)],
        compiler_params=params(),
        cost_estimate=cost(2 * tokens * width * dim, 2 * width * dim + 10 * tokens * dim),
    )(place, attn, *w, x, gain, router, chosen)


def expert_kernel(
    experts, half, own_ref, order_ref, xg_ref, ga_ref, gb_ref, wg_ref, wu_ref, wd_ref, ya_ref, yb_ref, back_ref, hg_ref, gp_ref
):
    rows, dim = ga_ref.shape
    hidden = wg_ref.shape[2]
    x = xg_ref[:, :dim]
    step = pl.program_id(0)
    g = jnp.where(step < half, ga_ref[...], gb_ref[...])
    gates = xg_ref[:, dim:].astype(F32)
    lane = lax.broadcasted_iota(jnp.int32, (rows, LANES), 1)
    gate_cols = jnp.zeros((rows, LANES), F32)
    for e in range(experts):
        mine = lane == own_ref[0] + e
        gate = jnp.sum(jnp.where(mine, gates, 0.0), axis=1, keepdims=True)
        pre_gate = dot(x, wg_ref[e])
        pre_up = dot(x, wu_ref[e])
        grad_hidden = dot(g, wd_ref[e], NT)
        sig = 1.0 / (1.0 + jnp.exp(-pre_gate))
        silu = pre_gate * sig
        h = (silu * pre_up).astype(BF).astype(F32)
        per_gate = jnp.sum(h * grad_hidden, axis=1, keepdims=True)
        gate_cols = jnp.where(mine, per_gate, gate_cols)
        hg_ref[:, e * hidden : (e + 1) * hidden] = (gate * h).astype(BF)
        gh = gate * grad_hidden
        base = 2 * e * hidden
        gp_ref[:, base : base + hidden] = (
            gh * pre_up * (sig * (1.0 + pre_gate * (1.0 - sig)))
        ).astype(BF)
        gp_ref[:, base + hidden : base + 2 * hidden] = (gh * silu).astype(BF)
    y = dot(hg_ref[:, :hidden], wd_ref[0])
    for e in range(1, experts):
        y += dot(hg_ref[:, e * hidden : (e + 1) * hidden], wd_ref[e])

    @pl.when(step < half)
    def _():
        ya_ref[...] = y.astype(BF)

    @pl.when(step >= half)
    def _():
        yb_ref[...] = y.astype(BF)

    back = None
    for e in range(experts):
        base = 2 * e * hidden
        part = dot(gp_ref[:, base : base + hidden], wg_ref[e], NT)
        part += dot(gp_ref[:, base + hidden : base + 2 * hidden], wu_ref[e], NT)
        back = part if back is None else back + part
    back_ref[:, :dim] = back.astype(BF)
    back_ref[:, dim:] = gate_cols.astype(BF)


def run_experts(own, order, xg, g, w_gate, w_up, w_down):
    rows = xg.shape[0]
    dim = g[0].shape[1]
    experts, _, hidden = w_gate.shape
    devices = order.shape[0]
    tile, half = rows // devices, devices // 2
    named = lambda width: pl.BlockSpec((tile, width), lambda i, own, order: (order[i], 0))
    first = lambda i: jnp.minimum(i, half - 1)
    second = lambda i: jnp.maximum(i - half, 0)
    return pl.pallas_call(
        functools.partial(expert_kernel, experts, half),
        name="run_experts",
        grid_spec=pltpu.PrefetchScalarGridSpec(
            num_scalar_prefetch=2,
            grid=(devices,),
            in_specs=[
                named(dim + LANES),
                pl.BlockSpec((tile, dim), lambda i, *_: (first(i), 0)),
                pl.BlockSpec((tile, dim), lambda i, *_: (second(i), 0)),
                whole(w_gate.shape),
                whole(w_up.shape),
                whole(w_down.shape),
            ],
            out_specs=[
                pl.BlockSpec((tile, dim), lambda i, *_: (first(i), 0)),
                pl.BlockSpec((tile, dim), lambda i, *_: (second(i), 0)),
                named(dim + LANES),
                pl.BlockSpec((tile, experts * hidden), lambda i, *_: (i, 0)),
                named(2 * experts * hidden),
            ],
        ),
        out_shape=[
            jax.ShapeDtypeStruct((rows // 2, dim), BF),
            jax.ShapeDtypeStruct((rows // 2, dim), BF),
            jax.ShapeDtypeStruct((rows, dim + LANES), BF),
            jax.ShapeDtypeStruct((rows, experts * hidden), BF),
            jax.ShapeDtypeStruct((rows, 2 * experts * hidden), BF),
        ],
        compiler_params=params(),
        cost_estimate=cost(
            12 * rows * dim * hidden * experts,
            2 * (4 * rows * dim + 3 * rows * experts * hidden + 3 * experts * dim * hidden),
            rows * experts * hidden,
        ),
    )(own, order, xg, *g, w_gate, w_up, w_down)


def wide_grad_kernel(steps, micros, *refs):
    a_refs, b_refs = refs[:micros], refs[micros : 2 * micros]
    out_ref, acc_ref = refs[2 * micros :]
    step = pl.program_id(0)
    for m in range(micros):

        @pl.when((step >= m * steps) & (step < (m + 1) * steps))
        def _(m=m):
            part = dot(a_refs[m][...], b_refs[m][...], TN)
            if m == 0:

                @pl.when(step == 0)
                def _():
                    acc_ref[...] = part

                @pl.when(step > 0)
                def _():
                    acc_ref[...] += part
            else:
                acc_ref[...] += part

    @pl.when(step == micros * steps - 1)
    def _():
        out_ref[...] = acc_ref[...].astype(BF)


def wide_grad(lefts, left_block, left_width, rights, right_block, right_width, tile=512):
    micros, rows = len(lefts), lefts[0].shape[0]
    steps = rows // tile

    def spec(m, width, column):
        return pl.BlockSpec(
            (tile, width), lambda i: (jnp.clip(i - m * steps, 0, steps - 1), column)
        )

    return pl.pallas_call(
        functools.partial(wide_grad_kernel, steps, micros),
        name="wide_grad",
        grid=(micros * steps,),
        in_specs=[spec(m, left_width, left_block) for m in range(micros)]
        + [spec(m, right_width, right_block) for m in range(micros)],
        out_specs=whole((left_width, right_width)),
        out_shape=jax.ShapeDtypeStruct((left_width, right_width), BF),
        scratch_shapes=[pltpu.VMEM((left_width, right_width), F32)],
        compiler_params=params(),
        cost_estimate=cost(
            2 * micros * rows * left_width * right_width,
            2 * (micros * rows * (left_width + right_width) + left_width * right_width),
        ),
    )(*lefts, *rights)


def down_grad_kernel(micros, devices, *refs):
    hg_refs, refs = refs[:micros], refs[micros:]
    ga_refs, gb_refs = refs[:micros], refs[micros : 2 * micros]
    out_ref, acc_ref = refs[2 * micros :]
    step = pl.program_id(0)
    g = [jnp.where(step < devices // 2, a[...], b[...]) for a, b in zip(ga_refs, gb_refs)]
    part = dot(jnp.concatenate(g), jnp.concatenate([r[...] for r in hg_refs]), TN)

    @pl.when(step == 0)
    def _():
        acc_ref[...] = part

    @pl.when(step > 0)
    def _():
        acc_ref[...] += part

    @pl.when(step == devices - 1)
    def _():
        out_ref[...] = acc_ref[...].astype(BF)


def down_grad(hgs, expert, hidden, gs, devices):
    micros, rows = len(hgs), hgs[0].shape[0]
    tile, half = rows // devices, devices // 2
    dim = gs[0][0].shape[1]
    return pl.pallas_call(
        functools.partial(down_grad_kernel, micros, devices),
        name="down_grad",
        grid=(devices,),
        in_specs=[pl.BlockSpec((tile, hidden), lambda i: (i, expert))] * micros
        + [pl.BlockSpec((tile, dim), lambda i: (jnp.minimum(i, half - 1), 0))] * micros
        + [pl.BlockSpec((tile, dim), lambda i: (jnp.maximum(i - half, 0), 0))] * micros,
        out_specs=whole((dim, hidden)),
        out_shape=jax.ShapeDtypeStruct((dim, hidden), BF),
        scratch_shapes=[pltpu.VMEM((dim, hidden), F32)],
        compiler_params=params(),
        cost_estimate=cost(2 * micros * rows * hidden * dim, 2 * micros * rows * (hidden + dim)),
    )(*hgs, *[g[0] for g in gs], *[g[1] for g in gs])


def before_kernel(
    steps, place_ref, ret_ref, res_ref, ge_ref, gout_ref, gain_ref, router_ref, wa_ref, wb_ref, gres_ref, ga_ref, gt_ref, small_ref, cut_ref, acc_ref
):
    dim = res_ref.shape[1]

    step = pl.program_id(0)
    tile = dim // steps

    @pl.when(step == 0)
    def _():
        ge = ge_ref[...]
        gg = ret_ref[:, dim:].astype(F32)
        gl = ge * (gg - jnp.sum(ge * gg, axis=-1, keepdims=True))
        high = gl.astype(BF)
        low = (gl - high.astype(F32)).astype(BF)
        router = router_ref[...]
        gn = ret_ref[:, :dim].astype(F32) + (dot(high, router, NT) + dot(low, router, NT))
        residual = res_ref[...]
        gain = gain_ref[...]
        inv = lax.rsqrt(jnp.mean(residual * residual, axis=-1, keepdims=True) + EPS)
        unit = residual * inv
        normed = (unit * gain).astype(BF)
        small_ref[:LANES] = dot(high, normed, TN) + dot(low, normed, TN)
        gain_row = jnp.sum(gn * unit, axis=0, keepdims=True)
        small_ref[LANES:] = jnp.broadcast_to(gain_row, (8, dim))
        u = gn * gain
        gres = gout_ref[...].astype(F32) + inv * (
            u - unit * jnp.mean(u * unit, axis=-1, keepdims=True)
        )
        gres_ref[...] = gres
        low_gres = gres.astype(BF)
        ga_ref[...] = low_gres
        for i in range(steps):
            cut_ref[i] = low_gres[:, i * tile : (i + 1) * tile]
        acc_ref[...] = jnp.zeros_like(acc_ref)

    acc_ref[...] += dot(in_order(place_ref, (wa_ref, wb_ref)), cut_ref[step], NT)

    @pl.when(step == steps - 1)
    def _():
        gt_ref[...] = acc_ref[...].astype(BF)


def before_attention(place, returned, residual, exact, gout, gain, router, w, first):
    tokens, dim = residual.shape
    width = 2 * w[0].shape[0] * w[0].shape[1]
    tile = 512
    steps = dim // tile
    return pl.pallas_call(
        functools.partial(before_kernel, steps),
        name="before_attention",
        grid=(steps,),
        in_specs=[
            smem(),
            whole((tokens, dim + LANES)),
            whole((tokens, dim)),
            whole((tokens, LANES)),
            whole((tokens, dim)),
            whole((1, dim)),
            whole((dim, LANES)),
            *w_columns(w, tile, lambda i: first // tile + i),
        ],
        out_specs=[
            whole((tokens, dim)),
            whole((tokens, dim)),
            whole((width, tokens)),
            whole((LANES + 8, dim)),
        ],
        out_shape=[
            jax.ShapeDtypeStruct((tokens, dim), F32),
            jax.ShapeDtypeStruct((tokens, dim), BF),
            jax.ShapeDtypeStruct((width, tokens), BF),
            jax.ShapeDtypeStruct((LANES + 8, dim), F32),
        ],
        scratch_shapes=[
            pltpu.VMEM((steps, tokens, tile), BF),
            pltpu.VMEM((width, tokens), F32),
        ],
        compiler_params=params(),
        cost_estimate=cost(2 * tokens * width * dim, 2 * width * dim + 14 * tokens * dim),
    )(place, returned, residual, exact, gout, gain, router, *w)


def last_kernel(
    q_steps, steps, place_ref, gq_ref, dkv_ref, qa_ref, qb_ref, kva_ref, kvb_ref, x_ref, gain_ref, gres_ref, din_ref, small_ref, acc_ref
):
    step = pl.program_id(0)

    @pl.when(step == 0)
    def _():
        acc_ref[...] = dot(gq_ref[...], in_order(place_ref, (qa_ref, qb_ref)), NT)

    @pl.when((step > 0) & (step < q_steps))
    def _():
        acc_ref[...] += dot(gq_ref[...], in_order(place_ref, (qa_ref, qb_ref)), NT)

    @pl.when(step >= q_steps)
    def _():
        acc_ref[...] += dot(dkv_ref[...], in_order(place_ref, (kva_ref, kvb_ref)), NT)

    @pl.when(step == steps - 1)
    def _():
        x = x_ref[...].astype(F32)
        gain = gain_ref[...]
        inv = lax.rsqrt(jnp.mean(x * x, axis=-1, keepdims=True) + EPS)
        unit = x * inv
        gn = acc_ref[...]
        small_ref[...] = jnp.broadcast_to(
            jnp.sum(gn * unit, axis=0, keepdims=True), small_ref.shape
        )
        w = gn * gain
        grad = inv * (w - unit * jnp.mean(w * unit, axis=-1, keepdims=True))
        din_ref[...] = (grad + gres_ref[...]).astype(BF)


def last_step(place, gq, dkv, w_q, w_kv, x, micro, gain, gres):
    tokens, dim = gres.shape
    tile = 512
    q_steps, kv_steps = gq.shape[1] // tile, dkv.shape[1] // tile
    steps = q_steps + kv_steps
    q_at = lambda i: (0, jnp.minimum(i, q_steps - 1))
    kv_at = lambda i: (0, jnp.maximum(i - q_steps, 0))
    return pl.pallas_call(
        functools.partial(last_kernel, q_steps, steps),
        name="last_step",
        grid=(steps,),
        in_specs=[
            smem(),
            pl.BlockSpec((tokens, tile), q_at),
            pl.BlockSpec((tokens, tile), kv_at),
            *w_columns(w_q, tile, lambda i: q_at(i)[1]),
            *w_columns(w_kv, tile, lambda i: kv_at(i)[1]),
            pl.BlockSpec((tokens, dim), lambda i: (micro, 0)),
            whole((1, dim)),
            whole((tokens, dim)),
        ],
        out_specs=[whole((tokens, dim)), whole((8, dim))],
        out_shape=[
            jax.ShapeDtypeStruct((tokens, dim), BF),
            jax.ShapeDtypeStruct((8, dim), F32),
        ],
        scratch_shapes=[pltpu.VMEM((tokens, dim), F32)],
        compiler_params=params(),
        cost_estimate=cost(
            2 * tokens * steps * tile * dim, 2 * steps * tile * dim + 12 * tokens * dim
        ),
    )(place, gq, dkv, *w_q, *w_kv, x, gain, gres)


def out_grad_kernel(micros, half, order_ref, *refs):
    t_refs, g_refs, (first_ref, second_ref) = refs[:micros], refs[micros : 2 * micros], refs[2 * micros :]
    step = pl.program_id(0)
    total = dot(t_refs[0][...], g_refs[0][...])
    for t_ref, g_ref in zip(t_refs[1:], g_refs[1:]):
        total += dot(t_ref[...], g_ref[...])

    @pl.when(step < half)
    def _():
        first_ref[...] = total.astype(BF)

    @pl.when(step >= half)
    def _():
        second_ref[...] = total.astype(BF)


def out_grad(order, heads_t, grads):
    micros, devices = len(heads_t), order.shape[0]
    width, tokens = heads_t[0].shape
    dim = grads[0].shape[1]
    tile, half = width // devices, devices // 2
    return pl.pallas_call(
        functools.partial(out_grad_kernel, micros, half),
        name="out_grad",
        grid_spec=pltpu.PrefetchScalarGridSpec(
            num_scalar_prefetch=1,
            grid=(devices,),
            in_specs=[pl.BlockSpec((tile, tokens), lambda i, order: (order[i], 0))] * micros
            + [whole((tokens, dim))] * micros,
            out_specs=[
                pl.BlockSpec((tile, dim), lambda i, order: (jnp.minimum(i, half - 1), 0)),
                pl.BlockSpec((tile, dim), lambda i, order: (jnp.maximum(i - half, 0), 0)),
            ],
        ),
        out_shape=[jax.ShapeDtypeStruct((width // 2, dim), BF)] * 2,
        compiler_params=params(),
        cost_estimate=cost(2 * micros * tokens * width * dim, 4 * width * dim),
    )(order, *heads_t, *grads)


def turn_kernel(kv_ref, cos_ref, sin_ref, out_ref):
    width = kv_ref.shape[2]
    key = rotate(kv_ref[0].astype(F32).T, cos_ref[...], sin_ref[...], -1)
    out_ref[:, :width] = key.T.astype(BF)
    out_ref[:, width:] = kv_ref[1]


def turn_back(kv, cosine, sine):
    _, tokens, width = kv.shape
    return pl.pallas_call(
        turn_kernel,
        name="turn_back",
        out_shape=jax.ShapeDtypeStruct((tokens, 2 * width), BF),
        compiler_params=params(),
        cost_estimate=cost(0, 8 * tokens * width),
    )(kv, cosine, sine)


def projection_kernel(micros, q_steps, steps, n_experts, normed_ref, *refs):
    gq_refs, refs = refs[:micros], refs[micros:]
    dkv_refs, refs = refs[:micros], refs[micros:]
    two_refs, refs = refs[:micros], refs[micros:]
    one_refs, (out_ref, turned_ref) = refs[:micros], refs[micros:]
    step = pl.program_id(0)
    tile = gq_refs[0].shape[1]

    @pl.when(step == 0)
    def _():
        turned_ref[...] = normed_ref[...].astype(F32).T.astype(BF)
        rows = functools.reduce(jnp.add, [r[:LANES] for r in two_refs])
        gain_two = functools.reduce(jnp.add, [r[LANES : LANES + 1] for r in two_refs])
        gain_one = functools.reduce(jnp.add, [r[:1] for r in one_refs])
        at = lax.broadcasted_iota(jnp.int32, rows.shape, 0)
        rows = jnp.where(at == n_experts, gain_one, rows)
        rows = jnp.where(at == n_experts + 1, gain_two, rows)
        out_ref[:, steps * tile :] = rows.T.astype(BF)

    q = jnp.concatenate([r[...] for r in gq_refs], axis=0)
    kv = jnp.concatenate([r[...] for r in dkv_refs], axis=0)
    g = jnp.where(step < q_steps, q, kv)
    out_ref[:, pl.ds(pl.multiple_of(step * tile, tile), tile)] = dot(turned_ref[...], g).astype(BF)


def projection_grads(normed, gqs, dkvs, twos, ones, n_experts):
    rows, dim = normed.shape
    micros, tokens, tile = len(gqs), gqs[0].shape[0], 512
    q_steps, kv_steps = gqs[0].shape[1] // tile, dkvs[0].shape[1] // tile
    steps = q_steps + kv_steps
    width = steps * tile + LANES
    return pl.pallas_call(
        functools.partial(projection_kernel, micros, q_steps, steps, n_experts),
        name="projection_grads",
        grid=(steps,),
        in_specs=[whole((rows, dim))]
        + [pl.BlockSpec((tokens, tile), lambda i: (0, jnp.minimum(i, q_steps - 1)))] * micros
        + [pl.BlockSpec((tokens, tile), lambda i: (0, jnp.maximum(i - q_steps, 0)))] * micros
        + [whole(twos[0].shape)] * micros
        + [whole(ones[0].shape)] * micros,
        out_specs=whole((dim, width)),
        out_shape=jax.ShapeDtypeStruct((dim, width), BF),
        scratch_shapes=[pltpu.VMEM((dim, rows), BF)],
        compiler_params=params(),
        cost_estimate=cost(2 * rows * dim * width, 2 * rows * (dim + width) + 2 * dim * width),
    )(normed, *gqs, *dkvs, *twos, *ones)


def add_low(a, b):
    return (a.astype(F32) + b.astype(F32)).astype(BF)


def line_sum(x, n):
    if n == 1:
        return x
    if n % 2:
        return lax.psum(x, "seq")
    half = n // 2
    at = lax.axis_index("seq")
    for k in range(half - 1):
        x = add_low(x, lax.ppermute(x, "seq", [(k, k + 1), (n - 1 - k, n - 2 - k)]))
    x = add_low(x, lax.ppermute(x, "seq", [(half - 1, half), (half, half - 1)]))
    for k in reversed(range(half - 1)):
        got = lax.ppermute(x, "seq", [(k + 1, k), (n - 2 - k, n - 1 - k)])
        x = jnp.where((at == k) | (at == n - 1 - k), got, x)
    return x


class Line:
    def __init__(self, n):
        self.n = n
        self.held = {}
        self.results = []

    def sums(self):
        at = lax.axis_index("seq")
        middle = (at == 1) | (at == 2)
        return [r[0] if len(r) == 1 else jnp.where(middle, *r) for r in self.results]

    def step(self, chunk, beside):
        n = self.n
        if n != 4:
            if chunk is not None:
                self.results.append((line_sum(chunk, n),))
            return
        at = lax.axis_index("seq")
        middle = (at == 1) | (at == 2)
        come, go = [(0, 1), (3, 2)], [(1, 0), (2, 3)]
        held, self.held = self.held, {}
        summed = held.get("summed")
        if summed is not None:
            summed = add_low(*summed)
        crossing = held.get("crossing")
        if crossing is not None:
            crossing = add_low(*crossing)
            self.held["summed"] = (crossing, lax.ppermute(crossing, "seq", [(1, 2), (2, 1)]))
        if chunk is not None and summed is not None and chunk.shape == summed.shape:
            sent = jnp.where(middle, summed, chunk)
            got = lax.ppermute(sent, "seq", come + go)
            self.results.append((sent, got))
            self.held["crossing"] = (chunk, got)
        else:
            if summed is not None:
                self.results.append((summed, lax.ppermute(summed, "seq", go)))
            if chunk is not None:
                self.held["crossing"] = (chunk, lax.ppermute(chunk, "seq", come))
        self.held, self.results = gate((self.held, self.results), beside)


def gate(x, *others):
    return lax.optimization_barrier((x, others))[0]


CORE, ALONG_X, ALONG_Y = 1, 2, 4


def swap(x, mask):
    return lax.ppermute(x, "fsdp", [(i, i ^ mask) for i in range(8)])


def gather_rows(x):
    return lax.all_gather(x, "fsdp", axis=0, tiled=True)


def assemble_kernel(x_ref, top_x_ref, low_y_ref, top_far_ref, low_far_ref, out_ref):
    rows = x_ref.shape[0]
    half = rows // 2
    out_ref[:rows] = x_ref[...]
    out_ref[rows : rows + half] = top_x_ref[...]
    out_ref[rows + half : 2 * rows] = low_far_ref[:half]
    out_ref[2 * rows : 2 * rows + half] = top_far_ref[:half]
    out_ref[2 * rows + half : 3 * rows] = low_y_ref[...]
    out_ref[3 * rows : 3 * rows + half] = top_far_ref[half:]
    out_ref[3 * rows + half :] = low_far_ref[half:]


def assemble(*pieces):
    rows, width = pieces[0].shape
    block = lambda n: pl.BlockSpec((n, width // 3), lambda i: (0, i))
    return pl.pallas_call(
        assemble_kernel,
        name="assemble",
        grid=(3,),
        in_specs=[block(p.shape[0]) for p in pieces],
        out_specs=block(4 * rows),
        out_shape=jax.ShapeDtypeStruct((4 * rows, width), pieces[0].dtype),
        compiler_params=params(),
        cost_estimate=cost(0, 16 * rows * width),
    )(*pieces)


def gather_near(x, n):
    if n != 8:
        every = gather_rows(x)
        half = every.shape[0] // 2
        return every[:half], every[half:]
    gather = Gather(x, n)
    gather.further()
    return gather.finish()


class Gather:
    def __init__(self, x, n):
        self.n, self.x = n, x
        if n != 8:
            self.halves = gather_near(x, n)
            self.near = self.far = ()
            return
        half = x.shape[0] // 2
        self.near = swap(x[:half], ALONG_X), swap(x[half:], ALONG_Y)

    def further(self, *others):
        if self.n != 8:
            return
        half = self.x.shape[0] // 2
        x, (top_x, low_y) = gate((self.x, self.near), *others)
        self.near = top_x, low_y
        top_far = swap(jnp.concatenate([x[:half], top_x]), ALONG_Y)
        low_far = swap(jnp.concatenate([x[half:], low_y]), ALONG_X)
        self.far = top_far, low_far

    def finish(self, *others):
        if self.n != 8:
            return self.halves
        near, far = gate((self.near, self.far), *others)
        mine = assemble(self.x, *near, *far)
        return mine, swap(mine, CORE)


class Scatter:
    def __init__(self, arrays, n):
        self.arrays, self.n, self.stage = list(arrays), n, 0
        self.rows = 2 * arrays[0][0].shape[0] // n

    def advance(self):
        held, self.stage = self.arrays, self.stage + 1
        rows, half = self.rows, self.rows // 2
        if self.n != 8:
            if self.stage == 1:
                self.arrays = [scatter_rows(jnp.concatenate(a)) for a in held]
            return
        if self.stage == 1:
            self.arrays = [add_low(mine, swap(other, CORE)) for mine, other in held]
        if self.stage == 2:
            tops = [a[k * rows : k * rows + half] for a in held for k in (2, 3)]
            lows = [a[k * rows + half : (k + 1) * rows] for a in held for k in (1, 3)]
            tops = swap(jnp.concatenate(tops), ALONG_Y)
            lows = swap(jnp.concatenate(lows), ALONG_X)
            self.arrays = []
            for i, a in enumerate(held):
                at = 2 * i * half
                self.arrays.append(
                    (
                        add_low(a[:half], tops[at : at + half]),
                        add_low(a[half:rows], lows[at : at + half]),
                        add_low(a[rows : rows + half], tops[at + half : at + rows]),
                        add_low(a[2 * rows + half : 3 * rows], lows[at + half : at + rows]),
                    )
                )
        if self.stage == 3:
            over_x = swap(jnp.concatenate([a[2] for a in held]), ALONG_X)
            over_y = swap(jnp.concatenate([a[3] for a in held]), ALONG_Y)
            self.arrays = [
                jnp.concatenate(
                    [
                        add_low(a[0], over_x[i * half : (i + 1) * half]),
                        add_low(a[1], over_y[i * half : (i + 1) * half]),
                    ]
                )
                for i, a in enumerate(held)
            ]


def block_order(n):
    at = jnp.arange(n, dtype=jnp.int32)
    if n != 8:
        return at
    return lax.axis_index("fsdp").astype(jnp.int32) ^ (2 * lax.rem(at, 4) + at // 4)


def block_places(n):
    if n != 8:
        return jnp.arange(n, dtype=jnp.int32)
    mask = lax.axis_index("fsdp").astype(jnp.int32) ^ jnp.arange(n, dtype=jnp.int32)
    return (mask >> 1) + 4 * (mask & 1)


def scatter_rows(x):
    return lax.psum_scatter(x, "fsdp", scatter_dimension=0, tiled=True)


def on_device(
    n_seq,
    n_fsdp,
    inputs,
    lengths,
    expert_ids,
    cotangent,
    gain_attn,
    w_query,
    key_projection,
    value_projection,
    w_out,
    gain_moe,
    router,
    w_gate,
    w_up,
    w_down,
):
    micros, local_seqs, tokens, dim = inputs.shape
    assert local_seqs == 1
    rows = micros * tokens
    experts, _, hidden = w_gate.shape
    n_experts = router.shape[1]
    kv_width = key_projection.shape[1]
    at = lax.axis_index("seq")
    own = (lax.axis_index("fsdp") * experts).astype(jnp.int32).reshape(1)

    small = jnp.concatenate(
        [router, gain_attn[:, None], gain_moe[:, None]], axis=1
    )
    small = jnp.pad(small, ((0, 0), (0, LANES - small.shape[1])))
    place, order = block_places(n_fsdp), block_order(n_fsdp)

    def weights(w):
        return [h.reshape(n_fsdp // 2, -1, h.shape[1]) for h in gather_near(w, n_fsdp)]

    w_kv = weights(jnp.concatenate([key_projection, value_projection, small], axis=1))
    router_all, rows_all = unpack(place, w_kv, 2 * kv_width // LANES, n_experts)
    gain_one = rows_all[n_experts : n_experts + 1]
    gain_two = rows_all[n_experts + 1 : n_experts + 2]

    positions = at * tokens + jnp.arange(tokens, dtype=jnp.int32)
    frequency = THETA ** (-(jnp.arange(HALF, dtype=F32) * 2.0) / HEAD)
    angles = frequency[:, None] * positions.astype(F32)[None, :]
    cosine, sine = jnp.cos(angles), jnp.sin(angles)
    cosine_all, sine_all = jnp.tile(cosine, (1, micros)), jnp.tile(sine, (1, micros))

    x = inputs.reshape(rows, dim)
    chosen = jnp.sum(
        (
            expert_ids.reshape(rows, TOPK)[:, :, None]
            == jnp.arange(LANES, dtype=jnp.int32)[None, None, :]
        ).astype(F32),
        axis=1,
    )
    valid = positions[None, :] < lengths[:, :1]
    gout = jnp.where(valid[:, :, None], cotangent.reshape(micros, tokens, dim), BF(0))
    infos = [
        jnp.stack([at.astype(jnp.int32), lengths[m, 0].astype(jnp.int32)]) for m in range(micros)
    ]

    kv, normed_one = kv_project(place, x, gain_one, w_kv, kv_width, cosine_all, sine_all)
    q_width = w_query.shape[1]
    w_gather = Gather(gate(jnp.concatenate([w_query, w_out], axis=1), kv), n_fsdp)
    w_gather.further()
    kvs = []
    for m in range(micros):
        mine = kv[m * tokens : (m + 1) * tokens]
        every = lax.all_gather(mine, "seq", axis=0, tiled=True)
        kvs.append(every.reshape(n_seq, tokens, 2 * kv_width))
    w_qo = [h.reshape(n_fsdp // 2, -1, h.shape[1]) for h in w_gather.finish(kvs[0], chosen, infos)]
    g_gathers = [Gather(gate(gout[0], w_gather.far), n_fsdp)]
    for m in range(1, micros):
        g_gathers.append(Gather(gate(gout[m], g_gathers[-1].near), n_fsdp))
    q_t = q_project(
        place, gate(normed_one, kvs[0]), w_qo, q_width, cosine_all, sine_all
    )

    state, xg_all = [], []
    for m in range(micros):
        if m == 0:
            info = gate(infos[m], g_gathers[0].near)
            g_gathers[0].further(q_t)
        else:
            info = gate(infos[m], state[-1][2])
        attn, attn_t, lse = attend(info, q_t, kvs[m], m, tokens)
        if m == 0:
            attn = gate(attn, g_gathers[0].far, [g.near for g in g_gathers[1:]])
            for g in g_gathers[1:]:
                g.further(g_gathers[0].far)
        else:
            attn = gate(attn, g_gathers[m].far)
        residual, xg, exact = after_attention(
            place, attn, w_qo, q_width, x, m, gain_two, router_all, chosen
        )
        state.append((attn_t, lse, residual, exact))
        xg_all.append(gather_rows(xg))

    g_all = [g.finish(state[-1][2]) for g in g_gathers]
    xg_all[0] = gate(xg_all[0], state[-1][2], g_all)
    passed, backs = [], []
    for m in range(micros):
        *y, back, hg, gp = run_experts(
            own, order, xg_all[m], g_all[m], w_gate, w_up, w_down
        )
        passed.append((xg_all[m], hg, gp))
        backs.append((scatter_rows(back), y))

    names = [(name, e) for name in ("down", "gate", "up") for e in range(experts)]

    def expert_grad(name, e, got):
        xs, hgs, gps = ([p[i] for p in got] for i in range(3))
        if name == "down":
            return down_grad(hgs, e, hidden, g_all, n_fsdp)
        return wide_grad(xs, 0, dim, gps, 2 * e + (name == "up"), hidden)

    line = Line(n_seq)
    found = [{} for _ in range(micros)]

    def to_heads(m):
        attn_t, lse, residual, exact = state[m]
        gres, g_attn, g_t, small_two = before_attention(
            place, backs[m][0], residual, exact, gout[m], gain_two, router_all, w_qo, q_width
        )
        found[m].update(gres=gres, g_attn=g_attn, g_t=g_t, small_two=small_two)

    def through_heads(m):
        attn_t, lse = state[m][:2]
        gq, by_owner = attend_back(
            infos[m], q_t, found[m]["g_t"], attn_t, lse, cosine, sine, kvs[m], m, tokens
        )
        found[m].update(gq=gq, by_owner=by_owner)

    owned = {}

    def to_owners(m):
        by_owner = found[m].pop("by_owner")
        shape = by_owner.shape
        owned[m] = lax.psum_scatter(
            by_owner.reshape(n_seq * shape[1] * tokens, shape[3]),
            "seq",
            scatter_dimension=0,
            tiled=True,
        ).reshape(shape[1:])

    def finish(m):
        f = found[m]
        f["dkv"] = turn_back(f["mine"], cosine, sine)
        f["din"], f["small_one"] = last_step(
            place, f["gq"], f["dkv"], w_qo, w_kv, x, m, gain_one, f["gres"]
        )

    def rest_grads():
        every = lambda name: [f[name] for f in found]
        return projection_grads(
            normed_one, every("gq"), every("dkv"), every("small_two"), every("small_one"), n_experts
        )

    n_grads = len(names)
    work = {
        0: [("grad", 1), (to_heads, 0)],
        1: [("grad", 2), (through_heads, 0)],
        2: [("grad", 3), (to_heads, 1), (through_heads, 1)],
        3: [("grad", 4), (finish, 0), ("grad", 5)],
        4: [(finish, 1)],
    }
    def widen(parts, turned):
        return jnp.stack([(p.T if turned else p).astype(F32) for p in parts])

    experts_out = []
    chunks = {0: expert_grad(*names[0], passed)}
    chunks.update({i: expert_grad(*names[i], passed) for i in range(6, n_grads)})
    slots = max(n_grads, 6)
    moe = Scatter([b[1] for b in backs], n_fsdp)
    for t in range(slots + 3):
        if t in (3, 4):
            found[t - 3]["mine"] = owned[t - 3]
        if t == 3:
            heads = Scatter([found[0].pop("out")], n_fsdp)
        if t == 7:
            found[0]["rest"] = rest
        held = (chunks, line.held, line.results, passed, found, moe.arrays)
        if t >= 3:
            *held, heads.arrays = lax.optimization_barrier((*held, heads.arrays))
        else:
            held = lax.optimization_barrier(held)
        chunks, line.held, line.results, passed, found, moe.arrays = held
        if t == 7:
            rest = lax.psum(found[0].pop("rest"), "seq")
        if len(line.results) in (experts, 2 * experts, 3 * experts) and len(experts_out) < 3:
            pair = line.sums()[-experts:]
            experts_out.append(widen(pair, len(experts_out) == 0))
            found[1]["wide"] = experts_out[-1]
        if t == slots:
            chunks[slots] = heads.arrays[0]
        sent = chunks.pop(t, None)
        if t in (2, 3):
            to_owners(t - 2)
        for kind, i in work.get(t, []):
            if kind != "grad":
                kind(i)
            elif i < n_grads:
                chunks[i] = expert_grad(*names[i], passed)
        if t == 2:
            found[0]["out"] = out_grad(
                order, [st[0] for st in state], [f["g_attn"] for f in found]
            )
        if t in (5, 6, 7):
            moe.advance()
        for _ in range(3 if t == 3 else 0):
            heads.advance()
        line.step(sent, (chunks, found))
        if t == 4:
            normed_one, line.held = lax.optimization_barrier((normed_one, line.held))
            rest = scatter_rows(rest_grads())
    rest = rest.astype(F32)
    totals = line.sums()
    for i in range(len(experts_out), 3):
        experts_out.append(widen(totals[i * experts : (i + 1) * experts], i == 0))
    d_out = totals[n_grads].astype(F32)

    outs = []
    for m in range(micros):
        outs.append(
            jnp.where(valid[m][:, None], state[m][2] + moe.arrays[m].astype(F32), 0.0).astype(BF)
        )
    grads = [f["din"] for f in found]
    assert len(totals) == n_grads + 1
    shape = (micros, 1, tokens, dim)
    ends = q_width + 2 * kv_width
    return (
        jnp.stack(outs).reshape(shape),
        jnp.stack(grads).reshape(shape),
        rest[:, ends + n_experts],
        rest[:, :q_width],
        rest[:, q_width : q_width + kv_width],
        rest[:, q_width + kv_width : ends],
        d_out,
        rest[:, ends + n_experts + 1],
        rest[:, ends : ends + n_experts],
        *experts_out[1:],
        experts_out[0],
    )


def solution(mesh):
    token_spec = P(None, "fsdp", "seq", None)
    row, matrix, cube = P("fsdp"), P("fsdp", None), P("fsdp", None, None)
    return jax.shard_map(
        functools.partial(on_device, mesh.shape["seq"], mesh.shape["fsdp"]),
        mesh=mesh,
        in_specs=(
            token_spec,
            P(None, "fsdp"),
            token_spec,
            token_spec,
            row,
            matrix,
            matrix,
            matrix,
            matrix,
            row,
            matrix,
            cube,
            cube,
            cube,
        ),
        out_specs=(
            token_spec,
            token_spec,
            row,
            matrix,
            matrix,
            matrix,
            matrix,
            row,
            matrix,
            cube,
            cube,
            cube,
        ),
        check_vma=False,
    )
```

```python
import functools

import jax
import jax.numpy as jnp
from jax import lax
from jax.experimental import pallas as pl
from jax.experimental.pallas import tpu as pltpu
from jax.sharding import PartitionSpec as P

HEAD = 64
HALF = HEAD // 2
GROUP = 3
TOPK = 8
EPS = 1e-06
THETA = 10000.0
NEGATIVE = -1e30
LANES = 128
SCALE = HEAD ** (-0.5)
BF = jnp.bfloat16
F32 = jnp.float32
VMEM_BYTES = 60 * 1024 * 1024

NN = (((1,), (0,)), ((), ()))
NT = (((1,), (1,)), ((), ()))
TN = (((0,), (0,)), ((), ()))


def dot(a, b, dims=NN):
    return lax.dot_general(a, b, dims, preferred_element_type=F32)


def params():
    return pltpu.CompilerParams(vmem_limit_bytes=VMEM_BYTES)


def cost(flops, moved, trans=0):
    parts = (int(v) // 10 for v in (flops, moved, trans))
    flops, moved, trans = parts
    return pl.CostEstimate(flops=flops, bytes_accessed=moved, transcendentals=trans)


def whole(shape):
    zeros = (0,) * len(shape)
    return pl.BlockSpec(shape, lambda *_: zeros)


def smem():
    return pl.BlockSpec(memory_space=pltpu.SMEM)


def pick(at, first_ref, second_ref, index=None):
    half = first_ref.shape[0]
    if index is None:
        index = lax.rem(at, half)
    return jnp.where(at < half, first_ref[index], second_ref[index])


def in_order(place_ref, w_refs):
    devices = 2 * w_refs[0].shape[0]
    return jnp.concatenate([pick(place_ref[j], *w_refs) for j in range(devices)], axis=0)


def rotate(rows, cosine, sine, sign):
    pieces = []
    for h in range(rows.shape[0] // HEAD):
        a = rows[h * HEAD : h * HEAD + HALF]
        b = rows[h * HEAD + HALF : (h + 1) * HEAD]
        if sign > 0:
            pieces += [a * cosine - b * sine, b * cosine + a * sine]
        else:
            pieces += [a * cosine + b * sine, b * cosine - a * sine]
    return jnp.concatenate(pieces, axis=0)


def unpack_kernel(n_experts, place_ref, wa_ref, wb_ref, router_ref, rows_ref):
    w = in_order(place_ref, (wa_ref, wb_ref))
    lane = lax.broadcasted_iota(jnp.int32, w.shape, 1)
    router_ref[...] = jnp.where(lane < n_experts, w.astype(F32), 0.0).astype(BF)
    rows_ref[...] = w.astype(F32).T


def unpack(place, w, block, n_experts):
    dim = 2 * w[0].shape[0] * w[0].shape[1]
    return pl.pallas_call(
        functools.partial(unpack_kernel, n_experts),
        name="unpack",
        grid=(1,),
        in_specs=[smem(), *w_columns(w, LANES, lambda i: block)],
        out_specs=[whole((dim, LANES)), whole((LANES, dim))],
        out_shape=[
            jax.ShapeDtypeStruct((dim, LANES), BF),
            jax.ShapeDtypeStruct((LANES, dim), F32),
        ],
        compiler_params=params(),
        cost_estimate=cost(0, 12 * dim * LANES),
    )(place, *w)


def kv_kernel(place_ref, x_ref, gain_ref, wa_ref, wb_ref, cos_ref, sin_ref, kv_ref, normed_ref):
    step = pl.program_id(0)

    @pl.when(step == 0)
    def _():
        x = x_ref[...].astype(F32)
        inv = lax.rsqrt(jnp.mean(x * x, axis=-1, keepdims=True) + EPS)
        normed_ref[...] = (x * inv * gain_ref[...]).astype(BF)
        r = dot(normed_ref[...], in_order(place_ref, (wa_ref, wb_ref)))
        r = rotate(r.T, cos_ref[...], sin_ref[...], 1)
        kv_ref[...] = r.T.astype(BF)

    @pl.when(step == 1)
    def _():
        kv_ref[...] = dot(normed_ref[...], in_order(place_ref, (wa_ref, wb_ref))).astype(BF)


def w_columns(w, tile, at):
    return [pl.BlockSpec((*half.shape[:2], tile), lambda *i: (0, 0, at(*i))) for half in w]


def kv_project(place, x, gain, w, width, cosine, sine):
    rows, dim = x.shape
    return pl.pallas_call(
        kv_kernel,
        name="kv_project",
        grid=(2,),
        in_specs=[
            smem(),
            whole((rows, dim)),
            whole((1, dim)),
            *w_columns(w, width, lambda i: i),
            whole((HALF, rows)),
            whole((HALF, rows)),
        ],
        out_specs=[pl.BlockSpec((rows, width), lambda i: (0, i)), whole((rows, dim))],
        out_shape=[
            jax.ShapeDtypeStruct((rows, 2 * width), BF),
            jax.ShapeDtypeStruct((rows, dim), BF),
        ],
        compiler_params=params(),
        cost_estimate=cost(2 * rows * dim * 2 * width, 2 * (2 * rows * dim + dim * 2 * width)),
    )(place, x, gain, *w, cosine, sine)


def q_kernel(place_ref, normed_ref, wa_ref, wb_ref, cos_ref, sin_ref, q_ref):
    r = dot(normed_ref[...], in_order(place_ref, (wa_ref, wb_ref)))
    r = rotate(r.T, cos_ref[...], sin_ref[...], 1)
    q_ref[...] = r.astype(BF) * BF(SCALE)


def q_project(place, normed, w, width, cosine, sine):
    rows, dim = normed.shape
    tile = 512
    return pl.pallas_call(
        q_kernel,
        name="q_project",
        grid=(width // tile,),
        in_specs=[
            smem(),
            whole((rows, dim)),
            *w_columns(w, tile, lambda i: i),
            whole((HALF, rows)),
            whole((HALF, rows)),
        ],
        out_specs=pl.BlockSpec((tile, rows), lambda i: (i, 0)),
        out_shape=jax.ShapeDtypeStruct((width, rows), BF),
        compiler_params=params(),
        cost_estimate=cost(2 * rows * dim * width, 2 * (2 * rows * dim + dim * width)),
    )(place, normed, *w, cosine, sine)


def side_by_side(ref, j):
    base = j * GROUP * HEAD
    return jnp.concatenate(
        [ref[base + h * HEAD : base + (h + 1) * HEAD, :] for h in range(GROUP)], axis=1
    )


def diagonal_mask(tokens, own_len):
    key = lax.broadcasted_iota(jnp.int32, (tokens, tokens), 0)
    query = lax.broadcasted_iota(jnp.int32, (tokens, tokens), 1)
    one = (key <= query) & (key < own_len)
    return jnp.concatenate([one.astype(jnp.int32)] * GROUP, axis=1) > 0


def attend_kernel(n, info_ref, q_ref, k_ref, v_ref, o_ref, ot_ref, lse_ref, m_ref, l_ref, acc_ref):
    tokens = q_ref.shape[1]
    d = pl.program_id(1)
    s = info_ref[0]
    own_len = info_ref[1] - s * tokens
    active = own_len > 0

    def pair(j):
        cols = slice(j * HEAD, (j + 1) * HEAD)
        scores = dot(k_ref[0, :, cols], side_by_side(q_ref, j))
        return scores, v_ref[0, :, cols].astype(F32).T.astype(BF)

    @pl.when(active & (d == 0))
    def _():
        mask = diagonal_mask(tokens, own_len)
        for j in range(2):
            scores, value_t = pair(j)
            scores = jnp.where(mask, scores, NEGATIVE)
            top = jnp.max(scores, axis=0, keepdims=True)
            p = jnp.exp(scores - top)
            l_ref[j : j + 1] = jnp.sum(p, axis=0, keepdims=True)
            acc_ref[j] = dot(value_t, p.astype(BF))
            m_ref[j : j + 1] = top

    @pl.when(active & (d > 0) & (d <= s))
    def _():
        for j in range(2):
            scores, value_t = pair(j)
            old = m_ref[j : j + 1]
            top = jnp.maximum(old, jnp.max(scores, axis=0, keepdims=True))
            keep = jnp.exp(old - top)
            p = jnp.exp(scores - top)
            l_ref[j : j + 1] = l_ref[j : j + 1] * keep + jnp.sum(p, axis=0, keepdims=True)
            acc_ref[j] = acc_ref[j] * keep + dot(value_t, p.astype(BF))
            m_ref[j : j + 1] = top

    @pl.when(active & (d == n - 1))
    def _():
        pieces = []
        for j in range(2):
            out = acc_ref[j] / l_ref[j : j + 1]
            lse_ref[j : j + 1] = m_ref[j : j + 1] + jnp.log(l_ref[j : j + 1])
            pieces += [out[:, h * tokens : (h + 1) * tokens] for h in range(GROUP)]
        out = jnp.concatenate(pieces, axis=0)
        ot_ref[...] = out.astype(BF)
        o_ref[...] = out.T.astype(BF)

    @pl.when(jnp.logical_not(active) & (d == 0))
    def _():
        o_ref[...] = jnp.zeros_like(o_ref)
        ot_ref[...] = jnp.zeros_like(ot_ref)
        lse_ref[...] = jnp.zeros_like(lse_ref)


def owner(info_ref, d, n):
    return lax.rem(info_ref[0] + n - d, n)


def attend(info, q_t, kv, micro, tokens):
    n = kv.shape[0]
    width = q_t.shape[0]
    kv_width = kv.shape[2] // 2
    steps = kv_width // LANES
    qw = width // steps
    return pl.pallas_call(
        functools.partial(attend_kernel, n),
        name="attend",
        grid_spec=pltpu.PrefetchScalarGridSpec(
            num_scalar_prefetch=1,
            grid=(steps, n),
            in_specs=[
                pl.BlockSpec((qw, tokens), lambda i, d, info: (i, micro)),
                pl.BlockSpec((1, tokens, LANES), lambda i, d, info: (owner(info, d, n), 0, i)),
                pl.BlockSpec(
                    (1, tokens, LANES), lambda i, d, info: (owner(info, d, n), 0, steps + i)
                ),
            ],
            out_specs=[
                pl.BlockSpec((tokens, qw), lambda i, d, info: (0, i)),
                pl.BlockSpec((qw, tokens), lambda i, d, info: (i, 0)),
                pl.BlockSpec((8, GROUP * tokens), lambda i, d, info: (i, 0)),
            ],
            scratch_shapes=[
                pltpu.VMEM((8, GROUP * tokens), F32),
                pltpu.VMEM((8, GROUP * tokens), F32),
                pltpu.VMEM((2, HEAD, GROUP * tokens), F32),
            ],
        ),
        out_shape=[
            jax.ShapeDtypeStruct((tokens, width), BF),
            jax.ShapeDtypeStruct((width, tokens), BF),
            jax.ShapeDtypeStruct((8 * steps, GROUP * tokens), F32),
        ],
        compiler_params=params(),
        cost_estimate=cost(
            4 * 4 * width * tokens * tokens * n,
            2 * (3 * width * tokens + n * tokens * 2 * kv_width),
            width // HEAD * tokens * tokens * n,
        ),
    )(info, q_t, kv, kv)


def attend_back_kernel(
    n, info_ref, q_ref, g_ref, o_ref, lse_ref, cos_ref, sin_ref, k_ref, v_ref, gq_ref, dkv_ref, acc_ref
):
    tokens = q_ref.shape[1]
    d = pl.program_id(1)
    s = info_ref[0]
    own_len = info_ref[1] - s * tokens
    active = own_len > 0

    def block(first):
        mask = diagonal_mask(tokens, own_len) if first else None
        dks, dvs = [], []
        for j in range(2):
            cols = slice(j * HEAD, (j + 1) * HEAD)
            key, value = k_ref[0, :, cols], v_ref[0, :, cols]
            query, grad = side_by_side(q_ref, j), side_by_side(g_ref, j)
            out = side_by_side(o_ref, j)
            inner = jnp.sum(grad.astype(F32) * out.astype(F32), axis=0, keepdims=True)
            p = jnp.exp(dot(key, query) - lse_ref[j : j + 1])
            if first:
                p = jnp.where(mask, p, 0.0)
            dp = dot(value, grad)
            ds = (p * (dp - inner)).astype(BF)
            dvs.append(dot(p.astype(BF), grad, NT))
            dks.append(dot(ds, query, NT))
            part = dot(key.astype(F32).T.astype(BF), ds)
            if first:
                acc_ref[j] = part
            else:
                acc_ref[j] += part
        dkv_ref[0, 0] = jnp.concatenate(dks, axis=1).astype(BF)
        dkv_ref[0, 1] = jnp.concatenate(dvs, axis=1).astype(BF)

    pl.when(active & (d == 0))(lambda: block(True))
    pl.when(active & (d > 0) & (d <= s))(lambda: block(False))

    @pl.when(active & (d == n - 1))
    def _():
        pieces = []
        for j in range(2):
            for h in range(GROUP):
                piece = acc_ref[j, :, h * tokens : (h + 1) * tokens] * SCALE
                pieces.append(piece.astype(BF).astype(F32))
        grad_q = rotate(jnp.concatenate(pieces, axis=0), cos_ref[...], sin_ref[...], -1)
        gq_ref[...] = grad_q.T.astype(BF)

    @pl.when(jnp.logical_not(active) | (d > s))
    def _():
        dkv_ref[...] = jnp.zeros_like(dkv_ref)

    @pl.when(jnp.logical_not(active) & (d == 0))
    def _():
        gq_ref[...] = jnp.zeros_like(gq_ref)


def attend_back(info, q_t, g_t, o_t, lse, cosine, sine, kv, micro, tokens):
    n = kv.shape[0]
    width = q_t.shape[0]
    kv_width = kv.shape[2] // 2
    steps = kv_width // LANES
    qw = width // steps
    transposed = pl.BlockSpec((qw, tokens), lambda i, d, info: (i, 0))
    return pl.pallas_call(
        functools.partial(attend_back_kernel, n),
        name="attend_back",
        grid_spec=pltpu.PrefetchScalarGridSpec(
            num_scalar_prefetch=1,
            grid=(steps, n),
            in_specs=[
            pl.BlockSpec((qw, tokens), lambda i, d, info: (i, micro)),
            transposed,
            transposed,
            pl.BlockSpec((8, GROUP * tokens), lambda i, d, info: (i, 0)),
            whole((HALF, tokens)),
            whole((HALF, tokens)),
            pl.BlockSpec((1, tokens, LANES), lambda i, d, info: (owner(info, d, n), 0, i)),
            pl.BlockSpec(
                (1, tokens, LANES), lambda i, d, info: (owner(info, d, n), 0, steps + i)
            ),
        ],
        out_specs=[
            pl.BlockSpec((tokens, qw), lambda i, d, info: (0, i)),
            pl.BlockSpec(
                (1, 2, tokens, LANES), lambda i, d, info: (owner(info, d, n), 0, 0, i)
            ),
        ],
            scratch_shapes=[pltpu.VMEM((2, HEAD, GROUP * tokens), F32)],
        ),
        out_shape=[
            jax.ShapeDtypeStruct((tokens, width), BF),
            jax.ShapeDtypeStruct((n, 2, tokens, kv_width), BF),
        ],
        compiler_params=params(),
        cost_estimate=cost(
            10 * 4 * width * tokens * tokens * n,
            2 * (4 * width * tokens + 2 * n * tokens * 2 * kv_width),
            width // HEAD * tokens * tokens * n,
        ),
    )(info, q_t, g_t, o_t, lse, cosine, sine, kv, kv)


def after_kernel(
    steps, place_ref, a_ref, wa_ref, wb_ref, x_ref, gain_ref, router_ref, chosen_ref, res_ref, xg_ref, ge_ref, acc_ref
):
    step = pl.program_id(0)
    acc_ref[step] = dot(a_ref[...], in_order(place_ref, (wa_ref, wb_ref)))

    @pl.when(step == steps - 1)
    def _():
        dim = x_ref.shape[1]
        product = jnp.concatenate([acc_ref[i] for i in range(steps)], axis=1)
        residual = x_ref[...].astype(F32) + product
        res_ref[...] = residual
        inv = lax.rsqrt(jnp.mean(residual * residual, axis=-1, keepdims=True) + EPS)
        normed = (residual * inv * gain_ref[...]).astype(BF)
        logits = dot(normed, router_ref[...])
        chosen = chosen_ref[...] > 0
        logits = jnp.where(chosen, logits, NEGATIVE)
        top = jnp.max(logits, axis=-1, keepdims=True)
        e = jnp.where(chosen, jnp.exp(logits - top), 0.0)
        exact = e / jnp.sum(e, axis=-1, keepdims=True)
        ge_ref[...] = exact
        xg_ref[:, :dim] = normed
        xg_ref[:, dim:] = exact.astype(BF)


def after_attention(place, attn, w, first, x, micro, gain, router, chosen):
    tokens, width = attn.shape
    dim = x.shape[1]
    tile = 512
    steps = dim // tile
    return pl.pallas_call(
        functools.partial(after_kernel, steps),
        name="after_attention",
        grid=(steps,),
        in_specs=[
            smem(),
            whole((tokens, width)),
            *w_columns(w, tile, lambda i: first // tile + i),
            pl.BlockSpec((tokens, dim), lambda i: (micro, 0)),
            whole((1, dim)),
            whole((dim, LANES)),
            pl.BlockSpec((tokens, LANES), lambda i: (micro, 0)),
        ],
        out_specs=[
            whole((tokens, dim)),
            whole((tokens, dim + LANES)),
            whole((tokens, LANES)),
        ],
        out_shape=[
            jax.ShapeDtypeStruct((tokens, dim), F32),
            jax.ShapeDtypeStruct((tokens, dim + LANES), BF),
            jax.ShapeDtypeStruct((tokens, LANES), F32),
        ],
        scratch_shapes=[pltpu.VMEM((steps, tokens, tile), F32)],
        compiler_params=params(),
        cost_estimate=cost(2 * tokens * width * dim, 2 * width * dim + 10 * tokens * dim),
    )(place, attn, *w, x, gain, router, chosen)


def expert_kernel(
    experts, half, own_ref, order_ref, xg_ref, ga_ref, gb_ref, wg_ref, wu_ref, wd_ref, ya_ref, yb_ref, back_ref, hg_ref, gp_ref
):
    rows, dim = ga_ref.shape
    hidden = wg_ref.shape[2]
    x = xg_ref[:, :dim]
    step = pl.program_id(0)
    g = jnp.where(step < half, ga_ref[...], gb_ref[...])
    gates = xg_ref[:, dim:].astype(F32)
    lane = lax.broadcasted_iota(jnp.int32, (rows, LANES), 1)
    gate_cols = jnp.zeros((rows, LANES), F32)
    for e in range(experts):
        mine = lane == own_ref[0] + e
        gate = jnp.sum(jnp.where(mine, gates, 0.0), axis=1, keepdims=True)
        pre_gate = dot(x, wg_ref[e])
        pre_up = dot(x, wu_ref[e])
        grad_hidden = dot(g, wd_ref[e], NT)
        sig = 1.0 / (1.0 + jnp.exp(-pre_gate))
        silu = pre_gate * sig
        h = (silu * pre_up).astype(BF).astype(F32)
        per_gate = jnp.sum(h * grad_hidden, axis=1, keepdims=True)
        gate_cols = jnp.where(mine, per_gate, gate_cols)
        hg_ref[:, e * hidden : (e + 1) * hidden] = (gate * h).astype(BF)
        gh = gate * grad_hidden
        base = 2 * e * hidden
        gp_ref[:, base : base + hidden] = (
            gh * pre_up * (sig * (1.0 + pre_gate * (1.0 - sig)))
        ).astype(BF)
        gp_ref[:, base + hidden : base + 2 * hidden] = (gh * silu).astype(BF)
    y = dot(hg_ref[:, :hidden], wd_ref[0])
    for e in range(1, experts):
        y += dot(hg_ref[:, e * hidden : (e + 1) * hidden], wd_ref[e])

    @pl.when(step < half)
    def _():
        ya_ref[...] = y.astype(BF)

    @pl.when(step >= half)
    def _():
        yb_ref[...] = y.astype(BF)

    back = None
    for e in range(experts):
        base = 2 * e * hidden
        part = dot(gp_ref[:, base : base + hidden], wg_ref[e], NT)
        part += dot(gp_ref[:, base + hidden : base + 2 * hidden], wu_ref[e], NT)
        back = part if back is None else back + part
    back_ref[:, :dim] = back.astype(BF)
    back_ref[:, dim:] = gate_cols.astype(BF)


def run_experts(own, order, xg, g, w_gate, w_up, w_down):
    rows = xg.shape[0]
    dim = g[0].shape[1]
    experts, _, hidden = w_gate.shape
    devices = order.shape[0]
    tile, half = rows // devices, devices // 2
    named = lambda width: pl.BlockSpec((tile, width), lambda i, own, order: (order[i], 0))
    first = lambda i: jnp.minimum(i, half - 1)
    second = lambda i: jnp.maximum(i - half, 0)
    return pl.pallas_call(
        functools.partial(expert_kernel, experts, half),
        name="run_experts",
        grid_spec=pltpu.PrefetchScalarGridSpec(
            num_scalar_prefetch=2,
            grid=(devices,),
            in_specs=[
                named(dim + LANES),
                pl.BlockSpec((tile, dim), lambda i, *_: (first(i), 0)),
                pl.BlockSpec((tile, dim), lambda i, *_: (second(i), 0)),
                whole(w_gate.shape),
                whole(w_up.shape),
                whole(w_down.shape),
            ],
            out_specs=[
                pl.BlockSpec((tile, dim), lambda i, *_: (first(i), 0)),
                pl.BlockSpec((tile, dim), lambda i, *_: (second(i), 0)),
                named(dim + LANES),
                pl.BlockSpec((tile, experts * hidden), lambda i, *_: (i, 0)),
                named(2 * experts * hidden),
            ],
        ),
        out_shape=[
            jax.ShapeDtypeStruct((rows // 2, dim), BF),
            jax.ShapeDtypeStruct((rows // 2, dim), BF),
            jax.ShapeDtypeStruct((rows, dim + LANES), BF),
            jax.ShapeDtypeStruct((rows, experts * hidden), BF),
            jax.ShapeDtypeStruct((rows, 2 * experts * hidden), BF),
        ],
        compiler_params=params(),
        cost_estimate=cost(
            12 * rows * dim * hidden * experts,
            2 * (4 * rows * dim + 3 * rows * experts * hidden + 3 * experts * dim * hidden),
            rows * experts * hidden,
        ),
    )(own, order, xg, *g, w_gate, w_up, w_down)


def wide_grad_kernel(steps, micros, *refs):
    a_refs, b_refs = refs[:micros], refs[micros : 2 * micros]
    out_ref, acc_ref = refs[2 * micros :]
    step = pl.program_id(0)
    for m in range(micros):

        @pl.when((step >= m * steps) & (step < (m + 1) * steps))
        def _(m=m):
            part = dot(a_refs[m][...], b_refs[m][...], TN)
            if m == 0:

                @pl.when(step == 0)
                def _():
                    acc_ref[...] = part

                @pl.when(step > 0)
                def _():
                    acc_ref[...] += part
            else:
                acc_ref[...] += part

    @pl.when(step == micros * steps - 1)
    def _():
        out_ref[...] = acc_ref[...].astype(BF)


def wide_grad(lefts, left_block, left_width, rights, right_block, right_width, tile=512):
    micros, rows = len(lefts), lefts[0].shape[0]
    steps = rows // tile

    def spec(m, width, column):
        return pl.BlockSpec(
            (tile, width), lambda i: (jnp.clip(i - m * steps, 0, steps - 1), column)
        )

    return pl.pallas_call(
        functools.partial(wide_grad_kernel, steps, micros),
        name="wide_grad",
        grid=(micros * steps,),
        in_specs=[spec(m, left_width, left_block) for m in range(micros)]
        + [spec(m, right_width, right_block) for m in range(micros)],
        out_specs=whole((left_width, right_width)),
        out_shape=jax.ShapeDtypeStruct((left_width, right_width), BF),
        scratch_shapes=[pltpu.VMEM((left_width, right_width), F32)],
        compiler_params=params(),
        cost_estimate=cost(
            2 * micros * rows * left_width * right_width,
            2 * (micros * rows * (left_width + right_width) + left_width * right_width),
        ),
    )(*lefts, *rights)


def down_grad_kernel(micros, devices, *refs):
    hg_refs, refs = refs[:micros], refs[micros:]
    ga_refs, gb_refs = refs[:micros], refs[micros : 2 * micros]
    out_ref, acc_ref = refs[2 * micros :]
    step = pl.program_id(0)
    g = [jnp.where(step < devices // 2, a[...], b[...]) for a, b in zip(ga_refs, gb_refs)]
    part = dot(jnp.concatenate(g), jnp.concatenate([r[...] for r in hg_refs]), TN)

    @pl.when(step == 0)
    def _():
        acc_ref[...] = part

    @pl.when(step > 0)
    def _():
        acc_ref[...] += part

    @pl.when(step == devices - 1)
    def _():
        out_ref[...] = acc_ref[...].astype(BF)


def down_grad(hgs, expert, hidden, gs, devices):
    micros, rows = len(hgs), hgs[0].shape[0]
    tile, half = rows // devices, devices // 2
    dim = gs[0][0].shape[1]
    return pl.pallas_call(
        functools.partial(down_grad_kernel, micros, devices),
        name="down_grad",
        grid=(devices,),
        in_specs=[pl.BlockSpec((tile, hidden), lambda i: (i, expert))] * micros
        + [pl.BlockSpec((tile, dim), lambda i: (jnp.minimum(i, half - 1), 0))] * micros
        + [pl.BlockSpec((tile, dim), lambda i: (jnp.maximum(i - half, 0), 0))] * micros,
        out_specs=whole((dim, hidden)),
        out_shape=jax.ShapeDtypeStruct((dim, hidden), BF),
        scratch_shapes=[pltpu.VMEM((dim, hidden), F32)],
        compiler_params=params(),
        cost_estimate=cost(2 * micros * rows * hidden * dim, 2 * micros * rows * (hidden + dim)),
    )(*hgs, *[g[0] for g in gs], *[g[1] for g in gs])


def before_kernel(
    steps, place_ref, ret_ref, res_ref, ge_ref, gout_ref, gain_ref, router_ref, wa_ref, wb_ref, gres_ref, ga_ref, gt_ref, small_ref, cut_ref, acc_ref
):
    dim = res_ref.shape[1]

    step = pl.program_id(0)
    tile = dim // steps

    @pl.when(step == 0)
    def _():
        ge = ge_ref[...]
        gg = ret_ref[:, dim:].astype(F32)
        gl = ge * (gg - jnp.sum(ge * gg, axis=-1, keepdims=True))
        high = gl.astype(BF)
        low = (gl - high.astype(F32)).astype(BF)
        router = router_ref[...]
        gn = ret_ref[:, :dim].astype(F32) + (dot(high, router, NT) + dot(low, router, NT))
        residual = res_ref[...]
        gain = gain_ref[...]
        inv = lax.rsqrt(jnp.mean(residual * residual, axis=-1, keepdims=True) + EPS)
        unit = residual * inv
        normed = (unit * gain).astype(BF)
        small_ref[:LANES] = dot(high, normed, TN) + dot(low, normed, TN)
        gain_row = jnp.sum(gn * unit, axis=0, keepdims=True)
        small_ref[LANES:] = jnp.broadcast_to(gain_row, (8, dim))
        u = gn * gain
        gres = gout_ref[...].astype(F32) + inv * (
            u - unit * jnp.mean(u * unit, axis=-1, keepdims=True)
        )
        gres_ref[...] = gres
        low_gres = gres.astype(BF)
        ga_ref[...] = low_gres
        for i in range(steps):
            cut_ref[i] = low_gres[:, i * tile : (i + 1) * tile]
        acc_ref[...] = jnp.zeros_like(acc_ref)

    acc_ref[...] += dot(in_order(place_ref, (wa_ref, wb_ref)), cut_ref[step], NT)

    @pl.when(step == steps - 1)
    def _():
        gt_ref[...] = acc_ref[...].astype(BF)


def before_attention(place, returned, residual, exact, gout, gain, router, w, first):
    tokens, dim = residual.shape
    width = 2 * w[0].shape[0] * w[0].shape[1]
    tile = 512
    steps = dim // tile
    return pl.pallas_call(
        functools.partial(before_kernel, steps),
        name="before_attention",
        grid=(steps,),
        in_specs=[
            smem(),
            whole((tokens, dim + LANES)),
            whole((tokens, dim)),
            whole((tokens, LANES)),
            whole((tokens, dim)),
            whole((1, dim)),
            whole((dim, LANES)),
            *w_columns(w, tile, lambda i: first // tile + i),
        ],
        out_specs=[
            whole((tokens, dim)),
            whole((tokens, dim)),
            whole((width, tokens)),
            whole((LANES + 8, dim)),
        ],
        out_shape=[
            jax.ShapeDtypeStruct((tokens, dim), F32),
            jax.ShapeDtypeStruct((tokens, dim), BF),
            jax.ShapeDtypeStruct((width, tokens), BF),
            jax.ShapeDtypeStruct((LANES + 8, dim), F32),
        ],
        scratch_shapes=[
            pltpu.VMEM((steps, tokens, tile), BF),
            pltpu.VMEM((width, tokens), F32),
        ],
        compiler_params=params(),
        cost_estimate=cost(2 * tokens * width * dim, 2 * width * dim + 14 * tokens * dim),
    )(place, returned, residual, exact, gout, gain, router, *w)


def last_kernel(
    q_steps, steps, place_ref, gq_ref, dkv_ref, qa_ref, qb_ref, kva_ref, kvb_ref, x_ref, gain_ref, gres_ref, din_ref, small_ref, acc_ref
):
    step = pl.program_id(0)

    @pl.when(step == 0)
    def _():
        acc_ref[...] = dot(gq_ref[...], in_order(place_ref, (qa_ref, qb_ref)), NT)

    @pl.when((step > 0) & (step < q_steps))
    def _():
        acc_ref[...] += dot(gq_ref[...], in_order(place_ref, (qa_ref, qb_ref)), NT)

    @pl.when(step >= q_steps)
    def _():
        acc_ref[...] += dot(dkv_ref[...], in_order(place_ref, (kva_ref, kvb_ref)), NT)

    @pl.when(step == steps - 1)
    def _():
        x = x_ref[...].astype(F32)
        gain = gain_ref[...]
        inv = lax.rsqrt(jnp.mean(x * x, axis=-1, keepdims=True) + EPS)
        unit = x * inv
        gn = acc_ref[...]
        small_ref[...] = jnp.broadcast_to(
            jnp.sum(gn * unit, axis=0, keepdims=True), small_ref.shape
        )
        w = gn * gain
        grad = inv * (w - unit * jnp.mean(w * unit, axis=-1, keepdims=True))
        din_ref[...] = (grad + gres_ref[...]).astype(BF)


def last_step(place, gq, dkv, w_q, w_kv, x, micro, gain, gres):
    tokens, dim = gres.shape
    tile = 512
    q_steps, kv_steps = gq.shape[1] // tile, dkv.shape[1] // tile
    steps = q_steps + kv_steps
    q_at = lambda i: (0, jnp.minimum(i, q_steps - 1))
    kv_at = lambda i: (0, jnp.maximum(i - q_steps, 0))
    return pl.pallas_call(
        functools.partial(last_kernel, q_steps, steps),
        name="last_step",
        grid=(steps,),
        in_specs=[
            smem(),
            pl.BlockSpec((tokens, tile), q_at),
            pl.BlockSpec((tokens, tile), kv_at),
            *w_columns(w_q, tile, lambda i: q_at(i)[1]),
            *w_columns(w_kv, tile, lambda i: kv_at(i)[1]),
            pl.BlockSpec((tokens, dim), lambda i: (micro, 0)),
            whole((1, dim)),
            whole((tokens, dim)),
        ],
        out_specs=[whole((tokens, dim)), whole((8, dim))],
        out_shape=[
            jax.ShapeDtypeStruct((tokens, dim), BF),
            jax.ShapeDtypeStruct((8, dim), F32),
        ],
        scratch_shapes=[pltpu.VMEM((tokens, dim), F32)],
        compiler_params=params(),
        cost_estimate=cost(
            2 * tokens * steps * tile * dim, 2 * steps * tile * dim + 12 * tokens * dim
        ),
    )(place, gq, dkv, *w_q, *w_kv, x, gain, gres)


def out_grad_kernel(micros, half, order_ref, *refs):
    t_refs, g_refs, (first_ref, second_ref) = refs[:micros], refs[micros : 2 * micros], refs[2 * micros :]
    step = pl.program_id(0)
    total = dot(t_refs[0][...], g_refs[0][...])
    for t_ref, g_ref in zip(t_refs[1:], g_refs[1:]):
        total += dot(t_ref[...], g_ref[...])

    @pl.when(step < half)
    def _():
        first_ref[...] = total.astype(BF)

    @pl.when(step >= half)
    def _():
        second_ref[...] = total.astype(BF)


def out_grad(order, heads_t, grads):
    micros, devices = len(heads_t), order.shape[0]
    width, tokens = heads_t[0].shape
    dim = grads[0].shape[1]
    tile, half = width // devices, devices // 2
    return pl.pallas_call(
        functools.partial(out_grad_kernel, micros, half),
        name="out_grad",
        grid_spec=pltpu.PrefetchScalarGridSpec(
            num_scalar_prefetch=1,
            grid=(devices,),
            in_specs=[pl.BlockSpec((tile, tokens), lambda i, order: (order[i], 0))] * micros
            + [whole((tokens, dim))] * micros,
            out_specs=[
                pl.BlockSpec((tile, dim), lambda i, order: (jnp.minimum(i, half - 1), 0)),
                pl.BlockSpec((tile, dim), lambda i, order: (jnp.maximum(i - half, 0), 0)),
            ],
        ),
        out_shape=[jax.ShapeDtypeStruct((width // 2, dim), BF)] * 2,
        compiler_params=params(),
        cost_estimate=cost(2 * micros * tokens * width * dim, 4 * width * dim),
    )(order, *heads_t, *grads)


def turn_kernel(kv_ref, cos_ref, sin_ref, out_ref):
    width = kv_ref.shape[2]
    key = rotate(kv_ref[0].astype(F32).T, cos_ref[...], sin_ref[...], -1)
    out_ref[:, :width] = key.T.astype(BF)
    out_ref[:, width:] = kv_ref[1]


def turn_back(kv, cosine, sine):
    _, tokens, width = kv.shape
    return pl.pallas_call(
        turn_kernel,
        name="turn_back",
        out_shape=jax.ShapeDtypeStruct((tokens, 2 * width), BF),
        compiler_params=params(),
        cost_estimate=cost(0, 8 * tokens * width),
    )(kv, cosine, sine)


def projection_kernel(micros, q_steps, steps, n_experts, normed_ref, *refs):
    gq_refs, refs = refs[:micros], refs[micros:]
    dkv_refs, refs = refs[:micros], refs[micros:]
    two_refs, refs = refs[:micros], refs[micros:]
    one_refs, (out_ref, turned_ref) = refs[:micros], refs[micros:]
    step = pl.program_id(0)
    tile = gq_refs[0].shape[1]

    @pl.when(step == 0)
    def _():
        turned_ref[...] = normed_ref[...].astype(F32).T.astype(BF)
        rows = functools.reduce(jnp.add, [r[:LANES] for r in two_refs])
        gain_two = functools.reduce(jnp.add, [r[LANES : LANES + 1] for r in two_refs])
        gain_one = functools.reduce(jnp.add, [r[:1] for r in one_refs])
        at = lax.broadcasted_iota(jnp.int32, rows.shape, 0)
        rows = jnp.where(at == n_experts, gain_one, rows)
        rows = jnp.where(at == n_experts + 1, gain_two, rows)
        out_ref[:, steps * tile :] = rows.T.astype(BF)

    q = jnp.concatenate([r[...] for r in gq_refs], axis=0)
    kv = jnp.concatenate([r[...] for r in dkv_refs], axis=0)
    g = jnp.where(step < q_steps, q, kv)
    out_ref[:, pl.ds(pl.multiple_of(step * tile, tile), tile)] = dot(turned_ref[...], g).astype(BF)


def projection_grads(normed, gqs, dkvs, twos, ones, n_experts):
    rows, dim = normed.shape
    micros, tokens, tile = len(gqs), gqs[0].shape[0], 512
    q_steps, kv_steps = gqs[0].shape[1] // tile, dkvs[0].shape[1] // tile
    steps = q_steps + kv_steps
    width = steps * tile + LANES
    return pl.pallas_call(
        functools.partial(projection_kernel, micros, q_steps, steps, n_experts),
        name="projection_grads",
        grid=(steps,),
        in_specs=[whole((rows, dim))]
        + [pl.BlockSpec((tokens, tile), lambda i: (0, jnp.minimum(i, q_steps - 1)))] * micros
        + [pl.BlockSpec((tokens, tile), lambda i: (0, jnp.maximum(i - q_steps, 0)))] * micros
        + [whole(twos[0].shape)] * micros
        + [whole(ones[0].shape)] * micros,
        out_specs=whole((dim, width)),
        out_shape=jax.ShapeDtypeStruct((dim, width), BF),
        scratch_shapes=[pltpu.VMEM((dim, rows), BF)],
        compiler_params=params(),
        cost_estimate=cost(2 * rows * dim * width, 2 * rows * (dim + width) + 2 * dim * width),
    )(normed, *gqs, *dkvs, *twos, *ones)


def add_low(a, b):
    return (a.astype(F32) + b.astype(F32)).astype(BF)


def line_sum(x, n):
    if n == 1:
        return x
    if n % 2:
        return lax.psum(x, "seq")
    half = n // 2
    at = lax.axis_index("seq")
    for k in range(half - 1):
        x = add_low(x, lax.ppermute(x, "seq", [(k, k + 1), (n - 1 - k, n - 2 - k)]))
    x = add_low(x, lax.ppermute(x, "seq", [(half - 1, half), (half, half - 1)]))
    for k in reversed(range(half - 1)):
        got = lax.ppermute(x, "seq", [(k + 1, k), (n - 2 - k, n - 1 - k)])
        x = jnp.where((at == k) | (at == n - 1 - k), got, x)
    return x


class Line:
    def __init__(self, n):
        self.n = n
        self.held = {}
        self.results = []

    def sums(self):
        at = lax.axis_index("seq")
        middle = (at == 1) | (at == 2)
        return [r[0] if len(r) == 1 else jnp.where(middle, *r) for r in self.results]

    def step(self, chunk, beside):
        n = self.n
        if n != 4:
            if chunk is not None:
                self.results.append((line_sum(chunk, n),))
            return
        at = lax.axis_index("seq")
        middle = (at == 1) | (at == 2)
        come, go = [(0, 1), (3, 2)], [(1, 0), (2, 3)]
        held, self.held = self.held, {}
        summed = held.get("summed")
        if summed is not None:
            summed = add_low(*summed)
        crossing = held.get("crossing")
        if crossing is not None:
            crossing = add_low(*crossing)
            self.held["summed"] = (crossing, lax.ppermute(crossing, "seq", [(1, 2), (2, 1)]))
        if chunk is not None and summed is not None and chunk.shape == summed.shape:
            sent = jnp.where(middle, summed, chunk)
            got = lax.ppermute(sent, "seq", come + go)
            self.results.append((sent, got))
            self.held["crossing"] = (chunk, got)
        else:
            if summed is not None:
                self.results.append((summed, lax.ppermute(summed, "seq", go)))
            if chunk is not None:
                self.held["crossing"] = (chunk, lax.ppermute(chunk, "seq", come))
        self.held, self.results = gate((self.held, self.results), beside)


def gate(x, *others):
    return lax.optimization_barrier((x, others))[0]


CORE, ALONG_X, ALONG_Y = 1, 2, 4


def swap(x, mask):
    return lax.ppermute(x, "fsdp", [(i, i ^ mask) for i in range(8)])


def gather_rows(x):
    return lax.all_gather(x, "fsdp", axis=0, tiled=True)


def assemble_kernel(x_ref, top_x_ref, low_y_ref, top_far_ref, low_far_ref, out_ref):
    rows = x_ref.shape[0]
    half = rows // 2
    out_ref[:rows] = x_ref[...]
    out_ref[rows : rows + half] = top_x_ref[...]
    out_ref[rows + half : 2 * rows] = low_far_ref[:half]
    out_ref[2 * rows : 2 * rows + half] = top_far_ref[:half]
    out_ref[2 * rows + half : 3 * rows] = low_y_ref[...]
    out_ref[3 * rows : 3 * rows + half] = top_far_ref[half:]
    out_ref[3 * rows + half :] = low_far_ref[half:]


def assemble(*pieces):
    rows, width = pieces[0].shape
    block = lambda n: pl.BlockSpec((n, width // 3), lambda i: (0, i))
    return pl.pallas_call(
        assemble_kernel,
        name="assemble",
        grid=(3,),
        in_specs=[block(p.shape[0]) for p in pieces],
        out_specs=block(4 * rows),
        out_shape=jax.ShapeDtypeStruct((4 * rows, width), pieces[0].dtype),
        compiler_params=params(),
        cost_estimate=cost(0, 16 * rows * width),
    )(*pieces)


def gather_near(x, n):
    if n != 8:
        every = gather_rows(x)
        half = every.shape[0] // 2
        return every[:half], every[half:]
    gather = Gather(x, n)
    gather.further()
    return gather.finish()


class Gather:
    def __init__(self, x, n):
        self.n, self.x = n, x
        if n != 8:
            self.halves = gather_near(x, n)
            self.near = self.far = ()
            return
        half = x.shape[0] // 2
        self.near = swap(x[:half], ALONG_X), swap(x[half:], ALONG_Y)

    def further(self, *others):
        if self.n != 8:
            return
        half = self.x.shape[0] // 2
        x, (top_x, low_y) = gate((self.x, self.near), *others)
        self.near = top_x, low_y
        top_far = swap(jnp.concatenate([x[:half], top_x]), ALONG_Y)
        low_far = swap(jnp.concatenate([x[half:], low_y]), ALONG_X)
        self.far = top_far, low_far

    def finish(self, *others):
        if self.n != 8:
            return self.halves
        near, far = gate((self.near, self.far), *others)
        mine = assemble(self.x, *near, *far)
        return mine, swap(mine, CORE)


class Scatter:
    def __init__(self, arrays, n):
        self.arrays, self.n, self.stage = list(arrays), n, 0
        self.rows = 2 * arrays[0][0].shape[0] // n

    def advance(self):
        held, self.stage = self.arrays, self.stage + 1
        rows, half = self.rows, self.rows // 2
        if self.n != 8:
            if self.stage == 1:
                self.arrays = [scatter_rows(jnp.concatenate(a)) for a in held]
            return
        if self.stage == 1:
            self.arrays = [add_low(mine, swap(other, CORE)) for mine, other in held]
        if self.stage == 2:
            tops = [a[k * rows : k * rows + half] for a in held for k in (2, 3)]
            lows = [a[k * rows + half : (k + 1) * rows] for a in held for k in (1, 3)]
            tops = swap(jnp.concatenate(tops), ALONG_Y)
            lows = swap(jnp.concatenate(lows), ALONG_X)
            self.arrays = []
            for i, a in enumerate(held):
                at = 2 * i * half
                self.arrays.append(
                    (
                        add_low(a[:half], tops[at : at + half]),
                        add_low(a[half:rows], lows[at : at + half]),
                        add_low(a[rows : rows + half], tops[at + half : at + rows]),
                        add_low(a[2 * rows + half : 3 * rows], lows[at + half : at + rows]),
                    )
                )
        if self.stage == 3:
            over_x = swap(jnp.concatenate([a[2] for a in held]), ALONG_X)
            over_y = swap(jnp.concatenate([a[3] for a in held]), ALONG_Y)
            self.arrays = [
                jnp.concatenate(
                    [
                        add_low(a[0], over_x[i * half : (i + 1) * half]),
                        add_low(a[1], over_y[i * half : (i + 1) * half]),
                    ]
                )
                for i, a in enumerate(held)
            ]


def block_order(n):
    at = jnp.arange(n, dtype=jnp.int32)
    if n != 8:
        return at
    return lax.axis_index("fsdp").astype(jnp.int32) ^ (2 * lax.rem(at, 4) + at // 4)


def block_places(n):
    if n != 8:
        return jnp.arange(n, dtype=jnp.int32)
    mask = lax.axis_index("fsdp").astype(jnp.int32) ^ jnp.arange(n, dtype=jnp.int32)
    return (mask >> 1) + 4 * (mask & 1)


def scatter_rows(x):
    return lax.psum_scatter(x, "fsdp", scatter_dimension=0, tiled=True)


def on_device(
    n_seq,
    n_fsdp,
    inputs,
    lengths,
    expert_ids,
    cotangent,
    gain_attn,
    w_query,
    key_projection,
    value_projection,
    w_out,
    gain_moe,
    router,
    w_gate,
    w_up,
    w_down,
):
    micros, local_seqs, tokens, dim = inputs.shape
    assert local_seqs == 1
    rows = micros * tokens
    experts, _, hidden = w_gate.shape
    n_experts = router.shape[1]
    kv_width = key_projection.shape[1]
    at = lax.axis_index("seq")
    own = (lax.axis_index("fsdp") * experts).astype(jnp.int32).reshape(1)

    small = jnp.concatenate(
        [router, gain_attn[:, None], gain_moe[:, None]], axis=1
    )
    small = jnp.pad(small, ((0, 0), (0, LANES - small.shape[1])))
    place, order = block_places(n_fsdp), block_order(n_fsdp)

    def weights(w):
        return [h.reshape(n_fsdp // 2, -1, h.shape[1]) for h in gather_near(w, n_fsdp)]

    w_kv = weights(jnp.concatenate([key_projection, value_projection, small], axis=1))
    router_all, rows_all = unpack(place, w_kv, 2 * kv_width // LANES, n_experts)
    gain_one = rows_all[n_experts : n_experts + 1]
    gain_two = rows_all[n_experts + 1 : n_experts + 2]

    positions = at * tokens + jnp.arange(tokens, dtype=jnp.int32)
    frequency = THETA ** (-(jnp.arange(HALF, dtype=F32) * 2.0) / HEAD)
    angles = frequency[:, None] * positions.astype(F32)[None, :]
    cosine, sine = jnp.cos(angles), jnp.sin(angles)
    cosine_all, sine_all = jnp.tile(cosine, (1, micros)), jnp.tile(sine, (1, micros))

    x = inputs.reshape(rows, dim)
    chosen = jnp.sum(
        (
            expert_ids.reshape(rows, TOPK)[:, :, None]
            == jnp.arange(LANES, dtype=jnp.int32)[None, None, :]
        ).astype(F32),
        axis=1,
    )
    valid = positions[None, :] < lengths[:, :1]
    gout = jnp.where(valid[:, :, None], cotangent.reshape(micros, tokens, dim), BF(0))
    infos = [
        jnp.stack([at.astype(jnp.int32), lengths[m, 0].astype(jnp.int32)]) for m in range(micros)
    ]

    kv, normed_one = kv_project(place, x, gain_one, w_kv, kv_width, cosine_all, sine_all)
    q_width = w_query.shape[1]
    w_gather = Gather(gate(jnp.concatenate([w_query, w_out], axis=1), kv), n_fsdp)
    w_gather.further()
    kvs = []
    for m in range(micros):
        mine = kv[m * tokens : (m + 1) * tokens]
        every = lax.all_gather(mine, "seq", axis=0, tiled=True)
        kvs.append(every.reshape(n_seq, tokens, 2 * kv_width))
    w_qo = [h.reshape(n_fsdp // 2, -1, h.shape[1]) for h in w_gather.finish(kvs[0], chosen, infos)]
    g_gathers = [Gather(gate(gout[0], w_gather.far), n_fsdp)]
    for m in range(1, micros):
        g_gathers.append(Gather(gate(gout[m], g_gathers[-1].near), n_fsdp))
    q_t = q_project(
        place, gate(normed_one, kvs[0]), w_qo, q_width, cosine_all, sine_all
    )

    state, xg_all = [], []
    for m in range(micros):
        if m == 0:
            info = gate(infos[m], g_gathers[0].near)
            g_gathers[0].further(q_t)
        else:
            info = gate(infos[m], state[-1][2])
        attn, attn_t, lse = attend(info, q_t, kvs[m], m, tokens)
        if m == 0:
            attn = gate(attn, g_gathers[0].far, [g.near for g in g_gathers[1:]])
            for g in g_gathers[1:]:
                g.further(g_gathers[0].far)
        else:
            attn = gate(attn, g_gathers[m].far)
        residual, xg, exact = after_attention(
            place, attn, w_qo, q_width, x, m, gain_two, router_all, chosen
        )
        state.append((attn_t, lse, residual, exact))
        xg_all.append(gather_rows(xg))

    g_all = [g.finish(state[-1][2]) for g in g_gathers]
    xg_all[0] = gate(xg_all[0], state[-1][2], g_all)
    passed, backs = [], []
    for m in range(micros):
        *y, back, hg, gp = run_experts(
            own, order, xg_all[m], g_all[m], w_gate, w_up, w_down
        )
        passed.append((xg_all[m], hg, gp))
        backs.append((scatter_rows(back), y))

    names = [(name, e) for name in ("down", "gate", "up") for e in range(experts)]

    def expert_grad(name, e, got):
        xs, hgs, gps = ([p[i] for p in got] for i in range(3))
        if name == "down":
            return down_grad(hgs, e, hidden, g_all, n_fsdp)
        return wide_grad(xs, 0, dim, gps, 2 * e + (name == "up"), hidden)

    line = Line(n_seq)
    found = [{} for _ in range(micros)]

    def to_heads(m):
        attn_t, lse, residual, exact = state[m]
        gres, g_attn, g_t, small_two = before_attention(
            place, backs[m][0], residual, exact, gout[m], gain_two, router_all, w_qo, q_width
        )
        found[m].update(gres=gres, g_attn=g_attn, g_t=g_t, small_two=small_two)

    def through_heads(m):
        attn_t, lse = state[m][:2]
        gq, by_owner = attend_back(
            infos[m], q_t, found[m]["g_t"], attn_t, lse, cosine, sine, kvs[m], m, tokens
        )
        found[m].update(gq=gq, by_owner=by_owner)

    owned = {}

    def to_owners(m):
        by_owner = found[m].pop("by_owner")
        shape = by_owner.shape
        owned[m] = lax.psum_scatter(
            by_owner.reshape(n_seq * shape[1] * tokens, shape[3]),
            "seq",
            scatter_dimension=0,
            tiled=True,
        ).reshape(shape[1:])

    def finish(m):
        f = found[m]
        f["dkv"] = turn_back(f["mine"], cosine, sine)
        f["din"], f["small_one"] = last_step(
            place, f["gq"], f["dkv"], w_qo, w_kv, x, m, gain_one, f["gres"]
        )

    def rest_grads():
        every = lambda name: [f[name] for f in found]
        return projection_grads(
            normed_one, every("gq"), every("dkv"), every("small_two"), every("small_one"), n_experts
        )

    n_grads = len(names)
    work = {
        0: [("grad", 1), (to_heads, 0)],
        1: [("grad", 2), (through_heads, 0)],
        2: [("grad", 3), (to_heads, 1), (through_heads, 1)],
        3: [("grad", 4), (finish, 0), ("grad", 5)],
        4: [(finish, 1)],
    }
    def widen(parts, turned):
        return jnp.stack([(p.T if turned else p).astype(F32) for p in parts])

    experts_out = []
    chunks = {0: expert_grad(*names[0], passed)}
    chunks.update({i: expert_grad(*names[i], passed) for i in range(6, n_grads)})
    slots = max(n_grads, 6)
    moe = Scatter([b[1] for b in backs], n_fsdp)
    for t in range(slots + 3):
        if t in (3, 4):
            found[t - 3]["mine"] = owned[t - 3]
        if t == 3:
            heads = Scatter([found[0].pop("out")], n_fsdp)
        if t == 7:
            found[0]["rest"] = rest
        held = (chunks, line.held, line.results, passed, found, moe.arrays)
        if t >= 3:
            *held, heads.arrays = lax.optimization_barrier((*held, heads.arrays))
        else:
            held = lax.optimization_barrier(held)
        chunks, line.held, line.results, passed, found, moe.arrays = held
        if t == 7:
            rest = lax.psum(found[0].pop("rest"), "seq")
        if len(line.results) in (experts, 2 * experts, 3 * experts) and len(experts_out) < 3:
            pair = line.sums()[-experts:]
            experts_out.append(widen(pair, len(experts_out) == 0))
            found[1]["wide"] = experts_out[-1]
        if t == slots:
            chunks[slots] = heads.arrays[0]
        sent = chunks.pop(t, None)
        if t in (2, 3):
            to_owners(t - 2)
        for kind, i in work.get(t, []):
            if kind != "grad":
                kind(i)
            elif i < n_grads:
                chunks[i] = expert_grad(*names[i], passed)
        if t == 2:
            found[0]["out"] = out_grad(
                order, [st[0] for st in state], [f["g_attn"] for f in found]
            )
        if t in (5, 6, 7):
            moe.advance()
        for _ in range(3 if t == 3 else 0):
            heads.advance()
        line.step(sent, (chunks, found))
        if t == 4:
            normed_one, line.held = lax.optimization_barrier((normed_one, line.held))
            rest = scatter_rows(rest_grads())
    rest = gate(rest, line.results).astype(F32)
    totals = line.sums()
    for i in range(len(experts_out), 3):
        experts_out.append(widen(totals[i * experts : (i + 1) * experts], i == 0))
    d_out = totals[n_grads].astype(F32)

    outs = []
    for m in range(micros):
        outs.append(
            jnp.where(valid[m][:, None], state[m][2] + moe.arrays[m].astype(F32), 0.0).astype(BF)
        )
    grads = [f["din"] for f in found]
    assert len(totals) == n_grads + 1
    shape = (micros, 1, tokens, dim)
    ends = q_width + 2 * kv_width
    return (
        jnp.stack(outs).reshape(shape),
        jnp.stack(grads).reshape(shape),
        rest[:, ends + n_experts],
        rest[:, :q_width],
        rest[:, q_width : q_width + kv_width],
        rest[:, q_width + kv_width : ends],
        d_out,
        rest[:, ends + n_experts + 1],
        rest[:, ends : ends + n_experts],
        *experts_out[1:],
        experts_out[0],
    )


def solution(mesh):
    token_spec = P(None, "fsdp", "seq", None)
    row, matrix, cube = P("fsdp"), P("fsdp", None), P("fsdp", None, None)
    return jax.shard_map(
        functools.partial(on_device, mesh.shape["seq"], mesh.shape["fsdp"]),
        mesh=mesh,
        in_specs=(
            token_spec,
            P(None, "fsdp"),
            token_spec,
            token_spec,
            row,
            matrix,
            matrix,
            matrix,
            matrix,
            row,
            matrix,
            cube,
            cube,
            cube,
        ),
        out_specs=(
            token_spec,
            token_spec,
            row,
            matrix,
            matrix,
            matrix,
            matrix,
            row,
            matrix,
            cube,
            cube,
            cube,
        ),
        check_vma=False,
    )
```

```python
import functools

import jax
import jax.numpy as jnp
from jax import lax
from jax.experimental import pallas as pl
from jax.experimental.pallas import tpu as pltpu
from jax.sharding import PartitionSpec as P

HEAD = 64
HALF = HEAD // 2
GROUP = 3
TOPK = 8
EPS = 1e-06
THETA = 10000.0
NEGATIVE = -1e30
LANES = 128
SCALE = HEAD ** (-0.5)
BF = jnp.bfloat16
F32 = jnp.float32
VMEM_BYTES = 60 * 1024 * 1024

NN = (((1,), (0,)), ((), ()))
NT = (((1,), (1,)), ((), ()))
TN = (((0,), (0,)), ((), ()))


def dot(a, b, dims=NN):
    return lax.dot_general(a, b, dims, preferred_element_type=F32)


def params():
    return pltpu.CompilerParams(vmem_limit_bytes=VMEM_BYTES)


def cost(flops, moved, trans=0):
    parts = (int(v) // 10 for v in (flops, moved, trans))
    flops, moved, trans = parts
    return pl.CostEstimate(flops=flops, bytes_accessed=moved, transcendentals=trans)


def whole(shape):
    zeros = (0,) * len(shape)
    return pl.BlockSpec(shape, lambda *_: zeros)


def smem():
    return pl.BlockSpec(memory_space=pltpu.SMEM)


def pick(at, first_ref, second_ref, index=None):
    half = first_ref.shape[0]
    if index is None:
        index = lax.rem(at, half)
    return jnp.where(at < half, first_ref[index], second_ref[index])


def in_order(place_ref, w_refs):
    devices = 2 * w_refs[0].shape[0]
    return jnp.concatenate([pick(place_ref[j], *w_refs) for j in range(devices)], axis=0)


def rotate(rows, cosine, sine, sign):
    pieces = []
    for h in range(rows.shape[0] // HEAD):
        a = rows[h * HEAD : h * HEAD + HALF]
        b = rows[h * HEAD + HALF : (h + 1) * HEAD]
        if sign > 0:
            pieces += [a * cosine - b * sine, b * cosine + a * sine]
        else:
            pieces += [a * cosine + b * sine, b * cosine - a * sine]
    return jnp.concatenate(pieces, axis=0)


def unpack_kernel(n_experts, place_ref, wa_ref, wb_ref, router_ref, rows_ref):
    w = in_order(place_ref, (wa_ref, wb_ref))
    lane = lax.broadcasted_iota(jnp.int32, w.shape, 1)
    router_ref[...] = jnp.where(lane < n_experts, w.astype(F32), 0.0).astype(BF)
    rows_ref[...] = w.astype(F32).T


def unpack(place, w, block, n_experts):
    dim = 2 * w[0].shape[0] * w[0].shape[1]
    return pl.pallas_call(
        functools.partial(unpack_kernel, n_experts),
        name="unpack",
        grid=(1,),
        in_specs=[smem(), *w_columns(w, LANES, lambda i: block)],
        out_specs=[whole((dim, LANES)), whole((LANES, dim))],
        out_shape=[
            jax.ShapeDtypeStruct((dim, LANES), BF),
            jax.ShapeDtypeStruct((LANES, dim), F32),
        ],
        compiler_params=params(),
        cost_estimate=cost(0, 12 * dim * LANES),
    )(place, *w)


def kv_kernel(place_ref, x_ref, gain_ref, wa_ref, wb_ref, cos_ref, sin_ref, kv_ref, normed_ref):
    step = pl.program_id(0)

    @pl.when(step == 0)
    def _():
        x = x_ref[...].astype(F32)
        inv = lax.rsqrt(jnp.mean(x * x, axis=-1, keepdims=True) + EPS)
        normed_ref[...] = (x * inv * gain_ref[...]).astype(BF)
        r = dot(normed_ref[...], in_order(place_ref, (wa_ref, wb_ref)))
        r = rotate(r.T, cos_ref[...], sin_ref[...], 1)
        kv_ref[...] = r.T.astype(BF)

    @pl.when(step == 1)
    def _():
        kv_ref[...] = dot(normed_ref[...], in_order(place_ref, (wa_ref, wb_ref))).astype(BF)


def w_columns(w, tile, at):
    return [pl.BlockSpec((*half.shape[:2], tile), lambda *i: (0, 0, at(*i))) for half in w]


def kv_project(place, x, gain, w, width, cosine, sine):
    rows, dim = x.shape
    return pl.pallas_call(
        kv_kernel,
        name="kv_project",
        grid=(2,),
        in_specs=[
            smem(),
            whole((rows, dim)),
            whole((1, dim)),
            *w_columns(w, width, lambda i: i),
            whole((HALF, rows)),
            whole((HALF, rows)),
        ],
        out_specs=[pl.BlockSpec((rows, width), lambda i: (0, i)), whole((rows, dim))],
        out_shape=[
            jax.ShapeDtypeStruct((rows, 2 * width), BF),
            jax.ShapeDtypeStruct((rows, dim), BF),
        ],
        compiler_params=params(),
        cost_estimate=cost(2 * rows * dim * 2 * width, 2 * (2 * rows * dim + dim * 2 * width)),
    )(place, x, gain, *w, cosine, sine)


def q_kernel(place_ref, normed_ref, wa_ref, wb_ref, cos_ref, sin_ref, q_ref):
    r = dot(normed_ref[...], in_order(place_ref, (wa_ref, wb_ref)))
    r = rotate(r.T, cos_ref[...], sin_ref[...], 1)
    q_ref[...] = r.astype(BF) * BF(SCALE)


def q_project(place, normed, w, width, cosine, sine):
    rows, dim = normed.shape
    tile = 512
    return pl.pallas_call(
        q_kernel,
        name="q_project",
        grid=(width // tile,),
        in_specs=[
            smem(),
            whole((rows, dim)),
            *w_columns(w, tile, lambda i: i),
            whole((HALF, rows)),
            whole((HALF, rows)),
        ],
        out_specs=pl.BlockSpec((tile, rows), lambda i: (i, 0)),
        out_shape=jax.ShapeDtypeStruct((width, rows), BF),
        compiler_params=params(),
        cost_estimate=cost(2 * rows * dim * width, 2 * (2 * rows * dim + dim * width)),
    )(place, normed, *w, cosine, sine)


def side_by_side(ref, j):
    base = j * GROUP * HEAD
    return jnp.concatenate(
        [ref[base + h * HEAD : base + (h + 1) * HEAD, :] for h in range(GROUP)], axis=1
    )


def diagonal_mask(tokens, own_len):
    key = lax.broadcasted_iota(jnp.int32, (tokens, tokens), 0)
    query = lax.broadcasted_iota(jnp.int32, (tokens, tokens), 1)
    one = (key <= query) & (key < own_len)
    return jnp.concatenate([one.astype(jnp.int32)] * GROUP, axis=1) > 0


def attend_kernel(n, info_ref, q_ref, k_ref, v_ref, o_ref, ot_ref, lse_ref, m_ref, l_ref, acc_ref):
    tokens = q_ref.shape[1]
    d = pl.program_id(1)
    s = info_ref[0]
    own_len = info_ref[1] - s * tokens
    active = own_len > 0

    def pair(j):
        cols = slice(j * HEAD, (j + 1) * HEAD)
        scores = dot(k_ref[0, :, cols], side_by_side(q_ref, j))
        return scores, v_ref[0, :, cols].astype(F32).T.astype(BF)

    @pl.when(active & (d == 0))
    def _():
        mask = diagonal_mask(tokens, own_len)
        for j in range(2):
            scores, value_t = pair(j)
            scores = jnp.where(mask, scores, NEGATIVE)
            top = jnp.max(scores, axis=0, keepdims=True)
            p = jnp.exp(scores - top)
            l_ref[j : j + 1] = jnp.sum(p, axis=0, keepdims=True)
            acc_ref[j] = dot(value_t, p.astype(BF))
            m_ref[j : j + 1] = top

    @pl.when(active & (d > 0) & (d <= s))
    def _():
        for j in range(2):
            scores, value_t = pair(j)
            old = m_ref[j : j + 1]
            top = jnp.maximum(old, jnp.max(scores, axis=0, keepdims=True))
            keep = jnp.exp(old - top)
            p = jnp.exp(scores - top)
            l_ref[j : j + 1] = l_ref[j : j + 1] * keep + jnp.sum(p, axis=0, keepdims=True)
            acc_ref[j] = acc_ref[j] * keep + dot(value_t, p.astype(BF))
            m_ref[j : j + 1] = top

    @pl.when(active & (d == n - 1))
    def _():
        pieces = []
        for j in range(2):
            out = acc_ref[j] / l_ref[j : j + 1]
            lse_ref[j : j + 1] = m_ref[j : j + 1] + jnp.log(l_ref[j : j + 1])
            pieces += [out[:, h * tokens : (h + 1) * tokens] for h in range(GROUP)]
        out = jnp.concatenate(pieces, axis=0)
        ot_ref[...] = out.astype(BF)
        o_ref[...] = out.T.astype(BF)

    @pl.when(jnp.logical_not(active) & (d == 0))
    def _():
        o_ref[...] = jnp.zeros_like(o_ref)
        ot_ref[...] = jnp.zeros_like(ot_ref)
        lse_ref[...] = jnp.zeros_like(lse_ref)


def owner(info_ref, d, n):
    return lax.rem(info_ref[0] + n - d, n)


def attend(info, q_t, kv, micro, tokens):
    n = kv.shape[0]
    width = q_t.shape[0]
    kv_width = kv.shape[2] // 2
    steps = kv_width // LANES
    qw = width // steps
    return pl.pallas_call(
        functools.partial(attend_kernel, n),
        name="attend",
        grid_spec=pltpu.PrefetchScalarGridSpec(
            num_scalar_prefetch=1,
            grid=(steps, n),
            in_specs=[
                pl.BlockSpec((qw, tokens), lambda i, d, info: (i, micro)),
                pl.BlockSpec((1, tokens, LANES), lambda i, d, info: (owner(info, d, n), 0, i)),
                pl.BlockSpec(
                    (1, tokens, LANES), lambda i, d, info: (owner(info, d, n), 0, steps + i)
                ),
            ],
            out_specs=[
                pl.BlockSpec((tokens, qw), lambda i, d, info: (0, i)),
                pl.BlockSpec((qw, tokens), lambda i, d, info: (i, 0)),
                pl.BlockSpec((8, GROUP * tokens), lambda i, d, info: (i, 0)),
            ],
            scratch_shapes=[
                pltpu.VMEM((8, GROUP * tokens), F32),
                pltpu.VMEM((8, GROUP * tokens), F32),
                pltpu.VMEM((2, HEAD, GROUP * tokens), F32),
            ],
        ),
        out_shape=[
            jax.ShapeDtypeStruct((tokens, width), BF),
            jax.ShapeDtypeStruct((width, tokens), BF),
            jax.ShapeDtypeStruct((8 * steps, GROUP * tokens), F32),
        ],
        compiler_params=params(),
        cost_estimate=cost(
            4 * 4 * width * tokens * tokens * n,
            2 * (3 * width * tokens + n * tokens * 2 * kv_width),
            width // HEAD * tokens * tokens * n,
        ),
    )(info, q_t, kv, kv)


def attend_back_kernel(
    n, info_ref, q_ref, g_ref, o_ref, lse_ref, cos_ref, sin_ref, k_ref, v_ref, gq_ref, dkv_ref, acc_ref
):
    tokens = q_ref.shape[1]
    d = pl.program_id(1)
    s = info_ref[0]
    own_len = info_ref[1] - s * tokens
    active = own_len > 0

    def block(first):
        mask = diagonal_mask(tokens, own_len) if first else None
        dks, dvs = [], []
        for j in range(2):
            cols = slice(j * HEAD, (j + 1) * HEAD)
            key, value = k_ref[0, :, cols], v_ref[0, :, cols]
            query, grad = side_by_side(q_ref, j), side_by_side(g_ref, j)
            out = side_by_side(o_ref, j)
            inner = jnp.sum(grad.astype(F32) * out.astype(F32), axis=0, keepdims=True)
            p = jnp.exp(dot(key, query) - lse_ref[j : j + 1])
            if first:
                p = jnp.where(mask, p, 0.0)
            dp = dot(value, grad)
            ds = (p * (dp - inner)).astype(BF)
            dvs.append(dot(p.astype(BF), grad, NT))
            dks.append(dot(ds, query, NT))
            part = dot(key.astype(F32).T.astype(BF), ds)
            if first:
                acc_ref[j] = part
            else:
                acc_ref[j] += part
        dkv_ref[0, 0] = jnp.concatenate(dks, axis=1).astype(BF)
        dkv_ref[0, 1] = jnp.concatenate(dvs, axis=1).astype(BF)

    pl.when(active & (d == 0))(lambda: block(True))
    pl.when(active & (d > 0) & (d <= s))(lambda: block(False))

    @pl.when(active & (d == n - 1))
    def _():
        pieces = []
        for j in range(2):
            for h in range(GROUP):
                piece = acc_ref[j, :, h * tokens : (h + 1) * tokens] * SCALE
                pieces.append(piece.astype(BF).astype(F32))
        grad_q = rotate(jnp.concatenate(pieces, axis=0), cos_ref[...], sin_ref[...], -1)
        gq_ref[...] = grad_q.T.astype(BF)

    @pl.when(jnp.logical_not(active) | (d > s))
    def _():
        dkv_ref[...] = jnp.zeros_like(dkv_ref)

    @pl.when(jnp.logical_not(active) & (d == 0))
    def _():
        gq_ref[...] = jnp.zeros_like(gq_ref)


def attend_back(info, q_t, g_t, o_t, lse, cosine, sine, kv, micro, tokens):
    n = kv.shape[0]
    width = q_t.shape[0]
    kv_width = kv.shape[2] // 2
    steps = kv_width // LANES
    qw = width // steps
    transposed = pl.BlockSpec((qw, tokens), lambda i, d, info: (i, 0))
    return pl.pallas_call(
        functools.partial(attend_back_kernel, n),
        name="attend_back",
        grid_spec=pltpu.PrefetchScalarGridSpec(
            num_scalar_prefetch=1,
            grid=(steps, n),
            in_specs=[
            pl.BlockSpec((qw, tokens), lambda i, d, info: (i, micro)),
            transposed,
            transposed,
            pl.BlockSpec((8, GROUP * tokens), lambda i, d, info: (i, 0)),
            whole((HALF, tokens)),
            whole((HALF, tokens)),
            pl.BlockSpec((1, tokens, LANES), lambda i, d, info: (owner(info, d, n), 0, i)),
            pl.BlockSpec(
                (1, tokens, LANES), lambda i, d, info: (owner(info, d, n), 0, steps + i)
            ),
        ],
        out_specs=[
            pl.BlockSpec((tokens, qw), lambda i, d, info: (0, i)),
            pl.BlockSpec(
                (1, 2, tokens, LANES), lambda i, d, info: (owner(info, d, n), 0, 0, i)
            ),
        ],
            scratch_shapes=[pltpu.VMEM((2, HEAD, GROUP * tokens), F32)],
        ),
        out_shape=[
            jax.ShapeDtypeStruct((tokens, width), BF),
            jax.ShapeDtypeStruct((n, 2, tokens, kv_width), BF),
        ],
        compiler_params=params(),
        cost_estimate=cost(
            10 * 4 * width * tokens * tokens * n,
            2 * (4 * width * tokens + 2 * n * tokens * 2 * kv_width),
            width // HEAD * tokens * tokens * n,
        ),
    )(info, q_t, g_t, o_t, lse, cosine, sine, kv, kv)


def after_kernel(
    steps, place_ref, a_ref, wa_ref, wb_ref, x_ref, gain_ref, router_ref, chosen_ref, res_ref, xg_ref, ge_ref, acc_ref
):
    step = pl.program_id(0)
    acc_ref[step] = dot(a_ref[...], in_order(place_ref, (wa_ref, wb_ref)))

    @pl.when(step == steps - 1)
    def _():
        dim = x_ref.shape[1]
        product = jnp.concatenate([acc_ref[i] for i in range(steps)], axis=1)
        residual = x_ref[...].astype(F32) + product
        res_ref[...] = residual
        inv = lax.rsqrt(jnp.mean(residual * residual, axis=-1, keepdims=True) + EPS)
        normed = (residual * inv * gain_ref[...]).astype(BF)
        logits = dot(normed, router_ref[...])
        chosen = chosen_ref[...] > 0
        logits = jnp.where(chosen, logits, NEGATIVE)
        top = jnp.max(logits, axis=-1, keepdims=True)
        e = jnp.where(chosen, jnp.exp(logits - top), 0.0)
        exact = e / jnp.sum(e, axis=-1, keepdims=True)
        ge_ref[...] = exact
        xg_ref[:, :dim] = normed
        xg_ref[:, dim:] = exact.astype(BF)


def after_attention(place, attn, w, first, x, micro, gain, router, chosen):
    tokens, width = attn.shape
    dim = x.shape[1]
    tile = 512
    steps = dim // tile
    return pl.pallas_call(
        functools.partial(after_kernel, steps),
        name="after_attention",
        grid=(steps,),
        in_specs=[
            smem(),
            whole((tokens, width)),
            *w_columns(w, tile, lambda i: first // tile + i),
            pl.BlockSpec((tokens, dim), lambda i: (micro, 0)),
            whole((1, dim)),
            whole((dim, LANES)),
            pl.BlockSpec((tokens, LANES), lambda i: (micro, 0)),
        ],
        out_specs=[
            whole((tokens, dim)),
            whole((tokens, dim + LANES)),
            whole((tokens, LANES)),
        ],
        out_shape=[
            jax.ShapeDtypeStruct((tokens, dim), F32),
            jax.ShapeDtypeStruct((tokens, dim + LANES), BF),
            jax.ShapeDtypeStruct((tokens, LANES), F32),
        ],
        scratch_shapes=[pltpu.VMEM((steps, tokens, tile), F32)],
        compiler_params=params(),
        cost_estimate=cost(2 * tokens * width * dim, 2 * width * dim + 10 * tokens * dim),
    )(place, attn, *w, x, gain, router, chosen)


def expert_kernel(
    experts, half, own_ref, order_ref, xg_ref, ga_ref, gb_ref, wg_ref, wu_ref, wd_ref, ya_ref, yb_ref, back_ref, hg_ref, gp_ref
):
    rows, dim = ga_ref.shape
    hidden = wg_ref.shape[2]
    x = xg_ref[:, :dim]
    step = pl.program_id(0)
    g = jnp.where(step < half, ga_ref[...], gb_ref[...])
    gates = xg_ref[:, dim:].astype(F32)
    lane = lax.broadcasted_iota(jnp.int32, (rows, LANES), 1)
    gate_cols = jnp.zeros((rows, LANES), F32)
    for e in range(experts):
        mine = lane == own_ref[0] + e
        gate = jnp.sum(jnp.where(mine, gates, 0.0), axis=1, keepdims=True)
        pre_gate = dot(x, wg_ref[e])
        pre_up = dot(x, wu_ref[e])
        grad_hidden = dot(g, wd_ref[e], NT)
        sig = 1.0 / (1.0 + jnp.exp(-pre_gate))
        silu = pre_gate * sig
        h = (silu * pre_up).astype(BF).astype(F32)
        per_gate = jnp.sum(h * grad_hidden, axis=1, keepdims=True)
        gate_cols = jnp.where(mine, per_gate, gate_cols)
        hg_ref[:, e * hidden : (e + 1) * hidden] = (gate * h).astype(BF)
        gh = gate * grad_hidden
        base = 2 * e * hidden
        gp_ref[:, base : base + hidden] = (
            gh * pre_up * (sig * (1.0 + pre_gate * (1.0 - sig)))
        ).astype(BF)
        gp_ref[:, base + hidden : base + 2 * hidden] = (gh * silu).astype(BF)
    y = dot(hg_ref[:, :hidden], wd_ref[0])
    for e in range(1, experts):
        y += dot(hg_ref[:, e * hidden : (e + 1) * hidden], wd_ref[e])

    @pl.when(step < half)
    def _():
        ya_ref[...] = y.astype(BF)

    @pl.when(step >= half)
    def _():
        yb_ref[...] = y.astype(BF)

    back = None
    for e in range(experts):
        base = 2 * e * hidden
        part = dot(gp_ref[:, base : base + hidden], wg_ref[e], NT)
        part += dot(gp_ref[:, base + hidden : base + 2 * hidden], wu_ref[e], NT)
        back = part if back is None else back + part
    back_ref[:, :dim] = back.astype(BF)
    back_ref[:, dim:] = gate_cols.astype(BF)


def run_experts(own, order, xg, g, w_gate, w_up, w_down):
    rows = xg.shape[0]
    dim = g[0].shape[1]
    experts, _, hidden = w_gate.shape
    devices = order.shape[0]
    tile, half = rows // devices, devices // 2
    named = lambda width: pl.BlockSpec((tile, width), lambda i, own, order: (order[i], 0))
    first = lambda i: jnp.minimum(i, half - 1)
    second = lambda i: jnp.maximum(i - half, 0)
    return pl.pallas_call(
        functools.partial(expert_kernel, experts, half),
        name="run_experts",
        grid_spec=pltpu.PrefetchScalarGridSpec(
            num_scalar_prefetch=2,
            grid=(devices,),
            in_specs=[
                named(dim + LANES),
                pl.BlockSpec((tile, dim), lambda i, *_: (first(i), 0)),
                pl.BlockSpec((tile, dim), lambda i, *_: (second(i), 0)),
                whole(w_gate.shape),
                whole(w_up.shape),
                whole(w_down.shape),
            ],
            out_specs=[
                pl.BlockSpec((tile, dim), lambda i, *_: (first(i), 0)),
                pl.BlockSpec((tile, dim), lambda i, *_: (second(i), 0)),
                named(dim + LANES),
                pl.BlockSpec((tile, experts * hidden), lambda i, *_: (i, 0)),
                named(2 * experts * hidden),
            ],
        ),
        out_shape=[
            jax.ShapeDtypeStruct((rows // 2, dim), BF),
            jax.ShapeDtypeStruct((rows // 2, dim), BF),
            jax.ShapeDtypeStruct((rows, dim + LANES), BF),
            jax.ShapeDtypeStruct((rows, experts * hidden), BF),
            jax.ShapeDtypeStruct((rows, 2 * experts * hidden), BF),
        ],
        compiler_params=params(),
        cost_estimate=cost(
            12 * rows * dim * hidden * experts,
            2 * (4 * rows * dim + 3 * rows * experts * hidden + 3 * experts * dim * hidden),
            rows * experts * hidden,
        ),
    )(own, order, xg, *g, w_gate, w_up, w_down)


def wide_grad_kernel(steps, micros, *refs):
    a_refs, b_refs = refs[:micros], refs[micros : 2 * micros]
    out_ref, acc_ref = refs[2 * micros :]
    step = pl.program_id(0)
    for m in range(micros):

        @pl.when((step >= m * steps) & (step < (m + 1) * steps))
        def _(m=m):
            part = dot(a_refs[m][...], b_refs[m][...], TN)
            if m == 0:

                @pl.when(step == 0)
                def _():
                    acc_ref[...] = part

                @pl.when(step > 0)
                def _():
                    acc_ref[...] += part
            else:
                acc_ref[...] += part

    @pl.when(step == micros * steps - 1)
    def _():
        out_ref[...] = acc_ref[...].astype(BF)


def wide_grad(lefts, left_block, left_width, rights, right_block, right_width, tile=512):
    micros, rows = len(lefts), lefts[0].shape[0]
    steps = rows // tile

    def spec(m, width, column):
        return pl.BlockSpec(
            (tile, width), lambda i: (jnp.clip(i - m * steps, 0, steps - 1), column)
        )

    return pl.pallas_call(
        functools.partial(wide_grad_kernel, steps, micros),
        name="wide_grad",
        grid=(micros * steps,),
        in_specs=[spec(m, left_width, left_block) for m in range(micros)]
        + [spec(m, right_width, right_block) for m in range(micros)],
        out_specs=whole((left_width, right_width)),
        out_shape=jax.ShapeDtypeStruct((left_width, right_width), BF),
        scratch_shapes=[pltpu.VMEM((left_width, right_width), F32)],
        compiler_params=params(),
        cost_estimate=cost(
            2 * micros * rows * left_width * right_width,
            2 * (micros * rows * (left_width + right_width) + left_width * right_width),
        ),
    )(*lefts, *rights)


def down_grad_kernel(micros, devices, *refs):
    hg_refs, refs = refs[:micros], refs[micros:]
    ga_refs, gb_refs = refs[:micros], refs[micros : 2 * micros]
    out_ref, acc_ref = refs[2 * micros :]
    step = pl.program_id(0)
    g = [jnp.where(step < devices // 2, a[...], b[...]) for a, b in zip(ga_refs, gb_refs)]
    part = dot(jnp.concatenate(g), jnp.concatenate([r[...] for r in hg_refs]), TN)

    @pl.when(step == 0)
    def _():
        acc_ref[...] = part

    @pl.when(step > 0)
    def _():
        acc_ref[...] += part

    @pl.when(step == devices - 1)
    def _():
        out_ref[...] = acc_ref[...].astype(BF)


def down_grad(hgs, expert, hidden, gs, devices):
    micros, rows = len(hgs), hgs[0].shape[0]
    tile, half = rows // devices, devices // 2
    dim = gs[0][0].shape[1]
    return pl.pallas_call(
        functools.partial(down_grad_kernel, micros, devices),
        name="down_grad",
        grid=(devices,),
        in_specs=[pl.BlockSpec((tile, hidden), lambda i: (i, expert))] * micros
        + [pl.BlockSpec((tile, dim), lambda i: (jnp.minimum(i, half - 1), 0))] * micros
        + [pl.BlockSpec((tile, dim), lambda i: (jnp.maximum(i - half, 0), 0))] * micros,
        out_specs=whole((dim, hidden)),
        out_shape=jax.ShapeDtypeStruct((dim, hidden), BF),
        scratch_shapes=[pltpu.VMEM((dim, hidden), F32)],
        compiler_params=params(),
        cost_estimate=cost(2 * micros * rows * hidden * dim, 2 * micros * rows * (hidden + dim)),
    )(*hgs, *[g[0] for g in gs], *[g[1] for g in gs])


def before_kernel(
    steps, place_ref, ret_ref, res_ref, ge_ref, gout_ref, gain_ref, router_ref, wa_ref, wb_ref, gres_ref, ga_ref, gt_ref, small_ref, cut_ref, acc_ref
):
    dim = res_ref.shape[1]

    step = pl.program_id(0)
    tile = dim // steps

    @pl.when(step == 0)
    def _():
        ge = ge_ref[...]
        gg = ret_ref[:, dim:].astype(F32)
        gl = ge * (gg - jnp.sum(ge * gg, axis=-1, keepdims=True))
        high = gl.astype(BF)
        low = (gl - high.astype(F32)).astype(BF)
        router = router_ref[...]
        gn = ret_ref[:, :dim].astype(F32) + (dot(high, router, NT) + dot(low, router, NT))
        residual = res_ref[...]
        gain = gain_ref[...]
        inv = lax.rsqrt(jnp.mean(residual * residual, axis=-1, keepdims=True) + EPS)
        unit = residual * inv
        normed = (unit * gain).astype(BF)
        small_ref[:LANES] = dot(high, normed, TN) + dot(low, normed, TN)
        gain_row = jnp.sum(gn * unit, axis=0, keepdims=True)
        small_ref[LANES:] = jnp.broadcast_to(gain_row, (8, dim))
        u = gn * gain
        gres = gout_ref[...].astype(F32) + inv * (
            u - unit * jnp.mean(u * unit, axis=-1, keepdims=True)
        )
        gres_ref[...] = gres
        low_gres = gres.astype(BF)
        ga_ref[...] = low_gres
        for i in range(steps):
            cut_ref[i] = low_gres[:, i * tile : (i + 1) * tile]
        acc_ref[...] = jnp.zeros_like(acc_ref)

    acc_ref[...] += dot(in_order(place_ref, (wa_ref, wb_ref)), cut_ref[step], NT)

    @pl.when(step == steps - 1)
    def _():
        gt_ref[...] = acc_ref[...].astype(BF)


def before_attention(place, returned, residual, exact, gout, gain, router, w, first):
    tokens, dim = residual.shape
    width = 2 * w[0].shape[0] * w[0].shape[1]
    tile = 512
    steps = dim // tile
    return pl.pallas_call(
        functools.partial(before_kernel, steps),
        name="before_attention",
        grid=(steps,),
        in_specs=[
            smem(),
            whole((tokens, dim + LANES)),
            whole((tokens, dim)),
            whole((tokens, LANES)),
            whole((tokens, dim)),
            whole((1, dim)),
            whole((dim, LANES)),
            *w_columns(w, tile, lambda i: first // tile + i),
        ],
        out_specs=[
            whole((tokens, dim)),
            whole((tokens, dim)),
            whole((width, tokens)),
            whole((LANES + 8, dim)),
        ],
        out_shape=[
            jax.ShapeDtypeStruct((tokens, dim), F32),
            jax.ShapeDtypeStruct((tokens, dim), BF),
            jax.ShapeDtypeStruct((width, tokens), BF),
            jax.ShapeDtypeStruct((LANES + 8, dim), F32),
        ],
        scratch_shapes=[
            pltpu.VMEM((steps, tokens, tile), BF),
            pltpu.VMEM((width, tokens), F32),
        ],
        compiler_params=params(),
        cost_estimate=cost(2 * tokens * width * dim, 2 * width * dim + 14 * tokens * dim),
    )(place, returned, residual, exact, gout, gain, router, *w)


def last_kernel(
    q_steps, steps, place_ref, gq_ref, dkv_ref, qa_ref, qb_ref, kva_ref, kvb_ref, x_ref, gain_ref, gres_ref, din_ref, small_ref, acc_ref
):
    step = pl.program_id(0)

    @pl.when(step == 0)
    def _():
        acc_ref[...] = dot(gq_ref[...], in_order(place_ref, (qa_ref, qb_ref)), NT)

    @pl.when((step > 0) & (step < q_steps))
    def _():
        acc_ref[...] += dot(gq_ref[...], in_order(place_ref, (qa_ref, qb_ref)), NT)

    @pl.when(step >= q_steps)
    def _():
        acc_ref[...] += dot(dkv_ref[...], in_order(place_ref, (kva_ref, kvb_ref)), NT)

    @pl.when(step == steps - 1)
    def _():
        x = x_ref[...].astype(F32)
        gain = gain_ref[...]
        inv = lax.rsqrt(jnp.mean(x * x, axis=-1, keepdims=True) + EPS)
        unit = x * inv
        gn = acc_ref[...]
        small_ref[...] = jnp.broadcast_to(
            jnp.sum(gn * unit, axis=0, keepdims=True), small_ref.shape
        )
        w = gn * gain
        grad = inv * (w - unit * jnp.mean(w * unit, axis=-1, keepdims=True))
        din_ref[...] = (grad + gres_ref[...]).astype(BF)


def last_step(place, gq, dkv, w_q, w_kv, x, micro, gain, gres):
    tokens, dim = gres.shape
    tile = 512
    q_steps, kv_steps = gq.shape[1] // tile, dkv.shape[1] // tile
    steps = q_steps + kv_steps
    q_at = lambda i: (0, jnp.minimum(i, q_steps - 1))
    kv_at = lambda i: (0, jnp.maximum(i - q_steps, 0))
    return pl.pallas_call(
        functools.partial(last_kernel, q_steps, steps),
        name="last_step",
        grid=(steps,),
        in_specs=[
            smem(),
            pl.BlockSpec((tokens, tile), q_at),
            pl.BlockSpec((tokens, tile), kv_at),
            *w_columns(w_q, tile, lambda i: q_at(i)[1]),
            *w_columns(w_kv, tile, lambda i: kv_at(i)[1]),
            pl.BlockSpec((tokens, dim), lambda i: (micro, 0)),
            whole((1, dim)),
            whole((tokens, dim)),
        ],
        out_specs=[whole((tokens, dim)), whole((8, dim))],
        out_shape=[
            jax.ShapeDtypeStruct((tokens, dim), BF),
            jax.ShapeDtypeStruct((8, dim), F32),
        ],
        scratch_shapes=[pltpu.VMEM((tokens, dim), F32)],
        compiler_params=params(),
        cost_estimate=cost(
            2 * tokens * steps * tile * dim, 2 * steps * tile * dim + 12 * tokens * dim
        ),
    )(place, gq, dkv, *w_q, *w_kv, x, gain, gres)


def out_grad_kernel(micros, half, order_ref, *refs):
    t_refs, g_refs, (first_ref, second_ref) = refs[:micros], refs[micros : 2 * micros], refs[2 * micros :]
    step = pl.program_id(0)
    total = dot(t_refs[0][...], g_refs[0][...])
    for t_ref, g_ref in zip(t_refs[1:], g_refs[1:]):
        total += dot(t_ref[...], g_ref[...])

    @pl.when(step < half)
    def _():
        first_ref[...] = total.astype(BF)

    @pl.when(step >= half)
    def _():
        second_ref[...] = total.astype(BF)


def out_grad(order, heads_t, grads):
    micros, devices = len(heads_t), order.shape[0]
    width, tokens = heads_t[0].shape
    dim = grads[0].shape[1]
    tile, half = width // devices, devices // 2
    return pl.pallas_call(
        functools.partial(out_grad_kernel, micros, half),
        name="out_grad",
        grid_spec=pltpu.PrefetchScalarGridSpec(
            num_scalar_prefetch=1,
            grid=(devices,),
            in_specs=[pl.BlockSpec((tile, tokens), lambda i, order: (order[i], 0))] * micros
            + [whole((tokens, dim))] * micros,
            out_specs=[
                pl.BlockSpec((tile, dim), lambda i, order: (jnp.minimum(i, half - 1), 0)),
                pl.BlockSpec((tile, dim), lambda i, order: (jnp.maximum(i - half, 0), 0)),
            ],
        ),
        out_shape=[jax.ShapeDtypeStruct((width // 2, dim), BF)] * 2,
        compiler_params=params(),
        cost_estimate=cost(2 * micros * tokens * width * dim, 4 * width * dim),
    )(order, *heads_t, *grads)


def turn_kernel(kv_ref, cos_ref, sin_ref, out_ref):
    width = kv_ref.shape[2]
    key = rotate(kv_ref[0].astype(F32).T, cos_ref[...], sin_ref[...], -1)
    out_ref[:, :width] = key.T.astype(BF)
    out_ref[:, width:] = kv_ref[1]


def turn_back(kv, cosine, sine):
    _, tokens, width = kv.shape
    return pl.pallas_call(
        turn_kernel,
        name="turn_back",
        out_shape=jax.ShapeDtypeStruct((tokens, 2 * width), BF),
        compiler_params=params(),
        cost_estimate=cost(0, 8 * tokens * width),
    )(kv, cosine, sine)


def projection_kernel(micros, q_steps, steps, n_experts, normed_ref, *refs):
    gq_refs, refs = refs[:micros], refs[micros:]
    dkv_refs, refs = refs[:micros], refs[micros:]
    two_refs, refs = refs[:micros], refs[micros:]
    one_refs, (out_ref, turned_ref) = refs[:micros], refs[micros:]
    step = pl.program_id(0)
    tile = gq_refs[0].shape[1]

    @pl.when(step == 0)
    def _():
        turned_ref[...] = normed_ref[...].astype(F32).T.astype(BF)
        rows = functools.reduce(jnp.add, [r[:LANES] for r in two_refs])
        gain_two = functools.reduce(jnp.add, [r[LANES : LANES + 1] for r in two_refs])
        gain_one = functools.reduce(jnp.add, [r[:1] for r in one_refs])
        at = lax.broadcasted_iota(jnp.int32, rows.shape, 0)
        rows = jnp.where(at == n_experts, gain_one, rows)
        rows = jnp.where(at == n_experts + 1, gain_two, rows)
        out_ref[:, steps * tile :] = rows.T.astype(BF)

    q = jnp.concatenate([r[...] for r in gq_refs], axis=0)
    kv = jnp.concatenate([r[...] for r in dkv_refs], axis=0)
    g = jnp.where(step < q_steps, q, kv)
    out_ref[:, pl.ds(pl.multiple_of(step * tile, tile), tile)] = dot(turned_ref[...], g).astype(BF)


def projection_grads(normed, gqs, dkvs, twos, ones, n_experts):
    rows, dim = normed.shape
    micros, tokens, tile = len(gqs), gqs[0].shape[0], 512
    q_steps, kv_steps = gqs[0].shape[1] // tile, dkvs[0].shape[1] // tile
    steps = q_steps + kv_steps
    width = steps * tile + LANES
    return pl.pallas_call(
        functools.partial(projection_kernel, micros, q_steps, steps, n_experts),
        name="projection_grads",
        grid=(steps,),
        in_specs=[whole((rows, dim))]
        + [pl.BlockSpec((tokens, tile), lambda i: (0, jnp.minimum(i, q_steps - 1)))] * micros
        + [pl.BlockSpec((tokens, tile), lambda i: (0, jnp.maximum(i - q_steps, 0)))] * micros
        + [whole(twos[0].shape)] * micros
        + [whole(ones[0].shape)] * micros,
        out_specs=whole((dim, width)),
        out_shape=jax.ShapeDtypeStruct((dim, width), BF),
        scratch_shapes=[pltpu.VMEM((dim, rows), BF)],
        compiler_params=params(),
        cost_estimate=cost(2 * rows * dim * width, 2 * rows * (dim + width) + 2 * dim * width),
    )(normed, *gqs, *dkvs, *twos, *ones)


def add_low(a, b):
    return a + b


def line_sum(x, n):
    if n == 1:
        return x
    if n % 2:
        return lax.psum(x, "seq")
    half = n // 2
    at = lax.axis_index("seq")
    for k in range(half - 1):
        x = add_low(x, lax.ppermute(x, "seq", [(k, k + 1), (n - 1 - k, n - 2 - k)]))
    x = add_low(x, lax.ppermute(x, "seq", [(half - 1, half), (half, half - 1)]))
    for k in reversed(range(half - 1)):
        got = lax.ppermute(x, "seq", [(k + 1, k), (n - 2 - k, n - 1 - k)])
        x = jnp.where((at == k) | (at == n - 1 - k), got, x)
    return x


class Line:
    def __init__(self, n):
        self.n = n
        self.held = {}
        self.results = []

    def sums(self):
        at = lax.axis_index("seq")
        middle = (at == 1) | (at == 2)
        return [r[0] if len(r) == 1 else jnp.where(middle, *r) for r in self.results]

    def step(self, chunk, beside):
        n = self.n
        if n != 4:
            if chunk is not None:
                self.results.append((line_sum(chunk, n),))
            return
        at = lax.axis_index("seq")
        middle = (at == 1) | (at == 2)
        come, go = [(0, 1), (3, 2)], [(1, 0), (2, 3)]
        held, self.held = self.held, {}
        summed = held.get("summed")
        if summed is not None:
            summed = add_low(*summed)
        crossing = held.get("crossing")
        if crossing is not None:
            crossing = add_low(*crossing)
            self.held["summed"] = (crossing, lax.ppermute(crossing, "seq", [(1, 2), (2, 1)]))
        if chunk is not None and summed is not None and chunk.shape == summed.shape:
            sent = jnp.where(middle, summed, chunk)
            got = lax.ppermute(sent, "seq", come + go)
            self.results.append((sent, got))
            self.held["crossing"] = (chunk, got)
        else:
            if summed is not None:
                self.results.append((summed, lax.ppermute(summed, "seq", go)))
            if chunk is not None:
                self.held["crossing"] = (chunk, lax.ppermute(chunk, "seq", come))
        self.held, self.results = gate((self.held, self.results), beside)


def gate(x, *others):
    return lax.optimization_barrier((x, others))[0]


CORE, ALONG_X, ALONG_Y = 1, 2, 4


def swap(x, mask):
    return lax.ppermute(x, "fsdp", [(i, i ^ mask) for i in range(8)])


def gather_rows(x):
    return lax.all_gather(x, "fsdp", axis=0, tiled=True)


def assemble_kernel(x_ref, top_x_ref, low_y_ref, top_far_ref, low_far_ref, out_ref):
    rows = x_ref.shape[0]
    half = rows // 2
    out_ref[:rows] = x_ref[...]
    out_ref[rows : rows + half] = top_x_ref[...]
    out_ref[rows + half : 2 * rows] = low_far_ref[:half]
    out_ref[2 * rows : 2 * rows + half] = top_far_ref[:half]
    out_ref[2 * rows + half : 3 * rows] = low_y_ref[...]
    out_ref[3 * rows : 3 * rows + half] = top_far_ref[half:]
    out_ref[3 * rows + half :] = low_far_ref[half:]


def assemble(*pieces):
    rows, width = pieces[0].shape
    block = lambda n: pl.BlockSpec((n, width // 3), lambda i: (0, i))
    return pl.pallas_call(
        assemble_kernel,
        name="assemble",
        grid=(3,),
        in_specs=[block(p.shape[0]) for p in pieces],
        out_specs=block(4 * rows),
        out_shape=jax.ShapeDtypeStruct((4 * rows, width), pieces[0].dtype),
        compiler_params=params(),
        cost_estimate=cost(0, 16 * rows * width),
    )(*pieces)


def gather_near(x, n):
    if n != 8:
        every = gather_rows(x)
        half = every.shape[0] // 2
        return every[:half], every[half:]
    gather = Gather(x, n)
    gather.further()
    return gather.finish()


class Gather:
    def __init__(self, x, n):
        self.n, self.x = n, x
        if n != 8:
            self.halves = gather_near(x, n)
            self.near = self.far = ()
            return
        half = x.shape[0] // 2
        self.near = swap(x[:half], ALONG_X), swap(x[half:], ALONG_Y)

    def further(self, *others):
        if self.n != 8:
            return
        half = self.x.shape[0] // 2
        x, (top_x, low_y) = gate((self.x, self.near), *others)
        self.near = top_x, low_y
        top_far = swap(jnp.concatenate([x[:half], top_x]), ALONG_Y)
        low_far = swap(jnp.concatenate([x[half:], low_y]), ALONG_X)
        self.far = top_far, low_far

    def finish(self, *others):
        if self.n != 8:
            return self.halves
        near, far = gate((self.near, self.far), *others)
        mine = assemble(self.x, *near, *far)
        return mine, swap(mine, CORE)


class Scatter:
    def __init__(self, arrays, n):
        self.arrays, self.n, self.stage = list(arrays), n, 0
        self.rows = 2 * arrays[0][0].shape[0] // n

    def advance(self):
        held, self.stage = self.arrays, self.stage + 1
        rows, half = self.rows, self.rows // 2
        if self.n != 8:
            if self.stage == 1:
                self.arrays = [scatter_rows(jnp.concatenate(a)) for a in held]
            return
        if self.stage == 1:
            self.arrays = [add_low(mine, swap(other, CORE)) for mine, other in held]
        if self.stage == 2:
            tops = [a[k * rows : k * rows + half] for a in held for k in (2, 3)]
            lows = [a[k * rows + half : (k + 1) * rows] for a in held for k in (1, 3)]
            tops = swap(jnp.concatenate(tops), ALONG_Y)
            lows = swap(jnp.concatenate(lows), ALONG_X)
            self.arrays = []
            for i, a in enumerate(held):
                at = 2 * i * half
                self.arrays.append(
                    (
                        add_low(a[:half], tops[at : at + half]),
                        add_low(a[half:rows], lows[at : at + half]),
                        add_low(a[rows : rows + half], tops[at + half : at + rows]),
                        add_low(a[2 * rows + half : 3 * rows], lows[at + half : at + rows]),
                    )
                )
        if self.stage == 3:
            over_x = swap(jnp.concatenate([a[2] for a in held]), ALONG_X)
            over_y = swap(jnp.concatenate([a[3] for a in held]), ALONG_Y)
            self.arrays = [
                jnp.concatenate(
                    [
                        add_low(a[0], over_x[i * half : (i + 1) * half]),
                        add_low(a[1], over_y[i * half : (i + 1) * half]),
                    ]
                )
                for i, a in enumerate(held)
            ]


def block_order(n):
    at = jnp.arange(n, dtype=jnp.int32)
    if n != 8:
        return at
    return lax.axis_index("fsdp").astype(jnp.int32) ^ (2 * lax.rem(at, 4) + at // 4)


def block_places(n):
    if n != 8:
        return jnp.arange(n, dtype=jnp.int32)
    mask = lax.axis_index("fsdp").astype(jnp.int32) ^ jnp.arange(n, dtype=jnp.int32)
    return (mask >> 1) + 4 * (mask & 1)


def scatter_rows(x):
    return lax.psum_scatter(x, "fsdp", scatter_dimension=0, tiled=True)


def on_device(
    n_seq,
    n_fsdp,
    inputs,
    lengths,
    expert_ids,
    cotangent,
    gain_attn,
    w_query,
    key_projection,
    value_projection,
    w_out,
    gain_moe,
    router,
    w_gate,
    w_up,
    w_down,
):
    micros, local_seqs, tokens, dim = inputs.shape
    assert local_seqs == 1
    rows = micros * tokens
    experts, _, hidden = w_gate.shape
    n_experts = router.shape[1]
    kv_width = key_projection.shape[1]
    at = lax.axis_index("seq")
    own = (lax.axis_index("fsdp") * experts).astype(jnp.int32).reshape(1)

    small = jnp.concatenate(
        [router, gain_attn[:, None], gain_moe[:, None]], axis=1
    )
    small = jnp.pad(small, ((0, 0), (0, LANES - small.shape[1])))
    place, order = block_places(n_fsdp), block_order(n_fsdp)

    def weights(w):
        return [h.reshape(n_fsdp // 2, -1, h.shape[1]) for h in gather_near(w, n_fsdp)]

    w_kv = weights(jnp.concatenate([key_projection, value_projection, small], axis=1))
    router_all, rows_all = unpack(place, w_kv, 2 * kv_width // LANES, n_experts)
    gain_one = rows_all[n_experts : n_experts + 1]
    gain_two = rows_all[n_experts + 1 : n_experts + 2]

    positions = at * tokens + jnp.arange(tokens, dtype=jnp.int32)
    frequency = THETA ** (-(jnp.arange(HALF, dtype=F32) * 2.0) / HEAD)
    angles = frequency[:, None] * positions.astype(F32)[None, :]
    cosine, sine = jnp.cos(angles), jnp.sin(angles)
    cosine_all, sine_all = jnp.tile(cosine, (1, micros)), jnp.tile(sine, (1, micros))

    x = inputs.reshape(rows, dim)
    chosen = jnp.sum(
        (
            expert_ids.reshape(rows, TOPK)[:, :, None]
            == jnp.arange(LANES, dtype=jnp.int32)[None, None, :]
        ).astype(F32),
        axis=1,
    )
    valid = positions[None, :] < lengths[:, :1]
    gout = jnp.where(valid[:, :, None], cotangent.reshape(micros, tokens, dim), BF(0))
    infos = [
        jnp.stack([at.astype(jnp.int32), lengths[m, 0].astype(jnp.int32)]) for m in range(micros)
    ]

    kv, normed_one = kv_project(place, x, gain_one, w_kv, kv_width, cosine_all, sine_all)
    q_width = w_query.shape[1]
    w_gather = Gather(gate(jnp.concatenate([w_query, w_out], axis=1), kv), n_fsdp)
    w_gather.further()
    kvs = []
    for m in range(micros):
        mine = kv[m * tokens : (m + 1) * tokens]
        every = lax.all_gather(mine, "seq", axis=0, tiled=True)
        kvs.append(every.reshape(n_seq, tokens, 2 * kv_width))
    w_qo = [h.reshape(n_fsdp // 2, -1, h.shape[1]) for h in w_gather.finish(kvs[0], chosen, infos)]
    g_gathers = [Gather(gate(gout[0], w_gather.far), n_fsdp)]
    for m in range(1, micros):
        g_gathers.append(Gather(gate(gout[m], g_gathers[-1].near), n_fsdp))
    q_t = q_project(
        place, gate(normed_one, kvs[0]), w_qo, q_width, cosine_all, sine_all
    )

    state, xg_all = [], []
    for m in range(micros):
        if m == 0:
            info = gate(infos[m], g_gathers[0].near)
            g_gathers[0].further(q_t)
        else:
            info = gate(infos[m], state[-1][2])
        attn, attn_t, lse = attend(info, q_t, kvs[m], m, tokens)
        if m == 0:
            attn = gate(attn, g_gathers[0].far, [g.near for g in g_gathers[1:]])
            for g in g_gathers[1:]:
                g.further(g_gathers[0].far)
        else:
            attn = gate(attn, g_gathers[m].far)
        residual, xg, exact = after_attention(
            place, attn, w_qo, q_width, x, m, gain_two, router_all, chosen
        )
        state.append((attn_t, lse, residual, exact))
        xg_all.append(gather_rows(xg))

    g_all = [g.finish(state[-1][2]) for g in g_gathers]
    xg_all[0] = gate(xg_all[0], state[-1][2], g_all)
    passed, backs = [], []
    for m in range(micros):
        *y, back, hg, gp = run_experts(
            own, order, xg_all[m], g_all[m], w_gate, w_up, w_down
        )
        passed.append((xg_all[m], hg, gp))
        backs.append((scatter_rows(back), y))

    names = [(name, e) for name in ("down", "gate", "up") for e in range(experts)]

    def expert_grad(name, e, got):
        xs, hgs, gps = ([p[i] for p in got] for i in range(3))
        if name == "down":
            return down_grad(hgs, e, hidden, g_all, n_fsdp)
        return wide_grad(xs, 0, dim, gps, 2 * e + (name == "up"), hidden)

    line = Line(n_seq)
    found = [{} for _ in range(micros)]

    def to_heads(m):
        attn_t, lse, residual, exact = state[m]
        gres, g_attn, g_t, small_two = before_attention(
            place, backs[m][0], residual, exact, gout[m], gain_two, router_all, w_qo, q_width
        )
        found[m].update(gres=gres, g_attn=g_attn, g_t=g_t, small_two=small_two)

    def through_heads(m):
        attn_t, lse = state[m][:2]
        gq, by_owner = attend_back(
            infos[m], q_t, found[m]["g_t"], attn_t, lse, cosine, sine, kvs[m], m, tokens
        )
        found[m].update(gq=gq, by_owner=by_owner)

    owned = {}

    def to_owners(m):
        by_owner = found[m].pop("by_owner")
        shape = by_owner.shape
        owned[m] = lax.psum_scatter(
            by_owner.reshape(n_seq * shape[1] * tokens, shape[3]),
            "seq",
            scatter_dimension=0,
            tiled=True,
        ).reshape(shape[1:])

    def finish(m):
        f = found[m]
        f["dkv"] = turn_back(f["mine"], cosine, sine)
        f["din"], f["small_one"] = last_step(
            place, f["gq"], f["dkv"], w_qo, w_kv, x, m, gain_one, f["gres"]
        )

    def rest_grads():
        every = lambda name: [f[name] for f in found]
        return projection_grads(
            normed_one, every("gq"), every("dkv"), every("small_two"), every("small_one"), n_experts
        )

    n_grads = len(names)
    work = {
        0: [("grad", 1), (to_heads, 0)],
        1: [("grad", 2), (through_heads, 0)],
        2: [("grad", 3), (to_heads, 1), (through_heads, 1)],
        3: [("grad", 4), (finish, 0), ("grad", 5)],
        4: [(finish, 1)],
    }
    def widen(parts, turned):
        return jnp.stack([(p.T if turned else p).astype(F32) for p in parts])

    experts_out = []
    chunks = {0: expert_grad(*names[0], passed)}
    chunks.update({i: expert_grad(*names[i], passed) for i in range(6, n_grads)})
    slots = max(n_grads, 6)
    moe = Scatter([b[1] for b in backs], n_fsdp)
    for t in range(slots + 3):
        if t in (3, 4):
            found[t - 3]["mine"] = owned[t - 3]
        if t == 3:
            heads = Scatter([found[0].pop("out")], n_fsdp)
        if t == 7:
            found[0]["rest"] = rest
        held = (chunks, line.held, line.results, passed, found, moe.arrays)
        if t >= 3:
            *held, heads.arrays = lax.optimization_barrier((*held, heads.arrays))
        else:
            held = lax.optimization_barrier(held)
        chunks, line.held, line.results, passed, found, moe.arrays = held
        if t == 7:
            rest = lax.psum(found[0].pop("rest"), "seq")
        if len(line.results) in (experts, 2 * experts, 3 * experts) and len(experts_out) < 3:
            pair = line.sums()[-experts:]
            experts_out.append(widen(pair, len(experts_out) == 0))
            found[1]["wide"] = experts_out[-1]
        if t == slots:
            chunks[slots] = heads.arrays[0]
        sent = chunks.pop(t, None)
        if t in (2, 3):
            to_owners(t - 2)
        for kind, i in work.get(t, []):
            if kind != "grad":
                kind(i)
            elif i < n_grads:
                chunks[i] = expert_grad(*names[i], passed)
        if t == 2:
            found[0]["out"] = out_grad(
                order, [st[0] for st in state], [f["g_attn"] for f in found]
            )
        if t in (5, 6, 7):
            moe.advance()
        for _ in range(3 if t == 3 else 0):
            heads.advance()
        line.step(sent, (chunks, found))
        if t == 4:
            normed_one, line.held = lax.optimization_barrier((normed_one, line.held))
            rest = scatter_rows(rest_grads())
    rest = rest.astype(F32)
    totals = line.sums()
    for i in range(len(experts_out), 3):
        experts_out.append(widen(totals[i * experts : (i + 1) * experts], i == 0))
    d_out = totals[n_grads].astype(F32)

    outs = []
    for m in range(micros):
        outs.append(
            jnp.where(valid[m][:, None], state[m][2] + moe.arrays[m].astype(F32), 0.0).astype(BF)
        )
    grads = [f["din"] for f in found]
    assert len(totals) == n_grads + 1
    shape = (micros, 1, tokens, dim)
    ends = q_width + 2 * kv_width
    return (
        jnp.stack(outs).reshape(shape),
        jnp.stack(grads).reshape(shape),
        rest[:, ends + n_experts],
        rest[:, :q_width],
        rest[:, q_width : q_width + kv_width],
        rest[:, q_width + kv_width : ends],
        d_out,
        rest[:, ends + n_experts + 1],
        rest[:, ends : ends + n_experts],
        *experts_out[1:],
        experts_out[0],
    )


def solution(mesh):
    token_spec = P(None, "fsdp", "seq", None)
    row, matrix, cube = P("fsdp"), P("fsdp", None), P("fsdp", None, None)
    return jax.shard_map(
        functools.partial(on_device, mesh.shape["seq"], mesh.shape["fsdp"]),
        mesh=mesh,
        in_specs=(
            token_spec,
            P(None, "fsdp"),
            token_spec,
            token_spec,
            row,
            matrix,
            matrix,
            matrix,
            matrix,
            row,
            matrix,
            cube,
            cube,
            cube,
        ),
        out_specs=(
            token_spec,
            token_spec,
            row,
            matrix,
            matrix,
            matrix,
            matrix,
            row,
            matrix,
            cube,
            cube,
            cube,
        ),
        check_vma=False,
    )
```

```python
import functools

import jax
import jax.numpy as jnp
from jax import lax
from jax.experimental import pallas as pl
from jax.experimental.pallas import tpu as pltpu
from jax.sharding import PartitionSpec as P

HEAD = 64
HALF = HEAD // 2
GROUP = 3
TOPK = 8
EPS = 1e-06
THETA = 10000.0
NEGATIVE = -1e30
LANES = 128
SCALE = HEAD ** (-0.5)
BF = jnp.bfloat16
F32 = jnp.float32
VMEM_BYTES = 60 * 1024 * 1024

NN = (((1,), (0,)), ((), ()))
NT = (((1,), (1,)), ((), ()))
TN = (((0,), (0,)), ((), ()))


def dot(a, b, dims=NN):
    return lax.dot_general(a, b, dims, preferred_element_type=F32)


def params():
    return pltpu.CompilerParams(vmem_limit_bytes=VMEM_BYTES)


def cost(flops, moved, trans=0):
    parts = (int(v) // 10 for v in (flops, moved, trans))
    flops, moved, trans = parts
    return pl.CostEstimate(flops=flops, bytes_accessed=moved, transcendentals=trans)


def whole(shape):
    zeros = (0,) * len(shape)
    return pl.BlockSpec(shape, lambda *_: zeros)


def smem():
    return pl.BlockSpec(memory_space=pltpu.SMEM)


def pick(at, first_ref, second_ref, index=None):
    half = first_ref.shape[0]
    if index is None:
        index = lax.rem(at, half)
    return jnp.where(at < half, first_ref[index], second_ref[index])


def in_order(place_ref, w_refs):
    devices = 2 * w_refs[0].shape[0]
    return jnp.concatenate([pick(place_ref[j], *w_refs) for j in range(devices)], axis=0)


def rotate(rows, cosine, sine, sign):
    pieces = []
    for h in range(rows.shape[0] // HEAD):
        a = rows[h * HEAD : h * HEAD + HALF]
        b = rows[h * HEAD + HALF : (h + 1) * HEAD]
        if sign > 0:
            pieces += [a * cosine - b * sine, b * cosine + a * sine]
        else:
            pieces += [a * cosine + b * sine, b * cosine - a * sine]
    return jnp.concatenate(pieces, axis=0)


def unpack_kernel(n_experts, place_ref, wa_ref, wb_ref, router_ref, rows_ref):
    w = in_order(place_ref, (wa_ref, wb_ref))
    lane = lax.broadcasted_iota(jnp.int32, w.shape, 1)
    router_ref[...] = jnp.where(lane < n_experts, w.astype(F32), 0.0).astype(BF)
    rows_ref[...] = w.astype(F32).T


def unpack(place, w, block, n_experts):
    dim = 2 * w[0].shape[0] * w[0].shape[1]
    return pl.pallas_call(
        functools.partial(unpack_kernel, n_experts),
        name="unpack",
        grid=(1,),
        in_specs=[smem(), *w_columns(w, LANES, lambda i: block)],
        out_specs=[whole((dim, LANES)), whole((LANES, dim))],
        out_shape=[
            jax.ShapeDtypeStruct((dim, LANES), BF),
            jax.ShapeDtypeStruct((LANES, dim), F32),
        ],
        compiler_params=params(),
        cost_estimate=cost(0, 12 * dim * LANES),
    )(place, *w)


def kv_kernel(place_ref, x_ref, gain_ref, wa_ref, wb_ref, cos_ref, sin_ref, kv_ref, normed_ref):
    step = pl.program_id(0)

    @pl.when(step == 0)
    def _():
        x = x_ref[...].astype(F32)
        inv = lax.rsqrt(jnp.mean(x * x, axis=-1, keepdims=True) + EPS)
        normed_ref[...] = (x * inv * gain_ref[...]).astype(BF)
        r = dot(normed_ref[...], in_order(place_ref, (wa_ref, wb_ref)))
        r = rotate(r.T, cos_ref[...], sin_ref[...], 1)
        kv_ref[...] = r.T.astype(BF)

    @pl.when(step == 1)
    def _():
        kv_ref[...] = dot(normed_ref[...], in_order(place_ref, (wa_ref, wb_ref))).astype(BF)


def w_columns(w, tile, at):
    return [pl.BlockSpec((*half.shape[:2], tile), lambda *i: (0, 0, at(*i))) for half in w]


def kv_project(place, x, gain, w, width, cosine, sine):
    rows, dim = x.shape
    return pl.pallas_call(
        kv_kernel,
        name="kv_project",
        grid=(2,),
        in_specs=[
            smem(),
            whole((rows, dim)),
            whole((1, dim)),
            *w_columns(w, width, lambda i: i),
            whole((HALF, rows)),
            whole((HALF, rows)),
        ],
        out_specs=[pl.BlockSpec((rows, width), lambda i: (0, i)), whole((rows, dim))],
        out_shape=[
            jax.ShapeDtypeStruct((rows, 2 * width), BF),
            jax.ShapeDtypeStruct((rows, dim), BF),
        ],
        compiler_params=params(),
        cost_estimate=cost(2 * rows * dim * 2 * width, 2 * (2 * rows * dim + dim * 2 * width)),
    )(place, x, gain, *w, cosine, sine)


def q_kernel(place_ref, normed_ref, wa_ref, wb_ref, cos_ref, sin_ref, q_ref):
    r = dot(normed_ref[...], in_order(place_ref, (wa_ref, wb_ref)))
    r = rotate(r.T, cos_ref[...], sin_ref[...], 1)
    q_ref[...] = r.astype(BF) * BF(SCALE)


def q_project(place, normed, w, width, cosine, sine):
    rows, dim = normed.shape
    tile = 512
    return pl.pallas_call(
        q_kernel,
        name="q_project",
        grid=(width // tile,),
        in_specs=[
            smem(),
            whole((rows, dim)),
            *w_columns(w, tile, lambda i: i),
            whole((HALF, rows)),
            whole((HALF, rows)),
        ],
        out_specs=pl.BlockSpec((tile, rows), lambda i: (i, 0)),
        out_shape=jax.ShapeDtypeStruct((width, rows), BF),
        compiler_params=params(),
        cost_estimate=cost(2 * rows * dim * width, 2 * (2 * rows * dim + dim * width)),
    )(place, normed, *w, cosine, sine)


def side_by_side(ref, j):
    base = j * GROUP * HEAD
    return jnp.concatenate(
        [ref[base + h * HEAD : base + (h + 1) * HEAD, :] for h in range(GROUP)], axis=1
    )


def diagonal_mask(tokens, own_len):
    key = lax.broadcasted_iota(jnp.int32, (tokens, tokens), 0)
    query = lax.broadcasted_iota(jnp.int32, (tokens, tokens), 1)
    one = (key <= query) & (key < own_len)
    return jnp.concatenate([one.astype(jnp.int32)] * GROUP, axis=1) > 0


def attend_kernel(n, info_ref, q_ref, k_ref, v_ref, o_ref, ot_ref, lse_ref, m_ref, l_ref, acc_ref):
    tokens = q_ref.shape[1]
    d = pl.program_id(1)
    s = info_ref[0]
    own_len = info_ref[1] - s * tokens
    active = own_len > 0

    def pair(j):
        cols = slice(j * HEAD, (j + 1) * HEAD)
        scores = dot(k_ref[0, :, cols], side_by_side(q_ref, j))
        return scores, v_ref[0, :, cols].astype(F32).T.astype(BF)

    @pl.when(active & (d == 0))
    def _():
        mask = diagonal_mask(tokens, own_len)
        for j in range(2):
            scores, value_t = pair(j)
            scores = jnp.where(mask, scores, NEGATIVE)
            top = jnp.max(scores, axis=0, keepdims=True)
            p = jnp.exp(scores - top)
            l_ref[j : j + 1] = jnp.sum(p, axis=0, keepdims=True)
            acc_ref[j] = dot(value_t, p.astype(BF))
            m_ref[j : j + 1] = top

    @pl.when(active & (d > 0) & (d <= s))
    def _():
        for j in range(2):
            scores, value_t = pair(j)
            old = m_ref[j : j + 1]
            top = jnp.maximum(old, jnp.max(scores, axis=0, keepdims=True))
            keep = jnp.exp(old - top)
            p = jnp.exp(scores - top)
            l_ref[j : j + 1] = l_ref[j : j + 1] * keep + jnp.sum(p, axis=0, keepdims=True)
            acc_ref[j] = acc_ref[j] * keep + dot(value_t, p.astype(BF))
            m_ref[j : j + 1] = top

    @pl.when(active & (d == n - 1))
    def _():
        pieces = []
        for j in range(2):
            out = acc_ref[j] / l_ref[j : j + 1]
            lse_ref[j : j + 1] = m_ref[j : j + 1] + jnp.log(l_ref[j : j + 1])
            pieces += [out[:, h * tokens : (h + 1) * tokens] for h in range(GROUP)]
        out = jnp.concatenate(pieces, axis=0)
        ot_ref[...] = out.astype(BF)
        o_ref[...] = out.T.astype(BF)

    @pl.when(jnp.logical_not(active) & (d == 0))
    def _():
        o_ref[...] = jnp.zeros_like(o_ref)
        ot_ref[...] = jnp.zeros_like(ot_ref)
        lse_ref[...] = jnp.zeros_like(lse_ref)


def owner(info_ref, d, n):
    return lax.rem(info_ref[0] + n - d, n)


def attend(info, q_t, kv, micro, tokens):
    n = kv.shape[0]
    width = q_t.shape[0]
    kv_width = kv.shape[2] // 2
    steps = kv_width // LANES
    qw = width // steps
    return pl.pallas_call(
        functools.partial(attend_kernel, n),
        name="attend",
        grid_spec=pltpu.PrefetchScalarGridSpec(
            num_scalar_prefetch=1,
            grid=(steps, n),
            in_specs=[
                pl.BlockSpec((qw, tokens), lambda i, d, info: (i, micro)),
                pl.BlockSpec((1, tokens, LANES), lambda i, d, info: (owner(info, d, n), 0, i)),
                pl.BlockSpec(
                    (1, tokens, LANES), lambda i, d, info: (owner(info, d, n), 0, steps + i)
                ),
            ],
            out_specs=[
                pl.BlockSpec((tokens, qw), lambda i, d, info: (0, i)),
                pl.BlockSpec((qw, tokens), lambda i, d, info: (i, 0)),
                pl.BlockSpec((8, GROUP * tokens), lambda i, d, info: (i, 0)),
            ],
            scratch_shapes=[
                pltpu.VMEM((8, GROUP * tokens), F32),
                pltpu.VMEM((8, GROUP * tokens), F32),
                pltpu.VMEM((2, HEAD, GROUP * tokens), F32),
            ],
        ),
        out_shape=[
            jax.ShapeDtypeStruct((tokens, width), BF),
            jax.ShapeDtypeStruct((width, tokens), BF),
            jax.ShapeDtypeStruct((8 * steps, GROUP * tokens), F32),
        ],
        compiler_params=params(),
        cost_estimate=cost(
            4 * 4 * width * tokens * tokens * n,
            2 * (3 * width * tokens + n * tokens * 2 * kv_width),
            width // HEAD * tokens * tokens * n,
        ),
    )(info, q_t, kv, kv)


def attend_back_kernel(
    n, info_ref, q_ref, g_ref, o_ref, lse_ref, cos_ref, sin_ref, k_ref, v_ref, gq_ref, dkv_ref, acc_ref
):
    tokens = q_ref.shape[1]
    d = pl.program_id(1)
    s = info_ref[0]
    own_len = info_ref[1] - s * tokens
    active = own_len > 0

    def block(first):
        mask = diagonal_mask(tokens, own_len) if first else None
        dks, dvs = [], []
        for j in range(2):
            cols = slice(j * HEAD, (j + 1) * HEAD)
            key, value = k_ref[0, :, cols], v_ref[0, :, cols]
            query, grad = side_by_side(q_ref, j), side_by_side(g_ref, j)
            out = side_by_side(o_ref, j)
            inner = jnp.sum(grad.astype(F32) * out.astype(F32), axis=0, keepdims=True)
            p = jnp.exp(dot(key, query) - lse_ref[j : j + 1])
            if first:
                p = jnp.where(mask, p, 0.0)
            dp = dot(value, grad)
            ds = (p * (dp - inner)).astype(BF)
            dvs.append(dot(p.astype(BF), grad, NT))
            dks.append(dot(ds, query, NT))
            part = dot(key.astype(F32).T.astype(BF), ds)
            if first:
                acc_ref[j] = part
            else:
                acc_ref[j] += part
        dkv_ref[0, 0] = jnp.concatenate(dks, axis=1).astype(BF)
        dkv_ref[0, 1] = jnp.concatenate(dvs, axis=1).astype(BF)

    pl.when(active & (d == 0))(lambda: block(True))
    pl.when(active & (d > 0) & (d <= s))(lambda: block(False))

    @pl.when(active & (d == n - 1))
    def _():
        pieces = []
        for j in range(2):
            for h in range(GROUP):
                piece = acc_ref[j, :, h * tokens : (h + 1) * tokens] * SCALE
                pieces.append(piece.astype(BF).astype(F32))
        grad_q = rotate(jnp.concatenate(pieces, axis=0), cos_ref[...], sin_ref[...], -1)
        gq_ref[...] = grad_q.T.astype(BF)

    @pl.when(jnp.logical_not(active) | (d > s))
    def _():
        dkv_ref[...] = jnp.zeros_like(dkv_ref)

    @pl.when(jnp.logical_not(active) & (d == 0))
    def _():
        gq_ref[...] = jnp.zeros_like(gq_ref)


def attend_back(info, q_t, g_t, o_t, lse, cosine, sine, kv, micro, tokens):
    n = kv.shape[0]
    width = q_t.shape[0]
    kv_width = kv.shape[2] // 2
    steps = kv_width // LANES
    qw = width // steps
    transposed = pl.BlockSpec((qw, tokens), lambda i, d, info: (i, 0))
    return pl.pallas_call(
        functools.partial(attend_back_kernel, n),
        name="attend_back",
        grid_spec=pltpu.PrefetchScalarGridSpec(
            num_scalar_prefetch=1,
            grid=(steps, n),
            in_specs=[
            pl.BlockSpec((qw, tokens), lambda i, d, info: (i, micro)),
            transposed,
            transposed,
            pl.BlockSpec((8, GROUP * tokens), lambda i, d, info: (i, 0)),
            whole((HALF, tokens)),
            whole((HALF, tokens)),
            pl.BlockSpec((1, tokens, LANES), lambda i, d, info: (owner(info, d, n), 0, i)),
            pl.BlockSpec(
                (1, tokens, LANES), lambda i, d, info: (owner(info, d, n), 0, steps + i)
            ),
        ],
        out_specs=[
            pl.BlockSpec((tokens, qw), lambda i, d, info: (0, i)),
            pl.BlockSpec(
                (1, 2, tokens, LANES), lambda i, d, info: (owner(info, d, n), 0, 0, i)
            ),
        ],
            scratch_shapes=[pltpu.VMEM((2, HEAD, GROUP * tokens), F32)],
        ),
        out_shape=[
            jax.ShapeDtypeStruct((tokens, width), BF),
            jax.ShapeDtypeStruct((n, 2, tokens, kv_width), BF),
        ],
        compiler_params=params(),
        cost_estimate=cost(
            10 * 4 * width * tokens * tokens * n,
            2 * (4 * width * tokens + 2 * n * tokens * 2 * kv_width),
            width // HEAD * tokens * tokens * n,
        ),
    )(info, q_t, g_t, o_t, lse, cosine, sine, kv, kv)


def after_kernel(
    steps, place_ref, a_ref, wa_ref, wb_ref, x_ref, gain_ref, router_ref, chosen_ref, res_ref, xg_ref, ge_ref, acc_ref
):
    step = pl.program_id(0)
    acc_ref[step] = dot(a_ref[...], in_order(place_ref, (wa_ref, wb_ref)))

    @pl.when(step == steps - 1)
    def _():
        dim = x_ref.shape[1]
        product = jnp.concatenate([acc_ref[i] for i in range(steps)], axis=1)
        residual = x_ref[...].astype(F32) + product
        res_ref[...] = residual
        inv = lax.rsqrt(jnp.mean(residual * residual, axis=-1, keepdims=True) + EPS)
        normed = (residual * inv * gain_ref[...]).astype(BF)
        logits = dot(normed, router_ref[...])
        chosen = chosen_ref[...] > 0
        logits = jnp.where(chosen, logits, NEGATIVE)
        top = jnp.max(logits, axis=-1, keepdims=True)
        e = jnp.where(chosen, jnp.exp(logits - top), 0.0)
        exact = e / jnp.sum(e, axis=-1, keepdims=True)
        ge_ref[...] = exact
        xg_ref[:, :dim] = normed
        xg_ref[:, dim:] = exact.astype(BF)


def after_attention(place, attn, w, first, x, micro, gain, router, chosen):
    tokens, width = attn.shape
    dim = x.shape[1]
    tile = 512
    steps = dim // tile
    return pl.pallas_call(
        functools.partial(after_kernel, steps),
        name="after_attention",
        grid=(steps,),
        in_specs=[
            smem(),
            whole((tokens, width)),
            *w_columns(w, tile, lambda i: first // tile + i),
            pl.BlockSpec((tokens, dim), lambda i: (micro, 0)),
            whole((1, dim)),
            whole((dim, LANES)),
            pl.BlockSpec((tokens, LANES), lambda i: (micro, 0)),
        ],
        out_specs=[
            whole((tokens, dim)),
            whole((tokens, dim + LANES)),
            whole((tokens, LANES)),
        ],
        out_shape=[
            jax.ShapeDtypeStruct((tokens, dim), F32),
            jax.ShapeDtypeStruct((tokens, dim + LANES), BF),
            jax.ShapeDtypeStruct((tokens, LANES), F32),
        ],
        scratch_shapes=[pltpu.VMEM((steps, tokens, tile), F32)],
        compiler_params=params(),
        cost_estimate=cost(2 * tokens * width * dim, 2 * width * dim + 10 * tokens * dim),
    )(place, attn, *w, x, gain, router, chosen)


def expert_kernel(
    experts, half, own_ref, order_ref, xg_ref, ga_ref, gb_ref, wg_ref, wu_ref, wd_ref, ya_ref, yb_ref, back_ref, hg_ref, gp_ref
):
    rows, dim = ga_ref.shape
    hidden = wg_ref.shape[2]
    x = xg_ref[:, :dim]
    step = pl.program_id(0)
    g = jnp.where(step < half, ga_ref[...], gb_ref[...])
    gates = xg_ref[:, dim:].astype(F32)
    lane = lax.broadcasted_iota(jnp.int32, (rows, LANES), 1)
    gate_cols = jnp.zeros((rows, LANES), F32)
    for e in range(experts):
        mine = lane == own_ref[0] + e
        gate = jnp.sum(jnp.where(mine, gates, 0.0), axis=1, keepdims=True)
        pre_gate = dot(x, wg_ref[e])
        pre_up = dot(x, wu_ref[e])
        grad_hidden = dot(g, wd_ref[e], NT)
        sig = 1.0 / (1.0 + jnp.exp(-pre_gate))
        silu = pre_gate * sig
        h = (silu * pre_up).astype(BF).astype(F32)
        per_gate = jnp.sum(h * grad_hidden, axis=1, keepdims=True)
        gate_cols = jnp.where(mine, per_gate, gate_cols)
        hg_ref[:, e * hidden : (e + 1) * hidden] = (gate * h).astype(BF)
        gh = gate * grad_hidden
        base = 2 * e * hidden
        gp_ref[:, base : base + hidden] = (
            gh * pre_up * (sig * (1.0 + pre_gate * (1.0 - sig)))
        ).astype(BF)
        gp_ref[:, base + hidden : base + 2 * hidden] = (gh * silu).astype(BF)
    y = dot(hg_ref[:, :hidden], wd_ref[0])
    for e in range(1, experts):
        y += dot(hg_ref[:, e * hidden : (e + 1) * hidden], wd_ref[e])

    @pl.when(step < half)
    def _():
        ya_ref[...] = y.astype(BF)

    @pl.when(step >= half)
    def _():
        yb_ref[...] = y.astype(BF)

    back = None
    for e in range(experts):
        base = 2 * e * hidden
        part = dot(gp_ref[:, base : base + hidden], wg_ref[e], NT)
        part += dot(gp_ref[:, base + hidden : base + 2 * hidden], wu_ref[e], NT)
        back = part if back is None else back + part
    back_ref[:, :dim] = back.astype(BF)
    back_ref[:, dim:] = gate_cols.astype(BF)


def run_experts(own, order, xg, g, w_gate, w_up, w_down):
    rows = xg.shape[0]
    dim = g[0].shape[1]
    experts, _, hidden = w_gate.shape
    devices = order.shape[0]
    tile, half = rows // devices, devices // 2
    named = lambda width: pl.BlockSpec((tile, width), lambda i, own, order: (order[i], 0))
    first = lambda i: jnp.minimum(i, half - 1)
    second = lambda i: jnp.maximum(i - half, 0)
    return pl.pallas_call(
        functools.partial(expert_kernel, experts, half),
        name="run_experts",
        grid_spec=pltpu.PrefetchScalarGridSpec(
            num_scalar_prefetch=2,
            grid=(devices,),
            in_specs=[
                named(dim + LANES),
                pl.BlockSpec((tile, dim), lambda i, *_: (first(i), 0)),
                pl.BlockSpec((tile, dim), lambda i, *_: (second(i), 0)),
                whole(w_gate.shape),
                whole(w_up.shape),
                whole(w_down.shape),
            ],
            out_specs=[
                pl.BlockSpec((tile, dim), lambda i, *_: (first(i), 0)),
                pl.BlockSpec((tile, dim), lambda i, *_: (second(i), 0)),
                named(dim + LANES),
                pl.BlockSpec((tile, experts * hidden), lambda i, *_: (i, 0)),
                named(2 * experts * hidden),
            ],
        ),
        out_shape=[
            jax.ShapeDtypeStruct((rows // 2, dim), BF),
            jax.ShapeDtypeStruct((rows // 2, dim), BF),
            jax.ShapeDtypeStruct((rows, dim + LANES), BF),
            jax.ShapeDtypeStruct((rows, experts * hidden), BF),
            jax.ShapeDtypeStruct((rows, 2 * experts * hidden), BF),
        ],
        compiler_params=params(),
        cost_estimate=cost(
            12 * rows * dim * hidden * experts,
            2 * (4 * rows * dim + 3 * rows * experts * hidden + 3 * experts * dim * hidden),
            rows * experts * hidden,
        ),
    )(own, order, xg, *g, w_gate, w_up, w_down)


def wide_grad_kernel(steps, micros, *refs):
    a_refs, b_refs = refs[:micros], refs[micros : 2 * micros]
    out_ref, acc_ref = refs[2 * micros :]
    step = pl.program_id(0)
    for m in range(micros):

        @pl.when((step >= m * steps) & (step < (m + 1) * steps))
        def _(m=m):
            part = dot(a_refs[m][...], b_refs[m][...], TN)
            if m == 0:

                @pl.when(step == 0)
                def _():
                    acc_ref[...] = part

                @pl.when(step > 0)
                def _():
                    acc_ref[...] += part
            else:
                acc_ref[...] += part

    @pl.when(step == micros * steps - 1)
    def _():
        out_ref[...] = acc_ref[...].astype(BF)


def wide_grad(lefts, left_block, left_width, rights, right_block, right_width, tile=512):
    micros, rows = len(lefts), lefts[0].shape[0]
    steps = rows // tile

    def spec(m, width, column):
        return pl.BlockSpec(
            (tile, width), lambda i: (jnp.clip(i - m * steps, 0, steps - 1), column)
        )

    return pl.pallas_call(
        functools.partial(wide_grad_kernel, steps, micros),
        name="wide_grad",
        grid=(micros * steps,),
        in_specs=[spec(m, left_width, left_block) for m in range(micros)]
        + [spec(m, right_width, right_block) for m in range(micros)],
        out_specs=whole((left_width, right_width)),
        out_shape=jax.ShapeDtypeStruct((left_width, right_width), BF),
        scratch_shapes=[pltpu.VMEM((left_width, right_width), F32)],
        compiler_params=params(),
        cost_estimate=cost(
            2 * micros * rows * left_width * right_width,
            2 * (micros * rows * (left_width + right_width) + left_width * right_width),
        ),
    )(*lefts, *rights)


def down_grad_kernel(micros, devices, *refs):
    hg_refs, refs = refs[:micros], refs[micros:]
    ga_refs, gb_refs = refs[:micros], refs[micros : 2 * micros]
    out_ref, acc_ref = refs[2 * micros :]
    step = pl.program_id(0)
    g = [jnp.where(step < devices // 2, a[...], b[...]) for a, b in zip(ga_refs, gb_refs)]
    part = dot(jnp.concatenate(g), jnp.concatenate([r[...] for r in hg_refs]), TN)

    @pl.when(step == 0)
    def _():
        acc_ref[...] = part

    @pl.when(step > 0)
    def _():
        acc_ref[...] += part

    @pl.when(step == devices - 1)
    def _():
        out_ref[...] = acc_ref[...].astype(BF)


def down_grad(hgs, expert, hidden, gs, devices):
    micros, rows = len(hgs), hgs[0].shape[0]
    tile, half = rows // devices, devices // 2
    dim = gs[0][0].shape[1]
    return pl.pallas_call(
        functools.partial(down_grad_kernel, micros, devices),
        name="down_grad",
        grid=(devices,),
        in_specs=[pl.BlockSpec((tile, hidden), lambda i: (i, expert))] * micros
        + [pl.BlockSpec((tile, dim), lambda i: (jnp.minimum(i, half - 1), 0))] * micros
        + [pl.BlockSpec((tile, dim), lambda i: (jnp.maximum(i - half, 0), 0))] * micros,
        out_specs=whole((dim, hidden)),
        out_shape=jax.ShapeDtypeStruct((dim, hidden), BF),
        scratch_shapes=[pltpu.VMEM((dim, hidden), F32)],
        compiler_params=params(),
        cost_estimate=cost(2 * micros * rows * hidden * dim, 2 * micros * rows * (hidden + dim)),
    )(*hgs, *[g[0] for g in gs], *[g[1] for g in gs])


def before_kernel(
    steps, place_ref, ret_ref, res_ref, ge_ref, gout_ref, gain_ref, router_ref, wa_ref, wb_ref, gres_ref, ga_ref, gt_ref, small_ref, cut_ref, acc_ref
):
    dim = res_ref.shape[1]

    step = pl.program_id(0)
    tile = dim // steps

    @pl.when(step == 0)
    def _():
        ge = ge_ref[...]
        gg = ret_ref[:, dim:].astype(F32)
        gl = ge * (gg - jnp.sum(ge * gg, axis=-1, keepdims=True))
        high = gl.astype(BF)
        low = (gl - high.astype(F32)).astype(BF)
        router = router_ref[...]
        gn = ret_ref[:, :dim].astype(F32) + (dot(high, router, NT) + dot(low, router, NT))
        residual = res_ref[...]
        gain = gain_ref[...]
        inv = lax.rsqrt(jnp.mean(residual * residual, axis=-1, keepdims=True) + EPS)
        unit = residual * inv
        normed = (unit * gain).astype(BF)
        small_ref[:LANES] = dot(high, normed, TN) + dot(low, normed, TN)
        gain_row = jnp.sum(gn * unit, axis=0, keepdims=True)
        small_ref[LANES:] = jnp.broadcast_to(gain_row, (8, dim))
        u = gn * gain
        gres = gout_ref[...].astype(F32) + inv * (
            u - unit * jnp.mean(u * unit, axis=-1, keepdims=True)
        )
        gres_ref[...] = gres
        low_gres = gres.astype(BF)
        ga_ref[...] = low_gres
        for i in range(steps):
            cut_ref[i] = low_gres[:, i * tile : (i + 1) * tile]
        acc_ref[...] = jnp.zeros_like(acc_ref)

    acc_ref[...] += dot(in_order(place_ref, (wa_ref, wb_ref)), cut_ref[step], NT)

    @pl.when(step == steps - 1)
    def _():
        gt_ref[...] = acc_ref[...].astype(BF)


def before_attention(place, returned, residual, exact, gout, gain, router, w, first):
    tokens, dim = residual.shape
    width = 2 * w[0].shape[0] * w[0].shape[1]
    tile = 512
    steps = dim // tile
    return pl.pallas_call(
        functools.partial(before_kernel, steps),
        name="before_attention",
        grid=(steps,),
        in_specs=[
            smem(),
            whole((tokens, dim + LANES)),
            whole((tokens, dim)),
            whole((tokens, LANES)),
            whole((tokens, dim)),
            whole((1, dim)),
            whole((dim, LANES)),
            *w_columns(w, tile, lambda i: first // tile + i),
        ],
        out_specs=[
            whole((tokens, dim)),
            whole((tokens, dim)),
            whole((width, tokens)),
            whole((LANES + 8, dim)),
        ],
        out_shape=[
            jax.ShapeDtypeStruct((tokens, dim), F32),
            jax.ShapeDtypeStruct((tokens, dim), BF),
            jax.ShapeDtypeStruct((width, tokens), BF),
            jax.ShapeDtypeStruct((LANES + 8, dim), F32),
        ],
        scratch_shapes=[
            pltpu.VMEM((steps, tokens, tile), BF),
            pltpu.VMEM((width, tokens), F32),
        ],
        compiler_params=params(),
        cost_estimate=cost(2 * tokens * width * dim, 2 * width * dim + 14 * tokens * dim),
    )(place, returned, residual, exact, gout, gain, router, *w)


def last_kernel(
    q_steps, steps, place_ref, gq_ref, dkv_ref, qa_ref, qb_ref, kva_ref, kvb_ref, x_ref, gain_ref, gres_ref, din_ref, small_ref, acc_ref
):
    step = pl.program_id(0)

    @pl.when(step == 0)
    def _():
        acc_ref[...] = dot(gq_ref[...], in_order(place_ref, (qa_ref, qb_ref)), NT)

    @pl.when((step > 0) & (step < q_steps))
    def _():
        acc_ref[...] += dot(gq_ref[...], in_order(place_ref, (qa_ref, qb_ref)), NT)

    @pl.when(step >= q_steps)
    def _():
        acc_ref[...] += dot(dkv_ref[...], in_order(place_ref, (kva_ref, kvb_ref)), NT)

    @pl.when(step == steps - 1)
    def _():
        x = x_ref[...].astype(F32)
        gain = gain_ref[...]
        inv = lax.rsqrt(jnp.mean(x * x, axis=-1, keepdims=True) + EPS)
        unit = x * inv
        gn = acc_ref[...]
        small_ref[...] = jnp.broadcast_to(
            jnp.sum(gn * unit, axis=0, keepdims=True), small_ref.shape
        )
        w = gn * gain
        grad = inv * (w - unit * jnp.mean(w * unit, axis=-1, keepdims=True))
        din_ref[...] = (grad + gres_ref[...]).astype(BF)


def last_step(place, gq, dkv, w_q, w_kv, x, micro, gain, gres):
    tokens, dim = gres.shape
    tile = 512
    q_steps, kv_steps = gq.shape[1] // tile, dkv.shape[1] // tile
    steps = q_steps + kv_steps
    q_at = lambda i: (0, jnp.minimum(i, q_steps - 1))
    kv_at = lambda i: (0, jnp.maximum(i - q_steps, 0))
    return pl.pallas_call(
        functools.partial(last_kernel, q_steps, steps),
        name="last_step",
        grid=(steps,),
        in_specs=[
            smem(),
            pl.BlockSpec((tokens, tile), q_at),
            pl.BlockSpec((tokens, tile), kv_at),
            *w_columns(w_q, tile, lambda i: q_at(i)[1]),
            *w_columns(w_kv, tile, lambda i: kv_at(i)[1]),
            pl.BlockSpec((tokens, dim), lambda i: (micro, 0)),
            whole((1, dim)),
            whole((tokens, dim)),
        ],
        out_specs=[whole((tokens, dim)), whole((8, dim))],
        out_shape=[
            jax.ShapeDtypeStruct((tokens, dim), BF),
            jax.ShapeDtypeStruct((8, dim), F32),
        ],
        scratch_shapes=[pltpu.VMEM((tokens, dim), F32)],
        compiler_params=params(),
        cost_estimate=cost(
            2 * tokens * steps * tile * dim, 2 * steps * tile * dim + 12 * tokens * dim
        ),
    )(place, gq, dkv, *w_q, *w_kv, x, gain, gres)


def out_grad_kernel(micros, half, order_ref, *refs):
    t_refs, g_refs, (first_ref, second_ref) = refs[:micros], refs[micros : 2 * micros], refs[2 * micros :]
    step = pl.program_id(0)
    total = dot(t_refs[0][...], g_refs[0][...])
    for t_ref, g_ref in zip(t_refs[1:], g_refs[1:]):
        total += dot(t_ref[...], g_ref[...])

    @pl.when(step < half)
    def _():
        first_ref[...] = total.astype(BF)

    @pl.when(step >= half)
    def _():
        second_ref[...] = total.astype(BF)


def out_grad(order, heads_t, grads):
    micros, devices = len(heads_t), order.shape[0]
    width, tokens = heads_t[0].shape
    dim = grads[0].shape[1]
    tile, half = width // devices, devices // 2
    return pl.pallas_call(
        functools.partial(out_grad_kernel, micros, half),
        name="out_grad",
        grid_spec=pltpu.PrefetchScalarGridSpec(
            num_scalar_prefetch=1,
            grid=(devices,),
            in_specs=[pl.BlockSpec((tile, tokens), lambda i, order: (order[i], 0))] * micros
            + [whole((tokens, dim))] * micros,
            out_specs=[
                pl.BlockSpec((tile, dim), lambda i, order: (jnp.minimum(i, half - 1), 0)),
                pl.BlockSpec((tile, dim), lambda i, order: (jnp.maximum(i - half, 0), 0)),
            ],
        ),
        out_shape=[jax.ShapeDtypeStruct((width // 2, dim), BF)] * 2,
        compiler_params=params(),
        cost_estimate=cost(2 * micros * tokens * width * dim, 4 * width * dim),
    )(order, *heads_t, *grads)


def turn_kernel(kv_ref, cos_ref, sin_ref, out_ref):
    width = kv_ref.shape[2]
    key = rotate(kv_ref[0].astype(F32).T, cos_ref[...], sin_ref[...], -1)
    out_ref[:, :width] = key.T.astype(BF)
    out_ref[:, width:] = kv_ref[1]


def turn_back(kv, cosine, sine):
    _, tokens, width = kv.shape
    return pl.pallas_call(
        turn_kernel,
        name="turn_back",
        out_shape=jax.ShapeDtypeStruct((tokens, 2 * width), BF),
        compiler_params=params(),
        cost_estimate=cost(0, 8 * tokens * width),
    )(kv, cosine, sine)


def projection_kernel(micros, q_steps, steps, n_experts, normed_ref, *refs):
    gq_refs, refs = refs[:micros], refs[micros:]
    dkv_refs, refs = refs[:micros], refs[micros:]
    two_refs, refs = refs[:micros], refs[micros:]
    one_refs, (out_ref, turned_ref) = refs[:micros], refs[micros:]
    step = pl.program_id(0)
    tile = gq_refs[0].shape[1]

    @pl.when(step == 0)
    def _():
        turned_ref[...] = normed_ref[...].astype(F32).T.astype(BF)
        rows = functools.reduce(jnp.add, [r[:LANES] for r in two_refs])
        gain_two = functools.reduce(jnp.add, [r[LANES : LANES + 1] for r in two_refs])
        gain_one = functools.reduce(jnp.add, [r[:1] for r in one_refs])
        at = lax.broadcasted_iota(jnp.int32, rows.shape, 0)
        rows = jnp.where(at == n_experts, gain_one, rows)
        rows = jnp.where(at == n_experts + 1, gain_two, rows)
        out_ref[:, steps * tile :] = rows.T.astype(BF)

    q = jnp.concatenate([r[...] for r in gq_refs], axis=0)
    kv = jnp.concatenate([r[...] for r in dkv_refs], axis=0)
    g = jnp.where(step < q_steps, q, kv)
    out_ref[:, pl.ds(pl.multiple_of(step * tile, tile), tile)] = dot(turned_ref[...], g).astype(BF)


def projection_grads(normed, gqs, dkvs, twos, ones, n_experts):
    rows, dim = normed.shape
    micros, tokens, tile = len(gqs), gqs[0].shape[0], 512
    q_steps, kv_steps = gqs[0].shape[1] // tile, dkvs[0].shape[1] // tile
    steps = q_steps + kv_steps
    width = steps * tile + LANES
    return pl.pallas_call(
        functools.partial(projection_kernel, micros, q_steps, steps, n_experts),
        name="projection_grads",
        grid=(steps,),
        in_specs=[whole((rows, dim))]
        + [pl.BlockSpec((tokens, tile), lambda i: (0, jnp.minimum(i, q_steps - 1)))] * micros
        + [pl.BlockSpec((tokens, tile), lambda i: (0, jnp.maximum(i - q_steps, 0)))] * micros
        + [whole(twos[0].shape)] * micros
        + [whole(ones[0].shape)] * micros,
        out_specs=whole((dim, width)),
        out_shape=jax.ShapeDtypeStruct((dim, width), BF),
        scratch_shapes=[pltpu.VMEM((dim, rows), BF)],
        compiler_params=params(),
        cost_estimate=cost(2 * rows * dim * width, 2 * rows * (dim + width) + 2 * dim * width),
    )(normed, *gqs, *dkvs, *twos, *ones)


def add_low(a, b):
    return (a.astype(F32) + b.astype(F32)).astype(BF)


def line_sum(x, n):
    if n == 1:
        return x
    if n % 2:
        return lax.psum(x, "seq")
    half = n // 2
    at = lax.axis_index("seq")
    for k in range(half - 1):
        x = add_low(x, lax.ppermute(x, "seq", [(k, k + 1), (n - 1 - k, n - 2 - k)]))
    x = add_low(x, lax.ppermute(x, "seq", [(half - 1, half), (half, half - 1)]))
    for k in reversed(range(half - 1)):
        got = lax.ppermute(x, "seq", [(k + 1, k), (n - 2 - k, n - 1 - k)])
        x = jnp.where((at == k) | (at == n - 1 - k), got, x)
    return x


class Line:
    def __init__(self, n):
        self.n = n
        self.held = {}
        self.results = []

    def sums(self):
        at = lax.axis_index("seq")
        middle = (at == 1) | (at == 2)
        return [r[0] if len(r) == 1 else jnp.where(middle, *r) for r in self.results]

    def step(self, chunk, beside):
        n = self.n
        if n != 4:
            if chunk is not None:
                self.results.append((line_sum(chunk, n),))
            return
        at = lax.axis_index("seq")
        middle = (at == 1) | (at == 2)
        come, go = [(0, 1), (3, 2)], [(1, 0), (2, 3)]
        held, self.held = self.held, {}
        summed = held.get("summed")
        if summed is not None:
            summed = add_low(*summed)
        crossing = held.get("crossing")
        if crossing is not None:
            crossing = add_low(*crossing)
            self.held["summed"] = (crossing, lax.ppermute(crossing, "seq", [(1, 2), (2, 1)]))
        if chunk is not None and summed is not None and chunk.shape == summed.shape:
            sent = jnp.where(middle, summed, chunk)
            got = lax.ppermute(sent, "seq", come + go)
            self.results.append((sent, got))
            self.held["crossing"] = (chunk, got)
        else:
            if summed is not None:
                self.results.append((summed, lax.ppermute(summed, "seq", go)))
            if chunk is not None:
                self.held["crossing"] = (chunk, lax.ppermute(chunk, "seq", come))
        self.held, self.results = gate((self.held, self.results), beside)


def gate(x, *others):
    return lax.optimization_barrier((x, others))[0]


CORE, ALONG_X, ALONG_Y = 1, 2, 4


def swap(x, mask):
    return lax.ppermute(x, "fsdp", [(i, i ^ mask) for i in range(8)])


def gather_rows(x):
    return lax.all_gather(x, "fsdp", axis=0, tiled=True)


def assemble_kernel(x_ref, top_x_ref, low_y_ref, top_far_ref, low_far_ref, out_ref):
    rows = x_ref.shape[0]
    half = rows // 2
    out_ref[:rows] = x_ref[...]
    out_ref[rows : rows + half] = top_x_ref[...]
    out_ref[rows + half : 2 * rows] = low_far_ref[:half]
    out_ref[2 * rows : 2 * rows + half] = top_far_ref[:half]
    out_ref[2 * rows + half : 3 * rows] = low_y_ref[...]
    out_ref[3 * rows : 3 * rows + half] = top_far_ref[half:]
    out_ref[3 * rows + half :] = low_far_ref[half:]


def assemble(*pieces):
    rows, width = pieces[0].shape
    block = lambda n: pl.BlockSpec((n, width // 3), lambda i: (0, i))
    return pl.pallas_call(
        assemble_kernel,
        name="assemble",
        grid=(3,),
        in_specs=[block(p.shape[0]) for p in pieces],
        out_specs=block(4 * rows),
        out_shape=jax.ShapeDtypeStruct((4 * rows, width), pieces[0].dtype),
        compiler_params=params(),
        cost_estimate=cost(0, 16 * rows * width),
    )(*pieces)


def gather_near(x, n):
    if n != 8:
        every = gather_rows(x)
        half = every.shape[0] // 2
        return every[:half], every[half:]
    gather = Gather(x, n)
    gather.further()
    return gather.finish()


class Gather:
    def __init__(self, x, n):
        self.n, self.x = n, x
        if n != 8:
            self.halves = gather_near(x, n)
            self.near = self.far = ()
            return
        half = x.shape[0] // 2
        self.near = swap(x[:half], ALONG_X), swap(x[half:], ALONG_Y)

    def further(self, *others):
        if self.n != 8:
            return
        half = self.x.shape[0] // 2
        x, (top_x, low_y) = gate((self.x, self.near), *others)
        self.near = top_x, low_y
        top_far = swap(jnp.concatenate([x[:half], top_x]), ALONG_Y)
        low_far = swap(jnp.concatenate([x[half:], low_y]), ALONG_X)
        self.far = top_far, low_far

    def finish(self, *others):
        if self.n != 8:
            return self.halves
        near, far = gate((self.near, self.far), *others)
        mine = assemble(self.x, *near, *far)
        return mine, swap(mine, CORE)


class Scatter:
    def __init__(self, arrays, n):
        self.arrays, self.n, self.stage = list(arrays), n, 0
        self.rows = 2 * arrays[0][0].shape[0] // n

    def advance(self):
        held, self.stage = self.arrays, self.stage + 1
        rows, half = self.rows, self.rows // 2
        if self.n != 8:
            if self.stage == 1:
                self.arrays = [scatter_rows(jnp.concatenate(a)) for a in held]
            return
        if self.stage == 1:
            self.arrays = [add_low(mine, swap(other, CORE)) for mine, other in held]
        if self.stage == 2:
            tops = [a[k * rows : k * rows + half] for a in held for k in (2, 3)]
            lows = [a[k * rows + half : (k + 1) * rows] for a in held for k in (1, 3)]
            tops = swap(jnp.concatenate(tops), ALONG_Y)
            lows = swap(jnp.concatenate(lows), ALONG_X)
            self.arrays = []
            for i, a in enumerate(held):
                at = 2 * i * half
                self.arrays.append(
                    (
                        add_low(a[:half], tops[at : at + half]),
                        add_low(a[half:rows], lows[at : at + half]),
                        add_low(a[rows : rows + half], tops[at + half : at + rows]),
                        add_low(a[2 * rows + half : 3 * rows], lows[at + half : at + rows]),
                    )
                )
        if self.stage == 3:
            over_x = swap(jnp.concatenate([a[2] for a in held]), ALONG_X)
            over_y = swap(jnp.concatenate([a[3] for a in held]), ALONG_Y)
            self.arrays = [
                jnp.concatenate(
                    [
                        add_low(a[0], over_x[i * half : (i + 1) * half]),
                        add_low(a[1], over_y[i * half : (i + 1) * half]),
                    ]
                )
                for i, a in enumerate(held)
            ]


def block_order(n):
    at = jnp.arange(n, dtype=jnp.int32)
    if n != 8:
        return at
    return lax.axis_index("fsdp").astype(jnp.int32) ^ (2 * lax.rem(at, 4) + at // 4)


def block_places(n):
    if n != 8:
        return jnp.arange(n, dtype=jnp.int32)
    mask = lax.axis_index("fsdp").astype(jnp.int32) ^ jnp.arange(n, dtype=jnp.int32)
    return (mask >> 1) + 4 * (mask & 1)


def scatter_rows(x):
    return lax.psum_scatter(x, "fsdp", scatter_dimension=0, tiled=True)


def on_device(
    n_seq,
    n_fsdp,
    inputs,
    lengths,
    expert_ids,
    cotangent,
    gain_attn,
    w_query,
    key_projection,
    value_projection,
    w_out,
    gain_moe,
    router,
    w_gate,
    w_up,
    w_down,
):
    micros, local_seqs, tokens, dim = inputs.shape
    assert local_seqs == 1
    rows = micros * tokens
    experts, _, hidden = w_gate.shape
    n_experts = router.shape[1]
    kv_width = key_projection.shape[1]
    at = lax.axis_index("seq")
    own = (lax.axis_index("fsdp") * experts).astype(jnp.int32).reshape(1)

    small = jnp.concatenate(
        [router, gain_attn[:, None], gain_moe[:, None]], axis=1
    )
    small = jnp.pad(small, ((0, 0), (0, LANES - small.shape[1])))
    place, order = block_places(n_fsdp), block_order(n_fsdp)

    def weights(w):
        return [h.reshape(n_fsdp // 2, -1, h.shape[1]) for h in gather_near(w, n_fsdp)]

    w_kv = weights(jnp.concatenate([key_projection, value_projection, small], axis=1))
    router_all, rows_all = unpack(place, w_kv, 2 * kv_width // LANES, n_experts)
    gain_one = rows_all[n_experts : n_experts + 1]
    gain_two = rows_all[n_experts + 1 : n_experts + 2]

    positions = at * tokens + jnp.arange(tokens, dtype=jnp.int32)
    frequency = THETA ** (-(jnp.arange(HALF, dtype=F32) * 2.0) / HEAD)
    angles = frequency[:, None] * positions.astype(F32)[None, :]
    cosine, sine = jnp.cos(angles), jnp.sin(angles)
    cosine_all, sine_all = jnp.tile(cosine, (1, micros)), jnp.tile(sine, (1, micros))

    x = inputs.reshape(rows, dim)
    chosen = jnp.sum(
        (
            expert_ids.reshape(rows, TOPK)[:, :, None]
            == jnp.arange(LANES, dtype=jnp.int32)[None, None, :]
        ).astype(F32),
        axis=1,
    )
    valid = positions[None, :] < lengths[:, :1]
    gout = jnp.where(valid[:, :, None], cotangent.reshape(micros, tokens, dim), BF(0))
    infos = [
        jnp.stack([at.astype(jnp.int32), lengths[m, 0].astype(jnp.int32)]) for m in range(micros)
    ]

    kv, normed_one = kv_project(place, x, gain_one, w_kv, kv_width, cosine_all, sine_all)
    q_width = w_query.shape[1]
    w_gather = Gather(gate(jnp.concatenate([w_query, w_out], axis=1), kv), n_fsdp)
    w_gather.further()
    kvs = []
    for m in range(micros):
        mine = kv[m * tokens : (m + 1) * tokens]
        every = lax.all_gather(mine, "seq", axis=0, tiled=True)
        kvs.append(every.reshape(n_seq, tokens, 2 * kv_width))
    w_qo = [h.reshape(n_fsdp // 2, -1, h.shape[1]) for h in w_gather.finish(kvs[0], chosen, infos)]
    g_gathers = [Gather(gate(gout[0], w_gather.far), n_fsdp)]
    for m in range(1, micros):
        g_gathers.append(Gather(gate(gout[m], g_gathers[-1].near), n_fsdp))
    q_t = q_project(
        place, gate(normed_one, kvs[0]), w_qo, q_width, cosine_all, sine_all
    )

    state, xg_all = [], []
    for m in range(micros):
        if m == 0:
            info = gate(infos[m], g_gathers[0].near)
            g_gathers[0].further(q_t)
        else:
            info = gate(infos[m], state[-1][2])
        attn, attn_t, lse = attend(info, q_t, kvs[m], m, tokens)
        if m == 0:
            attn = gate(attn, g_gathers[0].far, [g.near for g in g_gathers[1:]])
            for g in g_gathers[1:]:
                g.further(g_gathers[0].far)
        else:
            attn = gate(attn, g_gathers[m].far)
        residual, xg, exact = after_attention(
            place, attn, w_qo, q_width, x, m, gain_two, router_all, chosen
        )
        state.append((attn_t, lse, residual, exact))
        xg_all.append(gather_rows(xg))

    g_all = [g.finish(state[-1][2]) for g in g_gathers]
    xg_all[0] = gate(xg_all[0], state[-1][2], g_all)
    passed, backs = [], []
    for m in range(micros):
        *y, back, hg, gp = run_experts(
            own, order, xg_all[m], g_all[m], w_gate, w_up, w_down
        )
        passed.append((xg_all[m], hg, gp))
        backs.append((scatter_rows(back), y))

    names = [(name, e) for name in ("down", "gate", "up") for e in range(experts)]

    def expert_grad(name, e, got):
        xs, hgs, gps = ([p[i] for p in got] for i in range(3))
        if name == "down":
            return down_grad(hgs, e, hidden, g_all, n_fsdp)
        return wide_grad(xs, 0, dim, gps, 2 * e + (name == "up"), hidden)

    line = Line(n_seq)
    found = [{} for _ in range(micros)]

    def to_heads(m):
        attn_t, lse, residual, exact = state[m]
        gres, g_attn, g_t, small_two = before_attention(
            place, backs[m][0], residual, exact, gout[m], gain_two, router_all, w_qo, q_width
        )
        found[m].update(gres=gres, g_attn=g_attn, g_t=g_t, small_two=small_two)

    def through_heads(m):
        attn_t, lse = state[m][:2]
        gq, by_owner = attend_back(
            infos[m], q_t, found[m]["g_t"], attn_t, lse, cosine, sine, kvs[m], m, tokens
        )
        found[m].update(gq=gq, by_owner=by_owner)

    owned = {}

    def to_owners(m):
        by_owner = found[m].pop("by_owner")
        shape = by_owner.shape
        owned[m] = lax.psum_scatter(
            by_owner.reshape(n_seq * shape[1] * tokens, shape[3]),
            "seq",
            scatter_dimension=0,
            tiled=True,
        ).reshape(shape[1:])

    def finish(m):
        f = found[m]
        f["dkv"] = turn_back(f["mine"], cosine, sine)
        f["din"], f["small_one"] = last_step(
            place, f["gq"], f["dkv"], w_qo, w_kv, x, m, gain_one, f["gres"]
        )

    def rest_grads():
        every = lambda name: [f[name] for f in found]
        return projection_grads(
            normed_one, every("gq"), every("dkv"), every("small_two"), every("small_one"), n_experts
        )

    n_grads = len(names)
    work = {
        0: [("grad", 1), (to_heads, 0), (through_heads, 0)],
        1: [("grad", 2), ("grad", 3)],
        2: [(to_heads, 1), (through_heads, 1)],
        3: [("grad", 4), (finish, 0), ("grad", 5)],
        4: [(finish, 1)],
    }
    def widen(parts, turned):
        return jnp.stack([(p.T if turned else p).astype(F32) for p in parts])

    experts_out = []
    chunks = {0: expert_grad(*names[0], passed)}
    chunks.update({i: expert_grad(*names[i], passed) for i in range(6, n_grads)})
    slots = max(n_grads, 6)
    moe = Scatter([b[1] for b in backs], n_fsdp)
    for t in range(slots + 3):
        if t in (3, 4):
            found[t - 3]["mine"] = owned[t - 3]
        if t == 3:
            heads = Scatter([found[0].pop("out")], n_fsdp)
        if t == 7:
            found[0]["rest"] = rest
        held = (chunks, line.held, line.results, passed, found, moe.arrays)
        if t >= 3:
            *held, heads.arrays = lax.optimization_barrier((*held, heads.arrays))
        else:
            held = lax.optimization_barrier(held)
        chunks, line.held, line.results, passed, found, moe.arrays = held
        if t == 7:
            rest = lax.psum(found[0].pop("rest"), "seq")
        if len(line.results) in (experts, 2 * experts, 3 * experts) and len(experts_out) < 3:
            pair = line.sums()[-experts:]
            experts_out.append(widen(pair, len(experts_out) == 0))
            found[1]["wide"] = experts_out[-1]
        if t == slots:
            chunks[slots] = heads.arrays[0]
        sent = chunks.pop(t, None)
        if t in (1, 3):
            to_owners(t // 2)
        for kind, i in work.get(t, []):
            if kind != "grad":
                kind(i)
            elif i < n_grads:
                chunks[i] = expert_grad(*names[i], passed)
        if t == 2:
            found[0]["out"] = out_grad(
                order, [st[0] for st in state], [f["g_attn"] for f in found]
            )
        if t in (5, 6, 7):
            moe.advance()
        for _ in range(3 if t == 3 else 0):
            heads.advance()
        line.step(sent, (chunks, found))
        if t == 4:
            normed_one, line.held = lax.optimization_barrier((normed_one, line.held))
            rest = scatter_rows(rest_grads())
    rest = rest.astype(F32)
    totals = line.sums()
    for i in range(len(experts_out), 3):
        experts_out.append(widen(totals[i * experts : (i + 1) * experts], i == 0))
    d_out = totals[n_grads].astype(F32)

    outs = []
    for m in range(micros):
        outs.append(
            jnp.where(valid[m][:, None], state[m][2] + moe.arrays[m].astype(F32), 0.0).astype(BF)
        )
    grads = [f["din"] for f in found]
    assert len(totals) == n_grads + 1
    shape = (micros, 1, tokens, dim)
    ends = q_width + 2 * kv_width
    return (
        jnp.stack(outs).reshape(shape),
        jnp.stack(grads).reshape(shape),
        rest[:, ends + n_experts],
        rest[:, :q_width],
        rest[:, q_width : q_width + kv_width],
        rest[:, q_width + kv_width : ends],
        d_out,
        rest[:, ends + n_experts + 1],
        rest[:, ends : ends + n_experts],
        *experts_out[1:],
        experts_out[0],
    )


def solution(mesh):
    token_spec = P(None, "fsdp", "seq", None)
    row, matrix, cube = P("fsdp"), P("fsdp", None), P("fsdp", None, None)
    return jax.shard_map(
        functools.partial(on_device, mesh.shape["seq"], mesh.shape["fsdp"]),
        mesh=mesh,
        in_specs=(
            token_spec,
            P(None, "fsdp"),
            token_spec,
            token_spec,
            row,
            matrix,
            matrix,
            matrix,
            matrix,
            row,
            matrix,
            cube,
            cube,
            cube,
        ),
        out_specs=(
            token_spec,
            token_spec,
            row,
            matrix,
            matrix,
            matrix,
            matrix,
            row,
            matrix,
            cube,
            cube,
            cube,
        ),
        check_vma=False,
    )
```
